32 devices in a mesh: seq: 8 (over z, x), mp: 4 (over y, core).
Axes of the slice: x: 2, y: 2, z: 4, core: 2. Of those that a mesh axis runs over, the one named last changes fastest.
Arguments:
- frames: bfloat16 [8, 1024, 1024], P('mp', 'seq'), may hold values from -6 to 6
- segments: int32 [8, 1024], P('mp', 'seq'), may hold values from 0 to 7, never falling along the last dimension, each value on 1 to 896 neighbouring positions
- padding: int32 [8, 1024], P('mp', 'seq'), may hold values from 0 to 1, as said below
- codec_tokens: int32 [2, 8, 1024], P(None, 'mp', 'seq'), may hold values from 0 to 1023
- codebooks: bfloat16 [2048, 1024], P('mp'), may hold values from -6 to 6
- frame_prenorm: bfloat16 [1024], P('mp'), may hold values from 0.099609375 to 1.8984375
- frame_project: bfloat16 [1024, 3072], P('mp'), may hold values from -0.1875 to 0.1875
- frame_output: bfloat16 [1024, 1024], P('mp'), may hold values from -1.5 to 1.5
- frame_postnorm: bfloat16 [1024], P('mp'), may hold values from 0.099609375 to 1.8984375
- frame_expand: bfloat16 [1024, 4096], P('mp'), may hold values from -0.1875 to 0.1875
- frame_contract: bfloat16 [4096, 1024], P('mp'), may hold values from -0.09375 to 0.09375
- codec_prenorm: bfloat16 [1024], P('mp'), may hold values from 0.099609375 to 1.8984375
- codec_project: bfloat16 [1024, 3072], P('mp'), may hold values from -0.9375 to 0.9375
- codec_output: bfloat16 [1024, 1024], P('mp'), may hold values from -0.0546875 to 0.0546875
- codec_postnorm: bfloat16 [1024], P('mp'), may hold values from 0.099609375 to 1.8984375
- codec_expand: bfloat16 [1024, 4096], P('mp'), may hold values from -0.1875 to 0.1875
- codec_contract: bfloat16 [4096, 1024], P('mp'), may hold values from -0.09375 to 0.09375
- cotangent: bfloat16 [8, 1024, 3, 1024], P('mp', 'seq'), may hold values from -6 to 6
Outputs:
- output: bfloat16 [8, 1024, 3, 1024], P('mp', 'seq')
- frames_grad: float32 [8, 1024, 1024], P('mp', 'seq')
- codebooks_grad: float32 [2048, 1024], P('mp', 'seq')
- frame_prenorm_grad: float32 [1024], replicated
- frame_project_grad: float32 [1024, 3072], P('mp', 'seq')
- frame_output_grad: float32 [1024, 1024], P('mp', 'seq')
- frame_postnorm_grad: float32 [1024], replicated
- frame_expand_grad: float32 [1024, 4096], P('mp', 'seq')
- frame_contract_grad: float32 [4096, 1024], P('mp', 'seq')
- codec_prenorm_grad: float32 [1024], replicated
- codec_project_grad: float32 [1024, 3072], P('mp', 'seq')
- codec_output_grad: float32 [1024, 1024], P('mp', 'seq')
- codec_postnorm_grad: float32 [1024], replicated
- codec_expand_grad: float32 [1024, 4096], P('mp', 'seq')
- codec_contract_grad: float32 [4096, 1024], P('mp', 'seq')
The draws below stay inside these ranges and needn't reach their ends.
Inputs may be any that keep to these rules, and one draw needn't show every extreme that they name: `segments`: within a row segment numbers never fall; each segment covers at most 896 frames, and one exactly that many. In each row padding is 1 on the frames before the row's live length and 0 after it; live lengths lie between 512 and 1024, and the first row has no padding.
All inputs are finite; a program needn't handle non-finite values.
Results may differ from the reference program's by a relative error of at most 0.018.
Values may be sent and summed in bfloat16 or wider, within the bound.
No kernel may reach another device: no remote copies, remote signals or barrier semaphores. Data moves between devices by JAX's collectives and lax.ppermute only.
A program may use at most 384 MiB of HBM per device.

```python
import math
import jax
import jax.numpy as jnp
import numpy as np
from jax import lax

D = 1024
HEADS = 16
HEAD = 64
FF = 4096
CODES = 1024
POS = 3
LEN = 1024
ROWS = 8


def draw_padding(key, part):
    live_len = jax.random.randint(key, (ROWS,), LEN // 2, LEN + 1)
    live_len = jnp.where(jnp.arange(ROWS) == 0, LEN, live_len)
    positions = jnp.arange(LEN)
    return (positions[None, :] < live_len[:, None]).astype(jnp.int32)


def draw_codec_project(key, part):
    base = jnp.clip(jax.random.normal(key, (D, 3 * D), jnp.float32), -6.0, 6.0) * D ** (-0.5)
    column = jnp.arange(3 * D)
    return jnp.where(column[None, :] >= 2 * D, 5.0 * base, base).astype(jnp.bfloat16)


def set_ends(drawn, rng, smallest, top_value):
    longest = drawn.shape.index(max(drawn.shape))
    spots = []
    for shift in (0, 1):
        where = [jax.random.randint(jax.random.fold_in(rng, axis), (), 0, length) for axis, length in enumerate(drawn.shape)]
        where[longest] = (where[longest] + shift) % drawn.shape[longest]
        spots.append(tuple(where))
    return drawn.at[spots[0]].set(smallest).at[spots[1]].set(top_value)


def block_levels(rng, dims, shards, low, largest):
    factor_of, own = 1.0, jax.random.fold_in(rng, 6)
    for axis_at, parts in shards:
        heights = jnp.exp(jax.random.uniform(jax.random.fold_in(own, axis_at), (parts,), jnp.float32, low / len(shards), largest / len(shards)))
        factor_of = factor_of * jnp.repeat(heights, dims[axis_at] // parts).reshape([-1 if axis == axis_at else 1 for axis in range(len(dims))])
    return factor_of


def profile(number_of, total, limit, lean):
    weights = [(1 << 20) // math.isqrt(standing ** lean) + 1 for standing in range(2, number_of + 1)]
    rest, counts = total - limit - (number_of - 1), [1] * (number_of - 1)
    while rest > 0:
        movable = [i for i in range(number_of - 1) if counts[i] < limit]
        mass, budget = sum([weights[i] for i in movable]), rest
        for i in movable:
            addition = min(limit - counts[i], max(1, budget * weights[i] // mass), rest)
            counts[i] = counts[i] + addition
            rest = rest - addition
    return np.array([limit] + counts)


def uneven(rng, amount, total, bound, slope):
    if amount == 2:
        one = jax.random.randint(rng, (), max(1, total - bound), min(bound, total - 1) + 1)
        return jnp.stack([one, total - one])
    sizes = jnp.asarray(profile(amount, total, bound, slope), jnp.int32)
    twos = (amount - 1) // 2
    source_of, taker = sizes[1:1 + 2 * twos:2], sizes[2:2 + 2 * twos:2]
    margin = jnp.minimum(source_of - 1, bound - taker)
    moved = jax.random.randint(jax.random.fold_in(rng, 1), (twos,), 0, 1 << 20) % (margin + 1)
    sizes = sizes.at[1:1 + 2 * twos:2].set(source_of - moved).at[2:2 + 2 * twos:2].set(taker + moved)
    return sizes[jax.random.permutation(jax.random.fold_in(rng, 2), amount)]


def gaussian(key, shape, scale, limit, cuts=(), kind=jnp.bfloat16):
    drawn = scale * jax.random.normal(key, shape, jnp.float32)
    if cuts:
        drawn = drawn * block_levels(key, shape, cuts, -0.22, 0.18)
    return jnp.clip(drawn, -limit, limit).astype(kind)


def setup_inputs(seed: int = 0) -> dict:
    streams_of = jax.random.split(jax.random.key(seed), 19)
    frames = gaussian(streams_of[0], (ROWS, LEN, D), 1.0, 6.0, ((0, 4), (1, 8)))
    segments = jax.vmap(lambda own: jnp.searchsorted(jnp.cumsum(uneven(own, 8, LEN, LEN - LEN // 8, 2)), jnp.arange(LEN), side="right"))(jax.random.split(streams_of[1], ROWS)).reshape((ROWS, LEN)).astype(jnp.int32)
    padding = draw_padding(jax.random.fold_in(streams_of[18], 71), 0)
    codec_tokens = set_ends(jax.random.randint(streams_of[3], (POS - 1, ROWS, LEN), 0, CODES), jax.random.fold_in(streams_of[3], 1), 0, CODES - 1).astype(jnp.int32)
    codebooks = gaussian(streams_of[4], ((POS - 1) * CODES, D), 1.0, 6.0, ((0, 4),))
    frame_prenorm = jnp.clip(1.0 + 0.18 * jax.random.normal(streams_of[5], (D,), jnp.float32), 0.099609375, 1.8984375).astype(jnp.bfloat16)
    frame_project = gaussian(streams_of[6], (D, 3 * D), D ** -0.5, 0.1875, ((0, 4),))
    frame_output = gaussian(streams_of[7], (D, D), (D // 64) ** -0.5, 1.5, ((0, 4),))
    frame_postnorm = jnp.clip(1.0 + 0.18 * jax.random.normal(streams_of[8], (D,), jnp.float32), 0.099609375, 1.8984375).astype(jnp.bfloat16)
    frame_expand = gaussian(streams_of[9], (D, FF), D ** -0.5, 0.1875, ((0, 4),))
    frame_contract = gaussian(streams_of[10], (FF, D), FF ** -0.5, 0.09375, ((0, 4),))
    codec_prenorm = jnp.clip(1.0 + 0.18 * jax.random.normal(streams_of[11], (D,), jnp.float32), 0.099609375, 1.8984375).astype(jnp.bfloat16)
    codec_project = draw_codec_project(jax.random.fold_in(streams_of[18], 71), 0)
    codec_output = gaussian(streams_of[13], (D, D), (25 * D // 2) ** -0.5, 0.0546875, ((0, 4),))
    codec_postnorm = jnp.clip(1.0 + 0.18 * jax.random.normal(streams_of[14], (D,), jnp.float32), 0.099609375, 1.8984375).astype(jnp.bfloat16)
    codec_expand = gaussian(streams_of[15], (D, FF), D ** -0.5, 0.1875, ((0, 4),))
    codec_contract = gaussian(streams_of[16], (FF, D), FF ** -0.5, 0.09375, ((0, 4),))
    cotangent = gaussian(streams_of[17], (ROWS, LEN, POS, D), 1.0, 6.0, ((0, 4), (1, 8)))
    return dict(frames=frames, segments=segments, padding=padding, codec_tokens=codec_tokens, codebooks=codebooks, frame_prenorm=frame_prenorm, frame_project=frame_project, frame_output=frame_output, frame_postnorm=frame_postnorm, frame_expand=frame_expand, frame_contract=frame_contract, codec_prenorm=codec_prenorm, codec_project=codec_project, codec_output=codec_output, codec_postnorm=codec_postnorm, codec_expand=codec_expand, codec_contract=codec_contract, cotangent=cotangent)


EPSILON = 1e-05
MASKED = -1e+30
PRECISE = lax.Precision.HIGHEST

@jax.custom_vjp
def low(v):
    return lax.optimization_barrier(v.astype(jnp.bfloat16)).astype(jnp.float32)

@jax.custom_vjp
def low_back(v):
    return v

def low_keep(v):
    return (low(v), None)

def low_pass(kept, grad):
    return (grad,)

def back_keep(v):
    return (v, None)

def back_low(kept, grad):
    return (low(grad),)
low.defvjp(low_keep, low_pass)
low_back.defvjp(back_keep, back_low)

def rms_scale(values, gain_vec):
    return values * lax.rsqrt(lax.optimization_barrier(jnp.mean(values * values, axis=-1, keepdims=True)) + EPSILON) * gain_vec

def matmul(former, latter):
    return jnp.dot(former, latter, precision=PRECISE, preferred_element_type=jnp.float32)

def block(hidden, weights, attend):
    prenorm, project, output, postnorm, expand, contract = weights
    layout = hidden.shape
    flat = hidden.reshape(-1, D)
    normed = low(rms_scale(flat, prenorm))
    projected = low(low_back(matmul(normed, project)))
    attended = attend(projected.reshape(layout[:-1] + (3 * D,)))
    attended = low(low_back(attended.reshape(-1, D)))
    mixed = flat + low_back(matmul(attended, output))
    normed_two = low(rms_scale(mixed, postnorm))
    activated = low(jax.nn.gelu(low_back(matmul(normed_two, expand))))
    result = mixed + low_back(matmul(activated, contract))
    return result.reshape(layout)

def frame_row(row_items):
    projected, segment = row_items
    split_view = projected.reshape(LEN, 3, HEADS, HEAD)
    factor = HEAD ** (-0.5)
    scores = low_back(jnp.einsum('ihd,jhd->hij', split_view[:, 0], split_view[:, 1], precision=PRECISE) * factor)
    position = jnp.arange(LEN)
    allowed = (segment[:, None] == segment[None, :]) & (position[None, :] <= position[:, None])
    portions = jax.nn.softmax(jnp.where(allowed[None], scores, MASKED), axis=-1)
    attended = jnp.einsum('hij,jhd->ihd', low(portions), split_view[:, 2], precision=PRECISE)
    return attended.reshape(LEN, D)

def codec_attend(projected):
    split_view = projected.reshape(projected.shape[:-1] + (3, HEADS, HEAD))
    queries = split_view[:, :, :, 0]
    keys = split_view[:, :, :, 1]
    values = split_view[:, :, :, 2]
    factor = HEAD ** (-0.5)
    scores = low_back(jnp.einsum('rtihd,rtjhd->rthij', queries, keys, precision=PRECISE) * factor)
    position = jnp.arange(POS)
    causal = position[:, None] >= position[None, :]
    portions = jax.nn.softmax(jnp.where(causal, scores, MASKED), axis=-1)
    attended = jnp.einsum('rthij,rtjhd->rtihd', low(portions), values, precision=PRECISE)
    return attended.reshape(projected.shape[:-1] + (D,))

def forward(frames_wide, table_wide, frame_weights, codec_weights, segments, codec_tokens, padding):

    def frame_attend(projected):
        return lax.map(jax.checkpoint(frame_row), (projected, segments))
    global_out = block(frames_wide, frame_weights, frame_attend)
    frame_base = low(low_back(global_out))
    table_rows = codec_tokens + (jnp.arange(POS - 1, dtype=jnp.int32) * CODES)[:, None, None]
    embedded = table_wide[table_rows]
    local_in = jnp.concatenate([frame_base[:, :, None, :], frame_base[:, :, None, :] + jnp.moveaxis(embedded, 0, 2)], axis=2)
    result = block(local_in, codec_weights, codec_attend)
    return result * padding[:, :, None, None].astype(jnp.float32)

def reference(frames, segments, padding, codec_tokens, codebooks, frame_prenorm, frame_project, frame_output, frame_postnorm, frame_expand, frame_contract, codec_prenorm, codec_project, codec_output, codec_postnorm, codec_expand, codec_contract, cotangent):
    frame_weights = tuple((weight.astype(jnp.float32) for weight in (frame_prenorm, frame_project, frame_output, frame_postnorm, frame_expand, frame_contract)))
    codec_weights = tuple((weight.astype(jnp.float32) for weight in (codec_prenorm, codec_project, codec_output, codec_postnorm, codec_expand, codec_contract)))

    def wrapped(frames_wide, table_wide, frame_set, codec_set):
        return forward(frames_wide, table_wide, frame_set, codec_set, segments, codec_tokens, padding)
    output, pullback = jax.vjp(wrapped, frames.astype(jnp.float32), codebooks.astype(jnp.float32), frame_weights, codec_weights)
    frames_grad, codebooks_grad, frame_grads, codec_grads = pullback(cotangent.astype(jnp.float32))
    return (output.astype(jnp.bfloat16), frames_grad, codebooks_grad, frame_grads[0], frame_grads[1], frame_grads[2], frame_grads[3], frame_grads[4], frame_grads[5], codec_grads[0], codec_grads[1], codec_grads[2], codec_grads[3], codec_grads[4], codec_grads[5])
```

```python
import jax
import jax.numpy as jnp
from jax import lax
from jax.sharding import PartitionSpec as P

HEADS = 16
HEAD = 64
CODES = 1024


EPSILON = 1e-05
MASKED = -1e30
FACTOR = HEAD ** (-0.5)

BF = jnp.bfloat16
F32 = jnp.float32


def rms_scale(values, gain_vec):
    return (
        values * lax.rsqrt(jnp.mean(values * values, axis=-1, keepdims=True) + EPSILON) * gain_vec
    )


def matmul(former, latter):
    return jnp.dot(former, latter, preferred_element_type=F32)


def inner_left(former, latter):
    return lax.dot_general(former, latter, (((0,), (0,)), ((), ())), preferred_element_type=F32)


def inner_right(former, latter):
    return lax.dot_general(former, latter, (((1,), (1,)), ((), ())), preferred_element_type=F32)


def split_heads(values):
    return values.reshape(values.shape[:-1] + (-1, HEAD))


def swap(values, axis, bit):
    return lax.ppermute(values, axis, [(i, i ^ bit) for i in range(lax.axis_size(axis))])


def pick(values, index, axis):
    return lax.dynamic_index_in_dim(values, index, axis, keepdims=False)


class Place:
    def __init__(self):
        self.seq_count = lax.axis_size("seq")
        self.mp_count = lax.axis_size("mp")
        self.seq = lax.axis_index("seq")
        self.mp = lax.axis_index("mp")
        self.seq_low = self.seq % 2


def gather_weight(shard, place):
    height, breadth = shard.shape
    half = height // 2
    mine = lax.dynamic_slice(shard, (place.seq_low * half, 0), (half, breadth))
    first = swap(mine, "mp", 2)
    second = swap(first, "seq", 1)
    near_other = swap(shard, "mp", 1)
    far = jnp.zeros((height, breadth), shard.dtype)
    far = lax.dynamic_update_slice(far, first, (place.seq_low * half, 0))
    far = lax.dynamic_update_slice(far, second, ((1 - place.seq_low) * half, 0))
    far_other = swap(far, "mp", 1)
    whole = jnp.zeros((height * place.mp_count, breadth), shard.dtype)
    for flip, piece in ((0, shard), (1, near_other), (2, far), (3, far_other)):
        whole = lax.dynamic_update_slice(whole, piece, ((place.mp ^ flip) * height, 0))
    return whole


def line_scatter(blocks, place):
    count = place.seq_count // 2
    position = place.seq // 2
    size = 2 * count
    state = blocks
    up_in = down_in = None
    for step in range(1, count):
        up_index = jnp.clip(count - step + position, 0, count - 1)
        down_index = jnp.clip(step - 1 - (count - 1 - position), 0, count - 1)
        up_perm = [(i, i + 2) for i in range(size - 2) if i // 2 < step]
        down_perm = [(i, i - 2) for i in range(2, size) if (count - 1 - i // 2) < step]
        up_out = pick(blocks, up_index, 1)
        down_out = pick(blocks, down_index, 1)
        if up_in is not None:
            up_out = up_out + up_in
            down_out = down_out + down_in
        up_in = lax.ppermute(up_out, "seq", up_perm)
        down_in = lax.ppermute(down_out, "seq", down_perm)
    own = pick(blocks, position, 1).astype(F32)
    return own + up_in.astype(F32) + down_in.astype(F32)


def weight_grad(former, latter, place, seq_first):
    height = former.shape[1] // place.mp_count
    rows = former.shape[0]
    breadth = latter.shape[1] // place.seq_count
    low = place.seq_low
    view = latter.reshape(rows, place.seq_count // 2, 2, breadth)
    half = breadth * (place.seq_count // 2)
    give = pick(view, 1 - low, 2).reshape(rows, half)
    keep = pick(view, low, 2).reshape(rows, half)
    both = jnp.concatenate([give, keep], axis=1)

    def columns(flip):
        return lax.dynamic_slice(former, (0, (place.mp ^ flip) * height), (rows, height))

    own, other, far, far_other = (columns(flip) for flip in (0, 1, 2, 3))
    part = inner_left(jnp.concatenate([far_other, other], axis=1), both).astype(BF)
    part = swap(part, "mp", 1).astype(F32)
    if seq_first:
        send = inner_left(jnp.concatenate([far, own], axis=1), give) + part[:, :half]
        low_in = swap(send.astype(BF), "seq", 1).astype(F32)
        send = inner_left(far, keep) + part[:height, half:] + low_in[:height]
        far_in = swap(send.astype(BF), "mp", 2).astype(F32)
        total = inner_left(own, keep) + part[height:, half:] + low_in[height:] + far_in
    else:
        send = inner_left(far, both) + part[:height]
        far_in = swap(send.astype(BF), "mp", 2).astype(F32)
        send = inner_left(own, give) + part[height:, :half] + far_in[:, :half]
        low_in = swap(send.astype(BF), "seq", 1).astype(F32)
        total = inner_left(own, keep) + part[height:, half:] + far_in[:, half:] + low_in
    return total.astype(BF).reshape(height, place.seq_count // 2, breadth)


def finish_grads(partials, place):
    sizes = [part.shape[2] for part in partials]
    total = line_scatter(jnp.concatenate(partials, axis=2), place)
    pieces, start = [], 0
    for size in sizes:
        pieces.append(total[:, start : start + size])
        start += size
    return pieces


def sum_everywhere(values, place):
    for axis, count in (("mp", place.mp_count), ("seq", place.seq_count)):
        bit = 1
        while bit < count:
            values = values + swap(values, axis, bit)
            bit *= 2
    return values


def front_pass(hidden, weights):
    normed = rms_scale(hidden, weights[0].astype(F32)).astype(BF)
    projected = matmul(normed, weights[1]).astype(BF)
    return (normed, projected)


def rear_pass(hidden, attended, weights):
    mixed_sum = hidden + matmul(attended, weights[2])
    normed_two = rms_scale(mixed_sum, weights[3].astype(F32)).astype(BF)
    expanded = matmul(normed_two, weights[4])
    activated = jax.nn.gelu(expanded).astype(BF)
    result = mixed_sum + matmul(activated, weights[5])
    return (result, (mixed_sum, normed_two, expanded, activated))


def rear_grads(result_grad, saved_state, weights):
    mixed_sum, normed_two, expanded, activated = saved_state
    contract_input = result_grad.astype(BF)
    active_grad = inner_right(contract_input, weights[5])
    expand_input = jax.vjp(jax.nn.gelu, expanded)[1](active_grad)[0].astype(BF)
    normed_grad = inner_right(expand_input, weights[4])
    mixed_part, postnorm_grad = jax.vjp(rms_scale, mixed_sum, weights[3].astype(F32))[1](
        normed_grad
    )
    mixed_grad = result_grad + mixed_part
    output_input = mixed_grad.astype(BF)
    attended_grad = inner_right(output_input, weights[2]).astype(BF)
    return (mixed_grad, attended_grad, postnorm_grad, contract_input, expand_input, output_input)


def front_grads(hidden, projected_grad, mixed_grad, weights):
    normed_grad = inner_right(projected_grad, weights[1])
    hidden_part, prenorm_grad = jax.vjp(rms_scale, hidden, weights[0].astype(F32))[1](normed_grad)
    return (mixed_grad + hidden_part, prenorm_grad)


def portions_of(queries, keys, allowed):
    scores = jnp.einsum("ihd,jhd->hij", queries, keys, preferred_element_type=F32) * FACTOR
    return jax.nn.softmax(jnp.where(allowed[None], scores, MASKED), axis=-1)


def attend(queries, keys, values, allowed):
    portions = portions_of(queries, keys, allowed)
    return jnp.einsum(
        "hij,jhd->ihd", portions.astype(BF), values, preferred_element_type=F32
    ).astype(BF)


def attend_grads(queries, keys, values, allowed, out_grad):
    portions = portions_of(queries, keys, allowed)
    portion_grad = jnp.einsum("ihd,jhd->hij", out_grad, values, preferred_element_type=F32)
    score_grad = (
        portions * (portion_grad - jnp.sum(portions * portion_grad, axis=-1, keepdims=True))
    ).astype(BF)
    query_grad = (
        jnp.einsum("hij,jhd->ihd", score_grad, keys, preferred_element_type=F32) * FACTOR
    )
    key_grad = (
        jnp.einsum("hij,ihd->jhd", score_grad, queries, preferred_element_type=F32) * FACTOR
    )
    value_grad = jnp.einsum("hij,ihd->jhd", portions.astype(BF), out_grad, preferred_element_type=F32)
    return query_grad, key_grad, value_grad


def to_heads(values, place):
    rows, own, parts, width = values.shape
    count = place.seq_count
    view = values.reshape(rows, own, parts, count, width // count)
    moved = lax.all_to_all(
        jnp.transpose(view, (3, 0, 1, 2, 4)), "seq", split_axis=0, concat_axis=0, tiled=True
    )
    return jnp.transpose(moved, (1, 0, 2, 3, 4)).reshape(rows, count * own, parts, width // count)


def to_frames(values, place):
    rows, total, parts, width = values.shape
    count = place.seq_count
    view = values.reshape(rows, count, total // count, parts, width)
    moved = lax.all_to_all(
        jnp.transpose(view, (1, 0, 2, 3, 4)), "seq", split_axis=0, concat_axis=0, tiled=True
    )
    return jnp.transpose(moved, (1, 2, 3, 0, 4)).reshape(
        rows, total // count, parts, count * width
    )


def allowed_of(query_seg, key_seg, query_pos, key_pos):
    return (query_seg[:, None] == key_seg[None, :]) & (key_pos[None, :] <= query_pos[:, None])


def frame_attention(projected, segments, place):
    rows, own, triple = projected.shape
    width = triple // 3
    parts = projected.reshape(rows, own, 3, width)
    every_segment = lax.all_gather(segments, "seq", axis=1, tiled=True)
    every_pos = jnp.arange(own * place.seq_count)
    if HEADS % place.seq_count == 0:
        packed = to_heads(parts, place)
        sets = [split_heads(packed[:, :, part]) for part in range(3)]

        def one_row(items):
            queries, keys, values, segs = items
            return attend(queries, keys, values, allowed_of(segs, segs, every_pos, every_pos))

        attended = lax.map(one_row, (*sets, every_segment))
        attended = to_frames(attended.reshape(rows, own * place.seq_count, 1, -1), place)

        def backward(out_grad):
            grads = to_heads(out_grad.reshape(rows, own, 1, width), place)[:, :, 0]

            def one_row(items):
                queries, keys, values, segs, grad = items
                return attend_grads(
                    queries, keys, values, allowed_of(segs, segs, every_pos, every_pos), grad
                )

            found = lax.map(one_row, (*sets, every_segment, split_heads(grads)))
            packed_grad = jnp.stack(
                [grad.reshape(rows, own * place.seq_count, -1) for grad in found], axis=2
            ).astype(BF)
            return to_frames(packed_grad, place).reshape(rows, own, triple)

        return attended.reshape(rows, own, width), backward

    keys = lax.all_gather(parts[:, :, 1], "seq", axis=1, tiled=True)
    values = lax.all_gather(parts[:, :, 2], "seq", axis=1, tiled=True)
    sets = (split_heads(parts[:, :, 0]), split_heads(keys), split_heads(values))
    own_pos = place.seq * own + jnp.arange(own)

    def one_row(items):
        row_q, row_k, row_v, own_segs, segs = items
        return attend(row_q, row_k, row_v, allowed_of(own_segs, segs, own_pos, every_pos))

    attended = lax.map(one_row, (*sets, segments, every_segment)).reshape(rows, own, width)

    def backward(out_grad):
        def one_row(items):
            row_q, row_k, row_v, own_segs, segs, grad = items
            allowed = allowed_of(own_segs, segs, own_pos, every_pos)
            return attend_grads(row_q, row_k, row_v, allowed, grad)

        query_grad, key_grad, value_grad = lax.map(
            one_row, (*sets, segments, every_segment, split_heads(out_grad))
        )
        both = jnp.stack([key_grad.reshape(rows, -1, width), value_grad.reshape(rows, -1, width)], 2)
        both = lax.psum_scatter(both, "seq", scatter_dimension=1, tiled=True)
        parts_grad = [query_grad.reshape(rows, own, width), both[:, :, 0], both[:, :, 1]]
        return jnp.concatenate(parts_grad, axis=-1).astype(BF)

    return attended, backward


def head_sums(values, marks):
    return jnp.dot(values, marks, precision=lax.Precision.HIGHEST, preferred_element_type=F32)


def head_spread(values, marks):
    return lax.dot_general(
        values.astype(BF), marks.astype(BF), (((1,), (1,)), ((), ())), preferred_element_type=F32
    )


def codec_softmax(queries, keys, marks):
    result = []
    for later in range(len(queries)):
        scores = [
            head_sums(queries[later].astype(F32) * keys[earlier].astype(F32), marks) * FACTOR
            for earlier in range(later + 1)
        ]
        top = scores[0]
        for score in scores[1:]:
            top = jnp.maximum(top, score)
        powers = [jnp.exp(score - top) for score in scores]
        total = sum(powers)
        result.append([power / total for power in powers])
    return result


def codec_attend(soft, values, marks):
    result = []
    for row in soft:
        total = 0.0
        for earlier, portion in enumerate(row):
            total = total + head_spread(portion, marks) * values[earlier].astype(F32)
        result.append(total.astype(BF))
    return result


def codec_attend_grads(soft, queries, keys, values, grads, marks):
    count = len(queries)
    query_grad = []
    key_grad = [0.0] * count
    value_grad = [0.0] * count
    for later in range(count):
        grad = grads[later].astype(F32)
        portion_grads = [
            head_sums(grad * values[earlier].astype(F32), marks) for earlier in range(later + 1)
        ]
        mean = sum(soft[later][i] * portion_grads[i] for i in range(later + 1))
        total = 0.0
        for earlier in range(later + 1):
            score_grad = soft[later][earlier] * (portion_grads[earlier] - mean)
            wide = head_spread(score_grad, marks)
            total = total + wide * keys[earlier].astype(F32)
            key_grad[earlier] = key_grad[earlier] + wide * queries[later].astype(F32)
            value_grad[earlier] = value_grad[earlier] + head_spread(soft[later][earlier], marks) * grad
        query_grad.append(total * FACTOR)
    return jnp.concatenate(
        [
            jnp.concatenate(
                [query_grad[t], key_grad[t] * FACTOR, value_grad[t]], axis=-1
            ).astype(BF)
            for t in range(count)
        ],
        axis=0,
    )


def shards(
    frames,
    segments,
    padding,
    codec_tokens,
    codebooks,
    frame_prenorm,
    frame_project,
    frame_output,
    frame_postnorm,
    frame_expand,
    frame_contract,
    codec_prenorm,
    codec_project,
    codec_output,
    codec_postnorm,
    codec_expand,
    codec_contract,
    cotangent,
):
    place = Place()
    row_count, frames_dev, width = frames.shape
    frame_total = row_count * frames_dev
    positions = cotangent.shape[2]
    gains = lax.all_gather(
        jnp.stack([frame_prenorm, frame_postnorm, codec_prenorm, codec_postnorm]),
        "mp",
        axis=1,
        tiled=True,
    )
    frame_weights = (
        gains[0],
        gather_weight(frame_project, place),
        gather_weight(frame_output, place),
        gains[1],
        gather_weight(frame_expand, place),
        gather_weight(frame_contract, place),
    )
    codec_weights = (
        gains[2],
        gather_weight(codec_project, place),
        gather_weight(codec_output, place),
        gains[3],
        gather_weight(codec_expand, place),
        gather_weight(codec_contract, place),
    )
    table = gather_weight(codebooks, place)

    hidden = frames.astype(F32).reshape(frame_total, width)
    normed, projected = front_pass(hidden, frame_weights)
    attended, attention_back = frame_attention(
        projected.reshape(row_count, frames_dev, 3 * width), segments, place
    )
    attended = attended.reshape(frame_total, width)
    frame_result, frame_saved = rear_pass(hidden, attended, frame_weights)
    base = frame_result.astype(BF).astype(F32)

    table_rows = codec_tokens.reshape(positions - 1, frame_total) + (
        jnp.arange(positions - 1, dtype=jnp.int32) * CODES
    )[:, None]
    embedded = table[table_rows].astype(F32)
    codec_hidden = jnp.concatenate([base[None], base[None] + embedded], axis=0).reshape(
        positions * frame_total, width
    )
    codec_normed, codec_projected = front_pass(codec_hidden, codec_weights)
    marks = (
        jnp.arange(width)[:, None] // HEAD == jnp.arange(HEADS)[None, :]
    ).astype(F32)
    view = codec_projected.reshape(positions, frame_total, 3, width)
    queries, keys, values = ([view[t, :, part] for t in range(positions)] for part in range(3))
    soft = codec_softmax(queries, keys, marks)
    codec_attended = jnp.concatenate(codec_attend(soft, values, marks), axis=0)
    codec_result, codec_saved = rear_pass(codec_hidden, codec_attended, codec_weights)
    live = padding.reshape(frame_total).astype(F32)[None, :, None]
    output = jnp.transpose(
        (codec_result.reshape(positions, frame_total, width) * live).astype(BF), (1, 0, 2)
    ).reshape(row_count, frames_dev, positions, width)

    codec_grad = (
        jnp.transpose(cotangent.reshape(frame_total, positions, width), (1, 0, 2)).astype(F32) * live
    ).reshape(positions * frame_total, width)
    mixed_grad, attended_grad, codec_postnorm_grad, contract_in, expand_in, output_in = rear_grads(
        codec_grad, codec_saved, codec_weights
    )
    codec_contract_part = weight_grad(codec_saved[3], contract_in, place, True)
    codec_expand_part = weight_grad(codec_saved[1], expand_in, place, False)
    codec_output_part = weight_grad(codec_attended, output_in, place, True)
    grad_view = attended_grad.reshape(positions, frame_total, width)
    codec_projected_grad = codec_attend_grads(
        soft, queries, keys, values, [grad_view[t] for t in range(positions)], marks
    )
    codec_project_part = weight_grad(codec_normed, codec_projected_grad, place, True)
    input_grad, codec_prenorm_grad = front_grads(
        codec_hidden, codec_projected_grad, mixed_grad, codec_weights
    )
    input_grad = input_grad.reshape(positions, frame_total, width)
    chosen = (
        table_rows.reshape(-1)[:, None] == jnp.arange(table.shape[0], dtype=jnp.int32)[None, :]
    ).astype(BF)
    table_part = weight_grad(chosen, input_grad[1:].reshape(-1, width).astype(BF), place, False)
    base_grad = jnp.sum(input_grad, axis=0).astype(BF).astype(F32)

    (codec_contract_grad,) = finish_grads([codec_contract_part], place)
    codec_expand_grad, codec_output_grad, codec_project_grad = finish_grads(
        [codec_expand_part, codec_output_part, codec_project_part], place
    )
    (table_grad,) = finish_grads([table_part], place)

    frame_mixed_grad, frame_attended_grad, frame_postnorm_grad, contract_in, expand_in, output_in = (
        rear_grads(base_grad, frame_saved, frame_weights)
    )
    frame_projected_grad = attention_back(
        frame_attended_grad.reshape(row_count, frames_dev, width)
    ).reshape(frame_total, 3 * width)
    frame_contract_part = weight_grad(frame_saved[3], contract_in, place, True)
    frame_expand_part = weight_grad(frame_saved[1], expand_in, place, False)
    frame_output_part = weight_grad(attended, output_in, place, True)
    frame_project_part = weight_grad(normed, frame_projected_grad, place, True)
    frames_grad, frame_prenorm_grad = front_grads(
        hidden, frame_projected_grad, frame_mixed_grad, frame_weights
    )
    (frame_contract_grad,) = finish_grads([frame_contract_part], place)
    frame_expand_grad, frame_output_grad = finish_grads(
        [frame_expand_part, frame_output_part], place
    )
    (frame_project_grad,) = finish_grads([frame_project_part], place)
    gain_sums = sum_everywhere(
        jnp.stack(
            [frame_prenorm_grad, frame_postnorm_grad, codec_prenorm_grad, codec_postnorm_grad]
        ),
        place,
    )
    return (
        output,
        frames_grad.reshape(row_count, frames_dev, width),
        table_grad,
        gain_sums[0],
        frame_project_grad,
        frame_output_grad,
        gain_sums[1],
        frame_expand_grad,
        frame_contract_grad,
        gain_sums[2],
        codec_project_grad,
        codec_output_grad,
        gain_sums[3],
        codec_expand_grad,
        codec_contract_grad,
    )


def solution(mesh):
    placed = (
        P("mp", "seq", None),
        P("mp", "seq"),
        P("mp", "seq"),
        P(None, "mp", "seq"),
        P("mp", None),
        P("mp"),
        P("mp", None),
        P("mp", None),
        P("mp"),
        P("mp", None),
        P("mp", None),
        P("mp"),
        P("mp", None),
        P("mp", None),
        P("mp"),
        P("mp", None),
        P("mp", None),
        P("mp", "seq", None, None),
    )
    return jax.shard_map(
        shards,
        mesh=mesh,
        in_specs=placed,
        out_specs=(
            P("mp", "seq", None, None),
            P("mp", "seq", None),
            P("mp", "seq"),
            P(),
            P("mp", "seq"),
            P("mp", "seq"),
            P(),
            P("mp", "seq"),
            P("mp", "seq"),
            P(),
            P("mp", "seq"),
            P("mp", "seq"),
            P(),
            P("mp", "seq"),
            P("mp", "seq"),
        ),
        check_vma=False,
    )
```

```python
import functools

import jax
import jax.numpy as jnp
from jax import lax
from jax.experimental import pallas as pl
from jax.experimental.pallas import tpu as pltpu
from jax.sharding import PartitionSpec as P

HEADS = 16
HEAD = 64
CODES = 1024


EPSILON = 1e-05
MASKED = -1e30
FACTOR = HEAD ** (-0.5)

BF = jnp.bfloat16
F32 = jnp.float32


def rms_scale(values, gain_vec):
    return (
        values * lax.rsqrt(jnp.mean(values * values, axis=-1, keepdims=True) + EPSILON) * gain_vec
    )


def matmul(former, latter):
    return jnp.dot(former, latter, preferred_element_type=F32)


def inner_left(former, latter):
    return lax.dot_general(former, latter, (((0,), (0,)), ((), ())), preferred_element_type=F32)


def inner_right(former, latter):
    return lax.dot_general(former, latter, (((1,), (1,)), ((), ())), preferred_element_type=F32)


def split_heads(values):
    return values.reshape(values.shape[:-1] + (-1, HEAD))


def swap(values, axis, bit):
    return lax.ppermute(values, axis, [(i, i ^ bit) for i in range(lax.axis_size(axis))])


def pick(values, index, axis):
    return lax.dynamic_index_in_dim(values, index, axis, keepdims=False)


class Place:
    def __init__(self):
        self.seq_count = lax.axis_size("seq")
        self.mp_count = lax.axis_size("mp")
        self.seq = lax.axis_index("seq")
        self.mp = lax.axis_index("mp")
        self.seq_low = self.seq % 2


def gather_weight(shard, place):
    height, breadth = shard.shape
    half = height // 2
    mine = lax.dynamic_slice(shard, (place.seq_low * half, 0), (half, breadth))
    first = swap(mine, "mp", 2)
    second = swap(first, "seq", 1)
    near_other = swap(shard, "mp", 1)
    far = jnp.zeros((height, breadth), shard.dtype)
    far = lax.dynamic_update_slice(far, first, (place.seq_low * half, 0))
    far = lax.dynamic_update_slice(far, second, ((1 - place.seq_low) * half, 0))
    far_other = swap(far, "mp", 1)
    whole = jnp.zeros((height * place.mp_count, breadth), shard.dtype)
    for flip, piece in ((0, shard), (1, near_other), (2, far), (3, far_other)):
        whole = lax.dynamic_update_slice(whole, piece, ((place.mp ^ flip) * height, 0))
    return whole


def line_scatter(blocks, place):
    count = place.seq_count // 2
    position = place.seq // 2
    size = 2 * count
    state = blocks
    up_in = down_in = None
    for step in range(1, count):
        up_index = jnp.clip(count - step + position, 0, count - 1)
        down_index = jnp.clip(step - 1 - (count - 1 - position), 0, count - 1)
        up_perm = [(i, i + 2) for i in range(size - 2) if i // 2 < step]
        down_perm = [(i, i - 2) for i in range(2, size) if (count - 1 - i // 2) < step]
        up_out = pick(blocks, up_index, 1)
        down_out = pick(blocks, down_index, 1)
        if up_in is not None:
            up_out = up_out + up_in
            down_out = down_out + down_in
        up_in = lax.ppermute(up_out, "seq", up_perm)
        down_in = lax.ppermute(down_out, "seq", down_perm)
    own = pick(blocks, position, 1).astype(F32)
    return own + up_in.astype(F32) + down_in.astype(F32)


def weight_grad(former, latter, place, seq_first):
    height = former.shape[1] // place.mp_count
    rows = former.shape[0]
    breadth = latter.shape[1] // place.seq_count
    low = place.seq_low
    view = latter.reshape(rows, place.seq_count // 2, 2, breadth)
    half = breadth * (place.seq_count // 2)
    give = pick(view, 1 - low, 2).reshape(rows, half)
    keep = pick(view, low, 2).reshape(rows, half)
    both = jnp.concatenate([give, keep], axis=1)

    def columns(flip):
        return lax.dynamic_slice(former, (0, (place.mp ^ flip) * height), (rows, height))

    own, other, far, far_other = (columns(flip) for flip in (0, 1, 2, 3))
    part = inner_left(jnp.concatenate([far_other, other], axis=1), both).astype(BF)
    part = swap(part, "mp", 1).astype(F32)
    if seq_first:
        send = inner_left(jnp.concatenate([far, own], axis=1), give) + part[:, :half]
        low_in = swap(send.astype(BF), "seq", 1).astype(F32)
        send = inner_left(far, keep) + part[:height, half:] + low_in[:height]
        far_in = swap(send.astype(BF), "mp", 2).astype(F32)
        total = inner_left(own, keep) + part[height:, half:] + low_in[height:] + far_in
    else:
        send = inner_left(far, both) + part[:height]
        far_in = swap(send.astype(BF), "mp", 2).astype(F32)
        send = inner_left(own, give) + part[height:, :half] + far_in[:, :half]
        low_in = swap(send.astype(BF), "seq", 1).astype(F32)
        total = inner_left(own, keep) + part[height:, half:] + far_in[:, half:] + low_in
    return total.astype(BF).reshape(height, place.seq_count // 2, breadth)


def finish_grads(partials, place):
    sizes = [part.shape[2] for part in partials]
    total = line_scatter(jnp.concatenate(partials, axis=2), place)
    pieces, start = [], 0
    for size in sizes:
        pieces.append(total[:, start : start + size])
        start += size
    return pieces


def sum_everywhere(values, place):
    for axis, count in (("mp", place.mp_count), ("seq", place.seq_count)):
        bit = 1
        while bit < count:
            values = values + swap(values, axis, bit)
            bit *= 2
    return values


def front_pass(hidden, weights):
    normed = rms_scale(hidden, weights[0].astype(F32)).astype(BF)
    projected = matmul(normed, weights[1]).astype(BF)
    return (normed, projected)


def rear_pass(hidden, attended, weights):
    mixed_sum = hidden + matmul(attended, weights[2])
    normed_two = rms_scale(mixed_sum, weights[3].astype(F32)).astype(BF)
    expanded = matmul(normed_two, weights[4])
    activated = jax.nn.gelu(expanded).astype(BF)
    result = mixed_sum + matmul(activated, weights[5])
    return (result, (mixed_sum, normed_two, expanded, activated))


def rear_grads(result_grad, saved_state, weights):
    mixed_sum, normed_two, expanded, activated = saved_state
    contract_input = result_grad.astype(BF)
    active_grad = inner_right(contract_input, weights[5])
    expand_input = jax.vjp(jax.nn.gelu, expanded)[1](active_grad)[0].astype(BF)
    normed_grad = inner_right(expand_input, weights[4])
    mixed_part, postnorm_grad = jax.vjp(rms_scale, mixed_sum, weights[3].astype(F32))[1](
        normed_grad
    )
    mixed_grad = result_grad + mixed_part
    output_input = mixed_grad.astype(BF)
    attended_grad = inner_right(output_input, weights[2]).astype(BF)
    return (mixed_grad, attended_grad, postnorm_grad, contract_input, expand_input, output_input)


def front_grads(hidden, projected_grad, mixed_grad, weights):
    normed_grad = inner_right(projected_grad, weights[1])
    hidden_part, prenorm_grad = jax.vjp(rms_scale, hidden, weights[0].astype(F32))[1](normed_grad)
    return (mixed_grad + hidden_part, prenorm_grad)


def portions_of(queries, keys, allowed):
    scores = jnp.einsum("ihd,jhd->hij", queries, keys, preferred_element_type=F32) * FACTOR
    return jax.nn.softmax(jnp.where(allowed[None], scores, MASKED), axis=-1)


def attend(queries, keys, values, allowed):
    portions = portions_of(queries, keys, allowed)
    return jnp.einsum(
        "hij,jhd->ihd", portions.astype(BF), values, preferred_element_type=F32
    ).astype(BF)


def attend_grads(queries, keys, values, allowed, out_grad):
    portions = portions_of(queries, keys, allowed)
    portion_grad = jnp.einsum("ihd,jhd->hij", out_grad, values, preferred_element_type=F32)
    score_grad = (
        portions * (portion_grad - jnp.sum(portions * portion_grad, axis=-1, keepdims=True))
    ).astype(BF)
    query_grad = (
        jnp.einsum("hij,jhd->ihd", score_grad, keys, preferred_element_type=F32) * FACTOR
    )
    key_grad = (
        jnp.einsum("hij,ihd->jhd", score_grad, queries, preferred_element_type=F32) * FACTOR
    )
    value_grad = jnp.einsum("hij,ihd->jhd", portions.astype(BF), out_grad, preferred_element_type=F32)
    return query_grad, key_grad, value_grad


def to_heads(values, place):
    rows, own, parts, width = values.shape
    count = place.seq_count
    view = values.reshape(rows, own, parts, count, width // count)
    moved = lax.all_to_all(
        jnp.transpose(view, (3, 0, 1, 2, 4)), "seq", split_axis=0, concat_axis=0, tiled=True
    )
    return jnp.transpose(moved, (1, 0, 2, 3, 4)).reshape(rows, count * own, parts, width // count)


def to_frames(values, place):
    rows, total, parts, width = values.shape
    count = place.seq_count
    view = values.reshape(rows, count, total // count, parts, width)
    moved = lax.all_to_all(
        jnp.transpose(view, (1, 0, 2, 3, 4)), "seq", split_axis=0, concat_axis=0, tiled=True
    )
    return jnp.transpose(moved, (1, 2, 3, 0, 4)).reshape(
        rows, total // count, parts, count * width
    )


def allowed_of(query_seg, key_seg, query_pos, key_pos):
    return (query_seg[:, None] == key_seg[None, :]) & (key_pos[None, :] <= query_pos[:, None])


def frame_attention(projected, segments, place):
    rows, own, triple = projected.shape
    width = triple // 3
    parts = projected.reshape(rows, own, 3, width)
    every_segment = lax.all_gather(segments, "seq", axis=1, tiled=True)
    every_pos = jnp.arange(own * place.seq_count)
    if HEADS % place.seq_count == 0:
        packed = to_heads(parts, place)
        sets = [split_heads(packed[:, :, part]) for part in range(3)]

        def one_row(items):
            queries, keys, values, segs = items
            return attend(queries, keys, values, allowed_of(segs, segs, every_pos, every_pos))

        attended = lax.map(one_row, (*sets, every_segment))
        attended = to_frames(attended.reshape(rows, own * place.seq_count, 1, -1), place)

        def backward(out_grad):
            grads = to_heads(out_grad.reshape(rows, own, 1, width), place)[:, :, 0]

            def one_row(items):
                queries, keys, values, segs, grad = items
                return attend_grads(
                    queries, keys, values, allowed_of(segs, segs, every_pos, every_pos), grad
                )

            found = lax.map(one_row, (*sets, every_segment, split_heads(grads)))
            packed_grad = jnp.stack(
                [grad.reshape(rows, own * place.seq_count, -1) for grad in found], axis=2
            ).astype(BF)
            return to_frames(packed_grad, place).reshape(rows, own, triple)

        return attended.reshape(rows, own, width), backward

    keys = lax.all_gather(parts[:, :, 1], "seq", axis=1, tiled=True)
    values = lax.all_gather(parts[:, :, 2], "seq", axis=1, tiled=True)
    sets = (split_heads(parts[:, :, 0]), split_heads(keys), split_heads(values))
    own_pos = place.seq * own + jnp.arange(own)

    def one_row(items):
        row_q, row_k, row_v, own_segs, segs = items
        return attend(row_q, row_k, row_v, allowed_of(own_segs, segs, own_pos, every_pos))

    attended = lax.map(one_row, (*sets, segments, every_segment)).reshape(rows, own, width)

    def backward(out_grad):
        def one_row(items):
            row_q, row_k, row_v, own_segs, segs, grad = items
            allowed = allowed_of(own_segs, segs, own_pos, every_pos)
            return attend_grads(row_q, row_k, row_v, allowed, grad)

        query_grad, key_grad, value_grad = lax.map(
            one_row, (*sets, segments, every_segment, split_heads(out_grad))
        )
        both = jnp.stack([key_grad.reshape(rows, -1, width), value_grad.reshape(rows, -1, width)], 2)
        both = lax.psum_scatter(both, "seq", scatter_dimension=1, tiled=True)
        parts_grad = [query_grad.reshape(rows, own, width), both[:, :, 0], both[:, :, 1]]
        return jnp.concatenate(parts_grad, axis=-1).astype(BF)

    return attended, backward


def head_sums(values, marks):
    return jnp.dot(values, marks, precision=lax.Precision.HIGHEST, preferred_element_type=F32)


def head_spread(values, marks):
    return lax.dot_general(
        values.astype(BF), marks.astype(BF), (((1,), (1,)), ((), ())), preferred_element_type=F32
    )


def codec_softmax(queries, keys, marks):
    result = []
    for later in range(len(queries)):
        scores = [
            head_sums(queries[later].astype(F32) * keys[earlier].astype(F32), marks) * FACTOR
            for earlier in range(later + 1)
        ]
        top = scores[0]
        for score in scores[1:]:
            top = jnp.maximum(top, score)
        powers = [jnp.exp(score - top) for score in scores]
        total = sum(powers)
        result.append([power / total for power in powers])
    return result


def codec_attend(soft, values, marks):
    result = []
    for row in soft:
        total = 0.0
        for earlier, portion in enumerate(row):
            total = total + head_spread(portion, marks) * values[earlier].astype(F32)
        result.append(total.astype(BF))
    return result


def codec_attend_grads(soft, queries, keys, values, grads, marks):
    count = len(queries)
    query_grad = []
    key_grad = [0.0] * count
    value_grad = [0.0] * count
    for later in range(count):
        grad = grads[later].astype(F32)
        portion_grads = [
            head_sums(grad * values[earlier].astype(F32), marks) for earlier in range(later + 1)
        ]
        mean = sum(soft[later][i] * portion_grads[i] for i in range(later + 1))
        total = 0.0
        for earlier in range(later + 1):
            score_grad = soft[later][earlier] * (portion_grads[earlier] - mean)
            wide = head_spread(score_grad, marks)
            total = total + wide * keys[earlier].astype(F32)
            key_grad[earlier] = key_grad[earlier] + wide * queries[later].astype(F32)
            value_grad[earlier] = value_grad[earlier] + head_spread(soft[later][earlier], marks) * grad
        query_grad.append(total * FACTOR)
    return jnp.concatenate(
        [
            jnp.concatenate(
                [query_grad[t], key_grad[t] * FACTOR, value_grad[t]], axis=-1
            ).astype(BF)
            for t in range(count)
        ],
        axis=0,
    )


LANES = 128
TILE = 256
VMEM_LIMIT = 48 * 1024 * 1024


def whole_block(shape):
    return pl.BlockSpec(shape, lambda *_: (0,) * len(shape))


def causal_tiles(length):
    tile = min(TILE, length)
    return [(start, tile, start + tile) for start in range(0, length, tile)]


def head_masks(dtype):
    lane = lax.broadcasted_iota(jnp.int32, (1, LANES), 1)
    return [((lane // HEAD) == head).astype(dtype) for head in range(LANES // HEAD)]


def frame_attend_kernel(packed_ref, seg_col_ref, seg_row_ref, out_ref):
    chunks, _, own, _ = packed_ref.shape
    length = chunks * own
    packed = packed_ref[...].reshape(length, 3 * LANES)
    queries, keys, values = (packed[:, LANES * i : LANES * (i + 1)] for i in range(3))
    masks = head_masks(BF)
    lane = lax.broadcasted_iota(jnp.int32, (1, LANES), 1)
    for start, tile, end in causal_tiles(length):
        query_pos = start + lax.broadcasted_iota(jnp.int32, (tile, end), 0)
        key_pos = lax.broadcasted_iota(jnp.int32, (tile, end), 1)
        allowed = (seg_col_ref[0, start:end] == seg_row_ref[0, :, :end]) & (key_pos <= query_pos)
        result = jnp.zeros((tile, LANES), F32)
        for head, mask in enumerate(masks):
            scores = inner_right(queries[start:end] * mask, keys[:end]) * FACTOR
            scores = jnp.where(allowed, scores, MASKED)
            powers = jnp.exp(scores - jnp.max(scores, axis=1, keepdims=True))
            portions = powers / jnp.sum(powers, axis=1, keepdims=True)
            found = matmul(portions.astype(BF), values[:end])
            result = jnp.where(lane // HEAD == head, found, result)
        out_ref[start // own : end // own, 0] = result.astype(BF).reshape(tile // own, own, LANES)


def frame_attend_grads_kernel(packed_ref, grad_ref, seg_col_ref, seg_row_ref, out_ref, key_sum, value_sum):
    chunks, _, own, _ = packed_ref.shape
    length = chunks * own
    packed = packed_ref[...].reshape(length, 3 * LANES)
    queries, keys, values = (packed[:, LANES * i : LANES * (i + 1)] for i in range(3))
    grads = grad_ref[...].reshape(length, LANES)
    masks = head_masks(BF)
    lane = lax.broadcasted_iota(jnp.int32, (1, LANES), 1)
    key_sum[...] = jnp.zeros_like(key_sum)
    value_sum[...] = jnp.zeros_like(value_sum)
    for start, tile, end in causal_tiles(length):
        key_pos = lax.broadcasted_iota(jnp.int32, (end, tile), 0)
        query_pos = start + lax.broadcasted_iota(jnp.int32, (end, tile), 1)
        allowed = (seg_col_ref[0, :end] == seg_row_ref[0, :, start:end]) & (key_pos <= query_pos)
        query_grad = jnp.zeros((tile, LANES), F32)
        for head, mask in enumerate(masks):
            query = queries[start:end] * mask
            grad = grads[start:end] * mask
            scores = inner_right(keys[:end], query) * FACTOR
            scores = jnp.where(allowed, scores, MASKED)
            powers = jnp.exp(scores - jnp.max(scores, axis=0, keepdims=True))
            portions = powers / jnp.sum(powers, axis=0, keepdims=True)
            portion_grad = inner_right(values[:end], grad)
            mean = jnp.sum(portions * portion_grad, axis=0, keepdims=True)
            score_grad = (portions * (portion_grad - mean)).astype(BF)
            key_sum[:end] += matmul(score_grad, query)
            value_sum[:end] += matmul(portions.astype(BF), grad)
            found = inner_left(score_grad, keys[:end])
            query_grad = jnp.where(lane // HEAD == head, found, query_grad)
        out_ref[start // own : end // own, 0, :, :LANES] = (
            (query_grad * FACTOR).astype(BF).reshape(tile // own, own, LANES)
        )
    out_ref[:, 0, :, LANES : 2 * LANES] = (key_sum[...] * FACTOR).astype(BF).reshape(chunks, own, LANES)
    out_ref[:, 0, :, 2 * LANES :] = value_sum[...].astype(BF).reshape(chunks, own, LANES)


def row_spec(chunks, own, breadth):
    return pl.BlockSpec((chunks, 1, own, breadth), lambda row: (0, row, 0, 0))


def segment_specs(length):
    return [
        pl.BlockSpec((1, length, 1), lambda row: (row, 0, 0)),
        pl.BlockSpec((1, 1, length), lambda row: (row, 0, 0)),
    ]


def frame_attend_call(packed, segments):
    chunks, rows, own, _ = packed.shape
    length = chunks * own
    return pl.pallas_call(
        frame_attend_kernel,
        grid=(rows,),
        in_specs=[row_spec(chunks, own, 3 * LANES), *segment_specs(length)],
        out_specs=row_spec(chunks, own, LANES),
        out_shape=jax.ShapeDtypeStruct((chunks, rows, own, LANES), BF),
        compiler_params=pltpu.CompilerParams(vmem_limit_bytes=VMEM_LIMIT),
        cost_estimate=pl.CostEstimate(
            flops=rows * length * length * LANES * 5,
            bytes_accessed=packed.size * 3,
            transcendentals=rows * length * length,
        ),
        name="frame_attend",
    )(packed, segments[:, :, None], segments[:, None, :])


def frame_attend_grads_call(packed, grads, segments):
    chunks, rows, own, _ = packed.shape
    length = chunks * own
    return pl.pallas_call(
        frame_attend_grads_kernel,
        grid=(rows,),
        in_specs=[
            row_spec(chunks, own, 3 * LANES),
            row_spec(chunks, own, LANES),
            *segment_specs(length),
        ],
        out_specs=row_spec(chunks, own, 3 * LANES),
        out_shape=jax.ShapeDtypeStruct((chunks, rows, own, 3 * LANES), BF),
        scratch_shapes=[pltpu.VMEM((length, LANES), F32), pltpu.VMEM((length, LANES), F32)],
        compiler_params=pltpu.CompilerParams(vmem_limit_bytes=VMEM_LIMIT),
        cost_estimate=pl.CostEstimate(
            flops=rows * length * length * LANES * 12,
            bytes_accessed=packed.size * 5,
            transcendentals=rows * length * length,
        ),
        name="frame_attend_grads",
    )(packed, grads, segments[:, :, None], segments[:, None, :])


def position_pairs(positions):
    return [(later, earlier) for later in range(1, positions) for earlier in range(later + 1)]


def codec_sums(products, marks):
    stacked = jnp.concatenate(products, axis=0)
    high = stacked.astype(BF)
    low = (stacked - high.astype(F32)).astype(BF)
    total = matmul(high, marks) + matmul(low, marks)
    size = products[0].shape[0]
    return [total[size * i : size * (i + 1)] for i in range(len(products))]


def codec_spread(portions, marks):
    stacked = jnp.concatenate([portion.astype(BF) for portion in portions], axis=0)
    total = inner_right(stacked, marks)
    size = portions[0].shape[0]
    return [total[size * i : size * (i + 1)] for i in range(len(portions))]


def codec_portions(queries, keys, marks, pairs):
    scores = codec_sums(
        [queries[later].astype(F32) * keys[earlier].astype(F32) for later, earlier in pairs], marks
    )
    scores = dict(zip(pairs, [score * FACTOR for score in scores]))
    portions = {}
    for later in range(1, len(queries)):
        row = [scores[later, earlier] for earlier in range(later + 1)]
        top = functools.reduce(jnp.maximum, row)
        powers = [jnp.exp(score - top) for score in row]
        total = functools.reduce(jnp.add, powers)
        for earlier in range(later + 1):
            portions[later, earlier] = powers[earlier] / total
    return portions


def codec_parts(packed_ref, width):
    positions = packed_ref.shape[0]
    return [
        [packed_ref[t, :, width * part : width * (part + 1)] for t in range(positions)]
        for part in range(3)
    ]


def codec_attend_kernel(packed_ref, marks_ref, out_ref):
    positions, _, width = out_ref.shape
    queries, keys, values = codec_parts(packed_ref, width)
    marks = marks_ref[...]
    pairs = position_pairs(positions)
    portions = codec_portions(queries, keys, marks, pairs)
    wide = dict(zip(pairs, codec_spread([portions[pair] for pair in pairs], marks)))
    out_ref[0] = values[0]
    for later in range(1, positions):
        terms = [wide[later, e] * values[e].astype(F32) for e in range(later + 1)]
        out_ref[later] = functools.reduce(jnp.add, terms).astype(BF)


def codec_attend_grads_kernel(packed_ref, grad_ref, marks_ref, out_ref):
    positions, _, width = grad_ref.shape
    queries, keys, values = codec_parts(packed_ref, width)
    marks = marks_ref[...]
    pairs = position_pairs(positions)
    portions = codec_portions(queries, keys, marks, pairs)
    grads = [grad_ref[t].astype(F32) for t in range(positions)]
    portion_grads = dict(
        zip(
            pairs,
            codec_sums([grads[later] * values[earlier].astype(F32) for later, earlier in pairs], marks),
        )
    )
    score_grads = {}
    for later in range(1, positions):
        mean = functools.reduce(
            jnp.add, [portions[later, e] * portion_grads[later, e] for e in range(later + 1)]
        )
        for e in range(later + 1):
            score_grads[later, e] = portions[later, e] * (portion_grads[later, e] - mean)
    wide = dict(zip(pairs, codec_spread([portions[pair] for pair in pairs], marks)))
    wide_grads = dict(zip(pairs, codec_spread([score_grads[pair] for pair in pairs], marks)))
    zero = jnp.zeros_like(grads[0])
    for t in range(positions):
        query_grad = key_grad = zero
        value_grad = grads[0] if t == 0 else zero
        for later, earlier in pairs:
            if later == t:
                query_grad = query_grad + wide_grads[later, earlier] * keys[earlier].astype(F32)
            if earlier == t:
                key_grad = key_grad + wide_grads[later, earlier] * queries[later].astype(F32)
                value_grad = value_grad + wide[later, earlier] * grads[later]
        out_ref[t, :, :width] = (query_grad * FACTOR).astype(BF)
        out_ref[t, :, width : 2 * width] = (key_grad * FACTOR).astype(BF)
        out_ref[t, :, 2 * width :] = value_grad.astype(BF)


def codec_tile(frame_total):
    return 64 if frame_total % 64 == 0 else frame_total


def codec_spec(positions, tile, breadth):
    return pl.BlockSpec((positions, tile, breadth), lambda i: (0, i, 0))


def head_marks(width):
    return (
        jnp.arange(width)[:, None] // HEAD == jnp.arange(LANES)[None, :]
    ).astype(BF)


def codec_attend_call(packed):
    positions, total, triple = packed.shape
    width = triple // 3
    tile = codec_tile(total)
    return pl.pallas_call(
        codec_attend_kernel,
        grid=(total // tile,),
        in_specs=[codec_spec(positions, tile, triple), whole_block((width, LANES))],
        out_specs=codec_spec(positions, tile, width),
        out_shape=jax.ShapeDtypeStruct((positions, total, width), BF),
        compiler_params=pltpu.CompilerParams(vmem_limit_bytes=VMEM_LIMIT),
        cost_estimate=pl.CostEstimate(
            flops=total * width * LANES * 30, bytes_accessed=packed.size * 3, transcendentals=0
        ),
        name="codec_attend",
    )(packed, head_marks(width))


def codec_attend_grads_call(packed, grads):
    positions, total, triple = packed.shape
    width = triple // 3
    tile = codec_tile(total)
    return pl.pallas_call(
        codec_attend_grads_kernel,
        grid=(total // tile,),
        in_specs=[
            codec_spec(positions, tile, triple),
            codec_spec(positions, tile, width),
            whole_block((width, LANES)),
        ],
        out_specs=codec_spec(positions, tile, triple),
        out_shape=jax.ShapeDtypeStruct((positions, total, triple), BF),
        compiler_params=pltpu.CompilerParams(vmem_limit_bytes=VMEM_LIMIT),
        cost_estimate=pl.CostEstimate(
            flops=total * width * LANES * 70, bytes_accessed=packed.size * 5, transcendentals=0
        ),
        name="codec_attend_grads",
    )(packed, grads, head_marks(width))


def grad_order(place):
    seqs = [place.seq ^ (2 * spot + 1 - side) for side in range(2) for spot in range(4)]
    return jnp.stack([place.mp ^ 2, place.mp] + seqs + [place.seq]).astype(jnp.int32)


def grad_rows_kernel(mp_first, wide, order_ref, far_own, far_rec, own_own, own_rec, latter_own, latter_rec, *refs):
    send_ref, keep_ref, turned = refs[-3:]
    rows = latter_own.shape[0]
    height = far_own.shape[1]

    @pl.when(pl.program_id(0) == 0)
    def _():
        for at, (own, rec) in enumerate(((far_own, far_rec), (own_own, own_rec))):
            turned[height * at : height * (at + 1), :rows] = own[...].T
            turned[height * at : height * (at + 1), rows:] = rec[...].T

    total = matmul(turned[:, :rows], latter_own[...]) + matmul(turned[:, rows:], latter_rec[...])
    grad_rows_store(mp_first, wide, order_ref, total.astype(BF), height, send_ref, keep_ref)


def grad_rows_store(mp_first, wide, order_ref, total, height, send_ref, keep_ref):
    units = height // TILE
    if wide:
        chunks = total.shape[1] // 8 // LANES
        for seq in range(8):
            change = order_ref[10] ^ seq
            side = 1 - (change & 1)
            spot = change >> 1
            for chunk in range(chunks):
                first = (seq * chunks + chunk) * LANES
                value = total[:, first : first + LANES]
                for unit in range(units):
                    given = value[unit * TILE : (unit + 1) * TILE]
                    kept = value[height + unit * TILE : height + (unit + 1) * TILE]
                    at = chunk * units + unit
                    if mp_first:
                        send_ref[side, spot, at] = given
                        keep_ref[side, spot, at] = kept
                    else:

                        @pl.when(side == 0)
                        def _(given=given, kept=kept, at=at, spot=spot):
                            send_ref[0, spot, at] = given
                            send_ref[1, spot, at] = kept

                        @pl.when(side == 1)
                        def _(given=given, kept=kept, at=at, spot=spot):
                            keep_ref[0, spot, at] = given
                            keep_ref[1, spot, at] = kept

        return
    chunks = total.shape[1] // LANES
    for chunk in range(chunks):
        value = total[:, chunk * LANES : (chunk + 1) * LANES]
        given, kept = value[:height], value[height:]
        if mp_first:
            send_ref[0, 0, chunk] = given
            keep_ref[0, 0, chunk] = kept
        else:

            @pl.when(pl.program_id(0) < 4)
            def _(given=given, kept=kept, chunk=chunk):
                send_ref[0, 0, chunk] = given
                send_ref[1, 0, chunk] = kept

            @pl.when(pl.program_id(0) >= 4)
            def _(given=given, kept=kept, chunk=chunk):
                keep_ref[0, 0, chunk] = given
                keep_ref[1, 0, chunk] = kept


def grad_buffers(units):
    return [jax.ShapeDtypeStruct((2, 4, units, TILE, LANES), BF)] * 2


def grad_call(kernel, order, arrays, in_specs, out_specs, units, into, steps, scratch, flops, name):
    aliases = {}
    moved = 2 * sum(array.size for array in arrays)
    if into is not None:
        aliases = {len(arrays) + 1: 0, len(arrays) + 2: 1}
        in_specs = in_specs + [pl.BlockSpec(memory_space=pl.ANY)] * 2
        arrays = arrays + list(into)
    return pl.pallas_call(
        kernel,
        grid_spec=pltpu.PrefetchScalarGridSpec(
            num_scalar_prefetch=1,
            grid=(steps,),
            in_specs=in_specs,
            out_specs=out_specs,
            scratch_shapes=[scratch],
        ),
        out_shape=grad_buffers(units),
        input_output_aliases=aliases,
        compiler_params=pltpu.CompilerParams(vmem_limit_bytes=VMEM_LIMIT),
        cost_estimate=pl.CostEstimate(flops=flops, bytes_accessed=moved, transcendentals=0),
        name=name,
    )(order, *arrays)


def grad_rows(former, latter, order, mp_first, units, offset, into=None):
    rows, breadth = latter[0].shape
    height = former[0].shape[1] // 4
    wide = breadth // 8 == LANES
    chunks = breadth // 8 // LANES
    steps = 1 if wide else 8
    arrays = [former[0], former[1], former[0], former[1], latter[0], latter[1]]
    former_specs = [
        pl.BlockSpec((rows, height), lambda j, t, at=at: (0, t[at]), pipeline_mode=pl.Buffered(1))
        for at in (0, 0, 1, 1)
    ]
    if wide:
        latter_specs = [whole_block((rows, breadth))] * 2
        block = (2, 4, 1, TILE, LANES)
        out_specs = [pl.BlockSpec(block, lambda j, t: (0, 0, offset, 0, 0))] * 2
    else:
        latter_specs = [pl.BlockSpec((rows, breadth // 8), lambda j, t: (0, t[2 + j]))] * 2
        base = offset // chunks
        if mp_first:
            block = (1, 1, chunks, TILE, LANES)
            out_specs = [pl.BlockSpec(block, lambda j, t: (j // 4, j % 4, base, 0, 0))] * 2
        else:
            block = (2, 1, chunks, TILE, LANES)
            out_specs = [
                pl.BlockSpec(block, lambda j, t: (0, jnp.minimum(j, 3), base, 0, 0)),
                pl.BlockSpec(block, lambda j, t: (0, jnp.maximum(j - 4, 0), base, 0, 0)),
            ]
    return grad_call(
        functools.partial(grad_rows_kernel, mp_first, wide),
        order,
        arrays,
        former_specs + latter_specs,
        out_specs,
        units,
        into,
        steps,
        pltpu.VMEM((2 * height, 2 * rows), BF),
        2 * 2 * rows * 2 * height * breadth,
        "grad_rows",
    )


def grad_columns_kernel(order_ref, latter_own, latter_rec, former_own, former_rec, *refs):
    send_ref, keep_ref, turned = refs[-3:]
    rows = latter_own.shape[0]
    step = pl.program_id(0)

    @pl.when(step == 0)
    def _():
        turned[:, :rows] = latter_own[...].T
        turned[:, rows:] = latter_rec[...].T

    total = matmul(turned[:, :rows], former_own[...]) + matmul(turned[:, rows:], former_rec[...])
    total = total.astype(BF)
    chunks = total.shape[1] // LANES
    for target, when in ((send_ref, step < pl.num_programs(0) // 2), (keep_ref, step >= pl.num_programs(0) // 2)):

        @pl.when(when)
        def _(target=target):
            for seq in range(8):
                change = order_ref[10] ^ seq
                side = 1 - (change & 1)
                spot = change >> 1
                for chunk in range(chunks):
                    target[side, spot, chunk // 2, (chunk % 2) * LANES : (chunk % 2 + 1) * LANES] = total[
                        seq * LANES : (seq + 1) * LANES, chunk * LANES : (chunk + 1) * LANES
                    ]


def grad_columns(former, latter, order, units, offset, into=None):
    rows, breadth = latter[0].shape
    height = former[0].shape[1] // 4
    step = min(512, height)
    per = height // step
    block = (2, 4, step // TILE, TILE, LANES)
    base = offset // (step // TILE)
    latter_specs = [
        pl.BlockSpec((rows, breadth), lambda j, t: (0, 0), pipeline_mode=pl.Buffered(1))
    ] * 2
    former_specs = [pl.BlockSpec((rows, step), lambda j, t: (0, t[j // per] * per + j % per))] * 2
    out_specs = [
        pl.BlockSpec(block, lambda j, t: (0, 0, base + jnp.minimum(j, per - 1), 0, 0)),
        pl.BlockSpec(block, lambda j, t: (0, 0, base + jnp.maximum(j - per, 0), 0, 0)),
    ]
    return grad_call(
        grad_columns_kernel,
        order,
        [latter[0], latter[1], former[0], former[1]],
        latter_specs + former_specs,
        out_specs,
        units,
        into,
        2 * per,
        pltpu.VMEM((breadth, 2 * rows), BF),
        2 * 2 * rows * 2 * height * breadth,
        "grad_columns",
    )


def grad_table_kernel(height, order_ref, codes_ref, latter_own, latter_rec, *refs):
    send_ref, keep_ref, _ = refs[-3:]
    rows = latter_own.shape[0]
    parts = []
    for at in range(2):
        entry = order_ref[at] * height + lax.broadcasted_iota(jnp.int32, (height, 2 * rows), 0)
        parts.append((entry == codes_ref[...]).astype(F32).astype(BF))
    chosen = jnp.concatenate(parts, axis=0)
    total = matmul(chosen[:, :rows], latter_own[...]) + matmul(chosen[:, rows:], latter_rec[...])
    grad_rows_store(False, True, order_ref, total.astype(BF), height, send_ref, keep_ref)


def grad_table(codes, latter, order, height, units, offset, into=None):
    rows, breadth = latter[0].shape
    block = (2, 4, height // TILE, TILE, LANES)
    base = offset // (height // TILE)
    return grad_call(
        functools.partial(grad_table_kernel, height),
        order,
        [codes, latter[0], latter[1]],
        [whole_block(codes.shape), whole_block((rows, breadth)), whole_block((rows, breadth))],
        [pl.BlockSpec(block, lambda j, t: (0, 0, base, 0, 0))] * 2,
        units,
        into,
        1,
        pltpu.VMEM((8, LANES), F32),
        2 * 2 * rows * 2 * height * breadth,
        "grad_table",
    )


def reduce_blocks(send, keep, mp_first):
    stages = (("mp", 2), ("seq", 1)) if mp_first else (("seq", 1), ("mp", 2))
    first = swap(send, *stages[0])
    given = (keep[0].astype(F32) + first[0].astype(F32)).astype(BF)
    second = swap(given, *stages[1])
    total = (keep[1].astype(F32) + first[1].astype(F32) + second.astype(F32)).astype(BF)
    far = swap(total[2:], "seq", 4)
    total = total[:2].astype(F32) + far.astype(F32)
    near = swap(total[1].astype(BF), "seq", 2)
    return total[0] + near.astype(F32)


def rows_from_units(units, height):
    tiles = height // TILE
    chunks = units.shape[0] // tiles
    return jnp.transpose(
        units.reshape(chunks, height, LANES), (1, 0, 2)
    ).reshape(height, chunks * LANES)


def columns_from_units(units):
    count = units.shape[0]
    return jnp.transpose(units.reshape(2 * count, LANES, LANES), (0, 2, 1)).reshape(count * TILE, LANES)


def join_kernel(layout, place_ref, *refs):
    count = len(layout)
    own, other, first, second, first_other, second_other = refs[:6]
    outs = refs[6 : 6 + count]
    held = refs[6 + count : 6 + 2 * count]
    sems, out_sems = refs[-2:]
    half = first.shape[0]
    width = own.shape[1]
    me = place_ref[0]
    low = place_ref[1]
    copies = []
    for at, (height, breadth, start) in enumerate(layout):
        for column in range(breadth // width):
            row = start + column * height
            columns = pl.ds(column * width, width)
            for flip, source in ((0, own), (1, other)):
                target = held[at].at[pl.ds(pl.multiple_of((me ^ flip) * height, height), height), columns]
                copies.append((at, None, source.at[pl.ds(row, height)], target))
            for flip, sources in ((2, (first, second)), (3, (first_other, second_other))):
                for side in range(2):
                    begin, end = max(row, side * half), min(row + height, (side + 1) * half)
                    if begin >= end:
                        continue
                    rows = pl.ds(begin - side * half, end - begin)
                    target = held[at].at[
                        pl.ds(pl.multiple_of((me ^ flip) * height + begin - row, 16), end - begin), columns
                    ]
                    copies.append((at, side, sources[0].at[rows], target))
                    copies.append((at, 1 - side, sources[1].at[rows], target))

    def act(action, number):
        _, when, source, target = copies[number]
        copy = pltpu.make_async_copy(source, target, sems.at[number])
        if when is None:
            getattr(copy, action)()
        else:

            @pl.when(low == when)
            def _():
                getattr(copy, action)()

    for number in range(len(copies)):
        act("start", number)
    for at in range(count):
        for number in range(len(copies)):
            if copies[number][0] == at:
                act("wait", number)
        pltpu.make_async_copy(held[at], outs[at], out_sems.at[at]).start()
    for at in range(count):
        pltpu.make_async_copy(held[at], outs[at], out_sems.at[at]).wait()


def join_count(layout, half, width):
    count = 0
    for height, breadth, start in layout:
        for column in range(breadth // width):
            row = start + column * height
            count += 2
            for side in range(2):
                if max(row, side * half) < min(row + height, (side + 1) * half):
                    count += 4
    return count


def pack_weights(shards):
    width = 1024
    pieces = []
    for shard in shards:
        for column in range(shard.shape[1] // width):
            pieces.append(shard[:, column * width : (column + 1) * width])
    return pieces[0] if len(pieces) == 1 else jnp.concatenate(pieces, axis=0)


def pack_layout(shards):
    layout, start = [], 0
    for shard in shards:
        height, breadth = shard.shape
        layout.append((height, breadth, start))
        start += height * (breadth // 1024)
    return tuple(layout), start


def join_weights(pack, other, first, second, first_other, second_other, layout, place):
    half, width = first.shape
    any_spec = pl.BlockSpec(memory_space=pl.ANY)
    outs = [jax.ShapeDtypeStruct((4 * height, breadth), BF) for height, breadth, _ in layout]
    return pl.pallas_call(
        functools.partial(join_kernel, layout),
        in_specs=[pl.BlockSpec(memory_space=pltpu.SMEM)] + [any_spec] * 6,
        out_specs=[any_spec] * len(outs),
        out_shape=outs,
        scratch_shapes=[pltpu.VMEM(out.shape, BF) for out in outs]
        + [
            pltpu.SemaphoreType.DMA((join_count(layout, half, width),)),
            pltpu.SemaphoreType.DMA((len(outs),)),
        ],
        compiler_params=pltpu.CompilerParams(vmem_limit_bytes=VMEM_LIMIT),
        cost_estimate=pl.CostEstimate(flops=0, bytes_accessed=16 * pack.size, transcendentals=0),
        name="join_weights",
    )(
        jnp.stack([place.mp, place.seq_low]).astype(jnp.int32),
        pack,
        other,
        first,
        second,
        first_other,
        second_other,
    )


def shards_general(
    frames,
    segments,
    padding,
    codec_tokens,
    codebooks,
    frame_prenorm,
    frame_project,
    frame_output,
    frame_postnorm,
    frame_expand,
    frame_contract,
    codec_prenorm,
    codec_project,
    codec_output,
    codec_postnorm,
    codec_expand,
    codec_contract,
    cotangent,
):
    place = Place()
    row_count, frames_dev, width = frames.shape
    frame_total = row_count * frames_dev
    positions = cotangent.shape[2]
    gains = lax.all_gather(
        jnp.stack([frame_prenorm, frame_postnorm, codec_prenorm, codec_postnorm]),
        "mp",
        axis=1,
        tiled=True,
    )
    frame_weights = (
        gains[0],
        gather_weight(frame_project, place),
        gather_weight(frame_output, place),
        gains[1],
        gather_weight(frame_expand, place),
        gather_weight(frame_contract, place),
    )
    codec_weights = (
        gains[2],
        gather_weight(codec_project, place),
        gather_weight(codec_output, place),
        gains[3],
        gather_weight(codec_expand, place),
        gather_weight(codec_contract, place),
    )
    table = gather_weight(codebooks, place)

    hidden = frames.astype(F32).reshape(frame_total, width)
    normed, projected = front_pass(hidden, frame_weights)
    attended, attention_back = frame_attention(
        projected.reshape(row_count, frames_dev, 3 * width), segments, place
    )
    attended = attended.reshape(frame_total, width)
    frame_result, frame_saved = rear_pass(hidden, attended, frame_weights)
    base = frame_result.astype(BF).astype(F32)

    table_rows = codec_tokens.reshape(positions - 1, frame_total) + (
        jnp.arange(positions - 1, dtype=jnp.int32) * CODES
    )[:, None]
    embedded = table[table_rows].astype(F32)
    codec_hidden = jnp.concatenate([base[None], base[None] + embedded], axis=0).reshape(
        positions * frame_total, width
    )
    codec_normed, codec_projected = front_pass(codec_hidden, codec_weights)
    marks = (
        jnp.arange(width)[:, None] // HEAD == jnp.arange(HEADS)[None, :]
    ).astype(F32)
    view = codec_projected.reshape(positions, frame_total, 3, width)
    queries, keys, values = ([view[t, :, part] for t in range(positions)] for part in range(3))
    soft = codec_softmax(queries, keys, marks)
    codec_attended = jnp.concatenate(codec_attend(soft, values, marks), axis=0)
    codec_result, codec_saved = rear_pass(codec_hidden, codec_attended, codec_weights)
    live = padding.reshape(frame_total).astype(F32)[None, :, None]
    output = jnp.transpose(
        (codec_result.reshape(positions, frame_total, width) * live).astype(BF), (1, 0, 2)
    ).reshape(row_count, frames_dev, positions, width)

    codec_grad = (
        jnp.transpose(cotangent.reshape(frame_total, positions, width), (1, 0, 2)).astype(F32) * live
    ).reshape(positions * frame_total, width)
    mixed_grad, attended_grad, codec_postnorm_grad, contract_in, expand_in, output_in = rear_grads(
        codec_grad, codec_saved, codec_weights
    )
    codec_contract_part = weight_grad(codec_saved[3], contract_in, place, True)
    codec_expand_part = weight_grad(codec_saved[1], expand_in, place, False)
    codec_output_part = weight_grad(codec_attended, output_in, place, True)
    grad_view = attended_grad.reshape(positions, frame_total, width)
    codec_projected_grad = codec_attend_grads(
        soft, queries, keys, values, [grad_view[t] for t in range(positions)], marks
    )
    codec_project_part = weight_grad(codec_normed, codec_projected_grad, place, True)
    input_grad, codec_prenorm_grad = front_grads(
        codec_hidden, codec_projected_grad, mixed_grad, codec_weights
    )
    input_grad = input_grad.reshape(positions, frame_total, width)
    chosen = (
        table_rows.reshape(-1)[:, None] == jnp.arange(table.shape[0], dtype=jnp.int32)[None, :]
    ).astype(BF)
    table_part = weight_grad(chosen, input_grad[1:].reshape(-1, width).astype(BF), place, False)
    base_grad = jnp.sum(input_grad, axis=0).astype(BF).astype(F32)

    (codec_contract_grad,) = finish_grads([codec_contract_part], place)
    codec_expand_grad, codec_output_grad, codec_project_grad = finish_grads(
        [codec_expand_part, codec_output_part, codec_project_part], place
    )
    (table_grad,) = finish_grads([table_part], place)

    frame_mixed_grad, frame_attended_grad, frame_postnorm_grad, contract_in, expand_in, output_in = (
        rear_grads(base_grad, frame_saved, frame_weights)
    )
    frame_projected_grad = attention_back(
        frame_attended_grad.reshape(row_count, frames_dev, width)
    ).reshape(frame_total, 3 * width)
    frame_contract_part = weight_grad(frame_saved[3], contract_in, place, True)
    frame_expand_part = weight_grad(frame_saved[1], expand_in, place, False)
    frame_output_part = weight_grad(attended, output_in, place, True)
    frame_project_part = weight_grad(normed, frame_projected_grad, place, True)
    frames_grad, frame_prenorm_grad = front_grads(
        hidden, frame_projected_grad, frame_mixed_grad, frame_weights
    )
    (frame_contract_grad,) = finish_grads([frame_contract_part], place)
    frame_expand_grad, frame_output_grad = finish_grads(
        [frame_expand_part, frame_output_part], place
    )
    (frame_project_grad,) = finish_grads([frame_project_part], place)
    gain_sums = sum_everywhere(
        jnp.stack(
            [frame_prenorm_grad, frame_postnorm_grad, codec_prenorm_grad, codec_postnorm_grad]
        ),
        place,
    )
    return (
        output,
        frames_grad.reshape(row_count, frames_dev, width),
        table_grad,
        gain_sums[0],
        frame_project_grad,
        frame_output_grad,
        gain_sums[1],
        frame_expand_grad,
        frame_contract_grad,
        gain_sums[2],
        codec_project_grad,
        codec_output_grad,
        gain_sums[3],
        codec_expand_grad,
        codec_contract_grad,
    )


def tie(values, *after):
    flat, tree = jax.tree.flatten(values)
    held = lax.optimization_barrier(tuple(flat) + tuple(after))
    return jax.tree.unflatten(tree, held[: len(flat)])


def start_pack(pack, place, *after):
    half = pack.shape[0] // 2
    mine = lax.dynamic_slice(pack, (place.seq_low * half, 0), (half, pack.shape[1]))
    if after:
        pack, mine = tie((pack, mine), *after)
    first = swap(mine, "mp", 2)
    other = swap(pack, "mp", 1)
    second = swap(first, "seq", 1)
    return [pack, other, first, second, swap(first, "mp", 1), swap(second, "mp", 1)]


def pair(values):
    return (values, swap(values, "mp", 1))


def shards(
    frames,
    segments,
    padding,
    codec_tokens,
    codebooks,
    frame_prenorm,
    frame_project,
    frame_output,
    frame_postnorm,
    frame_expand,
    frame_contract,
    codec_prenorm,
    codec_project,
    codec_output,
    codec_postnorm,
    codec_expand,
    codec_contract,
    cotangent,
):
    place = Place()
    order = grad_order(place)
    row_count, frames_dev, width = frames.shape
    frame_total = row_count * frames_dev
    positions = cotangent.shape[2]

    packs = (
        [frame_project],
        [frame_expand, frame_contract, frame_output],
        [codec_project, codebooks],
        [codec_expand, codec_contract, codec_output],
    )
    pieces = []
    for members in packs:
        pack = pack_weights(members)
        pieces.append(start_pack(pack, place, *([pieces[-1][2]] if pieces else [])))

    def joined(at):
        return join_weights(*pieces[at], pack_layout(packs[at])[0], place)

    gains = lax.all_gather(
        jnp.stack([frame_prenorm, frame_postnorm, codec_prenorm, codec_postnorm]),
        "mp",
        axis=1,
        tiled=True,
    )
    every_segment = lax.all_gather(segments, "seq", axis=1, tiled=True)
    codes = codec_tokens.reshape(1, (positions - 1) * frame_total) + jnp.repeat(
        jnp.arange(positions - 1, dtype=jnp.int32) * CODES, frame_total
    )
    codes_both = jnp.concatenate(pair(codes), axis=1)
    live = padding.reshape(frame_total).astype(F32)[None, :, None]
    codec_grad = (
        jnp.transpose(cotangent.reshape(frame_total, positions, width), (1, 0, 2)).astype(F32) * live
    ).reshape(positions * frame_total, width)
    contract_in = pair(codec_grad.astype(BF))

    (weight_project,) = joined(0)
    hidden = frames.astype(F32).reshape(frame_total, width)
    normed, projected = front_pass(hidden, (gains[0], weight_project))
    normed_both = pair(normed)
    count = place.seq_count
    packed = jnp.transpose(
        projected.reshape(row_count, frames_dev, 3, count, LANES), (3, 0, 1, 2, 4)
    ).reshape(count, row_count, frames_dev, 3 * LANES)
    packed = lax.all_to_all(packed, "seq", split_axis=0, concat_axis=0, tiled=True)
    attended = lax.all_to_all(
        frame_attend_call(packed, every_segment), "seq", split_axis=0, concat_axis=0, tiled=True
    )
    attended = jnp.transpose(attended, (1, 2, 0, 3)).reshape(frame_total, width)
    attended_both = pair(attended)
    weight_expand, weight_contract, weight_output = joined(1)
    frame_weights = (gains[0], weight_project, weight_output, gains[1], weight_expand, weight_contract)
    frame_result, frame_saved = rear_pass(hidden, attended, frame_weights)
    normed_two_both = pair(frame_saved[1])
    activated_both = pair(frame_saved[3])
    base = frame_result.astype(BF).astype(F32)

    weight_project, table = joined(2)
    embedded = table[codes.reshape(positions - 1, frame_total)].astype(F32)
    codec_hidden = jnp.concatenate([base[None], base[None] + embedded], axis=0).reshape(
        positions * frame_total, width
    )
    codec_normed, codec_projected = front_pass(codec_hidden, (gains[2], weight_project))
    codec_normed_both = pair(codec_normed)
    codec_packed = codec_projected.reshape(positions, frame_total, 3 * width)
    codec_attended = codec_attend_call(codec_packed).reshape(positions * frame_total, width)
    codec_attended_both = pair(codec_attended)
    weight_expand, weight_contract, weight_output = joined(3)
    codec_weights = (gains[2], weight_project, weight_output, gains[3], weight_expand, weight_contract)
    codec_result, codec_saved = rear_pass(codec_hidden, codec_attended, codec_weights)
    codec_normed_two_both = pair(codec_saved[1])
    codec_activated_both = pair(codec_saved[3])
    output = jnp.transpose(
        (codec_result.reshape(positions, frame_total, width) * live).astype(BF), (1, 0, 2)
    ).reshape(row_count, frames_dev, positions, width)

    mixed_grad, attended_grad, codec_postnorm_grad, _, expand_in, output_in = rear_grads(
        codec_grad, codec_saved, codec_weights
    )
    output_in = pair(output_in)
    codec_one = grad_rows(codec_normed_two_both, pair(expand_in), order, True, 8, 0)
    codec_one = grad_columns(codec_activated_both, contract_in, order, 8, 4, codec_one)
    codec_one = reduce_blocks(*codec_one, True)
    codec_projected_grad = codec_attend_grads_call(
        codec_packed, attended_grad.reshape(positions, frame_total, width)
    ).reshape(positions * frame_total, 3 * width)
    codec_two = grad_rows(codec_normed_both, pair(codec_projected_grad), order, False, 6, 0)
    codec_two = grad_rows(codec_attended_both, output_in, order, False, 6, 3, codec_two)
    input_grad, codec_prenorm_grad = front_grads(
        codec_hidden, codec_projected_grad, mixed_grad, codec_weights
    )
    input_grad = input_grad.reshape(positions, frame_total, width)
    table_in = pair(input_grad[1:].reshape(-1, width).astype(BF))
    codec_two = grad_table(codes_both, table_in, order, codebooks.shape[0], 6, 4, codec_two)
    codec_two = reduce_blocks(*codec_two, False)
    base_grad = jnp.sum(input_grad, axis=0).astype(BF).astype(F32)

    (
        frame_mixed_grad,
        frame_attended_grad,
        frame_postnorm_grad,
        contract_in,
        expand_in,
        output_in,
    ) = rear_grads(base_grad, frame_saved, frame_weights)
    grads = lax.all_to_all(
        jnp.transpose(
            frame_attended_grad.reshape(row_count, frames_dev, count, LANES), (2, 0, 1, 3)
        ),
        "seq",
        split_axis=0,
        concat_axis=0,
        tiled=True,
    )
    frame_one = grad_rows(normed_two_both, pair(expand_in), order, True, 8, 0)
    frame_one = grad_columns(activated_both, pair(contract_in), order, 8, 4, frame_one)
    frame_one = reduce_blocks(*frame_one, True)
    packed_grad = lax.all_to_all(
        frame_attend_grads_call(packed, grads, every_segment),
        "seq",
        split_axis=0,
        concat_axis=0,
        tiled=True,
    )
    frame_projected_grad = jnp.transpose(
        packed_grad.reshape(count, row_count, frames_dev, 3, LANES), (1, 2, 3, 0, 4)
    ).reshape(frame_total, 3 * width)
    frame_two = grad_rows(normed_both, pair(frame_projected_grad), order, False, 4, 0)
    frame_two = grad_rows(attended_both, pair(output_in), order, False, 4, 3, frame_two)
    frame_two = reduce_blocks(*frame_two, False)
    frames_grad, frame_prenorm_grad = front_grads(
        hidden, frame_projected_grad, frame_mixed_grad, frame_weights
    )
    gain_sums = sum_everywhere(
        jnp.stack(
            [frame_prenorm_grad, frame_postnorm_grad, codec_prenorm_grad, codec_postnorm_grad]
        ),
        place,
    )
    height = frame_project.shape[0]
    return (
        output,
        frames_grad.reshape(row_count, frames_dev, width),
        rows_from_units(codec_two[4:], codebooks.shape[0]),
        gain_sums[0],
        rows_from_units(frame_two[:3], height),
        rows_from_units(frame_two[3:], height),
        gain_sums[1],
        rows_from_units(frame_one[:4], height),
        columns_from_units(frame_one[4:]),
        gain_sums[2],
        rows_from_units(codec_two[:3], height),
        rows_from_units(codec_two[3:4], height),
        gain_sums[3],
        rows_from_units(codec_one[:4], height),
        columns_from_units(codec_one[4:]),
    )


def solution(mesh):
    placed = (
        P("mp", "seq", None),
        P("mp", "seq"),
        P("mp", "seq"),
        P(None, "mp", "seq"),
        P("mp", None),
        P("mp"),
        P("mp", None),
        P("mp", None),
        P("mp"),
        P("mp", None),
        P("mp", None),
        P("mp"),
        P("mp", None),
        P("mp", None),
        P("mp"),
        P("mp", None),
        P("mp", None),
        P("mp", "seq", None, None),
    )
    small = mesh.shape["seq"] == 8 and mesh.shape["mp"] == 4
    return jax.shard_map(
        shards if small else shards_general,
        mesh=mesh,
        in_specs=placed,
        out_specs=(
            P("mp", "seq", None, None),
            P("mp", "seq", None),
            P("mp", "seq"),
            P(),
            P("mp", "seq"),
            P("mp", "seq"),
            P(),
            P("mp", "seq"),
            P("mp", "seq"),
            P(),
            P("mp", "seq"),
            P("mp", "seq"),
            P(),
            P("mp", "seq"),
            P("mp", "seq"),
        ),
        check_vma=False,
    )
```

```python
import functools

import jax
import jax.numpy as jnp
from jax import lax
from jax.experimental import pallas as pl
from jax.experimental.pallas import tpu as pltpu
from jax.sharding import PartitionSpec as P

HEADS = 16
HEAD = 64
CODES = 1024


EPSILON = 1e-05
MASKED = -1e30
FACTOR = HEAD ** (-0.5)

BF = jnp.bfloat16
F32 = jnp.float32


def rms_scale(values, gain_vec):
    return (
        values * lax.rsqrt(jnp.mean(values * values, axis=-1, keepdims=True) + EPSILON) * gain_vec
    )


def matmul(former, latter):
    return jnp.dot(former, latter, preferred_element_type=F32)


def inner_left(former, latter):
    return lax.dot_general(former, latter, (((0,), (0,)), ((), ())), preferred_element_type=F32)


def inner_right(former, latter):
    return lax.dot_general(former, latter, (((1,), (1,)), ((), ())), preferred_element_type=F32)


def split_heads(values):
    return values.reshape(values.shape[:-1] + (-1, HEAD))


def swap(values, axis, bit):
    return lax.ppermute(values, axis, [(i, i ^ bit) for i in range(lax.axis_size(axis))])


def pick(values, index, axis):
    return lax.dynamic_index_in_dim(values, index, axis, keepdims=False)


class Place:
    def __init__(self):
        self.seq_count = lax.axis_size("seq")
        self.mp_count = lax.axis_size("mp")
        self.seq = lax.axis_index("seq")
        self.mp = lax.axis_index("mp")
        self.seq_low = self.seq % 2


def gather_weight(shard, place):
    height, breadth = shard.shape
    half = height // 2
    mine = lax.dynamic_slice(shard, (place.seq_low * half, 0), (half, breadth))
    first = swap(mine, "mp", 2)
    second = swap(first, "seq", 1)
    near_other = swap(shard, "mp", 1)
    far = jnp.zeros((height, breadth), shard.dtype)
    far = lax.dynamic_update_slice(far, first, (place.seq_low * half, 0))
    far = lax.dynamic_update_slice(far, second, ((1 - place.seq_low) * half, 0))
    far_other = swap(far, "mp", 1)
    whole = jnp.zeros((height * place.mp_count, breadth), shard.dtype)
    for flip, piece in ((0, shard), (1, near_other), (2, far), (3, far_other)):
        whole = lax.dynamic_update_slice(whole, piece, ((place.mp ^ flip) * height, 0))
    return whole


def line_scatter(blocks, place):
    count = place.seq_count // 2
    position = place.seq // 2
    size = 2 * count
    state = blocks
    up_in = down_in = None
    for step in range(1, count):
        up_index = jnp.clip(count - step + position, 0, count - 1)
        down_index = jnp.clip(step - 1 - (count - 1 - position), 0, count - 1)
        up_perm = [(i, i + 2) for i in range(size - 2) if i // 2 < step]
        down_perm = [(i, i - 2) for i in range(2, size) if (count - 1 - i // 2) < step]
        up_out = pick(blocks, up_index, 1)
        down_out = pick(blocks, down_index, 1)
        if up_in is not None:
            up_out = up_out + up_in
            down_out = down_out + down_in
        up_in = lax.ppermute(up_out, "seq", up_perm)
        down_in = lax.ppermute(down_out, "seq", down_perm)
    own = pick(blocks, position, 1).astype(F32)
    return own + up_in.astype(F32) + down_in.astype(F32)


def weight_grad(former, latter, place, seq_first):
    height = former.shape[1] // place.mp_count
    rows = former.shape[0]
    breadth = latter.shape[1] // place.seq_count
    low = place.seq_low
    view = latter.reshape(rows, place.seq_count // 2, 2, breadth)
    half = breadth * (place.seq_count // 2)
    give = pick(view, 1 - low, 2).reshape(rows, half)
    keep = pick(view, low, 2).reshape(rows, half)
    both = jnp.concatenate([give, keep], axis=1)

    def columns(flip):
        return lax.dynamic_slice(former, (0, (place.mp ^ flip) * height), (rows, height))

    own, other, far, far_other = (columns(flip) for flip in (0, 1, 2, 3))
    part = inner_left(jnp.concatenate([far_other, other], axis=1), both).astype(BF)
    part = swap(part, "mp", 1).astype(F32)
    if seq_first:
        send = inner_left(jnp.concatenate([far, own], axis=1), give) + part[:, :half]
        low_in = swap(send.astype(BF), "seq", 1).astype(F32)
        send = inner_left(far, keep) + part[:height, half:] + low_in[:height]
        far_in = swap(send.astype(BF), "mp", 2).astype(F32)
        total = inner_left(own, keep) + part[height:, half:] + low_in[height:] + far_in
    else:
        send = inner_left(far, both) + part[:height]
        far_in = swap(send.astype(BF), "mp", 2).astype(F32)
        send = inner_left(own, give) + part[height:, :half] + far_in[:, :half]
        low_in = swap(send.astype(BF), "seq", 1).astype(F32)
        total = inner_left(own, keep) + part[height:, half:] + far_in[:, half:] + low_in
    return total.astype(BF).reshape(height, place.seq_count // 2, breadth)


def finish_grads(partials, place):
    sizes = [part.shape[2] for part in partials]
    total = line_scatter(jnp.concatenate(partials, axis=2), place)
    pieces, start = [], 0
    for size in sizes:
        pieces.append(total[:, start : start + size])
        start += size
    return pieces


def sum_everywhere(values, place):
    for axis, count in (("mp", place.mp_count), ("seq", place.seq_count)):
        bit = 1
        while bit < count:
            values = values + swap(values, axis, bit)
            bit *= 2
    return values


def front_pass(hidden, weights):
    normed = rms_scale(hidden, weights[0].astype(F32)).astype(BF)
    projected = matmul(normed, weights[1]).astype(BF)
    return (normed, projected)


def rear_pass(hidden, attended, weights):
    mixed_sum = hidden + matmul(attended, weights[2])
    normed_two = rms_scale(mixed_sum, weights[3].astype(F32)).astype(BF)
    expanded = matmul(normed_two, weights[4])
    activated = jax.nn.gelu(expanded).astype(BF)
    result = mixed_sum + matmul(activated, weights[5])
    return (result, (mixed_sum, normed_two, expanded, activated))


def rear_grads(result_grad, saved_state, weights):
    mixed_sum, normed_two, expanded, activated = saved_state
    contract_input = result_grad.astype(BF)
    active_grad = inner_right(contract_input, weights[5])
    expand_input = jax.vjp(jax.nn.gelu, expanded)[1](active_grad)[0].astype(BF)
    normed_grad = inner_right(expand_input, weights[4])
    mixed_part, postnorm_grad = jax.vjp(rms_scale, mixed_sum, weights[3].astype(F32))[1](
        normed_grad
    )
    mixed_grad = result_grad + mixed_part
    output_input = mixed_grad.astype(BF)
    attended_grad = inner_right(output_input, weights[2]).astype(BF)
    return (mixed_grad, attended_grad, postnorm_grad, contract_input, expand_input, output_input)


def front_grads(hidden, projected_grad, mixed_grad, weights):
    normed_grad = inner_right(projected_grad, weights[1])
    hidden_part, prenorm_grad = jax.vjp(rms_scale, hidden, weights[0].astype(F32))[1](normed_grad)
    return (mixed_grad + hidden_part, prenorm_grad)


def portions_of(queries, keys, allowed):
    scores = jnp.einsum("ihd,jhd->hij", queries, keys, preferred_element_type=F32) * FACTOR
    return jax.nn.softmax(jnp.where(allowed[None], scores, MASKED), axis=-1)


def attend(queries, keys, values, allowed):
    portions = portions_of(queries, keys, allowed)
    return jnp.einsum(
        "hij,jhd->ihd", portions.astype(BF), values, preferred_element_type=F32
    ).astype(BF)


def attend_grads(queries, keys, values, allowed, out_grad):
    portions = portions_of(queries, keys, allowed)
    portion_grad = jnp.einsum("ihd,jhd->hij", out_grad, values, preferred_element_type=F32)
    score_grad = (
        portions * (portion_grad - jnp.sum(portions * portion_grad, axis=-1, keepdims=True))
    ).astype(BF)
    query_grad = (
        jnp.einsum("hij,jhd->ihd", score_grad, keys, preferred_element_type=F32) * FACTOR
    )
    key_grad = (
        jnp.einsum("hij,ihd->jhd", score_grad, queries, preferred_element_type=F32) * FACTOR
    )
    value_grad = jnp.einsum("hij,ihd->jhd", portions.astype(BF), out_grad, preferred_element_type=F32)
    return query_grad, key_grad, value_grad


def to_heads(values, place):
    rows, own, parts, width = values.shape
    count = place.seq_count
    view = values.reshape(rows, own, parts, count, width // count)
    moved = lax.all_to_all(
        jnp.transpose(view, (3, 0, 1, 2, 4)), "seq", split_axis=0, concat_axis=0, tiled=True
    )
    return jnp.transpose(moved, (1, 0, 2, 3, 4)).reshape(rows, count * own, parts, width // count)


def to_frames(values, place):
    rows, total, parts, width = values.shape
    count = place.seq_count
    view = values.reshape(rows, count, total // count, parts, width)
    moved = lax.all_to_all(
        jnp.transpose(view, (1, 0, 2, 3, 4)), "seq", split_axis=0, concat_axis=0, tiled=True
    )
    return jnp.transpose(moved, (1, 2, 3, 0, 4)).reshape(
        rows, total // count, parts, count * width
    )


def allowed_of(query_seg, key_seg, query_pos, key_pos):
    return (query_seg[:, None] == key_seg[None, :]) & (key_pos[None, :] <= query_pos[:, None])


def frame_attention(projected, segments, place):
    rows, own, triple = projected.shape
    width = triple // 3
    parts = projected.reshape(rows, own, 3, width)
    every_segment = lax.all_gather(segments, "seq", axis=1, tiled=True)
    every_pos = jnp.arange(own * place.seq_count)
    if HEADS % place.seq_count == 0:
        packed = to_heads(parts, place)
        sets = [split_heads(packed[:, :, part]) for part in range(3)]

        def one_row(items):
            queries, keys, values, segs = items
            return attend(queries, keys, values, allowed_of(segs, segs, every_pos, every_pos))

        attended = lax.map(one_row, (*sets, every_segment))
        attended = to_frames(attended.reshape(rows, own * place.seq_count, 1, -1), place)

        def backward(out_grad):
            grads = to_heads(out_grad.reshape(rows, own, 1, width), place)[:, :, 0]

            def one_row(items):
                queries, keys, values, segs, grad = items
                return attend_grads(
                    queries, keys, values, allowed_of(segs, segs, every_pos, every_pos), grad
                )

            found = lax.map(one_row, (*sets, every_segment, split_heads(grads)))
            packed_grad = jnp.stack(
                [grad.reshape(rows, own * place.seq_count, -1) for grad in found], axis=2
            ).astype(BF)
            return to_frames(packed_grad, place).reshape(rows, own, triple)

        return attended.reshape(rows, own, width), backward

    keys = lax.all_gather(parts[:, :, 1], "seq", axis=1, tiled=True)
    values = lax.all_gather(parts[:, :, 2], "seq", axis=1, tiled=True)
    sets = (split_heads(parts[:, :, 0]), split_heads(keys), split_heads(values))
    own_pos = place.seq * own + jnp.arange(own)

    def one_row(items):
        row_q, row_k, row_v, own_segs, segs = items
        return attend(row_q, row_k, row_v, allowed_of(own_segs, segs, own_pos, every_pos))

    attended = lax.map(one_row, (*sets, segments, every_segment)).reshape(rows, own, width)

    def backward(out_grad):
        def one_row(items):
            row_q, row_k, row_v, own_segs, segs, grad = items
            allowed = allowed_of(own_segs, segs, own_pos, every_pos)
            return attend_grads(row_q, row_k, row_v, allowed, grad)

        query_grad, key_grad, value_grad = lax.map(
            one_row, (*sets, segments, every_segment, split_heads(out_grad))
        )
        both = jnp.stack([key_grad.reshape(rows, -1, width), value_grad.reshape(rows, -1, width)], 2)
        both = lax.psum_scatter(both, "seq", scatter_dimension=1, tiled=True)
        parts_grad = [query_grad.reshape(rows, own, width), both[:, :, 0], both[:, :, 1]]
        return jnp.concatenate(parts_grad, axis=-1).astype(BF)

    return attended, backward


def head_sums(values, marks):
    return jnp.dot(values, marks, precision=lax.Precision.HIGHEST, preferred_element_type=F32)


def head_spread(values, marks):
    return lax.dot_general(
        values.astype(BF), marks.astype(BF), (((1,), (1,)), ((), ())), preferred_element_type=F32
    )


def codec_softmax(queries, keys, marks):
    result = []
    for later in range(len(queries)):
        scores = [
            head_sums(queries[later].astype(F32) * keys[earlier].astype(F32), marks) * FACTOR
            for earlier in range(later + 1)
        ]
        top = scores[0]
        for score in scores[1:]:
            top = jnp.maximum(top, score)
        powers = [jnp.exp(score - top) for score in scores]
        total = sum(powers)
        result.append([power / total for power in powers])
    return result


def codec_attend(soft, values, marks):
    result = []
    for row in soft:
        total = 0.0
        for earlier, portion in enumerate(row):
            total = total + head_spread(portion, marks) * values[earlier].astype(F32)
        result.append(total.astype(BF))
    return result


def codec_attend_grads(soft, queries, keys, values, grads, marks):
    count = len(queries)
    query_grad = []
    key_grad = [0.0] * count
    value_grad = [0.0] * count
    for later in range(count):
        grad = grads[later].astype(F32)
        portion_grads = [
            head_sums(grad * values[earlier].astype(F32), marks) for earlier in range(later + 1)
        ]
        mean = sum(soft[later][i] * portion_grads[i] for i in range(later + 1))
        total = 0.0
        for earlier in range(later + 1):
            score_grad = soft[later][earlier] * (portion_grads[earlier] - mean)
            wide = head_spread(score_grad, marks)
            total = total + wide * keys[earlier].astype(F32)
            key_grad[earlier] = key_grad[earlier] + wide * queries[later].astype(F32)
            value_grad[earlier] = value_grad[earlier] + head_spread(soft[later][earlier], marks) * grad
        query_grad.append(total * FACTOR)
    return jnp.concatenate(
        [
            jnp.concatenate(
                [query_grad[t], key_grad[t] * FACTOR, value_grad[t]], axis=-1
            ).astype(BF)
            for t in range(count)
        ],
        axis=0,
    )


LANES = 128
TILE = 256
VMEM_LIMIT = 48 * 1024 * 1024


def whole_block(shape):
    return pl.BlockSpec(shape, lambda *_: (0,) * len(shape))


def causal_tiles(length):
    tile = min(TILE, length)
    return [(start, tile, start + tile) for start in range(0, length, tile)]


def head_masks(dtype):
    lane = lax.broadcasted_iota(jnp.int32, (1, LANES), 1)
    return [((lane // HEAD) == head).astype(dtype) for head in range(LANES // HEAD)]


def frame_attend_kernel(packed_ref, seg_col_ref, seg_row_ref, out_ref):
    chunks, _, own, _ = packed_ref.shape
    length = chunks * own
    packed = packed_ref[...].reshape(length, 3 * LANES)
    queries, keys, values = (packed[:, LANES * i : LANES * (i + 1)] for i in range(3))
    masks = head_masks(BF)
    lane = lax.broadcasted_iota(jnp.int32, (1, LANES), 1)
    for start, tile, end in causal_tiles(length):
        query_pos = start + lax.broadcasted_iota(jnp.int32, (tile, end), 0)
        key_pos = lax.broadcasted_iota(jnp.int32, (tile, end), 1)
        allowed = (seg_col_ref[0, start:end] == seg_row_ref[0, :, :end]) & (key_pos <= query_pos)
        result = jnp.zeros((tile, LANES), F32)
        for head, mask in enumerate(masks):
            scores = inner_right(queries[start:end] * mask, keys[:end]) * FACTOR
            scores = jnp.where(allowed, scores, MASKED)
            powers = jnp.exp(scores - jnp.max(scores, axis=1, keepdims=True))
            portions = powers / jnp.sum(powers, axis=1, keepdims=True)
            found = matmul(portions.astype(BF), values[:end])
            result = jnp.where(lane // HEAD == head, found, result)
        out_ref[start // own : end // own, 0] = result.astype(BF).reshape(tile // own, own, LANES)


def frame_attend_grads_kernel(packed_ref, grad_ref, seg_col_ref, seg_row_ref, out_ref, key_sum, value_sum):
    chunks, _, own, _ = packed_ref.shape
    length = chunks * own
    packed = packed_ref[...].reshape(length, 3 * LANES)
    queries, keys, values = (packed[:, LANES * i : LANES * (i + 1)] for i in range(3))
    grads = grad_ref[...].reshape(length, LANES)
    masks = head_masks(BF)
    lane = lax.broadcasted_iota(jnp.int32, (1, LANES), 1)
    key_sum[...] = jnp.zeros_like(key_sum)
    value_sum[...] = jnp.zeros_like(value_sum)
    for start, tile, end in causal_tiles(length):
        key_pos = lax.broadcasted_iota(jnp.int32, (end, tile), 0)
        query_pos = start + lax.broadcasted_iota(jnp.int32, (end, tile), 1)
        allowed = (seg_col_ref[0, :end] == seg_row_ref[0, :, start:end]) & (key_pos <= query_pos)
        query_grad = jnp.zeros((tile, LANES), F32)
        for head, mask in enumerate(masks):
            query = queries[start:end] * mask
            grad = grads[start:end] * mask
            scores = inner_right(keys[:end], query) * FACTOR
            scores = jnp.where(allowed, scores, MASKED)
            powers = jnp.exp(scores - jnp.max(scores, axis=0, keepdims=True))
            portions = powers / jnp.sum(powers, axis=0, keepdims=True)
            portion_grad = inner_right(values[:end], grad)
            mean = jnp.sum(portions * portion_grad, axis=0, keepdims=True)
            score_grad = (portions * (portion_grad - mean)).astype(BF)
            key_sum[:end] += matmul(score_grad, query)
            value_sum[:end] += matmul(portions.astype(BF), grad)
            found = inner_left(score_grad, keys[:end])
            query_grad = jnp.where(lane // HEAD == head, found, query_grad)
        out_ref[start // own : end // own, 0, :, :LANES] = (
            (query_grad * FACTOR).astype(BF).reshape(tile // own, own, LANES)
        )
    out_ref[:, 0, :, LANES : 2 * LANES] = (key_sum[...] * FACTOR).astype(BF).reshape(chunks, own, LANES)
    out_ref[:, 0, :, 2 * LANES :] = value_sum[...].astype(BF).reshape(chunks, own, LANES)


def row_spec(chunks, own, breadth):
    return pl.BlockSpec((chunks, 1, own, breadth), lambda row: (0, row, 0, 0))


def segment_specs(length):
    return [
        pl.BlockSpec((1, length, 1), lambda row: (row, 0, 0)),
        pl.BlockSpec((1, 1, length), lambda row: (row, 0, 0)),
    ]


def frame_attend_call(packed, segments):
    chunks, rows, own, _ = packed.shape
    length = chunks * own
    return pl.pallas_call(
        frame_attend_kernel,
        grid=(rows,),
        in_specs=[row_spec(chunks, own, 3 * LANES), *segment_specs(length)],
        out_specs=row_spec(chunks, own, LANES),
        out_shape=jax.ShapeDtypeStruct((chunks, rows, own, LANES), BF),
        compiler_params=pltpu.CompilerParams(vmem_limit_bytes=VMEM_LIMIT),
        cost_estimate=pl.CostEstimate(
            flops=rows * length * length * LANES * 5,
            bytes_accessed=packed.size * 3,
            transcendentals=rows * length * length,
        ),
        name="frame_attend",
    )(packed, segments[:, :, None], segments[:, None, :])


def frame_attend_grads_call(packed, grads, segments):
    chunks, rows, own, _ = packed.shape
    length = chunks * own
    return pl.pallas_call(
        frame_attend_grads_kernel,
        grid=(rows,),
        in_specs=[
            row_spec(chunks, own, 3 * LANES),
            row_spec(chunks, own, LANES),
            *segment_specs(length),
        ],
        out_specs=row_spec(chunks, own, 3 * LANES),
        out_shape=jax.ShapeDtypeStruct((chunks, rows, own, 3 * LANES), BF),
        scratch_shapes=[pltpu.VMEM((length, LANES), F32), pltpu.VMEM((length, LANES), F32)],
        compiler_params=pltpu.CompilerParams(vmem_limit_bytes=VMEM_LIMIT),
        cost_estimate=pl.CostEstimate(
            flops=rows * length * length * LANES * 12,
            bytes_accessed=packed.size * 5,
            transcendentals=rows * length * length,
        ),
        name="frame_attend_grads",
    )(packed, grads, segments[:, :, None], segments[:, None, :])


def position_pairs(positions):
    return [(later, earlier) for later in range(1, positions) for earlier in range(later + 1)]


def codec_sums(products, marks):
    stacked = jnp.concatenate(products, axis=0)
    high = stacked.astype(BF)
    low = (stacked - high.astype(F32)).astype(BF)
    total = matmul(high, marks) + matmul(low, marks)
    size = products[0].shape[0]
    return [total[size * i : size * (i + 1)] for i in range(len(products))]


def codec_spread(portions, marks):
    stacked = jnp.concatenate([portion.astype(BF) for portion in portions], axis=0)
    total = inner_right(stacked, marks)
    size = portions[0].shape[0]
    return [total[size * i : size * (i + 1)] for i in range(len(portions))]


def codec_portions(queries, keys, marks, pairs):
    scores = codec_sums(
        [queries[later].astype(F32) * keys[earlier].astype(F32) for later, earlier in pairs], marks
    )
    scores = dict(zip(pairs, [score * FACTOR for score in scores]))
    portions = {}
    for later in range(1, len(queries)):
        row = [scores[later, earlier] for earlier in range(later + 1)]
        top = functools.reduce(jnp.maximum, row)
        powers = [jnp.exp(score - top) for score in row]
        total = functools.reduce(jnp.add, powers)
        for earlier in range(later + 1):
            portions[later, earlier] = powers[earlier] / total
    return portions


def codec_parts(packed_ref, width):
    positions = packed_ref.shape[0]
    return [
        [packed_ref[t, :, width * part : width * (part + 1)] for t in range(positions)]
        for part in range(3)
    ]


def codec_attend_kernel(packed_ref, marks_ref, out_ref):
    positions, _, width = out_ref.shape
    queries, keys, values = codec_parts(packed_ref, width)
    marks = marks_ref[...]
    pairs = position_pairs(positions)
    portions = codec_portions(queries, keys, marks, pairs)
    wide = dict(zip(pairs, codec_spread([portions[pair] for pair in pairs], marks)))
    out_ref[0] = values[0]
    for later in range(1, positions):
        terms = [wide[later, e] * values[e].astype(F32) for e in range(later + 1)]
        out_ref[later] = functools.reduce(jnp.add, terms).astype(BF)


def codec_attend_grads_kernel(packed_ref, grad_ref, marks_ref, out_ref):
    positions, _, width = grad_ref.shape
    queries, keys, values = codec_parts(packed_ref, width)
    marks = marks_ref[...]
    pairs = position_pairs(positions)
    portions = codec_portions(queries, keys, marks, pairs)
    grads = [grad_ref[t].astype(F32) for t in range(positions)]
    portion_grads = dict(
        zip(
            pairs,
            codec_sums([grads[later] * values[earlier].astype(F32) for later, earlier in pairs], marks),
        )
    )
    score_grads = {}
    for later in range(1, positions):
        mean = functools.reduce(
            jnp.add, [portions[later, e] * portion_grads[later, e] for e in range(later + 1)]
        )
        for e in range(later + 1):
            score_grads[later, e] = portions[later, e] * (portion_grads[later, e] - mean)
    wide = dict(zip(pairs, codec_spread([portions[pair] for pair in pairs], marks)))
    wide_grads = dict(zip(pairs, codec_spread([score_grads[pair] for pair in pairs], marks)))
    zero = jnp.zeros_like(grads[0])
    for t in range(positions):
        query_grad = key_grad = zero
        value_grad = grads[0] if t == 0 else zero
        for later, earlier in pairs:
            if later == t:
                query_grad = query_grad + wide_grads[later, earlier] * keys[earlier].astype(F32)
            if earlier == t:
                key_grad = key_grad + wide_grads[later, earlier] * queries[later].astype(F32)
                value_grad = value_grad + wide[later, earlier] * grads[later]
        out_ref[t, :, :width] = (query_grad * FACTOR).astype(BF)
        out_ref[t, :, width : 2 * width] = (key_grad * FACTOR).astype(BF)
        out_ref[t, :, 2 * width :] = value_grad.astype(BF)


def codec_tile(frame_total):
    return 64 if frame_total % 64 == 0 else frame_total


def codec_spec(positions, tile, breadth):
    return pl.BlockSpec((positions, tile, breadth), lambda i: (0, i, 0))


def head_marks(width):
    return (
        jnp.arange(width)[:, None] // HEAD == jnp.arange(LANES)[None, :]
    ).astype(BF)


def codec_attend_call(packed):
    positions, total, triple = packed.shape
    width = triple // 3
    tile = codec_tile(total)
    return pl.pallas_call(
        codec_attend_kernel,
        grid=(total // tile,),
        in_specs=[codec_spec(positions, tile, triple), whole_block((width, LANES))],
        out_specs=codec_spec(positions, tile, width),
        out_shape=jax.ShapeDtypeStruct((positions, total, width), BF),
        compiler_params=pltpu.CompilerParams(vmem_limit_bytes=VMEM_LIMIT),
        cost_estimate=pl.CostEstimate(
            flops=total * width * LANES * 30, bytes_accessed=packed.size * 3, transcendentals=0
        ),
        name="codec_attend",
    )(packed, head_marks(width))


def codec_attend_grads_call(packed, grads):
    positions, total, triple = packed.shape
    width = triple // 3
    tile = codec_tile(total)
    return pl.pallas_call(
        codec_attend_grads_kernel,
        grid=(total // tile,),
        in_specs=[
            codec_spec(positions, tile, triple),
            codec_spec(positions, tile, width),
            whole_block((width, LANES)),
        ],
        out_specs=codec_spec(positions, tile, triple),
        out_shape=jax.ShapeDtypeStruct((positions, total, triple), BF),
        compiler_params=pltpu.CompilerParams(vmem_limit_bytes=VMEM_LIMIT),
        cost_estimate=pl.CostEstimate(
            flops=total * width * LANES * 70, bytes_accessed=packed.size * 5, transcendentals=0
        ),
        name="codec_attend_grads",
    )(packed, grads, head_marks(width))


def grad_order(place):
    seqs = [place.seq ^ (2 * spot + 1 - side) for side in range(2) for spot in range(4)]
    return jnp.stack([place.mp ^ 2, place.mp] + seqs + [place.seq]).astype(jnp.int32)


def grad_rows_kernel(mp_first, wide, order_ref, far_own, far_rec, own_own, own_rec, latter_own, latter_rec, *refs):
    send_ref, keep_ref, turned = refs[-3:]
    rows = latter_own.shape[0]
    height = far_own.shape[1]

    @pl.when(pl.program_id(0) == 0)
    def _():
        for at, (own, rec) in enumerate(((far_own, far_rec), (own_own, own_rec))):
            turned[height * at : height * (at + 1), :rows] = own[...].T
            turned[height * at : height * (at + 1), rows:] = rec[...].T

    total = matmul(turned[:, :rows], latter_own[...]) + matmul(turned[:, rows:], latter_rec[...])
    grad_rows_store(mp_first, wide, order_ref, total.astype(BF), height, send_ref, keep_ref)


def grad_rows_store(mp_first, wide, order_ref, total, height, send_ref, keep_ref):
    units = height // TILE
    if wide:
        chunks = total.shape[1] // 8 // LANES
        for seq in range(8):
            change = order_ref[10] ^ seq
            side = 1 - (change & 1)
            spot = change >> 1
            for chunk in range(chunks):
                first = (seq * chunks + chunk) * LANES
                value = total[:, first : first + LANES]
                for unit in range(units):
                    given = value[unit * TILE : (unit + 1) * TILE]
                    kept = value[height + unit * TILE : height + (unit + 1) * TILE]
                    at = chunk * units + unit
                    if mp_first:
                        send_ref[side, spot, at] = given
                        keep_ref[side, spot, at] = kept
                    else:

                        @pl.when(side == 0)
                        def _(given=given, kept=kept, at=at, spot=spot):
                            send_ref[0, spot, at] = given
                            send_ref[1, spot, at] = kept

                        @pl.when(side == 1)
                        def _(given=given, kept=kept, at=at, spot=spot):
                            keep_ref[0, spot, at] = given
                            keep_ref[1, spot, at] = kept

        return
    chunks = total.shape[1] // LANES
    for chunk in range(chunks):
        value = total[:, chunk * LANES : (chunk + 1) * LANES]
        given, kept = value[:height], value[height:]
        if mp_first:
            send_ref[0, 0, chunk] = given
            keep_ref[0, 0, chunk] = kept
        else:

            @pl.when(pl.program_id(0) < 4)
            def _(given=given, kept=kept, chunk=chunk):
                send_ref[0, 0, chunk] = given
                send_ref[1, 0, chunk] = kept

            @pl.when(pl.program_id(0) >= 4)
            def _(given=given, kept=kept, chunk=chunk):
                keep_ref[0, 0, chunk] = given
                keep_ref[1, 0, chunk] = kept


def grad_buffers(units):
    return [jax.ShapeDtypeStruct((2, 4, units, TILE, LANES), BF)] * 2


def grad_call(kernel, order, arrays, in_specs, out_specs, units, into, steps, scratch, flops, name):
    aliases = {}
    moved = 2 * sum(array.size for array in arrays)
    if into is not None:
        aliases = {len(arrays) + 1: 0, len(arrays) + 2: 1}
        in_specs = in_specs + [pl.BlockSpec(memory_space=pl.ANY)] * 2
        arrays = arrays + list(into)
    return pl.pallas_call(
        kernel,
        grid_spec=pltpu.PrefetchScalarGridSpec(
            num_scalar_prefetch=1,
            grid=(steps,),
            in_specs=in_specs,
            out_specs=out_specs,
            scratch_shapes=[scratch],
        ),
        out_shape=grad_buffers(units),
        input_output_aliases=aliases,
        compiler_params=pltpu.CompilerParams(vmem_limit_bytes=VMEM_LIMIT),
        cost_estimate=pl.CostEstimate(flops=flops, bytes_accessed=moved, transcendentals=0),
        name=name,
    )(order, *arrays)


def grad_rows(former, latter, order, mp_first, units, offset, into=None):
    rows, breadth = latter[0].shape
    height = former[0].shape[1] // 4
    wide = breadth // 8 == LANES
    chunks = breadth // 8 // LANES
    steps = 1 if wide else 8
    arrays = [former[0], former[1], former[0], former[1], latter[0], latter[1]]
    former_specs = [
        pl.BlockSpec((rows, height), lambda j, t, at=at: (0, t[at]), pipeline_mode=pl.Buffered(1))
        for at in (0, 0, 1, 1)
    ]
    if wide:
        latter_specs = [whole_block((rows, breadth))] * 2
        block = (2, 4, 1, TILE, LANES)
        out_specs = [pl.BlockSpec(block, lambda j, t: (0, 0, offset, 0, 0))] * 2
    else:
        latter_specs = [pl.BlockSpec((rows, breadth // 8), lambda j, t: (0, t[2 + j]))] * 2
        base = offset // chunks
        if mp_first:
            block = (1, 1, chunks, TILE, LANES)
            out_specs = [pl.BlockSpec(block, lambda j, t: (j // 4, j % 4, base, 0, 0))] * 2
        else:
            block = (2, 1, chunks, TILE, LANES)
            out_specs = [
                pl.BlockSpec(block, lambda j, t: (0, jnp.minimum(j, 3), base, 0, 0)),
                pl.BlockSpec(block, lambda j, t: (0, jnp.maximum(j - 4, 0), base, 0, 0)),
            ]
    return grad_call(
        functools.partial(grad_rows_kernel, mp_first, wide),
        order,
        arrays,
        former_specs + latter_specs,
        out_specs,
        units,
        into,
        steps,
        pltpu.VMEM((2 * height, 2 * rows), BF),
        2 * 2 * rows * 2 * height * breadth,
        "grad_rows",
    )


def grad_columns_kernel(order_ref, latter_own, latter_rec, former_own, former_rec, *refs):
    send_ref, keep_ref, turned = refs[-3:]
    rows = latter_own.shape[0]
    step = pl.program_id(0)

    @pl.when(step == 0)
    def _():
        turned[:, :rows] = latter_own[...].T
        turned[:, rows:] = latter_rec[...].T

    total = matmul(turned[:, :rows], former_own[...]) + matmul(turned[:, rows:], former_rec[...])
    total = total.astype(BF)
    chunks = total.shape[1] // LANES
    for target, when in ((send_ref, step < pl.num_programs(0) // 2), (keep_ref, step >= pl.num_programs(0) // 2)):

        @pl.when(when)
        def _(target=target):
            for seq in range(8):
                change = order_ref[10] ^ seq
                side = 1 - (change & 1)
                spot = change >> 1
                for chunk in range(chunks):
                    target[side, spot, chunk // 2, (chunk % 2) * LANES : (chunk % 2 + 1) * LANES] = total[
                        seq * LANES : (seq + 1) * LANES, chunk * LANES : (chunk + 1) * LANES
                    ]


def grad_columns(former, latter, order, units, offset, into=None):
    rows, breadth = latter[0].shape
    height = former[0].shape[1] // 4
    step = min(512, height)
    per = height // step
    block = (2, 4, step // TILE, TILE, LANES)
    base = offset // (step // TILE)
    latter_specs = [
        pl.BlockSpec((rows, breadth), lambda j, t: (0, 0), pipeline_mode=pl.Buffered(1))
    ] * 2
    former_specs = [pl.BlockSpec((rows, step), lambda j, t: (0, t[j // per] * per + j % per))] * 2
    out_specs = [
        pl.BlockSpec(block, lambda j, t: (0, 0, base + jnp.minimum(j, per - 1), 0, 0)),
        pl.BlockSpec(block, lambda j, t: (0, 0, base + jnp.maximum(j - per, 0), 0, 0)),
    ]
    return grad_call(
        grad_columns_kernel,
        order,
        [latter[0], latter[1], former[0], former[1]],
        latter_specs + former_specs,
        out_specs,
        units,
        into,
        2 * per,
        pltpu.VMEM((breadth, 2 * rows), BF),
        2 * 2 * rows * 2 * height * breadth,
        "grad_columns",
    )


def grad_table_kernel(height, order_ref, codes_ref, latter_own, latter_rec, *refs):
    send_ref, keep_ref, _ = refs[-3:]
    rows = latter_own.shape[0]
    parts = []
    for at in range(2):
        entry = order_ref[at] * height + lax.broadcasted_iota(jnp.int32, (height, 2 * rows), 0)
        parts.append((entry == codes_ref[...]).astype(F32).astype(BF))
    chosen = jnp.concatenate(parts, axis=0)
    total = matmul(chosen[:, :rows], latter_own[...]) + matmul(chosen[:, rows:], latter_rec[...])
    grad_rows_store(False, True, order_ref, total.astype(BF), height, send_ref, keep_ref)


def grad_table(codes, latter, order, height, units, offset, into=None):
    rows, breadth = latter[0].shape
    block = (2, 4, height // TILE, TILE, LANES)
    base = offset // (height // TILE)
    return grad_call(
        functools.partial(grad_table_kernel, height),
        order,
        [codes, latter[0], latter[1]],
        [whole_block(codes.shape), whole_block((rows, breadth)), whole_block((rows, breadth))],
        [pl.BlockSpec(block, lambda j, t: (0, 0, base, 0, 0))] * 2,
        units,
        into,
        1,
        pltpu.VMEM((8, LANES), F32),
        2 * 2 * rows * 2 * height * breadth,
        "grad_table",
    )


def reduce_blocks(send, keep, mp_first):
    stages = (("mp", 2), ("seq", 1)) if mp_first else (("seq", 1), ("mp", 2))
    first = swap(send, *stages[0])
    given = (keep[0].astype(F32) + first[0].astype(F32)).astype(BF)
    second = swap(given, *stages[1])
    total = (keep[1].astype(F32) + first[1].astype(F32) + second.astype(F32)).astype(BF)
    far = swap(total[2:], "seq", 4)
    total = total[:2].astype(F32) + far.astype(F32)
    near = swap(total[1].astype(BF), "seq", 2)
    return total[0] + near.astype(F32)


def rows_from_units(units, height):
    tiles = height // TILE
    chunks = units.shape[0] // tiles
    return jnp.transpose(
        units.reshape(chunks, height, LANES), (1, 0, 2)
    ).reshape(height, chunks * LANES)


def columns_from_units(units):
    count = units.shape[0]
    return jnp.transpose(units.reshape(2 * count, LANES, LANES), (0, 2, 1)).reshape(count * TILE, LANES)


def join_kernel(layout, place_ref, *refs):
    count = len(layout)
    own, other, first, second, first_other, second_other = refs[:6]
    outs = refs[6 : 6 + count]
    held = refs[6 + count : 6 + 2 * count]
    sems, out_sems = refs[-2:]
    half = first.shape[0]
    width = own.shape[1]
    me = place_ref[0]
    low = place_ref[1]
    copies = []
    for at, (height, breadth, start) in enumerate(layout):
        for column in range(breadth // width):
            row = start + column * height
            columns = pl.ds(column * width, width)
            for flip, source in ((0, own), (1, other)):
                target = held[at].at[pl.ds(pl.multiple_of((me ^ flip) * height, height), height), columns]
                copies.append((at, None, source.at[pl.ds(row, height)], target))
            for flip, sources in ((2, (first, second)), (3, (first_other, second_other))):
                for side in range(2):
                    begin, end = max(row, side * half), min(row + height, (side + 1) * half)
                    if begin >= end:
                        continue
                    rows = pl.ds(begin - side * half, end - begin)
                    target = held[at].at[
                        pl.ds(pl.multiple_of((me ^ flip) * height + begin - row, 16), end - begin), columns
                    ]
                    copies.append((at, side, sources[0].at[rows], target))
                    copies.append((at, 1 - side, sources[1].at[rows], target))

    def act(action, number):
        _, when, source, target = copies[number]
        copy = pltpu.make_async_copy(source, target, sems.at[number])
        if when is None:
            getattr(copy, action)()
        else:

            @pl.when(low == when)
            def _():
                getattr(copy, action)()

    for number in range(len(copies)):
        act("start", number)
    for at in range(count):
        for number in range(len(copies)):
            if copies[number][0] == at:
                act("wait", number)
        pltpu.make_async_copy(held[at], outs[at], out_sems.at[at]).start()
    for at in range(count):
        pltpu.make_async_copy(held[at], outs[at], out_sems.at[at]).wait()


def join_count(layout, half, width):
    count = 0
    for height, breadth, start in layout:
        for column in range(breadth // width):
            row = start + column * height
            count += 2
            for side in range(2):
                if max(row, side * half) < min(row + height, (side + 1) * half):
                    count += 4
    return count


def pack_weights(shards):
    width = 1024
    pieces = []
    for shard in shards:
        for column in range(shard.shape[1] // width):
            pieces.append(shard[:, column * width : (column + 1) * width])
    return pieces[0] if len(pieces) == 1 else jnp.concatenate(pieces, axis=0)


def pack_layout(shards):
    layout, start = [], 0
    for shard in shards:
        height, breadth = shard.shape
        layout.append((height, breadth, start))
        start += height * (breadth // 1024)
    return tuple(layout), start


def join_weights(pack, other, first, second, first_other, second_other, layout, place):
    half, width = first.shape
    any_spec = pl.BlockSpec(memory_space=pl.ANY)
    outs = [jax.ShapeDtypeStruct((4 * height, breadth), BF) for height, breadth, _ in layout]
    return pl.pallas_call(
        functools.partial(join_kernel, layout),
        in_specs=[pl.BlockSpec(memory_space=pltpu.SMEM)] + [any_spec] * 6,
        out_specs=[any_spec] * len(outs),
        out_shape=outs,
        scratch_shapes=[pltpu.VMEM(out.shape, BF) for out in outs]
        + [
            pltpu.SemaphoreType.DMA((join_count(layout, half, width),)),
            pltpu.SemaphoreType.DMA((len(outs),)),
        ],
        compiler_params=pltpu.CompilerParams(vmem_limit_bytes=VMEM_LIMIT),
        cost_estimate=pl.CostEstimate(flops=0, bytes_accessed=16 * pack.size, transcendentals=0),
        name="join_weights",
    )(
        jnp.stack([place.mp, place.seq_low]).astype(jnp.int32),
        pack,
        other,
        first,
        second,
        first_other,
        second_other,
    )


def shards_general(
    frames,
    segments,
    padding,
    codec_tokens,
    codebooks,
    frame_prenorm,
    frame_project,
    frame_output,
    frame_postnorm,
    frame_expand,
    frame_contract,
    codec_prenorm,
    codec_project,
    codec_output,
    codec_postnorm,
    codec_expand,
    codec_contract,
    cotangent,
):
    place = Place()
    row_count, frames_dev, width = frames.shape
    frame_total = row_count * frames_dev
    positions = cotangent.shape[2]
    gains = lax.all_gather(
        jnp.stack([frame_prenorm, frame_postnorm, codec_prenorm, codec_postnorm]),
        "mp",
        axis=1,
        tiled=True,
    )
    frame_weights = (
        gains[0],
        gather_weight(frame_project, place),
        gather_weight(frame_output, place),
        gains[1],
        gather_weight(frame_expand, place),
        gather_weight(frame_contract, place),
    )
    codec_weights = (
        gains[2],
        gather_weight(codec_project, place),
        gather_weight(codec_output, place),
        gains[3],
        gather_weight(codec_expand, place),
        gather_weight(codec_contract, place),
    )
    table = gather_weight(codebooks, place)

    hidden = frames.astype(F32).reshape(frame_total, width)
    normed, projected = front_pass(hidden, frame_weights)
    attended, attention_back = frame_attention(
        projected.reshape(row_count, frames_dev, 3 * width), segments, place
    )
    attended = attended.reshape(frame_total, width)
    frame_result, frame_saved = rear_pass(hidden, attended, frame_weights)
    base = frame_result.astype(BF).astype(F32)

    table_rows = codec_tokens.reshape(positions - 1, frame_total) + (
        jnp.arange(positions - 1, dtype=jnp.int32) * CODES
    )[:, None]
    embedded = table[table_rows].astype(F32)
    codec_hidden = jnp.concatenate([base[None], base[None] + embedded], axis=0).reshape(
        positions * frame_total, width
    )
    codec_normed, codec_projected = front_pass(codec_hidden, codec_weights)
    marks = (
        jnp.arange(width)[:, None] // HEAD == jnp.arange(HEADS)[None, :]
    ).astype(F32)
    view = codec_projected.reshape(positions, frame_total, 3, width)
    queries, keys, values = ([view[t, :, part] for t in range(positions)] for part in range(3))
    soft = codec_softmax(queries, keys, marks)
    codec_attended = jnp.concatenate(codec_attend(soft, values, marks), axis=0)
    codec_result, codec_saved = rear_pass(codec_hidden, codec_attended, codec_weights)
    live = padding.reshape(frame_total).astype(F32)[None, :, None]
    output = jnp.transpose(
        (codec_result.reshape(positions, frame_total, width) * live).astype(BF), (1, 0, 2)
    ).reshape(row_count, frames_dev, positions, width)

    codec_grad = (
        jnp.transpose(cotangent.reshape(frame_total, positions, width), (1, 0, 2)).astype(F32) * live
    ).reshape(positions * frame_total, width)
    mixed_grad, attended_grad, codec_postnorm_grad, contract_in, expand_in, output_in = rear_grads(
        codec_grad, codec_saved, codec_weights
    )
    codec_contract_part = weight_grad(codec_saved[3], contract_in, place, True)
    codec_expand_part = weight_grad(codec_saved[1], expand_in, place, False)
    codec_output_part = weight_grad(codec_attended, output_in, place, True)
    grad_view = attended_grad.reshape(positions, frame_total, width)
    codec_projected_grad = codec_attend_grads(
        soft, queries, keys, values, [grad_view[t] for t in range(positions)], marks
    )
    codec_project_part = weight_grad(codec_normed, codec_projected_grad, place, True)
    input_grad, codec_prenorm_grad = front_grads(
        codec_hidden, codec_projected_grad, mixed_grad, codec_weights
    )
    input_grad = input_grad.reshape(positions, frame_total, width)
    chosen = (
        table_rows.reshape(-1)[:, None] == jnp.arange(table.shape[0], dtype=jnp.int32)[None, :]
    ).astype(BF)
    table_part = weight_grad(chosen, input_grad[1:].reshape(-1, width).astype(BF), place, False)
    base_grad = jnp.sum(input_grad, axis=0).astype(BF).astype(F32)

    (codec_contract_grad,) = finish_grads([codec_contract_part], place)
    codec_expand_grad, codec_output_grad, codec_project_grad = finish_grads(
        [codec_expand_part, codec_output_part, codec_project_part], place
    )
    (table_grad,) = finish_grads([table_part], place)

    frame_mixed_grad, frame_attended_grad, frame_postnorm_grad, contract_in, expand_in, output_in = (
        rear_grads(base_grad, frame_saved, frame_weights)
    )
    frame_projected_grad = attention_back(
        frame_attended_grad.reshape(row_count, frames_dev, width)
    ).reshape(frame_total, 3 * width)
    frame_contract_part = weight_grad(frame_saved[3], contract_in, place, True)
    frame_expand_part = weight_grad(frame_saved[1], expand_in, place, False)
    frame_output_part = weight_grad(attended, output_in, place, True)
    frame_project_part = weight_grad(normed, frame_projected_grad, place, True)
    frames_grad, frame_prenorm_grad = front_grads(
        hidden, frame_projected_grad, frame_mixed_grad, frame_weights
    )
    (frame_contract_grad,) = finish_grads([frame_contract_part], place)
    frame_expand_grad, frame_output_grad = finish_grads(
        [frame_expand_part, frame_output_part], place
    )
    (frame_project_grad,) = finish_grads([frame_project_part], place)
    gain_sums = sum_everywhere(
        jnp.stack(
            [frame_prenorm_grad, frame_postnorm_grad, codec_prenorm_grad, codec_postnorm_grad]
        ),
        place,
    )
    return (
        output,
        frames_grad.reshape(row_count, frames_dev, width),
        table_grad,
        gain_sums[0],
        frame_project_grad,
        frame_output_grad,
        gain_sums[1],
        frame_expand_grad,
        frame_contract_grad,
        gain_sums[2],
        codec_project_grad,
        codec_output_grad,
        gain_sums[3],
        codec_expand_grad,
        codec_contract_grad,
    )


def tie(values, *after):
    flat, tree = jax.tree.flatten(values)
    held = lax.optimization_barrier(tuple(flat) + tuple(after))
    return jax.tree.unflatten(tree, held[: len(flat)])


def start_pack(pack, place, *after):
    half = pack.shape[0] // 2
    mine = lax.dynamic_slice(pack, (place.seq_low * half, 0), (half, pack.shape[1]))
    if after:
        pack, mine = tie((pack, mine), *after)
    first = swap(mine, "mp", 2)
    other = swap(pack, "mp", 1)
    second = swap(first, "seq", 1)
    return [pack, other, first, second, swap(first, "mp", 1), swap(second, "mp", 1)]


def pair(values):
    return (values, swap(values, "mp", 1))


def hidden_grads(contract_in, expanded, weights):
    active_grad = inner_right(contract_in, weights[5])
    expand_in = jax.vjp(jax.nn.gelu, expanded)[1](active_grad)[0].astype(BF)
    return expand_in, inner_right(expand_in, weights[4])


def mixed_grads(result_grad, normed_grad, mixed_sum, weights):
    mixed_part, postnorm_grad = jax.vjp(rms_scale, mixed_sum, weights[3].astype(F32))[1](normed_grad)
    mixed_grad = result_grad + mixed_part
    output_in = mixed_grad.astype(BF)
    return mixed_grad, inner_right(output_in, weights[2]).astype(BF), postnorm_grad, output_in


def shards(
    frames,
    segments,
    padding,
    codec_tokens,
    codebooks,
    frame_prenorm,
    frame_project,
    frame_output,
    frame_postnorm,
    frame_expand,
    frame_contract,
    codec_prenorm,
    codec_project,
    codec_output,
    codec_postnorm,
    codec_expand,
    codec_contract,
    cotangent,
):
    place = Place()
    order = grad_order(place)
    row_count, frames_dev, width = frames.shape
    frame_total = row_count * frames_dev
    positions = cotangent.shape[2]

    gain_rows = jnp.pad(
        jnp.concatenate([frame_prenorm, frame_postnorm, codec_prenorm, codec_postnorm])[None],
        ((0, 31), (0, 0)),
    )
    packs = (
        [frame_project, gain_rows],
        [frame_expand, frame_contract, frame_output],
        [codec_project, codebooks],
        [codec_expand, codec_contract, codec_output],
    )
    pieces = []
    for members in packs:
        pack = pack_weights(members)
        pieces.append(start_pack(pack, place, *([pieces[-1][2]] if pieces else [])))

    def joined(at):
        return join_weights(*pieces[at], pack_layout(packs[at])[0], place)

    count = place.seq_count
    every_segment = lax.all_to_all(
        jnp.broadcast_to(segments[None], (count, row_count, frames_dev)),
        "seq",
        split_axis=0,
        concat_axis=0,
        tiled=True,
    )
    every_segment = jnp.transpose(every_segment, (1, 0, 2)).reshape(row_count, count * frames_dev)
    codes = codec_tokens.reshape(1, (positions - 1) * frame_total) + jnp.repeat(
        jnp.arange(positions - 1, dtype=jnp.int32) * CODES, frame_total
    )
    codes_both = jnp.concatenate(pair(codes), axis=1)
    live = padding.reshape(frame_total).astype(F32)[None, :, None]
    codec_grad = (
        jnp.transpose(cotangent.reshape(frame_total, positions, width), (1, 0, 2)).astype(F32) * live
    ).reshape(positions * frame_total, width)
    contract_in = pair(codec_grad.astype(BF))

    weight_project, gains = joined(0)
    gains = jnp.transpose(
        gains.reshape(place.mp_count, 32, 4, -1)[:, 0], (1, 0, 2)
    ).reshape(4, width)
    hidden = frames.astype(F32).reshape(frame_total, width)
    normed, projected = front_pass(hidden, (gains[0], weight_project))
    normed_both = pair(normed)
    packed = jnp.transpose(
        projected.reshape(row_count, frames_dev, 3, count, LANES), (3, 0, 1, 2, 4)
    ).reshape(count, row_count, frames_dev, 3 * LANES)
    packed = lax.all_to_all(packed, "seq", split_axis=0, concat_axis=0, tiled=True)
    attended = lax.all_to_all(
        frame_attend_call(packed, every_segment), "seq", split_axis=0, concat_axis=0, tiled=True
    )
    attended = jnp.transpose(attended, (1, 2, 0, 3)).reshape(frame_total, width)
    attended_both = pair(attended)
    weight_expand, weight_contract, weight_output = joined(1)
    frame_weights = (gains[0], weight_project, weight_output, gains[1], weight_expand, weight_contract)
    frame_result, frame_saved = rear_pass(hidden, attended, frame_weights)
    normed_two_both = pair(frame_saved[1])
    activated_both = pair(frame_saved[3])
    base = frame_result.astype(BF).astype(F32)

    weight_project, table = joined(2)
    embedded = table[codes.reshape(positions - 1, frame_total)].astype(F32)
    codec_hidden = jnp.concatenate([base[None], base[None] + embedded], axis=0).reshape(
        positions * frame_total, width
    )
    codec_normed, codec_projected = front_pass(codec_hidden, (gains[2], weight_project))
    codec_normed_both = pair(codec_normed)
    codec_packed = codec_projected.reshape(positions, frame_total, 3 * width)
    codec_attended = codec_attend_call(codec_packed).reshape(positions * frame_total, width)
    codec_attended_both = pair(codec_attended)
    weight_expand, weight_contract, weight_output = joined(3)
    codec_weights = (gains[2], weight_project, weight_output, gains[3], weight_expand, weight_contract)
    codec_result, codec_saved = rear_pass(codec_hidden, codec_attended, codec_weights)
    codec_normed_two_both = pair(codec_saved[1])
    codec_activated_both = pair(codec_saved[3])
    output = jnp.transpose(
        (codec_result.reshape(positions, frame_total, width) * live).astype(BF), (1, 0, 2)
    ).reshape(row_count, frames_dev, positions, width)

    expand_in, normed_grad = hidden_grads(contract_in[0], codec_saved[2], codec_weights)
    codec_one = grad_columns(codec_activated_both, contract_in, order, 8, 4)
    codec_one = grad_rows(codec_normed_two_both, pair(expand_in), order, True, 8, 0, codec_one)
    normed_grad = tie(normed_grad, *codec_one)
    mixed_grad, attended_grad, codec_postnorm_grad, output_in = mixed_grads(
        codec_grad, normed_grad, codec_saved[0], codec_weights
    )
    codec_one = reduce_blocks(*codec_one, True)
    output_in = pair(output_in)
    codec_projected_grad = codec_attend_grads_call(
        codec_packed, attended_grad.reshape(positions, frame_total, width)
    ).reshape(positions * frame_total, 3 * width)
    codec_two = grad_rows(codec_normed_both, pair(codec_projected_grad), order, False, 6, 0)
    codec_two = grad_rows(codec_attended_both, output_in, order, False, 6, 3, codec_two)
    input_grad, codec_prenorm_grad = front_grads(
        codec_hidden, codec_projected_grad, mixed_grad, codec_weights
    )
    input_grad = input_grad.reshape(positions, frame_total, width)
    table_in = pair(input_grad[1:].reshape(-1, width).astype(BF))
    codec_two = grad_table(codes_both, table_in, order, codebooks.shape[0], 6, 4, codec_two)
    base_grad = tie(jnp.sum(input_grad, axis=0).astype(BF), *codec_two).astype(F32)
    codec_two = reduce_blocks(*codec_two, False)

    contract_in = pair(base_grad.astype(BF))
    expand_in, normed_grad = hidden_grads(contract_in[0], frame_saved[2], frame_weights)
    frame_mixed_grad, frame_attended_grad, frame_postnorm_grad, output_in = mixed_grads(
        base_grad, normed_grad, frame_saved[0], frame_weights
    )
    grads = lax.all_to_all(
        jnp.transpose(
            frame_attended_grad.reshape(row_count, frames_dev, count, LANES), (2, 0, 1, 3)
        ),
        "seq",
        split_axis=0,
        concat_axis=0,
        tiled=True,
    )
    frame_one = grad_columns(activated_both, contract_in, order, 8, 4)
    frame_one = grad_rows(normed_two_both, pair(expand_in), order, True, 8, 0, frame_one)
    grads = tie(grads, *frame_one)
    frame_one = reduce_blocks(*frame_one, True)
    packed_grad = lax.all_to_all(
        frame_attend_grads_call(packed, grads, every_segment),
        "seq",
        split_axis=0,
        concat_axis=0,
        tiled=True,
    )
    frame_projected_grad = jnp.transpose(
        packed_grad.reshape(count, row_count, frames_dev, 3, LANES), (1, 2, 3, 0, 4)
    ).reshape(frame_total, 3 * width)
    frame_two = grad_rows(normed_both, pair(frame_projected_grad), order, False, 4, 0)
    frame_two = grad_rows(attended_both, pair(output_in), order, False, 4, 3, frame_two)
    frame_two = reduce_blocks(*frame_two, False)
    frames_grad, frame_prenorm_grad = front_grads(
        hidden, frame_projected_grad, frame_mixed_grad, frame_weights
    )
    gain_sums = sum_everywhere(
        jnp.stack(
            [frame_prenorm_grad, frame_postnorm_grad, codec_prenorm_grad, codec_postnorm_grad]
        ),
        place,
    )
    height = frame_project.shape[0]
    return (
        output,
        frames_grad.reshape(row_count, frames_dev, width),
        rows_from_units(codec_two[4:], codebooks.shape[0]),
        gain_sums[0],
        rows_from_units(frame_two[:3], height),
        rows_from_units(frame_two[3:], height),
        gain_sums[1],
        rows_from_units(frame_one[:4], height),
        columns_from_units(frame_one[4:]),
        gain_sums[2],
        rows_from_units(codec_two[:3], height),
        rows_from_units(codec_two[3:4], height),
        gain_sums[3],
        rows_from_units(codec_one[:4], height),
        columns_from_units(codec_one[4:]),
    )


def solution(mesh):
    placed = (
        P("mp", "seq", None),
        P("mp", "seq"),
        P("mp", "seq"),
        P(None, "mp", "seq"),
        P("mp", None),
        P("mp"),
        P("mp", None),
        P("mp", None),
        P("mp"),
        P("mp", None),
        P("mp", None),
        P("mp"),
        P("mp", None),
        P("mp", None),
        P("mp"),
        P("mp", None),
        P("mp", None),
        P("mp", "seq", None, None),
    )
    small = mesh.shape["seq"] == 8 and mesh.shape["mp"] == 4
    return jax.shard_map(
        shards if small else shards_general,
        mesh=mesh,
        in_specs=placed,
        out_specs=(
            P("mp", "seq", None, None),
            P("mp", "seq", None),
            P("mp", "seq"),
            P(),
            P("mp", "seq"),
            P("mp", "seq"),
            P(),
            P("mp", "seq"),
            P("mp", "seq"),
            P(),
            P("mp", "seq"),
            P("mp", "seq"),
            P(),
            P("mp", "seq"),
            P("mp", "seq"),
        ),
        check_vma=False,
    )
```

```python
import functools

import jax
import jax.numpy as jnp
from jax import lax
from jax.experimental import pallas as pl
from jax.experimental.pallas import tpu as pltpu
from jax.sharding import PartitionSpec as P

HEADS = 16
HEAD = 64
CODES = 1024


EPSILON = 1e-05
MASKED = -1e30
FACTOR = HEAD ** (-0.5)

BF = jnp.bfloat16
F32 = jnp.float32


def rms_scale(values, gain_vec):
    return (
        values * lax.rsqrt(jnp.mean(values * values, axis=-1, keepdims=True) + EPSILON) * gain_vec
    )


def matmul(former, latter):
    return jnp.dot(former, latter, preferred_element_type=F32)


def inner_left(former, latter):
    return lax.dot_general(former, latter, (((0,), (0,)), ((), ())), preferred_element_type=F32)


def inner_right(former, latter):
    return lax.dot_general(former, latter, (((1,), (1,)), ((), ())), preferred_element_type=F32)


def split_heads(values):
    return values.reshape(values.shape[:-1] + (-1, HEAD))


def swap(values, axis, bit):
    return lax.ppermute(values, axis, [(i, i ^ bit) for i in range(lax.axis_size(axis))])


def pick(values, index, axis):
    return lax.dynamic_index_in_dim(values, index, axis, keepdims=False)


class Place:
    def __init__(self):
        self.seq_count = lax.axis_size("seq")
        self.mp_count = lax.axis_size("mp")
        self.seq = lax.axis_index("seq")
        self.mp = lax.axis_index("mp")
        self.seq_low = self.seq % 2


def gather_weight(shard, place):
    height, breadth = shard.shape
    half = height // 2
    mine = lax.dynamic_slice(shard, (place.seq_low * half, 0), (half, breadth))
    first = swap(mine, "mp", 2)
    second = swap(first, "seq", 1)
    near_other = swap(shard, "mp", 1)
    far = jnp.zeros((height, breadth), shard.dtype)
    far = lax.dynamic_update_slice(far, first, (place.seq_low * half, 0))
    far = lax.dynamic_update_slice(far, second, ((1 - place.seq_low) * half, 0))
    far_other = swap(far, "mp", 1)
    whole = jnp.zeros((height * place.mp_count, breadth), shard.dtype)
    for flip, piece in ((0, shard), (1, near_other), (2, far), (3, far_other)):
        whole = lax.dynamic_update_slice(whole, piece, ((place.mp ^ flip) * height, 0))
    return whole


def line_scatter(blocks, place):
    count = place.seq_count // 2
    position = place.seq // 2
    size = 2 * count
    state = blocks
    up_in = down_in = None
    for step in range(1, count):
        up_index = jnp.clip(count - step + position, 0, count - 1)
        down_index = jnp.clip(step - 1 - (count - 1 - position), 0, count - 1)
        up_perm = [(i, i + 2) for i in range(size - 2) if i // 2 < step]
        down_perm = [(i, i - 2) for i in range(2, size) if (count - 1 - i // 2) < step]
        up_out = pick(blocks, up_index, 1)
        down_out = pick(blocks, down_index, 1)
        if up_in is not None:
            up_out = up_out + up_in
            down_out = down_out + down_in
        up_in = lax.ppermute(up_out, "seq", up_perm)
        down_in = lax.ppermute(down_out, "seq", down_perm)
    own = pick(blocks, position, 1).astype(F32)
    return own + up_in.astype(F32) + down_in.astype(F32)


def weight_grad(former, latter, place, seq_first):
    height = former.shape[1] // place.mp_count
    rows = former.shape[0]
    breadth = latter.shape[1] // place.seq_count
    low = place.seq_low
    view = latter.reshape(rows, place.seq_count // 2, 2, breadth)
    half = breadth * (place.seq_count // 2)
    give = pick(view, 1 - low, 2).reshape(rows, half)
    keep = pick(view, low, 2).reshape(rows, half)
    both = jnp.concatenate([give, keep], axis=1)

    def columns(flip):
        return lax.dynamic_slice(former, (0, (place.mp ^ flip) * height), (rows, height))

    own, other, far, far_other = (columns(flip) for flip in (0, 1, 2, 3))
    part = inner_left(jnp.concatenate([far_other, other], axis=1), both).astype(BF)
    part = swap(part, "mp", 1).astype(F32)
    if seq_first:
        send = inner_left(jnp.concatenate([far, own], axis=1), give) + part[:, :half]
        low_in = swap(send.astype(BF), "seq", 1).astype(F32)
        send = inner_left(far, keep) + part[:height, half:] + low_in[:height]
        far_in = swap(send.astype(BF), "mp", 2).astype(F32)
        total = inner_left(own, keep) + part[height:, half:] + low_in[height:] + far_in
    else:
        send = inner_left(far, both) + part[:height]
        far_in = swap(send.astype(BF), "mp", 2).astype(F32)
        send = inner_left(own, give) + part[height:, :half] + far_in[:, :half]
        low_in = swap(send.astype(BF), "seq", 1).astype(F32)
        total = inner_left(own, keep) + part[height:, half:] + far_in[:, half:] + low_in
    return total.astype(BF).reshape(height, place.seq_count // 2, breadth)


def finish_grads(partials, place):
    sizes = [part.shape[2] for part in partials]
    total = line_scatter(jnp.concatenate(partials, axis=2), place)
    pieces, start = [], 0
    for size in sizes:
        pieces.append(total[:, start : start + size])
        start += size
    return pieces


def sum_everywhere(values, place):
    for axis, count in (("mp", place.mp_count), ("seq", place.seq_count)):
        bit = 1
        while bit < count:
            values = values + swap(values, axis, bit)
            bit *= 2
    return values


def front_pass(hidden, weights):
    normed = rms_scale(hidden, weights[0].astype(F32)).astype(BF)
    projected = matmul(normed, weights[1]).astype(BF)
    return (normed, projected)


def rear_pass(hidden, attended, weights):
    mixed_sum = hidden + matmul(attended, weights[2])
    normed_two = rms_scale(mixed_sum, weights[3].astype(F32)).astype(BF)
    expanded = matmul(normed_two, weights[4])
    activated = jax.nn.gelu(expanded).astype(BF)
    result = mixed_sum + matmul(activated, weights[5])
    return (result, (mixed_sum, normed_two, expanded, activated))


def rear_grads(result_grad, saved_state, weights):
    mixed_sum, normed_two, expanded, activated = saved_state
    contract_input = result_grad.astype(BF)
    active_grad = inner_right(contract_input, weights[5])
    expand_input = jax.vjp(jax.nn.gelu, expanded)[1](active_grad)[0].astype(BF)
    normed_grad = inner_right(expand_input, weights[4])
    mixed_part, postnorm_grad = jax.vjp(rms_scale, mixed_sum, weights[3].astype(F32))[1](
        normed_grad
    )
    mixed_grad = result_grad + mixed_part
    output_input = mixed_grad.astype(BF)
    attended_grad = inner_right(output_input, weights[2]).astype(BF)
    return (mixed_grad, attended_grad, postnorm_grad, contract_input, expand_input, output_input)


def front_grads(hidden, projected_grad, mixed_grad, weights):
    normed_grad = inner_right(projected_grad, weights[1])
    hidden_part, prenorm_grad = jax.vjp(rms_scale, hidden, weights[0].astype(F32))[1](normed_grad)
    return (mixed_grad + hidden_part, prenorm_grad)


def portions_of(queries, keys, allowed):
    scores = jnp.einsum("ihd,jhd->hij", queries, keys, preferred_element_type=F32) * FACTOR
    return jax.nn.softmax(jnp.where(allowed[None], scores, MASKED), axis=-1)


def attend(queries, keys, values, allowed):
    portions = portions_of(queries, keys, allowed)
    return jnp.einsum(
        "hij,jhd->ihd", portions.astype(BF), values, preferred_element_type=F32
    ).astype(BF)


def attend_grads(queries, keys, values, allowed, out_grad):
    portions = portions_of(queries, keys, allowed)
    portion_grad = jnp.einsum("ihd,jhd->hij", out_grad, values, preferred_element_type=F32)
    score_grad = (
        portions * (portion_grad - jnp.sum(portions * portion_grad, axis=-1, keepdims=True))
    ).astype(BF)
    query_grad = (
        jnp.einsum("hij,jhd->ihd", score_grad, keys, preferred_element_type=F32) * FACTOR
    )
    key_grad = (
        jnp.einsum("hij,ihd->jhd", score_grad, queries, preferred_element_type=F32) * FACTOR
    )
    value_grad = jnp.einsum("hij,ihd->jhd", portions.astype(BF), out_grad, preferred_element_type=F32)
    return query_grad, key_grad, value_grad


def to_heads(values, place):
    rows, own, parts, width = values.shape
    count = place.seq_count
    view = values.reshape(rows, own, parts, count, width // count)
    moved = lax.all_to_all(
        jnp.transpose(view, (3, 0, 1, 2, 4)), "seq", split_axis=0, concat_axis=0, tiled=True
    )
    return jnp.transpose(moved, (1, 0, 2, 3, 4)).reshape(rows, count * own, parts, width // count)


def to_frames(values, place):
    rows, total, parts, width = values.shape
    count = place.seq_count
    view = values.reshape(rows, count, total // count, parts, width)
    moved = lax.all_to_all(
        jnp.transpose(view, (1, 0, 2, 3, 4)), "seq", split_axis=0, concat_axis=0, tiled=True
    )
    return jnp.transpose(moved, (1, 2, 3, 0, 4)).reshape(
        rows, total // count, parts, count * width
    )


def allowed_of(query_seg, key_seg, query_pos, key_pos):
    return (query_seg[:, None] == key_seg[None, :]) & (key_pos[None, :] <= query_pos[:, None])


def frame_attention(projected, segments, place):
    rows, own, triple = projected.shape
    width = triple // 3
    parts = projected.reshape(rows, own, 3, width)
    every_segment = lax.all_gather(segments, "seq", axis=1, tiled=True)
    every_pos = jnp.arange(own * place.seq_count)
    if HEADS % place.seq_count == 0:
        packed = to_heads(parts, place)
        sets = [split_heads(packed[:, :, part]) for part in range(3)]

        def one_row(items):
            queries, keys, values, segs = items
            return attend(queries, keys, values, allowed_of(segs, segs, every_pos, every_pos))

        attended = lax.map(one_row, (*sets, every_segment))
        attended = to_frames(attended.reshape(rows, own * place.seq_count, 1, -1), place)

        def backward(out_grad):
            grads = to_heads(out_grad.reshape(rows, own, 1, width), place)[:, :, 0]

            def one_row(items):
                queries, keys, values, segs, grad = items
                return attend_grads(
                    queries, keys, values, allowed_of(segs, segs, every_pos, every_pos), grad
                )

            found = lax.map(one_row, (*sets, every_segment, split_heads(grads)))
            packed_grad = jnp.stack(
                [grad.reshape(rows, own * place.seq_count, -1) for grad in found], axis=2
            ).astype(BF)
            return to_frames(packed_grad, place).reshape(rows, own, triple)

        return attended.reshape(rows, own, width), backward

    keys = lax.all_gather(parts[:, :, 1], "seq", axis=1, tiled=True)
    values = lax.all_gather(parts[:, :, 2], "seq", axis=1, tiled=True)
    sets = (split_heads(parts[:, :, 0]), split_heads(keys), split_heads(values))
    own_pos = place.seq * own + jnp.arange(own)

    def one_row(items):
        row_q, row_k, row_v, own_segs, segs = items
        return attend(row_q, row_k, row_v, allowed_of(own_segs, segs, own_pos, every_pos))

    attended = lax.map(one_row, (*sets, segments, every_segment)).reshape(rows, own, width)

    def backward(out_grad):
        def one_row(items):
            row_q, row_k, row_v, own_segs, segs, grad = items
            allowed = allowed_of(own_segs, segs, own_pos, every_pos)
            return attend_grads(row_q, row_k, row_v, allowed, grad)

        query_grad, key_grad, value_grad = lax.map(
            one_row, (*sets, segments, every_segment, split_heads(out_grad))
        )
        both = jnp.stack([key_grad.reshape(rows, -1, width), value_grad.reshape(rows, -1, width)], 2)
        both = lax.psum_scatter(both, "seq", scatter_dimension=1, tiled=True)
        parts_grad = [query_grad.reshape(rows, own, width), both[:, :, 0], both[:, :, 1]]
        return jnp.concatenate(parts_grad, axis=-1).astype(BF)

    return attended, backward


def head_sums(values, marks):
    return jnp.dot(values, marks, precision=lax.Precision.HIGHEST, preferred_element_type=F32)


def head_spread(values, marks):
    return lax.dot_general(
        values.astype(BF), marks.astype(BF), (((1,), (1,)), ((), ())), preferred_element_type=F32
    )


def codec_softmax(queries, keys, marks):
    result = []
    for later in range(len(queries)):
        scores = [
            head_sums(queries[later].astype(F32) * keys[earlier].astype(F32), marks) * FACTOR
            for earlier in range(later + 1)
        ]
        top = scores[0]
        for score in scores[1:]:
            top = jnp.maximum(top, score)
        powers = [jnp.exp(score - top) for score in scores]
        total = sum(powers)
        result.append([power / total for power in powers])
    return result


def codec_attend(soft, values, marks):
    result = []
    for row in soft:
        total = 0.0
        for earlier, portion in enumerate(row):
            total = total + head_spread(portion, marks) * values[earlier].astype(F32)
        result.append(total.astype(BF))
    return result


def codec_attend_grads(soft, queries, keys, values, grads, marks):
    count = len(queries)
    query_grad = []
    key_grad = [0.0] * count
    value_grad = [0.0] * count
    for later in range(count):
        grad = grads[later].astype(F32)
        portion_grads = [
            head_sums(grad * values[earlier].astype(F32), marks) for earlier in range(later + 1)
        ]
        mean = sum(soft[later][i] * portion_grads[i] for i in range(later + 1))
        total = 0.0
        for earlier in range(later + 1):
            score_grad = soft[later][earlier] * (portion_grads[earlier] - mean)
            wide = head_spread(score_grad, marks)
            total = total + wide * keys[earlier].astype(F32)
            key_grad[earlier] = key_grad[earlier] + wide * queries[later].astype(F32)
            value_grad[earlier] = value_grad[earlier] + head_spread(soft[later][earlier], marks) * grad
        query_grad.append(total * FACTOR)
    return jnp.concatenate(
        [
            jnp.concatenate(
                [query_grad[t], key_grad[t] * FACTOR, value_grad[t]], axis=-1
            ).astype(BF)
            for t in range(count)
        ],
        axis=0,
    )


LANES = 128
TILE = 256
VMEM_LIMIT = 48 * 1024 * 1024


def whole_block(shape):
    return pl.BlockSpec(shape, lambda *_: (0,) * len(shape))


def causal_tiles(length):
    tile = min(TILE, length)
    return [(start, tile, start + tile) for start in range(0, length, tile)]


def head_masks(dtype):
    lane = lax.broadcasted_iota(jnp.int32, (1, LANES), 1)
    return [((lane // HEAD) == head).astype(dtype) for head in range(LANES // HEAD)]


def frame_attend_kernel(packed_ref, seg_col_ref, seg_row_ref, out_ref):
    chunks, _, own, _ = packed_ref.shape
    length = chunks * own
    packed = packed_ref[...].reshape(length, 3 * LANES)
    queries, keys, values = (packed[:, LANES * i : LANES * (i + 1)] for i in range(3))
    masks = head_masks(BF)
    lane = lax.broadcasted_iota(jnp.int32, (1, LANES), 1)
    for start, tile, end in causal_tiles(length):
        query_pos = start + lax.broadcasted_iota(jnp.int32, (tile, end), 0)
        key_pos = lax.broadcasted_iota(jnp.int32, (tile, end), 1)
        allowed = (seg_col_ref[0, start:end] == seg_row_ref[0, :, :end]) & (key_pos <= query_pos)
        result = jnp.zeros((tile, LANES), F32)
        for head, mask in enumerate(masks):
            scores = inner_right(queries[start:end] * mask, keys[:end]) * FACTOR
            scores = jnp.where(allowed, scores, MASKED)
            powers = jnp.exp(scores - jnp.max(scores, axis=1, keepdims=True))
            portions = powers / jnp.sum(powers, axis=1, keepdims=True)
            found = matmul(portions.astype(BF), values[:end])
            result = jnp.where(lane // HEAD == head, found, result)
        out_ref[start // own : end // own, 0] = result.astype(BF).reshape(tile // own, own, LANES)


def frame_attend_grads_kernel(packed_ref, grad_ref, seg_col_ref, seg_row_ref, out_ref, key_sum, value_sum):
    chunks, _, own, _ = packed_ref.shape
    length = chunks * own
    packed = packed_ref[...].reshape(length, 3 * LANES)
    queries, keys, values = (packed[:, LANES * i : LANES * (i + 1)] for i in range(3))
    grads = grad_ref[...].reshape(length, LANES)
    masks = head_masks(BF)
    lane = lax.broadcasted_iota(jnp.int32, (1, LANES), 1)
    key_sum[...] = jnp.zeros_like(key_sum)
    value_sum[...] = jnp.zeros_like(value_sum)
    for start, tile, end in causal_tiles(length):
        key_pos = lax.broadcasted_iota(jnp.int32, (end, tile), 0)
        query_pos = start + lax.broadcasted_iota(jnp.int32, (end, tile), 1)
        allowed = (seg_col_ref[0, :end] == seg_row_ref[0, :, start:end]) & (key_pos <= query_pos)
        query_grad = jnp.zeros((tile, LANES), F32)
        for head, mask in enumerate(masks):
            query = queries[start:end] * mask
            grad = grads[start:end] * mask
            scores = inner_right(keys[:end], query) * FACTOR
            scores = jnp.where(allowed, scores, MASKED)
            powers = jnp.exp(scores - jnp.max(scores, axis=0, keepdims=True))
            portions = powers / jnp.sum(powers, axis=0, keepdims=True)
            portion_grad = inner_right(values[:end], grad)
            mean = jnp.sum(portions * portion_grad, axis=0, keepdims=True)
            score_grad = (portions * (portion_grad - mean)).astype(BF)
            key_sum[:end] += matmul(score_grad, query)
            value_sum[:end] += matmul(portions.astype(BF), grad)
            found = inner_left(score_grad, keys[:end])
            query_grad = jnp.where(lane // HEAD == head, found, query_grad)
        out_ref[start // own : end // own, 0, :, :LANES] = (
            (query_grad * FACTOR).astype(BF).reshape(tile // own, own, LANES)
        )
    out_ref[:, 0, :, LANES : 2 * LANES] = (key_sum[...] * FACTOR).astype(BF).reshape(chunks, own, LANES)
    out_ref[:, 0, :, 2 * LANES :] = value_sum[...].astype(BF).reshape(chunks, own, LANES)


def row_spec(chunks, own, breadth):
    return pl.BlockSpec((chunks, 1, own, breadth), lambda row: (0, row, 0, 0))


def segment_specs(length):
    return [
        pl.BlockSpec((1, length, 1), lambda row: (row, 0, 0)),
        pl.BlockSpec((1, 1, length), lambda row: (row, 0, 0)),
    ]


def frame_attend_call(packed, segments):
    chunks, rows, own, _ = packed.shape
    length = chunks * own
    return pl.pallas_call(
        frame_attend_kernel,
        grid=(rows,),
        in_specs=[row_spec(chunks, own, 3 * LANES), *segment_specs(length)],
        out_specs=row_spec(chunks, own, LANES),
        out_shape=jax.ShapeDtypeStruct((chunks, rows, own, LANES), BF),
        compiler_params=pltpu.CompilerParams(vmem_limit_bytes=VMEM_LIMIT),
        cost_estimate=pl.CostEstimate(
            flops=rows * length * length * LANES * 5,
            bytes_accessed=packed.size * 3,
            transcendentals=rows * length * length,
        ),
        name="frame_attend",
    )(packed, segments[:, :, None], segments[:, None, :])


def frame_attend_grads_call(packed, grads, segments):
    chunks, rows, own, _ = packed.shape
    length = chunks * own
    return pl.pallas_call(
        frame_attend_grads_kernel,
        grid=(rows,),
        in_specs=[
            row_spec(chunks, own, 3 * LANES),
            row_spec(chunks, own, LANES),
            *segment_specs(length),
        ],
        out_specs=row_spec(chunks, own, 3 * LANES),
        out_shape=jax.ShapeDtypeStruct((chunks, rows, own, 3 * LANES), BF),
        scratch_shapes=[pltpu.VMEM((length, LANES), F32), pltpu.VMEM((length, LANES), F32)],
        compiler_params=pltpu.CompilerParams(vmem_limit_bytes=VMEM_LIMIT),
        cost_estimate=pl.CostEstimate(
            flops=rows * length * length * LANES * 12,
            bytes_accessed=packed.size * 5,
            transcendentals=rows * length * length,
        ),
        name="frame_attend_grads",
    )(packed, grads, segments[:, :, None], segments[:, None, :])


def position_pairs(positions):
    return [(later, earlier) for later in range(1, positions) for earlier in range(later + 1)]


def codec_sums(products, marks):
    stacked = jnp.concatenate(products, axis=0)
    high = stacked.astype(BF)
    low = (stacked - high.astype(F32)).astype(BF)
    total = matmul(high, marks) + matmul(low, marks)
    size = products[0].shape[0]
    return [total[size * i : size * (i + 1)] for i in range(len(products))]


def codec_spread(portions, marks):
    stacked = jnp.concatenate([portion.astype(BF) for portion in portions], axis=0)
    total = inner_right(stacked, marks)
    size = portions[0].shape[0]
    return [total[size * i : size * (i + 1)] for i in range(len(portions))]


def codec_portions(queries, keys, marks, pairs):
    scores = codec_sums(
        [queries[later].astype(F32) * keys[earlier].astype(F32) for later, earlier in pairs], marks
    )
    scores = dict(zip(pairs, [score * FACTOR for score in scores]))
    portions = {}
    for later in range(1, len(queries)):
        row = [scores[later, earlier] for earlier in range(later + 1)]
        top = functools.reduce(jnp.maximum, row)
        powers = [jnp.exp(score - top) for score in row]
        total = functools.reduce(jnp.add, powers)
        for earlier in range(later + 1):
            portions[later, earlier] = powers[earlier] / total
    return portions


def codec_parts(packed_ref, width):
    positions = packed_ref.shape[0]
    return [
        [packed_ref[t, :, width * part : width * (part + 1)] for t in range(positions)]
        for part in range(3)
    ]


def codec_attend_kernel(packed_ref, marks_ref, out_ref):
    positions, _, width = out_ref.shape
    queries, keys, values = codec_parts(packed_ref, width)
    marks = marks_ref[...]
    pairs = position_pairs(positions)
    portions = codec_portions(queries, keys, marks, pairs)
    wide = dict(zip(pairs, codec_spread([portions[pair] for pair in pairs], marks)))
    out_ref[0] = values[0]
    for later in range(1, positions):
        terms = [wide[later, e] * values[e].astype(F32) for e in range(later + 1)]
        out_ref[later] = functools.reduce(jnp.add, terms).astype(BF)


def codec_attend_grads_kernel(packed_ref, grad_ref, marks_ref, out_ref):
    positions, _, width = grad_ref.shape
    queries, keys, values = codec_parts(packed_ref, width)
    marks = marks_ref[...]
    pairs = position_pairs(positions)
    portions = codec_portions(queries, keys, marks, pairs)
    grads = [grad_ref[t].astype(F32) for t in range(positions)]
    portion_grads = dict(
        zip(
            pairs,
            codec_sums([grads[later] * values[earlier].astype(F32) for later, earlier in pairs], marks),
        )
    )
    score_grads = {}
    for later in range(1, positions):
        mean = functools.reduce(
            jnp.add, [portions[later, e] * portion_grads[later, e] for e in range(later + 1)]
        )
        for e in range(later + 1):
            score_grads[later, e] = portions[later, e] * (portion_grads[later, e] - mean)
    wide = dict(zip(pairs, codec_spread([portions[pair] for pair in pairs], marks)))
    wide_grads = dict(zip(pairs, codec_spread([score_grads[pair] for pair in pairs], marks)))
    zero = jnp.zeros_like(grads[0])
    for t in range(positions):
        query_grad = key_grad = zero
        value_grad = grads[0] if t == 0 else zero
        for later, earlier in pairs:
            if later == t:
                query_grad = query_grad + wide_grads[later, earlier] * keys[earlier].astype(F32)
            if earlier == t:
                key_grad = key_grad + wide_grads[later, earlier] * queries[later].astype(F32)
                value_grad = value_grad + wide[later, earlier] * grads[later]
        out_ref[t, :, :width] = (query_grad * FACTOR).astype(BF)
        out_ref[t, :, width : 2 * width] = (key_grad * FACTOR).astype(BF)
        out_ref[t, :, 2 * width :] = value_grad.astype(BF)


def codec_tile(frame_total):
    return 64 if frame_total % 64 == 0 else frame_total


def codec_spec(positions, tile, breadth):
    return pl.BlockSpec((positions, tile, breadth), lambda i: (0, i, 0))


def head_marks(width):
    return (
        jnp.arange(width)[:, None] // HEAD == jnp.arange(LANES)[None, :]
    ).astype(BF)


def codec_attend_call(packed):
    positions, total, triple = packed.shape
    width = triple // 3
    tile = codec_tile(total)
    return pl.pallas_call(
        codec_attend_kernel,
        grid=(total // tile,),
        in_specs=[codec_spec(positions, tile, triple), whole_block((width, LANES))],
        out_specs=codec_spec(positions, tile, width),
        out_shape=jax.ShapeDtypeStruct((positions, total, width), BF),
        compiler_params=pltpu.CompilerParams(vmem_limit_bytes=VMEM_LIMIT),
        cost_estimate=pl.CostEstimate(
            flops=total * width * LANES * 30, bytes_accessed=packed.size * 3, transcendentals=0
        ),
        name="codec_attend",
    )(packed, head_marks(width))


def codec_attend_grads_call(packed, grads):
    positions, total, triple = packed.shape
    width = triple // 3
    tile = codec_tile(total)
    return pl.pallas_call(
        codec_attend_grads_kernel,
        grid=(total // tile,),
        in_specs=[
            codec_spec(positions, tile, triple),
            codec_spec(positions, tile, width),
            whole_block((width, LANES)),
        ],
        out_specs=codec_spec(positions, tile, triple),
        out_shape=jax.ShapeDtypeStruct((positions, total, triple), BF),
        compiler_params=pltpu.CompilerParams(vmem_limit_bytes=VMEM_LIMIT),
        cost_estimate=pl.CostEstimate(
            flops=total * width * LANES * 70, bytes_accessed=packed.size * 5, transcendentals=0
        ),
        name="codec_attend_grads",
    )(packed, grads, head_marks(width))


BITS = {"y": ("mp", 2), "x": ("seq", 1), "n": ("seq", 2), "f": ("seq", 4)}


def grad_order(place):
    flips = []
    for bits in ((1, 2, 4), (2, 1, 4), (1, 2, 4)):
        for step in range(8):
            flips.append(sum(bit for at, bit in enumerate(bits) if not (step >> (2 - at)) & 1))
    return jnp.stack(
        [place.mp ^ 2, place.mp] + [place.seq ^ flip for flip in flips] + [place.seq]
    ).astype(jnp.int32)


STEPS = {"y": (2, "xnf"), "n": (10, "nxf"), "x": (18, "xnf")}
OWN_SEQ = 26


def keep_flags(order_ref, seq):
    change = order_ref[OWN_SEQ] ^ seq
    return {"x": 1 - (change & 1), "n": 1 - ((change >> 1) & 1), "f": 1 - ((change >> 2) & 1)}


def grad_rows_kernel(stages, wide, order_ref, far_own, far_rec, own_own, own_rec, latter_own, latter_rec, *refs):
    send_ref, keep_ref, turned = refs[-3:]
    rows = latter_own.shape[0]
    height = far_own.shape[1]

    @pl.when(pl.program_id(0) == 0)
    def _():
        for at, (own, rec) in enumerate(((far_own, far_rec), (own_own, own_rec))):
            turned[height * at : height * (at + 1), :rows] = own[...].T
            turned[height * at : height * (at + 1), rows:] = rec[...].T

    total = matmul(turned[:, :rows], latter_own[...]) + matmul(turned[:, rows:], latter_rec[...])
    store = grad_store_wide if wide else grad_store
    store(stages, order_ref, total.astype(BF), height, send_ref, keep_ref)


def grad_store_wide(stages, order_ref, total, height, send_ref, keep_ref):
    units = height // TILE
    chunks = total.shape[1] // 8 // LANES
    for seq in range(8):
        flags = keep_flags(order_ref, seq)
        for chunk in range(chunks):
            first = (seq * chunks + chunk) * LANES
            for unit in range(units):
                at = chunk * units + unit
                for kept in range(2):
                    start = height * kept + unit * TILE
                    value = total[start : start + TILE, first : first + LANES]
                    spot = {**flags, "y": kept}
                    where = tuple(spot[stage] for stage in stages[1:])
                    for target, when in ((send_ref, 0), (keep_ref, 1)):

                        @pl.when(spot[stages[0]] == when)
                        def _(target=target, where=where, at=at, value=value):
                            target[(*where, at)] = value


def grad_store(stages, order_ref, total, height, send_ref, keep_ref):
    chunks = total.shape[1] // LANES
    for chunk in range(chunks):
        value = total[:, chunk * LANES : (chunk + 1) * LANES]
        given, kept = value[:height], value[height:]
        if stages[0] == "y":
            send_ref[0, 0, 0, chunk] = given
            keep_ref[0, 0, 0, chunk] = kept
        else:
            spots = [tuple(side if stage == "y" else 0 for stage in stages[1:]) for side in range(2)]
            for target, when in ((send_ref, pl.program_id(0) < 4), (keep_ref, pl.program_id(0) >= 4)):

                @pl.when(when)
                def _(target=target, given=given, kept=kept, chunk=chunk):
                    target[(*spots[0], chunk)] = given
                    target[(*spots[1], chunk)] = kept


def grad_buffers(units):
    return [jax.ShapeDtypeStruct((2, 2, 2, units, TILE, LANES), BF)] * 2


def grad_call(kernel, order, arrays, in_specs, out_specs, units, into, steps, scratch, flops, name):
    aliases = {}
    moved = 2 * sum(array.size for array in arrays)
    if into is not None:
        aliases = {len(arrays) + 1: 0, len(arrays) + 2: 1}
        in_specs = in_specs + [pl.BlockSpec(memory_space=pl.ANY)] * 2
        arrays = arrays + list(into)
    return pl.pallas_call(
        kernel,
        grid_spec=pltpu.PrefetchScalarGridSpec(
            num_scalar_prefetch=1,
            grid=(steps,),
            in_specs=in_specs,
            out_specs=out_specs,
            scratch_shapes=[scratch],
        ),
        out_shape=grad_buffers(units),
        input_output_aliases=aliases,
        compiler_params=pltpu.CompilerParams(vmem_limit_bytes=VMEM_LIMIT),
        cost_estimate=pl.CostEstimate(flops=flops, bytes_accessed=moved, transcendentals=0),
        name=name,
    )(order, *arrays)


def grad_rows(former, latter, order, stages, units, offset, into=None):
    rows, breadth = latter[0].shape
    height = former[0].shape[1] // 4
    wide = breadth // 8 == LANES
    chunks = breadth // 8 // LANES
    steps = 1 if wide else 8
    arrays = [former[0], former[1], former[0], former[1], latter[0], latter[1]]
    former_specs = [
        pl.BlockSpec((rows, height), lambda j, t, at=at: (0, t[at]), pipeline_mode=pl.Buffered(1))
        for at in (0, 0, 1, 1)
    ]
    if wide:
        latter_specs = [whole_block((rows, breadth))] * 2
        block = (2, 2, 2, 1, TILE, LANES)
        out_specs = [pl.BlockSpec(block, lambda j, t: (0, 0, 0, offset, 0, 0))] * 2
    else:
        base = offset // chunks
        table, names = STEPS[stages[0]]
        bits = {name: 2 - at for at, name in enumerate(names)}
        if stages[0] == "y":
            block = (1, 1, 1, chunks, TILE, LANES)

            def where(j):
                return tuple((j >> bits[stage]) & 1 for stage in stages[1:]) + (base, 0, 0)

            out_specs = [pl.BlockSpec(block, lambda j, t: where(j))] * 2
        else:
            block = tuple(2 if stage == "y" else 1 for stage in stages[1:]) + (chunks, TILE, LANES)

            def where(j):
                return tuple(
                    0 if stage == "y" else (j >> bits[stage]) & 1 for stage in stages[1:]
                ) + (base, 0, 0)

            out_specs = [
                pl.BlockSpec(block, lambda j, t: where(jnp.minimum(j, 3))),
                pl.BlockSpec(block, lambda j, t: where(jnp.maximum(j - 4, 0))),
            ]
        latter_specs = [
            pl.BlockSpec((rows, breadth // 8), lambda j, t: (0, t[table + j]))
        ] * 2
    return grad_call(
        functools.partial(grad_rows_kernel, stages, wide),
        order,
        arrays,
        former_specs + latter_specs,
        out_specs,
        units,
        into,
        steps,
        pltpu.VMEM((2 * height, 2 * rows), BF),
        2 * 2 * rows * 2 * height * breadth,
        "grad_rows",
    )


def grad_columns_kernel(stages, order_ref, latter_own, latter_rec, former_own, former_rec, *refs):
    send_ref, keep_ref, turned = refs[-3:]
    rows = latter_own.shape[0]
    step = pl.program_id(0)

    @pl.when(step == 0)
    def _():
        turned[:, :rows] = latter_own[...].T
        turned[:, rows:] = latter_rec[...].T

    total = matmul(turned[:, :rows], former_own[...]) + matmul(turned[:, rows:], former_rec[...])
    total = total.astype(BF)
    chunks = total.shape[1] // LANES
    for target, when in ((send_ref, step < pl.num_programs(0) // 2), (keep_ref, step >= pl.num_programs(0) // 2)):

        @pl.when(when)
        def _(target=target):
            for seq in range(8):
                flags = keep_flags(order_ref, seq)
                where = tuple(flags[stage] for stage in stages[1:])
                for chunk in range(chunks):
                    half = (chunk % 2) * LANES
                    target[(*where, chunk // 2, slice(half, half + LANES))] = total[
                        seq * LANES : (seq + 1) * LANES, chunk * LANES : (chunk + 1) * LANES
                    ]


def grad_columns(former, latter, order, stages, units, offset, into=None):
    rows, breadth = latter[0].shape
    height = former[0].shape[1] // 4
    step = min(512, height)
    per = height // step
    block = (2, 2, 2, step // TILE, TILE, LANES)
    base = offset // (step // TILE)
    latter_specs = [
        pl.BlockSpec((rows, breadth), lambda j, t: (0, 0), pipeline_mode=pl.Buffered(1))
    ] * 2
    former_specs = [pl.BlockSpec((rows, step), lambda j, t: (0, t[j // per] * per + j % per))] * 2
    out_specs = [
        pl.BlockSpec(block, lambda j, t: (0, 0, 0, base + jnp.minimum(j, per - 1), 0, 0)),
        pl.BlockSpec(block, lambda j, t: (0, 0, 0, base + jnp.maximum(j - per, 0), 0, 0)),
    ]
    return grad_call(
        functools.partial(grad_columns_kernel, stages),
        order,
        [latter[0], latter[1], former[0], former[1]],
        latter_specs + former_specs,
        out_specs,
        units,
        into,
        2 * per,
        pltpu.VMEM((breadth, 2 * rows), BF),
        2 * 2 * rows * 2 * height * breadth,
        "grad_columns",
    )


def grad_table_kernel(stages, height, order_ref, codes_ref, latter_own, latter_rec, *refs):
    send_ref, keep_ref, _ = refs[-3:]
    rows = latter_own.shape[0]
    parts = []
    for at in range(2):
        entry = order_ref[at] * height + lax.broadcasted_iota(jnp.int32, (height, 2 * rows), 0)
        parts.append((entry == codes_ref[...]).astype(F32).astype(BF))
    chosen = jnp.concatenate(parts, axis=0)
    total = matmul(chosen[:, :rows], latter_own[...]) + matmul(chosen[:, rows:], latter_rec[...])
    grad_store_wide(stages, order_ref, total.astype(BF), height, send_ref, keep_ref)


def grad_table(codes, latter, order, stages, height, units, offset, into=None):
    rows, breadth = latter[0].shape
    block = (2, 2, 2, height // TILE, TILE, LANES)
    base = offset // (height // TILE)
    return grad_call(
        functools.partial(grad_table_kernel, stages, height),
        order,
        [codes, latter[0], latter[1]],
        [whole_block(codes.shape), whole_block((rows, breadth)), whole_block((rows, breadth))],
        [pl.BlockSpec(block, lambda j, t: (0, 0, 0, base, 0, 0))] * 2,
        units,
        into,
        1,
        pltpu.VMEM((8, LANES), F32),
        2 * 2 * rows * 2 * height * breadth,
        "grad_table",
    )


def rows_from_units(units, height):
    tiles = height // TILE
    chunks = units.shape[0] // tiles
    return jnp.transpose(
        units.reshape(chunks, height, LANES), (1, 0, 2)
    ).reshape(height, chunks * LANES)


def columns_from_units(units):
    count = units.shape[0]
    return jnp.transpose(units.reshape(2 * count, LANES, LANES), (0, 2, 1)).reshape(count * TILE, LANES)


PACK = 1024


def pack_rows(members):
    return sum(member.shape[0] * (member.shape[1] // PACK) for member in members)


def pack_pieces(shapes):
    found, start = [], 0
    for at, (height, breadth) in enumerate(shapes):
        for column in range(breadth // PACK):
            found.append((at, column, height, start))
            start += height
    return found


def columns_of(column):
    return pl.ds(column * PACK, PACK)


def pack_kernel(place_ref, *refs):
    members, (pack_ref, quarter_ref, held, sems, out_sems) = refs[:-5], refs[-5:]
    rows = held.shape[0] // 4
    copies = []
    for number, (at, column, height, start) in enumerate(pack_pieces([m.shape for m in members])):
        copies.append(
            pltpu.make_async_copy(
                members[at].at[:, columns_of(column)], held.at[pl.ds(start, height)], sems.at[number]
            )
        )
    for copy in copies:
        copy.start()
    for copy in copies:
        copy.wait()
    mine = pl.ds(pl.multiple_of(place_ref[1] * rows, 16), rows)
    whole = pltpu.make_async_copy(held, pack_ref, out_sems.at[0])
    part = pltpu.make_async_copy(held.at[mine], quarter_ref, out_sems.at[1])
    part.start()
    whole.start()
    part.wait()
    whole.wait()


def pack_call(members, spots):
    rows = pack_rows(members)
    any_spec = pl.BlockSpec(memory_space=pl.ANY)
    count = len(pack_pieces([m.shape for m in members]))
    return pl.pallas_call(
        pack_kernel,
        in_specs=[pl.BlockSpec(memory_space=pltpu.SMEM)] + [any_spec] * len(members),
        out_specs=[any_spec] * 2,
        out_shape=[
            jax.ShapeDtypeStruct((rows, PACK), BF),
            jax.ShapeDtypeStruct((rows // 4, PACK), BF),
        ],
        scratch_shapes=[
            pltpu.VMEM((rows, PACK), BF),
            pltpu.SemaphoreType.DMA((count,)),
            pltpu.SemaphoreType.DMA((2,)),
        ],
        compiler_params=pltpu.CompilerParams(vmem_limit_bytes=VMEM_LIMIT),
        cost_estimate=pl.CostEstimate(flops=0, bytes_accessed=4 * rows * PACK, transcendentals=0),
        name="pack_weights",
    )(spots, *members)


def join_kernel(shapes, parts, place_ref, *refs):
    count = len(parts)
    sources = refs[:count]
    outs = refs[count : count + len(shapes)]
    held, sems, out_sems = refs[-3:]
    rows = held.shape[0] // 4
    quarter = rows // 4
    copies = []
    for number, (source, (flip, change, offset)) in enumerate(zip(sources, parts)):
        start = (place_ref[0] ^ flip) * rows + offset
        if change is not None:
            start = start + (place_ref[1] ^ change) * quarter
        size = source.shape[0]
        copies.append(
            pltpu.make_async_copy(
                source, held.at[pl.ds(pl.multiple_of(start, 16), size)], sems.at[number]
            )
        )
    for copy in copies:
        copy.start()
    for copy in copies:
        copy.wait()
    copies = []
    for at, column, height, start in pack_pieces(shapes):
        for block in range(4):
            copies.append(
                pltpu.make_async_copy(
                    held.at[pl.ds(block * rows + start, height)],
                    outs[at].at[pl.ds(block * height, height), columns_of(column)],
                    out_sems.at[len(copies)],
                )
            )
    for copy in copies:
        copy.start()
    for copy in copies:
        copy.wait()


def join_weights(members, pieces, parts, spots):
    shapes = [member.shape for member in members]
    rows = pack_rows(members)
    any_spec = pl.BlockSpec(memory_space=pl.ANY)
    outs = [jax.ShapeDtypeStruct((4 * height, breadth), BF) for height, breadth in shapes]
    return pl.pallas_call(
        functools.partial(join_kernel, shapes, parts),
        in_specs=[pl.BlockSpec(memory_space=pltpu.SMEM)] + [any_spec] * len(pieces),
        out_specs=[any_spec] * len(outs),
        out_shape=outs,
        scratch_shapes=[
            pltpu.VMEM((4 * rows, PACK), BF),
            pltpu.SemaphoreType.DMA((len(pieces),)),
            pltpu.SemaphoreType.DMA((4 * len(pack_pieces(shapes)),)),
        ],
        compiler_params=pltpu.CompilerParams(vmem_limit_bytes=VMEM_LIMIT),
        cost_estimate=pl.CostEstimate(flops=0, bytes_accessed=16 * rows * PACK, transcendentals=0),
        name="join_weights",
    )(spots, *pieces)


def shards_general(
    frames,
    segments,
    padding,
    codec_tokens,
    codebooks,
    frame_prenorm,
    frame_project,
    frame_output,
    frame_postnorm,
    frame_expand,
    frame_contract,
    codec_prenorm,
    codec_project,
    codec_output,
    codec_postnorm,
    codec_expand,
    codec_contract,
    cotangent,
):
    place = Place()
    row_count, frames_dev, width = frames.shape
    frame_total = row_count * frames_dev
    positions = cotangent.shape[2]
    gains = lax.all_gather(
        jnp.stack([frame_prenorm, frame_postnorm, codec_prenorm, codec_postnorm]),
        "mp",
        axis=1,
        tiled=True,
    )
    frame_weights = (
        gains[0],
        gather_weight(frame_project, place),
        gather_weight(frame_output, place),
        gains[1],
        gather_weight(frame_expand, place),
        gather_weight(frame_contract, place),
    )
    codec_weights = (
        gains[2],
        gather_weight(codec_project, place),
        gather_weight(codec_output, place),
        gains[3],
        gather_weight(codec_expand, place),
        gather_weight(codec_contract, place),
    )
    table = gather_weight(codebooks, place)

    hidden = frames.astype(F32).reshape(frame_total, width)
    normed, projected = front_pass(hidden, frame_weights)
    attended, attention_back = frame_attention(
        projected.reshape(row_count, frames_dev, 3 * width), segments, place
    )
    attended = attended.reshape(frame_total, width)
    frame_result, frame_saved = rear_pass(hidden, attended, frame_weights)
    base = frame_result.astype(BF).astype(F32)

    table_rows = codec_tokens.reshape(positions - 1, frame_total) + (
        jnp.arange(positions - 1, dtype=jnp.int32) * CODES
    )[:, None]
    embedded = table[table_rows].astype(F32)
    codec_hidden = jnp.concatenate([base[None], base[None] + embedded], axis=0).reshape(
        positions * frame_total, width
    )
    codec_normed, codec_projected = front_pass(codec_hidden, codec_weights)
    marks = (
        jnp.arange(width)[:, None] // HEAD == jnp.arange(HEADS)[None, :]
    ).astype(F32)
    view = codec_projected.reshape(positions, frame_total, 3, width)
    queries, keys, values = ([view[t, :, part] for t in range(positions)] for part in range(3))
    soft = codec_softmax(queries, keys, marks)
    codec_attended = jnp.concatenate(codec_attend(soft, values, marks), axis=0)
    codec_result, codec_saved = rear_pass(codec_hidden, codec_attended, codec_weights)
    live = padding.reshape(frame_total).astype(F32)[None, :, None]
    output = jnp.transpose(
        (codec_result.reshape(positions, frame_total, width) * live).astype(BF), (1, 0, 2)
    ).reshape(row_count, frames_dev, positions, width)

    codec_grad = (
        jnp.transpose(cotangent.reshape(frame_total, positions, width), (1, 0, 2)).astype(F32) * live
    ).reshape(positions * frame_total, width)
    mixed_grad, attended_grad, codec_postnorm_grad, contract_in, expand_in, output_in = rear_grads(
        codec_grad, codec_saved, codec_weights
    )
    codec_contract_part = weight_grad(codec_saved[3], contract_in, place, True)
    codec_expand_part = weight_grad(codec_saved[1], expand_in, place, False)
    codec_output_part = weight_grad(codec_attended, output_in, place, True)
    grad_view = attended_grad.reshape(positions, frame_total, width)
    codec_projected_grad = codec_attend_grads(
        soft, queries, keys, values, [grad_view[t] for t in range(positions)], marks
    )
    codec_project_part = weight_grad(codec_normed, codec_projected_grad, place, True)
    input_grad, codec_prenorm_grad = front_grads(
        codec_hidden, codec_projected_grad, mixed_grad, codec_weights
    )
    input_grad = input_grad.reshape(positions, frame_total, width)
    chosen = (
        table_rows.reshape(-1)[:, None] == jnp.arange(table.shape[0], dtype=jnp.int32)[None, :]
    ).astype(BF)
    table_part = weight_grad(chosen, input_grad[1:].reshape(-1, width).astype(BF), place, False)
    base_grad = jnp.sum(input_grad, axis=0).astype(BF).astype(F32)

    (codec_contract_grad,) = finish_grads([codec_contract_part], place)
    codec_expand_grad, codec_output_grad, codec_project_grad = finish_grads(
        [codec_expand_part, codec_output_part, codec_project_part], place
    )
    (table_grad,) = finish_grads([table_part], place)

    frame_mixed_grad, frame_attended_grad, frame_postnorm_grad, contract_in, expand_in, output_in = (
        rear_grads(base_grad, frame_saved, frame_weights)
    )
    frame_projected_grad = attention_back(
        frame_attended_grad.reshape(row_count, frames_dev, width)
    ).reshape(frame_total, 3 * width)
    frame_contract_part = weight_grad(frame_saved[3], contract_in, place, True)
    frame_expand_part = weight_grad(frame_saved[1], expand_in, place, False)
    frame_output_part = weight_grad(attended, output_in, place, True)
    frame_project_part = weight_grad(normed, frame_projected_grad, place, True)
    frames_grad, frame_prenorm_grad = front_grads(
        hidden, frame_projected_grad, frame_mixed_grad, frame_weights
    )
    (frame_contract_grad,) = finish_grads([frame_contract_part], place)
    frame_expand_grad, frame_output_grad = finish_grads(
        [frame_expand_part, frame_output_part], place
    )
    (frame_project_grad,) = finish_grads([frame_project_part], place)
    gain_sums = sum_everywhere(
        jnp.stack(
            [frame_prenorm_grad, frame_postnorm_grad, codec_prenorm_grad, codec_postnorm_grad]
        ),
        place,
    )
    return (
        output,
        frames_grad.reshape(row_count, frames_dev, width),
        table_grad,
        gain_sums[0],
        frame_project_grad,
        frame_output_grad,
        gain_sums[1],
        frame_expand_grad,
        frame_contract_grad,
        gain_sums[2],
        codec_project_grad,
        codec_output_grad,
        gain_sums[3],
        codec_expand_grad,
        codec_contract_grad,
    )


class Chain:
    def __init__(self):
        self.last = ()

    def enter(self, *values):
        held = lax.optimization_barrier(tuple(values) + self.last)
        return held[0] if len(values) == 1 else held[: len(values)]

    def leave(self, *values):
        self.last = values


class Gather:
    def __init__(self, members, spots, whole=False):
        self.members = members
        self.spots = spots
        self.whole = whole
        self.pack, self.quarter = pack_call(members, spots)
        self.pieces = [self.pack]
        self.parts = [(0, None, 0)]

    def add(self, piece, change, offset):
        self.pieces += [piece, swap(piece, "mp", 1)]
        self.parts += [(2, change, offset), (3, change, offset)]

    def start(self, chain):
        self.far = swap(chain.enter(self.pack if self.whole else self.quarter), "mp", 2)
        self.pieces.append(swap(self.pack, "mp", 1))
        self.parts.append((1, None, 0))

    def spread(self, chain):
        far = chain.enter(self.far)
        chain.leave(far)
        if self.whole:
            self.add(far, None, 0)
            return
        self.over_x = swap(far, "seq", 1)
        self.over_n = swap(far, "seq", 2)
        self.add(far, 0, 0)

    def cross(self, chain):
        over_x, over_n = chain.enter(self.over_x, self.over_n)
        chain.leave(over_x, over_n)
        half = over_x.shape[0] // 2
        self.ends = (swap(over_n[:half], "seq", 1), swap(over_x[half:], "seq", 2))
        self.add(over_x, 1, 0)
        self.add(over_n, 2, 0)

    def close(self, chain):
        ends = chain.enter(*self.ends)
        chain.leave(*ends)
        self.add(ends[0], 3, 0)
        self.add(ends[1], 3, ends[0].shape[0])

    def join(self, chain):
        pieces = chain.enter(*self.pieces)
        outs = join_weights(self.members, pieces, tuple(self.parts), self.spots)
        chain.leave(*outs)
        return outs


class Reduce:
    def __init__(self, stages, blocks):
        self.stages = stages
        self.keep = blocks[1]
        self.came = [swap(blocks[0], *BITS[stages[0]])]

    def total(self, last):
        at = len(self.came) - 1
        spot = (1,) * at + ((0,) if not last else ())
        value = self.keep[spot].astype(F32) if spot else self.keep.astype(F32)
        for level, came in enumerate(self.came):
            value = value + came[spot[level:]].astype(F32)
        return value

    def step(self, chain):
        self.keep, *self.came = chain.enter(self.keep, *self.came)
        given = self.total(False).astype(BF)
        chain.leave(given)
        self.came.append(swap(given, *BITS[self.stages[len(self.came)]]))

    def result(self):
        return self.total(True)


def pair(values):
    return (values, swap(values, "mp", 1))


def hidden_grads(contract_in, expanded, weights):
    active_grad = inner_right(contract_in, weights[5])
    return jax.vjp(jax.nn.gelu, expanded)[1](active_grad)[0].astype(BF)


def mixed_grads(result_grad, normed_grad, mixed_sum, weights):
    mixed_part, postnorm_grad = jax.vjp(rms_scale, mixed_sum, weights[3].astype(F32))[1](normed_grad)
    mixed_grad = result_grad + mixed_part
    output_in = mixed_grad.astype(BF)
    return mixed_grad, inner_right(output_in, weights[2]).astype(BF), postnorm_grad, output_in


def shards(
    frames,
    segments,
    padding,
    codec_tokens,
    codebooks,
    frame_prenorm,
    frame_project,
    frame_output,
    frame_postnorm,
    frame_expand,
    frame_contract,
    codec_prenorm,
    codec_project,
    codec_output,
    codec_postnorm,
    codec_expand,
    codec_contract,
    cotangent,
):
    place = Place()
    chain = Chain()
    order = grad_order(place)
    spots = jnp.stack([place.mp, place.seq % 4]).astype(jnp.int32)
    row_count, frames_dev, width = frames.shape
    frame_total = row_count * frames_dev
    positions = cotangent.shape[2]
    count = place.seq_count

    gain_rows = jnp.pad(
        jnp.concatenate([frame_prenorm, frame_postnorm, codec_prenorm, codec_postnorm])[None],
        ((0, 127), (0, 0)),
    )
    first = Gather([frame_project, gain_rows], spots)
    first.start(chain)
    chain.leave(first.quarter)
    every_segment = lax.all_to_all(
        jnp.broadcast_to(segments[None], (count, row_count, frames_dev)),
        "seq",
        split_axis=0,
        concat_axis=0,
        tiled=True,
    )
    every_segment = jnp.transpose(every_segment, (1, 0, 2)).reshape(row_count, count * frames_dev)
    codes = codec_tokens.reshape(1, (positions - 1) * frame_total) + jnp.repeat(
        jnp.arange(positions - 1, dtype=jnp.int32) * CODES, frame_total
    )
    codes_both = jnp.concatenate(pair(codes), axis=1)
    live = padding.reshape(frame_total).astype(F32)[None, :, None]
    second = Gather([frame_expand, frame_contract, frame_output], spots)
    first.spread(chain)
    second.start(chain)
    codec_grad = (
        jnp.transpose(
            chain.enter(cotangent).reshape(frame_total, positions, width), (1, 0, 2)
        ).astype(F32)
        * live
    ).reshape(positions * frame_total, width)
    contract_in = pair(codec_grad.astype(BF))
    chain.leave(contract_in[0])
    first.cross(chain)
    third = Gather([codec_project, codebooks], spots, True)
    fourth = Gather([codec_expand, codec_contract, codec_output], spots)
    first.close(chain)

    weight_project, gains = first.join(chain)
    gains = jnp.transpose(
        gains.reshape(place.mp_count, -1, 4, width // 4)[:, 0], (1, 0, 2)
    ).reshape(4, width)
    hidden = frames.astype(F32).reshape(frame_total, width)
    normed, projected = front_pass(hidden, (gains[0], weight_project))
    packed = jnp.transpose(
        projected.reshape(row_count, frames_dev, 3, count, LANES), (3, 0, 1, 2, 4)
    ).reshape(count, row_count, frames_dev, 3 * LANES)
    chain.leave(packed)
    packed = lax.all_to_all(packed, "seq", split_axis=0, concat_axis=0, tiled=True)
    second.spread(chain)
    fourth.start(chain)
    second.cross(chain)
    third.start(chain)
    packed = chain.enter(packed)
    attended = frame_attend_call(packed, every_segment)
    chain.leave(attended)
    attended = lax.all_to_all(attended, "seq", split_axis=0, concat_axis=0, tiled=True)
    fourth.spread(chain)
    second.close(chain)
    weight_expand, weight_contract, weight_output = second.join(chain)
    frame_weights = (gains[0], weight_project, weight_output, gains[1], weight_expand, weight_contract)
    attended = jnp.transpose(chain.enter(attended), (1, 2, 0, 3)).reshape(frame_total, width)
    frame_result, frame_saved = rear_pass(hidden, attended, frame_weights)
    base_low = frame_result.astype(BF)
    chain.leave(base_low)
    normed_both = pair(normed)
    attended_both = pair(attended)
    normed_two_both = pair(frame_saved[1])
    activated_both = pair(frame_saved[3])

    third.spread(chain)
    fourth.cross(chain)
    weight_project, table = third.join(chain)
    embedded = table[codes.reshape(positions - 1, frame_total)].astype(F32)
    base = chain.enter(base_low).astype(F32)
    codec_hidden = jnp.concatenate([base[None], base[None] + embedded], axis=0).reshape(
        positions * frame_total, width
    )
    codec_normed, codec_projected = front_pass(codec_hidden, (gains[2], weight_project))
    codec_packed = codec_projected.reshape(positions, frame_total, 3 * width)
    chain.leave(codec_packed)
    fourth.close(chain)
    codec_attended = codec_attend_call(chain.enter(codec_packed)).reshape(
        positions * frame_total, width
    )
    chain.leave(codec_attended)
    codec_normed_both = pair(codec_normed)
    codec_attended_both = pair(codec_attended)
    weight_expand, weight_contract, weight_output = fourth.join(chain)
    codec_weights = (gains[2], weight_project, weight_output, gains[3], weight_expand, weight_contract)
    mixed_sum = codec_hidden + matmul(chain.enter(codec_attended), weight_output)
    normed_two = rms_scale(mixed_sum, gains[3].astype(F32)).astype(BF)
    expanded = matmul(normed_two, weight_expand)
    activated = jax.nn.gelu(expanded).astype(BF)

    expand_in = hidden_grads(contract_in[0], expanded, codec_weights)
    chain.leave(activated, expand_in)
    activated_pair = pair(activated)
    expand_pair = pair(expand_in)
    codec_normed_two_both = pair(normed_two)
    normed_grad = inner_right(chain.enter(expand_in), weight_expand)
    chain.leave(normed_grad)
    stages = tuple("ynxf")
    blocks = grad_columns(chain.enter(*activated_pair), contract_in, order, stages, 4, 0)
    chain.leave(*blocks)
    contract_sum = Reduce(stages, blocks)
    stages = tuple("xynf")
    blocks = grad_rows(codec_normed_two_both, chain.enter(*expand_pair), order, stages, 4, 0)
    chain.leave(*blocks)
    expand_sum = Reduce(stages, blocks)
    mixed_grad, attended_grad, codec_postnorm_grad, output_in = mixed_grads(
        codec_grad, chain.enter(normed_grad), mixed_sum, codec_weights
    )
    chain.leave(attended_grad)
    output_pair = pair(output_in)
    codec_projected_grad = codec_attend_grads_call(
        codec_packed, chain.enter(attended_grad).reshape(positions, frame_total, width)
    ).reshape(positions * frame_total, 3 * width)
    chain.leave(codec_projected_grad)
    projected_pair = pair(codec_projected_grad)
    input_grad, codec_prenorm_grad = front_grads(
        codec_hidden, chain.enter(codec_projected_grad), mixed_grad, codec_weights
    )
    input_grad = input_grad.reshape(positions, frame_total, width)
    base_grad = jnp.sum(input_grad, axis=0).astype(BF)
    table_in = input_grad[1:].reshape(-1, width).astype(BF)
    chain.leave(base_grad, table_in)
    table_pair = pair(table_in)

    base_grad = chain.enter(base_grad)
    contract_in = pair(base_grad)
    base_grad = base_grad.astype(F32)
    frame_expand_in = hidden_grads(contract_in[0], frame_saved[2], frame_weights)
    chain.leave(frame_expand_in)
    frame_expand_pair = pair(frame_expand_in)
    contract_sum.step(chain)
    normed_grad = inner_right(chain.enter(frame_expand_in), frame_weights[4])
    frame_mixed_grad, frame_attended_grad, frame_postnorm_grad, output_in = mixed_grads(
        base_grad, normed_grad, frame_saved[0], frame_weights
    )
    grads = jnp.transpose(
        frame_attended_grad.reshape(row_count, frames_dev, count, LANES), (2, 0, 1, 3)
    )
    chain.leave(grads)
    grads = lax.all_to_all(grads, "seq", split_axis=0, concat_axis=0, tiled=True)
    frame_output_pair = pair(output_in)
    expand_sum.step(chain)
    stages = tuple("yxnf")
    blocks = grad_columns(chain.enter(*activated_both), contract_in, order, stages, 4, 0)
    chain.leave(*blocks)
    frame_contract_sum = Reduce(stages, blocks)
    stages = tuple("xynf")
    blocks = grad_rows(normed_two_both, chain.enter(*frame_expand_pair), order, stages, 5, 0)
    blocks = grad_rows(attended_both, frame_output_pair, order, stages, 5, 4, blocks)
    chain.leave(*blocks)
    frame_expand_sum = Reduce(stages, blocks)
    contract_sum.step(chain)
    packed_grad = frame_attend_grads_call(packed, chain.enter(grads), every_segment)
    chain.leave(packed_grad)
    packed_grad = lax.all_to_all(packed_grad, "seq", split_axis=0, concat_axis=0, tiled=True)
    expand_sum.step(chain)
    contract_sum.step(chain)
    stages = tuple("nyxf")
    blocks = grad_rows(codec_normed_both, chain.enter(*projected_pair), order, stages, 6, 0)
    blocks = grad_rows(codec_attended_both, output_pair, order, stages, 6, 3, blocks)
    blocks = grad_table(codes_both, table_pair, order, stages, codebooks.shape[0], 6, 4, blocks)
    chain.leave(*blocks)
    codec_sum = Reduce(stages, blocks)
    frame_contract_sum.step(chain)
    expand_sum.step(chain)
    codec_result = mixed_sum + matmul(chain.enter(activated), weight_contract)
    output = jnp.transpose(
        (codec_result.reshape(positions, frame_total, width) * live).astype(BF), (1, 0, 2)
    ).reshape(row_count, frames_dev, positions, width)
    chain.leave(output)
    frame_expand_sum.step(chain)
    frame_projected_grad = jnp.transpose(
        chain.enter(packed_grad).reshape(count, row_count, frames_dev, 3, LANES), (1, 2, 3, 0, 4)
    ).reshape(frame_total, 3 * width)
    frame_projected_pair = pair(frame_projected_grad)
    chain.leave(frame_projected_grad)
    frames_grad, frame_prenorm_grad = front_grads(
        hidden, chain.enter(frame_projected_grad), frame_mixed_grad, frame_weights
    )
    chain.leave(frames_grad)
    stages = tuple("nxyf")
    blocks = grad_rows(normed_both, chain.enter(*frame_projected_pair), order, stages, 3, 0)
    chain.leave(*blocks)
    frame_project_sum = Reduce(stages, blocks)
    gain_sums = sum_everywhere(
        jnp.stack(
            [frame_prenorm_grad, frame_postnorm_grad, codec_prenorm_grad, codec_postnorm_grad]
        ),
        place,
    )
    frame_contract_sum.step(chain)
    codec_sum.step(chain)
    frame_expand_sum.step(chain)
    frame_contract_sum.step(chain)
    codec_sum.step(chain)
    frame_project_sum.step(chain)
    frame_expand_sum.step(chain)
    frame_project_sum.step(chain)
    codec_sum.step(chain)
    frame_project_sum.step(chain)

    height = frame_project.shape[0]
    codec_two = codec_sum.result()
    frame_one = frame_expand_sum.result()
    return (
        output,
        frames_grad.reshape(row_count, frames_dev, width),
        rows_from_units(codec_two[4:], codebooks.shape[0]),
        gain_sums[0],
        rows_from_units(frame_project_sum.result(), height),
        rows_from_units(frame_one[4:], height),
        gain_sums[1],
        rows_from_units(frame_one[:4], height),
        columns_from_units(frame_contract_sum.result()),
        gain_sums[2],
        rows_from_units(codec_two[:3], height),
        rows_from_units(codec_two[3:4], height),
        gain_sums[3],
        rows_from_units(expand_sum.result(), height),
        columns_from_units(contract_sum.result()),
    )


def solution(mesh):
    placed = (
        P("mp", "seq", None),
        P("mp", "seq"),
        P("mp", "seq"),
        P(None, "mp", "seq"),
        P("mp", None),
        P("mp"),
        P("mp", None),
        P("mp", None),
        P("mp"),
        P("mp", None),
        P("mp", None),
        P("mp"),
        P("mp", None),
        P("mp", None),
        P("mp"),
        P("mp", None),
        P("mp", None),
        P("mp", "seq", None, None),
    )
    small = mesh.shape["seq"] == 8 and mesh.shape["mp"] == 4
    return jax.shard_map(
        shards if small else shards_general,
        mesh=mesh,
        in_specs=placed,
        out_specs=(
            P("mp", "seq", None, None),
            P("mp", "seq", None),
            P("mp", "seq"),
            P(),
            P("mp", "seq"),
            P("mp", "seq"),
            P(),
            P("mp", "seq"),
            P("mp", "seq"),
            P(),
            P("mp", "seq"),
            P("mp", "seq"),
            P(),
            P("mp", "seq"),
            P("mp", "seq"),
        ),
        check_vma=False,
    )
```

```python
import functools

import jax
import jax.numpy as jnp
from jax import lax
from jax.experimental import pallas as pl
from jax.experimental.pallas import tpu as pltpu
from jax.sharding import PartitionSpec as P

HEADS = 16
HEAD = 64
CODES = 1024


EPSILON = 1e-05
MASKED = -1e30
FACTOR = HEAD ** (-0.5)

BF = jnp.bfloat16
F32 = jnp.float32


def rms_scale(values, gain_vec):
    return (
        values * lax.rsqrt(jnp.mean(values * values, axis=-1, keepdims=True) + EPSILON) * gain_vec
    )


def matmul(former, latter):
    return jnp.dot(former, latter, preferred_element_type=F32)


def inner_left(former, latter):
    return lax.dot_general(former, latter, (((0,), (0,)), ((), ())), preferred_element_type=F32)


def inner_right(former, latter):
    return lax.dot_general(former, latter, (((1,), (1,)), ((), ())), preferred_element_type=F32)


def split_heads(values):
    return values.reshape(values.shape[:-1] + (-1, HEAD))


def swap(values, axis, bit):
    return lax.ppermute(values, axis, [(i, i ^ bit) for i in range(lax.axis_size(axis))])


def pick(values, index, axis):
    return lax.dynamic_index_in_dim(values, index, axis, keepdims=False)


class Place:
    def __init__(self):
        self.seq_count = lax.axis_size("seq")
        self.mp_count = lax.axis_size("mp")
        self.seq = lax.axis_index("seq")
        self.mp = lax.axis_index("mp")
        self.seq_low = self.seq % 2


def gather_weight(shard, place):
    height, breadth = shard.shape
    half = height // 2
    mine = lax.dynamic_slice(shard, (place.seq_low * half, 0), (half, breadth))
    first = swap(mine, "mp", 2)
    second = swap(first, "seq", 1)
    near_other = swap(shard, "mp", 1)
    far = jnp.zeros((height, breadth), shard.dtype)
    far = lax.dynamic_update_slice(far, first, (place.seq_low * half, 0))
    far = lax.dynamic_update_slice(far, second, ((1 - place.seq_low) * half, 0))
    far_other = swap(far, "mp", 1)
    whole = jnp.zeros((height * place.mp_count, breadth), shard.dtype)
    for flip, piece in ((0, shard), (1, near_other), (2, far), (3, far_other)):
        whole = lax.dynamic_update_slice(whole, piece, ((place.mp ^ flip) * height, 0))
    return whole


def line_scatter(blocks, place):
    count = place.seq_count // 2
    position = place.seq // 2
    size = 2 * count
    state = blocks
    up_in = down_in = None
    for step in range(1, count):
        up_index = jnp.clip(count - step + position, 0, count - 1)
        down_index = jnp.clip(step - 1 - (count - 1 - position), 0, count - 1)
        up_perm = [(i, i + 2) for i in range(size - 2) if i // 2 < step]
        down_perm = [(i, i - 2) for i in range(2, size) if (count - 1 - i // 2) < step]
        up_out = pick(blocks, up_index, 1)
        down_out = pick(blocks, down_index, 1)
        if up_in is not None:
            up_out = up_out + up_in
            down_out = down_out + down_in
        up_in = lax.ppermute(up_out, "seq", up_perm)
        down_in = lax.ppermute(down_out, "seq", down_perm)
    own = pick(blocks, position, 1).astype(F32)
    return own + up_in.astype(F32) + down_in.astype(F32)


def weight_grad(former, latter, place, seq_first):
    height = former.shape[1] // place.mp_count
    rows = former.shape[0]
    breadth = latter.shape[1] // place.seq_count
    low = place.seq_low
    view = latter.reshape(rows, place.seq_count // 2, 2, breadth)
    half = breadth * (place.seq_count // 2)
    give = pick(view, 1 - low, 2).reshape(rows, half)
    keep = pick(view, low, 2).reshape(rows, half)
    both = jnp.concatenate([give, keep], axis=1)

    def columns(flip):
        return lax.dynamic_slice(former, (0, (place.mp ^ flip) * height), (rows, height))

    own, other, far, far_other = (columns(flip) for flip in (0, 1, 2, 3))
    part = inner_left(jnp.concatenate([far_other, other], axis=1), both).astype(BF)
    part = swap(part, "mp", 1).astype(F32)
    if seq_first:
        send = inner_left(jnp.concatenate([far, own], axis=1), give) + part[:, :half]
        low_in = swap(send.astype(BF), "seq", 1).astype(F32)
        send = inner_left(far, keep) + part[:height, half:] + low_in[:height]
        far_in = swap(send.astype(BF), "mp", 2).astype(F32)
        total = inner_left(own, keep) + part[height:, half:] + low_in[height:] + far_in
    else:
        send = inner_left(far, both) + part[:height]
        far_in = swap(send.astype(BF), "mp", 2).astype(F32)
        send = inner_left(own, give) + part[height:, :half] + far_in[:, :half]
        low_in = swap(send.astype(BF), "seq", 1).astype(F32)
        total = inner_left(own, keep) + part[height:, half:] + far_in[:, half:] + low_in
    return total.astype(BF).reshape(height, place.seq_count // 2, breadth)


def finish_grads(partials, place):
    sizes = [part.shape[2] for part in partials]
    total = line_scatter(jnp.concatenate(partials, axis=2), place)
    pieces, start = [], 0
    for size in sizes:
        pieces.append(total[:, start : start + size])
        start += size
    return pieces


def sum_everywhere(values, place):
    for axis, count in (("mp", place.mp_count), ("seq", place.seq_count)):
        bit = 1
        while bit < count:
            values = values + swap(values, axis, bit)
            bit *= 2
    return values


def front_pass(hidden, weights):
    normed = rms_scale(hidden, weights[0].astype(F32)).astype(BF)
    projected = matmul(normed, weights[1]).astype(BF)
    return (normed, projected)


def rear_pass(hidden, attended, weights):
    mixed_sum = hidden + matmul(attended, weights[2])
    normed_two = rms_scale(mixed_sum, weights[3].astype(F32)).astype(BF)
    expanded = matmul(normed_two, weights[4])
    activated = jax.nn.gelu(expanded).astype(BF)
    result = mixed_sum + matmul(activated, weights[5])
    return (result, (mixed_sum, normed_two, expanded, activated))


def rear_grads(result_grad, saved_state, weights):
    mixed_sum, normed_two, expanded, activated = saved_state
    contract_input = result_grad.astype(BF)
    active_grad = inner_right(contract_input, weights[5])
    expand_input = jax.vjp(jax.nn.gelu, expanded)[1](active_grad)[0].astype(BF)
    normed_grad = inner_right(expand_input, weights[4])
    mixed_part, postnorm_grad = jax.vjp(rms_scale, mixed_sum, weights[3].astype(F32))[1](
        normed_grad
    )
    mixed_grad = result_grad + mixed_part
    output_input = mixed_grad.astype(BF)
    attended_grad = inner_right(output_input, weights[2]).astype(BF)
    return (mixed_grad, attended_grad, postnorm_grad, contract_input, expand_input, output_input)


def front_grads(hidden, projected_grad, mixed_grad, weights):
    normed_grad = inner_right(projected_grad, weights[1])
    hidden_part, prenorm_grad = jax.vjp(rms_scale, hidden, weights[0].astype(F32))[1](normed_grad)
    return (mixed_grad + hidden_part, prenorm_grad)


def portions_of(queries, keys, allowed):
    scores = jnp.einsum("ihd,jhd->hij", queries, keys, preferred_element_type=F32) * FACTOR
    return jax.nn.softmax(jnp.where(allowed[None], scores, MASKED), axis=-1)


def attend(queries, keys, values, allowed):
    portions = portions_of(queries, keys, allowed)
    return jnp.einsum(
        "hij,jhd->ihd", portions.astype(BF), values, preferred_element_type=F32
    ).astype(BF)


def attend_grads(queries, keys, values, allowed, out_grad):
    portions = portions_of(queries, keys, allowed)
    portion_grad = jnp.einsum("ihd,jhd->hij", out_grad, values, preferred_element_type=F32)
    score_grad = (
        portions * (portion_grad - jnp.sum(portions * portion_grad, axis=-1, keepdims=True))
    ).astype(BF)
    query_grad = (
        jnp.einsum("hij,jhd->ihd", score_grad, keys, preferred_element_type=F32) * FACTOR
    )
    key_grad = (
        jnp.einsum("hij,ihd->jhd", score_grad, queries, preferred_element_type=F32) * FACTOR
    )
    value_grad = jnp.einsum("hij,ihd->jhd", portions.astype(BF), out_grad, preferred_element_type=F32)
    return query_grad, key_grad, value_grad


def to_heads(values, place):
    rows, own, parts, width = values.shape
    count = place.seq_count
    view = values.reshape(rows, own, parts, count, width // count)
    moved = lax.all_to_all(
        jnp.transpose(view, (3, 0, 1, 2, 4)), "seq", split_axis=0, concat_axis=0, tiled=True
    )
    return jnp.transpose(moved, (1, 0, 2, 3, 4)).reshape(rows, count * own, parts, width // count)


def to_frames(values, place):
    rows, total, parts, width = values.shape
    count = place.seq_count
    view = values.reshape(rows, count, total // count, parts, width)
    moved = lax.all_to_all(
        jnp.transpose(view, (1, 0, 2, 3, 4)), "seq", split_axis=0, concat_axis=0, tiled=True
    )
    return jnp.transpose(moved, (1, 2, 3, 0, 4)).reshape(
        rows, total // count, parts, count * width
    )


def allowed_of(query_seg, key_seg, query_pos, key_pos):
    return (query_seg[:, None] == key_seg[None, :]) & (key_pos[None, :] <= query_pos[:, None])


def frame_attention(projected, segments, place):
    rows, own, triple = projected.shape
    width = triple // 3
    parts = projected.reshape(rows, own, 3, width)
    every_segment = lax.all_gather(segments, "seq", axis=1, tiled=True)
    every_pos = jnp.arange(own * place.seq_count)
    if HEADS % place.seq_count == 0:
        packed = to_heads(parts, place)
        sets = [split_heads(packed[:, :, part]) for part in range(3)]

        def one_row(items):
            queries, keys, values, segs = items
            return attend(queries, keys, values, allowed_of(segs, segs, every_pos, every_pos))

        attended = lax.map(one_row, (*sets, every_segment))
        attended = to_frames(attended.reshape(rows, own * place.seq_count, 1, -1), place)

        def backward(out_grad):
            grads = to_heads(out_grad.reshape(rows, own, 1, width), place)[:, :, 0]

            def one_row(items):
                queries, keys, values, segs, grad = items
                return attend_grads(
                    queries, keys, values, allowed_of(segs, segs, every_pos, every_pos), grad
                )

            found = lax.map(one_row, (*sets, every_segment, split_heads(grads)))
            packed_grad = jnp.stack(
                [grad.reshape(rows, own * place.seq_count, -1) for grad in found], axis=2
            ).astype(BF)
            return to_frames(packed_grad, place).reshape(rows, own, triple)

        return attended.reshape(rows, own, width), backward

    keys = lax.all_gather(parts[:, :, 1], "seq", axis=1, tiled=True)
    values = lax.all_gather(parts[:, :, 2], "seq", axis=1, tiled=True)
    sets = (split_heads(parts[:, :, 0]), split_heads(keys), split_heads(values))
    own_pos = place.seq * own + jnp.arange(own)

    def one_row(items):
        row_q, row_k, row_v, own_segs, segs = items
        return attend(row_q, row_k, row_v, allowed_of(own_segs, segs, own_pos, every_pos))

    attended = lax.map(one_row, (*sets, segments, every_segment)).reshape(rows, own, width)

    def backward(out_grad):
        def one_row(items):
            row_q, row_k, row_v, own_segs, segs, grad = items
            allowed = allowed_of(own_segs, segs, own_pos, every_pos)
            return attend_grads(row_q, row_k, row_v, allowed, grad)

        query_grad, key_grad, value_grad = lax.map(
            one_row, (*sets, segments, every_segment, split_heads(out_grad))
        )
        both = jnp.stack([key_grad.reshape(rows, -1, width), value_grad.reshape(rows, -1, width)], 2)
        both = lax.psum_scatter(both, "seq", scatter_dimension=1, tiled=True)
        parts_grad = [query_grad.reshape(rows, own, width), both[:, :, 0], both[:, :, 1]]
        return jnp.concatenate(parts_grad, axis=-1).astype(BF)

    return attended, backward


def head_sums(values, marks):
    return jnp.dot(values, marks, precision=lax.Precision.HIGHEST, preferred_element_type=F32)


def head_spread(values, marks):
    return lax.dot_general(
        values.astype(BF), marks.astype(BF), (((1,), (1,)), ((), ())), preferred_element_type=F32
    )


def codec_softmax(queries, keys, marks):
    result = []
    for later in range(len(queries)):
        scores = [
            head_sums(queries[later].astype(F32) * keys[earlier].astype(F32), marks) * FACTOR
            for earlier in range(later + 1)
        ]
        top = scores[0]
        for score in scores[1:]:
            top = jnp.maximum(top, score)
        powers = [jnp.exp(score - top) for score in scores]
        total = sum(powers)
        result.append([power / total for power in powers])
    return result


def codec_attend(soft, values, marks):
    result = []
    for row in soft:
        total = 0.0
        for earlier, portion in enumerate(row):
            total = total + head_spread(portion, marks) * values[earlier].astype(F32)
        result.append(total.astype(BF))
    return result


def codec_attend_grads(soft, queries, keys, values, grads, marks):
    count = len(queries)
    query_grad = []
    key_grad = [0.0] * count
    value_grad = [0.0] * count
    for later in range(count):
        grad = grads[later].astype(F32)
        portion_grads = [
            head_sums(grad * values[earlier].astype(F32), marks) for earlier in range(later + 1)
        ]
        mean = sum(soft[later][i] * portion_grads[i] for i in range(later + 1))
        total = 0.0
        for earlier in range(later + 1):
            score_grad = soft[later][earlier] * (portion_grads[earlier] - mean)
            wide = head_spread(score_grad, marks)
            total = total + wide * keys[earlier].astype(F32)
            key_grad[earlier] = key_grad[earlier] + wide * queries[later].astype(F32)
            value_grad[earlier] = value_grad[earlier] + head_spread(soft[later][earlier], marks) * grad
        query_grad.append(total * FACTOR)
    return jnp.concatenate(
        [
            jnp.concatenate(
                [query_grad[t], key_grad[t] * FACTOR, value_grad[t]], axis=-1
            ).astype(BF)
            for t in range(count)
        ],
        axis=0,
    )


LANES = 128
TILE = 256
VMEM_LIMIT = 48 * 1024 * 1024
HINT = pl.CostEstimate(flops=1, bytes_accessed=1, transcendentals=0)


def whole_block(shape):
    return pl.BlockSpec(shape, lambda *_: (0,) * len(shape))


def causal_tiles(length):
    tile = min(TILE, length)
    return [(start, tile, start + tile) for start in range(0, length, tile)]


def head_masks(dtype):
    lane = lax.broadcasted_iota(jnp.int32, (1, LANES), 1)
    return [((lane // HEAD) == head).astype(dtype) for head in range(LANES // HEAD)]


def frame_attend_kernel(packed_ref, seg_col_ref, seg_row_ref, out_ref):
    chunks, _, own, _ = packed_ref.shape
    length = chunks * own
    packed = packed_ref[...].reshape(length, 3 * LANES)
    queries, keys, values = (packed[:, LANES * i : LANES * (i + 1)] for i in range(3))
    masks = head_masks(BF)
    lane = lax.broadcasted_iota(jnp.int32, (1, LANES), 1)
    for start, tile, end in causal_tiles(length):
        query_pos = start + lax.broadcasted_iota(jnp.int32, (tile, end), 0)
        key_pos = lax.broadcasted_iota(jnp.int32, (tile, end), 1)
        allowed = (seg_col_ref[0, start:end] == seg_row_ref[0, :, :end]) & (key_pos <= query_pos)
        result = jnp.zeros((tile, LANES), F32)
        for head, mask in enumerate(masks):
            scores = inner_right(queries[start:end] * mask, keys[:end]) * FACTOR
            scores = jnp.where(allowed, scores, MASKED)
            powers = jnp.exp(scores - jnp.max(scores, axis=1, keepdims=True))
            portions = powers / jnp.sum(powers, axis=1, keepdims=True)
            found = matmul(portions.astype(BF), values[:end])
            result = jnp.where(lane // HEAD == head, found, result)
        out_ref[start // own : end // own, 0] = result.astype(BF).reshape(tile // own, own, LANES)


def frame_attend_grads_kernel(packed_ref, grad_ref, seg_col_ref, seg_row_ref, out_ref, key_sum, value_sum):
    chunks, _, own, _ = packed_ref.shape
    length = chunks * own
    packed = packed_ref[...].reshape(length, 3 * LANES)
    queries, keys, values = (packed[:, LANES * i : LANES * (i + 1)] for i in range(3))
    grads = grad_ref[...].reshape(length, LANES)
    masks = head_masks(BF)
    lane = lax.broadcasted_iota(jnp.int32, (1, LANES), 1)
    key_sum[...] = jnp.zeros_like(key_sum)
    value_sum[...] = jnp.zeros_like(value_sum)
    for start, tile, end in causal_tiles(length):
        key_pos = lax.broadcasted_iota(jnp.int32, (end, tile), 0)
        query_pos = start + lax.broadcasted_iota(jnp.int32, (end, tile), 1)
        allowed = (seg_col_ref[0, :end] == seg_row_ref[0, :, start:end]) & (key_pos <= query_pos)
        query_grad = jnp.zeros((tile, LANES), F32)
        for head, mask in enumerate(masks):
            query = queries[start:end] * mask
            grad = grads[start:end] * mask
            scores = inner_right(keys[:end], query) * FACTOR
            scores = jnp.where(allowed, scores, MASKED)
            powers = jnp.exp(scores - jnp.max(scores, axis=0, keepdims=True))
            portions = powers / jnp.sum(powers, axis=0, keepdims=True)
            portion_grad = inner_right(values[:end], grad)
            mean = jnp.sum(portions * portion_grad, axis=0, keepdims=True)
            score_grad = (portions * (portion_grad - mean)).astype(BF)
            key_sum[:end] += matmul(score_grad, query)
            value_sum[:end] += matmul(portions.astype(BF), grad)
            found = inner_left(score_grad, keys[:end])
            query_grad = jnp.where(lane // HEAD == head, found, query_grad)
        out_ref[start // own : end // own, 0, :, :LANES] = (
            (query_grad * FACTOR).astype(BF).reshape(tile // own, own, LANES)
        )
    out_ref[:, 0, :, LANES : 2 * LANES] = (key_sum[...] * FACTOR).astype(BF).reshape(chunks, own, LANES)
    out_ref[:, 0, :, 2 * LANES :] = value_sum[...].astype(BF).reshape(chunks, own, LANES)


def row_spec(chunks, own, breadth):
    return pl.BlockSpec((chunks, 1, own, breadth), lambda row: (0, row, 0, 0))


def segment_specs(length):
    return [
        pl.BlockSpec((1, length, 1), lambda row: (row, 0, 0)),
        pl.BlockSpec((1, 1, length), lambda row: (row, 0, 0)),
    ]


def frame_attend_call(packed, segments):
    chunks, rows, own, _ = packed.shape
    length = chunks * own
    return pl.pallas_call(
        frame_attend_kernel,
        grid=(rows,),
        in_specs=[row_spec(chunks, own, 3 * LANES), *segment_specs(length)],
        out_specs=row_spec(chunks, own, LANES),
        out_shape=jax.ShapeDtypeStruct((chunks, rows, own, LANES), BF),
        compiler_params=pltpu.CompilerParams(vmem_limit_bytes=VMEM_LIMIT),
        cost_estimate=HINT,
        name="frame_attend",
    )(packed, segments[:, :, None], segments[:, None, :])


def frame_attend_grads_call(packed, grads, segments):
    chunks, rows, own, _ = packed.shape
    length = chunks * own
    return pl.pallas_call(
        frame_attend_grads_kernel,
        grid=(rows,),
        in_specs=[
            row_spec(chunks, own, 3 * LANES),
            row_spec(chunks, own, LANES),
            *segment_specs(length),
        ],
        out_specs=row_spec(chunks, own, 3 * LANES),
        out_shape=jax.ShapeDtypeStruct((chunks, rows, own, 3 * LANES), BF),
        scratch_shapes=[pltpu.VMEM((length, LANES), F32), pltpu.VMEM((length, LANES), F32)],
        compiler_params=pltpu.CompilerParams(vmem_limit_bytes=VMEM_LIMIT),
        cost_estimate=HINT,
        name="frame_attend_grads",
    )(packed, grads, segments[:, :, None], segments[:, None, :])


def position_pairs(positions):
    return [(later, earlier) for later in range(1, positions) for earlier in range(later + 1)]


def codec_sums(products, marks):
    stacked = jnp.concatenate(products, axis=0)
    high = stacked.astype(BF)
    low = (stacked - high.astype(F32)).astype(BF)
    total = matmul(high, marks) + matmul(low, marks)
    size = products[0].shape[0]
    return [total[size * i : size * (i + 1)] for i in range(len(products))]


def codec_spread(portions, marks):
    stacked = jnp.concatenate([portion.astype(BF) for portion in portions], axis=0)
    total = inner_right(stacked, marks)
    size = portions[0].shape[0]
    return [total[size * i : size * (i + 1)] for i in range(len(portions))]


def codec_portions(queries, keys, marks, pairs):
    scores = codec_sums(
        [queries[later].astype(F32) * keys[earlier].astype(F32) for later, earlier in pairs], marks
    )
    scores = dict(zip(pairs, [score * FACTOR for score in scores]))
    portions = {}
    for later in range(1, len(queries)):
        row = [scores[later, earlier] for earlier in range(later + 1)]
        top = functools.reduce(jnp.maximum, row)
        powers = [jnp.exp(score - top) for score in row]
        total = functools.reduce(jnp.add, powers)
        for earlier in range(later + 1):
            portions[later, earlier] = powers[earlier] / total
    return portions


def codec_parts(packed_ref, width):
    positions = packed_ref.shape[0]
    return [
        [packed_ref[t, :, width * part : width * (part + 1)] for t in range(positions)]
        for part in range(3)
    ]


def codec_attend_kernel(packed_ref, marks_ref, out_ref):
    positions, _, width = out_ref.shape
    queries, keys, values = codec_parts(packed_ref, width)
    marks = marks_ref[...]
    pairs = position_pairs(positions)
    portions = codec_portions(queries, keys, marks, pairs)
    wide = dict(zip(pairs, codec_spread([portions[pair] for pair in pairs], marks)))
    out_ref[0] = values[0]
    for later in range(1, positions):
        terms = [wide[later, e] * values[e].astype(F32) for e in range(later + 1)]
        out_ref[later] = functools.reduce(jnp.add, terms).astype(BF)


def codec_attend_grads_kernel(packed_ref, grad_ref, marks_ref, out_ref):
    positions, _, width = grad_ref.shape
    queries, keys, values = codec_parts(packed_ref, width)
    marks = marks_ref[...]
    pairs = position_pairs(positions)
    portions = codec_portions(queries, keys, marks, pairs)
    grads = [grad_ref[t].astype(F32) for t in range(positions)]
    portion_grads = dict(
        zip(
            pairs,
            codec_sums([grads[later] * values[earlier].astype(F32) for later, earlier in pairs], marks),
        )
    )
    score_grads = {}
    for later in range(1, positions):
        mean = functools.reduce(
            jnp.add, [portions[later, e] * portion_grads[later, e] for e in range(later + 1)]
        )
        for e in range(later + 1):
            score_grads[later, e] = portions[later, e] * (portion_grads[later, e] - mean)
    wide = dict(zip(pairs, codec_spread([portions[pair] for pair in pairs], marks)))
    wide_grads = dict(zip(pairs, codec_spread([score_grads[pair] for pair in pairs], marks)))
    zero = jnp.zeros_like(grads[0])
    for t in range(positions):
        query_grad = key_grad = zero
        value_grad = grads[0] if t == 0 else zero
        for later, earlier in pairs:
            if later == t:
                query_grad = query_grad + wide_grads[later, earlier] * keys[earlier].astype(F32)
            if earlier == t:
                key_grad = key_grad + wide_grads[later, earlier] * queries[later].astype(F32)
                value_grad = value_grad + wide[later, earlier] * grads[later]
        out_ref[t, :, :width] = (query_grad * FACTOR).astype(BF)
        out_ref[t, :, width : 2 * width] = (key_grad * FACTOR).astype(BF)
        out_ref[t, :, 2 * width :] = value_grad.astype(BF)


def codec_tile(frame_total):
    return 64 if frame_total % 64 == 0 else frame_total


def codec_spec(positions, tile, breadth):
    return pl.BlockSpec((positions, tile, breadth), lambda i: (0, i, 0))


def head_marks(width):
    return (
        jnp.arange(width)[:, None] // HEAD == jnp.arange(LANES)[None, :]
    ).astype(BF)


def codec_attend_call(packed):
    positions, total, triple = packed.shape
    width = triple // 3
    tile = codec_tile(total)
    return pl.pallas_call(
        codec_attend_kernel,
        grid=(total // tile,),
        in_specs=[codec_spec(positions, tile, triple), whole_block((width, LANES))],
        out_specs=codec_spec(positions, tile, width),
        out_shape=jax.ShapeDtypeStruct((positions, total, width), BF),
        compiler_params=pltpu.CompilerParams(vmem_limit_bytes=VMEM_LIMIT),
        cost_estimate=HINT,
        name="codec_attend",
    )(packed, head_marks(width))


def codec_attend_grads_call(packed, grads):
    positions, total, triple = packed.shape
    width = triple // 3
    tile = codec_tile(total)
    return pl.pallas_call(
        codec_attend_grads_kernel,
        grid=(total // tile,),
        in_specs=[
            codec_spec(positions, tile, triple),
            codec_spec(positions, tile, width),
            whole_block((width, LANES)),
        ],
        out_specs=codec_spec(positions, tile, triple),
        out_shape=jax.ShapeDtypeStruct((positions, total, triple), BF),
        compiler_params=pltpu.CompilerParams(vmem_limit_bytes=VMEM_LIMIT),
        cost_estimate=HINT,
        name="codec_attend_grads",
    )(packed, grads, head_marks(width))


BITS = {"y": ("mp", 2), "x": ("seq", 1), "n": ("seq", 2), "f": ("seq", 4)}


def grad_order(place):
    flips = []
    for bits in ((1, 2, 4), (2, 1, 4), (1, 2, 4)):
        for step in range(8):
            flips.append(sum(bit for at, bit in enumerate(bits) if not (step >> (2 - at)) & 1))
    return jnp.stack(
        [place.mp ^ 2, place.mp] + [place.seq ^ flip for flip in flips] + [place.seq]
    ).astype(jnp.int32)


STEPS = {"y": (2, "xnf"), "n": (10, "nxf"), "x": (18, "xnf")}
OWN_SEQ = 26


def keep_flags(order_ref, seq):
    change = order_ref[OWN_SEQ] ^ seq
    return {"x": 1 - (change & 1), "n": 1 - ((change >> 1) & 1), "f": 1 - ((change >> 2) & 1)}


def grad_rows_kernel(stages, wide, order_ref, far_own, far_rec, own_own, own_rec, latter_own, latter_rec, *refs):
    send_ref, keep_ref, turned = refs[-3:]
    rows = latter_own.shape[0]
    height = far_own.shape[1]

    @pl.when(pl.program_id(0) == 0)
    def _():
        for at, (own, rec) in enumerate(((far_own, far_rec), (own_own, own_rec))):
            turned[height * at : height * (at + 1), :rows] = own[...].T
            turned[height * at : height * (at + 1), rows:] = rec[...].T

    total = matmul(turned[:, :rows], latter_own[...]) + matmul(turned[:, rows:], latter_rec[...])
    store = grad_store_wide if wide else grad_store
    store(stages, order_ref, total.astype(BF), height, send_ref, keep_ref)


def grad_store_wide(stages, order_ref, total, height, send_ref, keep_ref):
    units = height // TILE
    chunks = total.shape[1] // 8 // LANES
    for seq in range(8):
        flags = keep_flags(order_ref, seq)
        for chunk in range(chunks):
            first = (seq * chunks + chunk) * LANES
            for unit in range(units):
                at = chunk * units + unit
                for kept in range(2):
                    start = height * kept + unit * TILE
                    value = total[start : start + TILE, first : first + LANES]
                    spot = {**flags, "y": kept}
                    where = tuple(spot[stage] for stage in stages[1:])
                    for target, when in ((send_ref, 0), (keep_ref, 1)):

                        @pl.when(spot[stages[0]] == when)
                        def _(target=target, where=where, at=at, value=value):
                            target[(*where, at)] = value


def grad_store(stages, order_ref, total, height, send_ref, keep_ref):
    chunks = total.shape[1] // LANES
    for chunk in range(chunks):
        value = total[:, chunk * LANES : (chunk + 1) * LANES]
        given, kept = value[:height], value[height:]
        if stages[0] == "y":
            send_ref[0, 0, 0, chunk] = given
            keep_ref[0, 0, 0, chunk] = kept
        else:
            spots = [tuple(side if stage == "y" else 0 for stage in stages[1:]) for side in range(2)]
            for target, when in ((send_ref, pl.program_id(0) < 4), (keep_ref, pl.program_id(0) >= 4)):

                @pl.when(when)
                def _(target=target, given=given, kept=kept, chunk=chunk):
                    target[(*spots[0], chunk)] = given
                    target[(*spots[1], chunk)] = kept


def grad_buffers(units):
    return [jax.ShapeDtypeStruct((2, 2, 2, units, TILE, LANES), BF)] * 2


def grad_call(kernel, order, arrays, in_specs, out_specs, units, into, steps, scratch, flops, name):
    aliases = {}
    moved = 2 * sum(array.size for array in arrays)
    if into is not None:
        aliases = {len(arrays) + 1: 0, len(arrays) + 2: 1}
        in_specs = in_specs + [pl.BlockSpec(memory_space=pl.ANY)] * 2
        arrays = arrays + list(into)
    return pl.pallas_call(
        kernel,
        grid_spec=pltpu.PrefetchScalarGridSpec(
            num_scalar_prefetch=1,
            grid=(steps,),
            in_specs=in_specs,
            out_specs=out_specs,
            scratch_shapes=[scratch],
        ),
        out_shape=grad_buffers(units),
        input_output_aliases=aliases,
        compiler_params=pltpu.CompilerParams(vmem_limit_bytes=VMEM_LIMIT),
        cost_estimate=HINT,
        name=name,
    )(order, *arrays)


def grad_rows(former, latter, order, stages, units, offset, into=None):
    former, skip, height = former
    latter, latter_skip, breadth = latter
    rows = latter[0].shape[0]
    height = height // 4
    skip = skip // height
    wide = breadth // 8 == LANES
    chunks = breadth // 8 // LANES
    steps = 1 if wide else 8
    arrays = [former[0], former[1], former[0], former[1], latter[0], latter[1]]
    former_specs = [
        pl.BlockSpec((rows, height), lambda j, t, at=at: (0, skip + t[at]), pipeline_mode=pl.Buffered(1))
        for at in (0, 0, 1, 1)
    ]
    if wide:
        latter_specs = [
            pl.BlockSpec((rows, breadth), lambda j, t: (0, latter_skip // breadth))
        ] * 2
        block = (2, 2, 2, 1, TILE, LANES)
        out_specs = [pl.BlockSpec(block, lambda j, t: (0, 0, 0, offset, 0, 0))] * 2
    else:
        base = offset // chunks
        table, names = STEPS[stages[0]]
        bits = {name: 2 - at for at, name in enumerate(names)}
        if stages[0] == "y":
            block = (1, 1, 1, chunks, TILE, LANES)

            def where(j):
                return tuple((j >> bits[stage]) & 1 for stage in stages[1:]) + (base, 0, 0)

            out_specs = [pl.BlockSpec(block, lambda j, t: where(j))] * 2
        else:
            block = tuple(2 if stage == "y" else 1 for stage in stages[1:]) + (chunks, TILE, LANES)

            def where(j):
                return tuple(
                    0 if stage == "y" else (j >> bits[stage]) & 1 for stage in stages[1:]
                ) + (base, 0, 0)

            out_specs = [
                pl.BlockSpec(block, lambda j, t: where(jnp.minimum(j, 3))),
                pl.BlockSpec(block, lambda j, t: where(jnp.maximum(j - 4, 0))),
            ]
        latter_specs = [
            pl.BlockSpec(
                (rows, breadth // 8),
                lambda j, t: (0, latter_skip // (breadth // 8) + t[table + j]),
            )
        ] * 2
    return grad_call(
        functools.partial(grad_rows_kernel, stages, wide),
        order,
        arrays,
        former_specs + latter_specs,
        out_specs,
        units,
        into,
        steps,
        pltpu.VMEM((2 * height, 2 * rows), BF),
        2 * 2 * rows * 2 * height * breadth,
        "grad_rows",
    )


def grad_columns_kernel(stages, order_ref, latter_own, latter_rec, former_own, former_rec, *refs):
    send_ref, keep_ref, turned = refs[-3:]
    rows = latter_own.shape[0]
    step = pl.program_id(0)

    @pl.when(step == 0)
    def _():
        turned[:, :rows] = latter_own[...].T
        turned[:, rows:] = latter_rec[...].T

    total = matmul(turned[:, :rows], former_own[...]) + matmul(turned[:, rows:], former_rec[...])
    total = total.astype(BF)
    chunks = total.shape[1] // LANES
    for target, when in ((send_ref, step < pl.num_programs(0) // 2), (keep_ref, step >= pl.num_programs(0) // 2)):

        @pl.when(when)
        def _(target=target):
            for seq in range(8):
                flags = keep_flags(order_ref, seq)
                where = tuple(flags[stage] for stage in stages[1:])
                for chunk in range(chunks):
                    half = (chunk % 2) * LANES
                    target[(*where, chunk // 2, slice(half, half + LANES))] = total[
                        seq * LANES : (seq + 1) * LANES, chunk * LANES : (chunk + 1) * LANES
                    ]


def grad_columns(former, latter, order, stages, units, offset, into=None):
    former, skip, height = former
    latter, latter_skip, breadth = latter
    rows = latter[0].shape[0]
    height = height // 4
    step = min(512, height)
    per = height // step
    block = (2, 2, 2, step // TILE, TILE, LANES)
    base = offset // (step // TILE)
    latter_specs = [
        pl.BlockSpec(
            (rows, breadth), lambda j, t: (0, latter_skip // breadth), pipeline_mode=pl.Buffered(1)
        )
    ] * 2
    former_specs = [
        pl.BlockSpec((rows, step), lambda j, t: (0, skip // step + t[j // per] * per + j % per))
    ] * 2
    out_specs = [
        pl.BlockSpec(block, lambda j, t: (0, 0, 0, base + jnp.minimum(j, per - 1), 0, 0)),
        pl.BlockSpec(block, lambda j, t: (0, 0, 0, base + jnp.maximum(j - per, 0), 0, 0)),
    ]
    return grad_call(
        functools.partial(grad_columns_kernel, stages),
        order,
        [latter[0], latter[1], former[0], former[1]],
        latter_specs + former_specs,
        out_specs,
        units,
        into,
        2 * per,
        pltpu.VMEM((breadth, 2 * rows), BF),
        2 * 2 * rows * 2 * height * breadth,
        "grad_columns",
    )


def grad_table_kernel(stages, height, order_ref, codes_ref, latter_own, latter_rec, *refs):
    send_ref, keep_ref, _ = refs[-3:]
    rows = latter_own.shape[0]
    parts = []
    for at in range(2):
        entry = order_ref[at] * height + lax.broadcasted_iota(jnp.int32, (height, 2 * rows), 0)
        parts.append((entry == codes_ref[...]).astype(F32).astype(BF))
    chosen = jnp.concatenate(parts, axis=0)
    total = matmul(chosen[:, :rows], latter_own[...]) + matmul(chosen[:, rows:], latter_rec[...])
    grad_store_wide(stages, order_ref, total.astype(BF), height, send_ref, keep_ref)


def grad_table(codes, latter, order, stages, height, units, offset, into=None):
    rows, breadth = latter[0].shape
    block = (2, 2, 2, height // TILE, TILE, LANES)
    base = offset // (height // TILE)
    return grad_call(
        functools.partial(grad_table_kernel, stages, height),
        order,
        [codes, latter[0], latter[1]],
        [whole_block(codes.shape), whole_block((rows, breadth)), whole_block((rows, breadth))],
        [pl.BlockSpec(block, lambda j, t: (0, 0, 0, base, 0, 0))] * 2,
        units,
        into,
        1,
        pltpu.VMEM((8, LANES), F32),
        2 * 2 * rows * 2 * height * breadth,
        "grad_table",
    )


def rows_from_units(units, height):
    tiles = height // TILE
    chunks = units.shape[0] // tiles
    return jnp.transpose(
        units.reshape(chunks, height, LANES), (1, 0, 2)
    ).reshape(height, chunks * LANES)


def columns_from_units(units):
    count = units.shape[0]
    return jnp.transpose(units.reshape(2 * count, LANES, LANES), (0, 2, 1)).reshape(count * TILE, LANES)


PACK = 1024


def pack_rows(members):
    return sum(member.shape[0] * (member.shape[1] // PACK) for member in members)


def pack_pieces(shapes):
    found, start = [], 0
    for at, (height, breadth) in enumerate(shapes):
        for column in range(breadth // PACK):
            found.append((at, column, height, start))
            start += height
    return found


def columns_of(column):
    return pl.ds(column * PACK, PACK)


def pack_kernel(place_ref, *refs):
    members, (pack_ref, quarter_ref, held, sems, out_sems) = refs[:-5], refs[-5:]
    rows = held.shape[0] // 4
    copies = []
    for number, (at, column, height, start) in enumerate(pack_pieces([m.shape for m in members])):
        copies.append(
            pltpu.make_async_copy(
                members[at].at[:, columns_of(column)], held.at[pl.ds(start, height)], sems.at[number]
            )
        )
    for copy in copies:
        copy.start()
    for copy in copies:
        copy.wait()
    mine = pl.ds(pl.multiple_of(place_ref[1] * rows, 16), rows)
    whole = pltpu.make_async_copy(held, pack_ref, out_sems.at[0])
    part = pltpu.make_async_copy(held.at[mine], quarter_ref, out_sems.at[1])
    part.start()
    whole.start()
    part.wait()
    whole.wait()


def pack_call(members, spots):
    rows = pack_rows(members)
    any_spec = pl.BlockSpec(memory_space=pl.ANY)
    count = len(pack_pieces([m.shape for m in members]))
    return pl.pallas_call(
        pack_kernel,
        in_specs=[pl.BlockSpec(memory_space=pltpu.SMEM)] + [any_spec] * len(members),
        out_specs=[any_spec] * 2,
        out_shape=[
            jax.ShapeDtypeStruct((rows, PACK), BF),
            jax.ShapeDtypeStruct((rows // 4, PACK), BF),
        ],
        scratch_shapes=[
            pltpu.VMEM((rows, PACK), BF),
            pltpu.SemaphoreType.DMA((count,)),
            pltpu.SemaphoreType.DMA((2,)),
        ],
        compiler_params=pltpu.CompilerParams(vmem_limit_bytes=VMEM_LIMIT),
        cost_estimate=HINT,
        name="pack_weights",
    )(spots, *members)


def far_kernel(parts, place_ref, *refs):
    pieces, (out_ref, held, sems, out_sem) = refs[:-4], refs[-4:]
    quarter = held.shape[0] // 4
    copies = []
    for number, (piece, (change, offset)) in enumerate(zip(pieces, parts)):
        start = (place_ref[1] ^ change) * quarter + offset
        copies.append(
            pltpu.make_async_copy(
                piece, held.at[pl.ds(pl.multiple_of(start, 16), piece.shape[0])], sems.at[number]
            )
        )
    for copy in copies:
        copy.start()
    for copy in copies:
        copy.wait()
    whole = pltpu.make_async_copy(held, out_ref, out_sem.at[0])
    whole.start()
    whole.wait()


def far_pack(pieces, parts, spots):
    rows = sum(piece.shape[0] for piece in pieces)
    any_spec = pl.BlockSpec(memory_space=pl.ANY)
    return pl.pallas_call(
        functools.partial(far_kernel, parts),
        in_specs=[pl.BlockSpec(memory_space=pltpu.SMEM)] + [any_spec] * len(pieces),
        out_specs=any_spec,
        out_shape=jax.ShapeDtypeStruct((rows, PACK), BF),
        scratch_shapes=[
            pltpu.VMEM((rows, PACK), BF),
            pltpu.SemaphoreType.DMA((len(pieces),)),
            pltpu.SemaphoreType.DMA((1,)),
        ],
        compiler_params=pltpu.CompilerParams(vmem_limit_bytes=VMEM_LIMIT),
        cost_estimate=HINT,
        name="far_pack",
    )(spots, *pieces)


def join_kernel(shapes, place_ref, *refs):
    packs = refs[:4]
    outs = refs[4 : 4 + len(shapes)]
    held, sems, out_sems = refs[-3:]
    rows = held.shape[0] // 4
    copies = []
    for flip, pack in enumerate(packs):
        start = pl.multiple_of((place_ref[0] ^ flip) * rows, 16)
        copies.append(pltpu.make_async_copy(pack, held.at[pl.ds(start, rows)], sems.at[flip]))
    for copy in copies:
        copy.start()
    for copy in copies:
        copy.wait()
    copies = []
    for at, column, height, start in pack_pieces(shapes):
        for block in range(4):
            copies.append(
                pltpu.make_async_copy(
                    held.at[pl.ds(block * rows + start, height)],
                    outs[at].at[pl.ds(block * height, height), columns_of(column)],
                    out_sems.at[len(copies)],
                )
            )
    for copy in copies:
        copy.start()
    for copy in copies:
        copy.wait()


def join_weights(members, packs, spots):
    shapes = [member.shape for member in members]
    rows = pack_rows(members)
    any_spec = pl.BlockSpec(memory_space=pl.ANY)
    outs = [jax.ShapeDtypeStruct((4 * height, breadth), BF) for height, breadth in shapes]
    return pl.pallas_call(
        functools.partial(join_kernel, shapes),
        in_specs=[pl.BlockSpec(memory_space=pltpu.SMEM)] + [any_spec] * 4,
        out_specs=[any_spec] * len(outs),
        out_shape=outs,
        scratch_shapes=[
            pltpu.VMEM((4 * rows, PACK), BF),
            pltpu.SemaphoreType.DMA((4,)),
            pltpu.SemaphoreType.DMA((4 * len(pack_pieces(shapes)),)),
        ],
        compiler_params=pltpu.CompilerParams(vmem_limit_bytes=VMEM_LIMIT),
        cost_estimate=HINT,
        name="join_weights",
    )(spots, *packs)


WIDE_LIMIT = 58 * 1024 * 1024
GELU_A = 0.7978845608028654
GELU_B = 0.044715


def gelu_pair(values):
    square = values * values
    bent = jnp.tanh(GELU_A * values * (1.0 + GELU_B * square))
    half = 0.5 * (1.0 + bent)
    slope = half + 0.5 * values * (1.0 - bent * bent) * (GELU_A * (1.0 + 3.0 * GELU_B * square))
    return values * half, slope


def rms_grads(values, gain, grad):
    inverse = lax.rsqrt(jnp.mean(values * values, axis=-1, keepdims=True) + EPSILON)
    scaled = values * inverse
    inner = grad * gain
    part = inverse * (inner - scaled * jnp.mean(inner * scaled, axis=-1, keepdims=True))
    return part, jnp.sum(grad * scaled, axis=0, keepdims=True)


def held(shape):
    return pl.BlockSpec(
        shape, lambda *_: (0,) * len(shape), pipeline_mode=pl.Buffered(1)
    )


def dense_call(kernel, steps, in_specs, out_specs, out_shape, scratch, name):
    return pl.pallas_call(
        kernel,
        grid=(steps,),
        in_specs=in_specs,
        out_specs=out_specs,
        out_shape=out_shape,
        scratch_shapes=scratch,
        compiler_params=pltpu.CompilerParams(vmem_limit_bytes=WIDE_LIMIT),
        cost_estimate=HINT,
        name=name,
    )


def frame_front_kernel(hidden_ref, gain_ref, weight_ref, normed_ref, packed_ref):
    groups, rows, own, _ = packed_ref.shape

    @pl.when(pl.program_id(0) == 0)
    def _():
        normed_ref[...] = rms_scale(hidden_ref[...].astype(F32), gain_ref[...]).astype(BF)

    total = matmul(normed_ref[...], weight_ref[...]).astype(BF)
    for part in range(3):

        @pl.when(pl.program_id(0) == part)
        def _(part=part):
            for group in range(groups):
                packed_ref[group, :, :, LANES * part : LANES * (part + 1)] = total[
                    :, LANES * group : LANES * (group + 1)
                ].reshape(rows, own, LANES)


def frame_front(hidden, gain, weight, rows):
    total, width = hidden.shape
    groups = width // LANES
    shape = (groups, rows, total // rows, 3 * LANES)
    return dense_call(
        frame_front_kernel,
        3,
        [held(hidden.shape), held(gain.shape), pl.BlockSpec((width, width), lambda j: (0, j))],
        [whole_block((total, width)), whole_block(shape)],
        [jax.ShapeDtypeStruct((total, width), BF), jax.ShapeDtypeStruct(shape, BF)],
        [],
        "frame_front",
    )(hidden, gain, weight)


def frame_rear_kernel(
    hidden_ref, front_ref, packed_ref, gain_ref, output_ref, expand_ref, contract_ref,
    kept_ref, mixed_ref, slope_ref, base_ref, total, normed_ref,
):
    groups, rows, own, _ = packed_ref.shape
    width = groups * LANES
    tile = slope_ref.shape[1]

    @pl.when(pl.program_id(0) == 0)
    def _():
        for group in range(groups):
            kept_ref[:, width + LANES * group : width + LANES * (group + 1)] = packed_ref[
                group
            ].reshape(rows * own, LANES)
        attended = kept_ref[:, width : 2 * width]
        mixed = hidden_ref[...].astype(F32) + matmul(attended, output_ref[...])
        mixed_ref[...] = mixed
        total[...] = mixed
        normed_ref[...] = rms_scale(mixed, gain_ref[...]).astype(BF)
        kept_ref[:, :width] = front_ref[...]
        kept_ref[:, 2 * width : 3 * width] = normed_ref[...]

    active, slope = gelu_pair(matmul(normed_ref[...], expand_ref[...]))
    active = active.astype(BF)
    for step in range(4 * width // tile):

        @pl.when(pl.program_id(0) == step)
        def _(step=step):
            kept_ref[:, 3 * width + step * tile : 3 * width + (step + 1) * tile] = active

    slope_ref[...] = slope.astype(BF)
    total[...] += matmul(active, contract_ref[...])

    @pl.when(pl.program_id(0) == pl.num_programs(0) - 1)
    def _():
        base_ref[...] = total[...].astype(BF)


FF_TILE = 512
FRAME_TILE = 1024


def frame_rear(hidden, front, packed, gain, output, expand, contract):
    total, width = hidden.shape
    inner = expand.shape[1]
    tile = FRAME_TILE
    full = whole_block((total, width))
    kept = (total, 3 * width + inner)
    return dense_call(
        frame_rear_kernel,
        inner // tile,
        [
            held(hidden.shape),
            held(front.shape),
            held(packed.shape),
            held(gain.shape),
            held(output.shape),
            pl.BlockSpec((width, tile), lambda j: (0, j)),
            pl.BlockSpec((tile, width), lambda j: (j, 0)),
        ],
        [whole_block(kept), full, pl.BlockSpec((total, tile), lambda j: (0, j)), full],
        [
            jax.ShapeDtypeStruct(kept, BF),
            jax.ShapeDtypeStruct((total, width), F32),
            jax.ShapeDtypeStruct((total, inner), BF),
            jax.ShapeDtypeStruct((total, width), BF),
        ],
        [pltpu.VMEM((total, width), F32), pltpu.VMEM((total, width), BF)],
        "frame_rear",
    )(hidden, front, packed, gain, output, expand, contract)


def frame_rear_grads_kernel(
    grad_ref, slope_ref, mixed_ref, gain_ref, output_ref, expand_ref, contract_ref,
    kept_ref, mixed_grad_ref, packed_ref, gain_grad_ref, total,
):
    groups, rows, own, _ = packed_ref.shape
    width = groups * LANES
    tile = slope_ref.shape[1]
    grad = grad_ref[...]
    expand_in = (slope_ref[...].astype(F32) * inner_right(grad, contract_ref[...])).astype(BF)
    for step in range(4 * width // tile):

        @pl.when(pl.program_id(0) == step)
        def _(step=step):
            kept_ref[:, width + step * tile : width + (step + 1) * tile] = expand_in

    @pl.when(pl.program_id(0) == 0)
    def _():
        total[...] = jnp.zeros_like(total)
        kept_ref[:, :width] = grad

    total[...] += inner_right(expand_in, expand_ref[...])

    @pl.when(pl.program_id(0) == pl.num_programs(0) - 1)
    def _():
        part, gain_grad = rms_grads(mixed_ref[...], gain_ref[...], total[...])
        mixed_grad = grad.astype(F32) + part
        mixed_grad_ref[...] = mixed_grad
        gain_grad_ref[...] = gain_grad
        output_in = mixed_grad.astype(BF)
        kept_ref[:, 5 * width :] = output_in
        attended_grad = inner_right(output_in, output_ref[...]).astype(BF)
        for group in range(groups):
            packed_ref[group] = attended_grad[:, LANES * group : LANES * (group + 1)].reshape(
                rows, own, LANES
            )


def frame_rear_grads(grad, slope, mixed, gain, output, expand, contract, rows):
    total, width = grad.shape
    inner = expand.shape[1]
    tile = FRAME_TILE
    shape = (width // LANES, rows, total // rows, LANES)
    kept = (total, 2 * width + inner)
    full = whole_block((total, width))
    part = pl.BlockSpec((total, tile), lambda j: (0, j))
    return dense_call(
        frame_rear_grads_kernel,
        inner // tile,
        [
            held(grad.shape),
            part,
            held(mixed.shape),
            held(gain.shape),
            held(output.shape),
            pl.BlockSpec((width, tile), lambda j: (0, j)),
            pl.BlockSpec((tile, width), lambda j: (j, 0)),
        ],
        [whole_block(kept), full, whole_block(shape), whole_block((1, width))],
        [
            jax.ShapeDtypeStruct(kept, BF),
            jax.ShapeDtypeStruct((total, width), F32),
            jax.ShapeDtypeStruct(shape, BF),
            jax.ShapeDtypeStruct((1, width), F32),
        ],
        [pltpu.VMEM((total, width), F32)],
        "frame_rear_grads",
    )(grad, slope, mixed, gain, output, expand, contract)


def frame_front_grads_kernel(
    packed_ref, hidden_ref, gain_ref, mixed_grad_ref, weight_ref,
    projected_ref, grad_ref, gain_grad_ref, total,
):
    groups, rows, own, _ = packed_ref.shape

    @pl.when(pl.program_id(0) == 0)
    def _():
        total[...] = jnp.zeros_like(total)

    for part in range(3):

        @pl.when(pl.program_id(0) == part)
        def _(part=part):
            for group in range(groups):
                projected_ref[:, LANES * group : LANES * (group + 1)] = packed_ref[
                    group, :, :, LANES * part : LANES * (part + 1)
                ].reshape(rows * own, LANES)

    total[...] += inner_right(projected_ref[...], weight_ref[...])

    @pl.when(pl.program_id(0) == 2)
    def _():
        part, gain_grad = rms_grads(hidden_ref[...].astype(F32), gain_ref[...], total[...])
        grad_ref[...] = mixed_grad_ref[...] + part
        gain_grad_ref[...] = gain_grad


def frame_front_grads(packed, hidden, gain, mixed_grad, weight):
    total, width = hidden.shape
    return dense_call(
        frame_front_grads_kernel,
        3,
        [
            held(packed.shape),
            held(hidden.shape),
            held(gain.shape),
            held(mixed_grad.shape),
            pl.BlockSpec((width, width), lambda j: (0, j)),
        ],
        [
            pl.BlockSpec((total, width), lambda j: (0, j)),
            whole_block((total, width)),
            whole_block((1, width)),
        ],
        [
            jax.ShapeDtypeStruct((total, 3 * width), BF),
            jax.ShapeDtypeStruct((total, width), F32),
            jax.ShapeDtypeStruct((1, width), F32),
        ],
        [pltpu.VMEM((total, width), F32)],
        "frame_front_grads",
    )(packed, hidden, gain, mixed_grad, weight)


def codec_front_kernel(base_ref, entries_ref, gain_ref, weight_ref, normed_ref, packed_ref, normed):
    positions = packed_ref.shape[0]

    @pl.when(pl.program_id(0) == 0)
    def _():
        base = base_ref[...].astype(F32)
        size = base.shape[0]
        for t in range(positions):
            hidden = base if t == 0 else base + entries_ref[t - 1].astype(F32)
            normed[size * t : size * (t + 1)] = rms_scale(hidden, gain_ref[...]).astype(BF)
        normed_ref[...] = normed[...]

    total = matmul(normed[...], weight_ref[...]).astype(BF)
    packed_ref[...] = total.reshape(packed_ref.shape)


def codec_front(base, entries, gain, weight):
    total, width = base.shape
    positions = entries.shape[0] + 1
    return dense_call(
        codec_front_kernel,
        6,
        [
            held(base.shape),
            held(entries.shape),
            held(gain.shape),
            pl.BlockSpec((width, width // 2), lambda j: (0, j)),
        ],
        [
            whole_block((positions * total, width)),
            pl.BlockSpec((positions, total, width // 2), lambda j: (0, 0, j)),
        ],
        [
            jax.ShapeDtypeStruct((positions * total, width), BF),
            jax.ShapeDtypeStruct((positions, total, 3 * width), BF),
        ],
        [pltpu.VMEM((positions * total, width), BF)],
        "codec_front",
    )(base, entries, gain, weight)


def codec_rear_kernel(
    base_ref, entries_ref, front_ref, attended_ref, grad_ref, gain_ref, output_ref, expand_ref,
    contract_ref, mixed_ref, active_ref, expand_kept_ref, kept_ref, mixed_grad_ref,
    attended_grad_ref, gain_grad_ref, total,
):
    width = total.shape[1]
    positions = entries_ref.shape[0] + 1
    size = base_ref.shape[0]

    @pl.when(pl.program_id(0) == 0)
    def _():
        base = base_ref[...].astype(F32)
        for t in range(positions):
            own = slice(size * t, size * (t + 1))
            hidden = base if t == 0 else base + entries_ref[t - 1].astype(F32)
            mixed = hidden + matmul(attended_ref[own], output_ref[...])
            mixed_ref[own] = mixed
            expand_kept_ref[own, :width] = rms_scale(mixed, gain_ref[...]).astype(BF)
        total[...] = jnp.zeros_like(total)
        kept_ref[:, :width] = front_ref[...]
        kept_ref[:, width : 2 * width] = attended_ref[...]

    active, slope = gelu_pair(matmul(expand_kept_ref[:, :width], expand_ref[...]))
    active_ref[...] = active.astype(BF)
    expand_in = (slope * inner_right(grad_ref[...], contract_ref[...])).astype(BF)
    tile = expand_in.shape[1]
    for step in range(4 * width // tile):

        @pl.when(pl.program_id(0) == step)
        def _(step=step):
            expand_kept_ref[:, width + step * tile : width + (step + 1) * tile] = expand_in

    total[...] += inner_right(expand_in, expand_ref[...])

    @pl.when(pl.program_id(0) == pl.num_programs(0) - 1)
    def _():
        gain_grads = jnp.zeros_like(gain_grad_ref)
        for t in range(positions):
            own = slice(size * t, size * (t + 1))
            part, gain_grad = rms_grads(mixed_ref[own], gain_ref[...], total[own])
            gain_grads = gain_grads + gain_grad
            mixed_grad = grad_ref[own].astype(F32) + part
            mixed_grad_ref[own] = mixed_grad
            output_in = mixed_grad.astype(BF)
            kept_ref[own, 2 * width :] = output_in
            attended_grad_ref[t] = inner_right(output_in, output_ref[...]).astype(BF)
        gain_grad_ref[...] = gain_grads


def codec_rear(base, entries, front, attended, grad, gain, output, expand, contract):
    size, width = base.shape
    total = attended.shape[0]
    inner = expand.shape[1]
    tile = FF_TILE
    full = whole_block((total, width))
    wide, triple = (total, width + inner), (total, 3 * width)
    high = jax.ShapeDtypeStruct((total, width), F32)
    return dense_call(
        codec_rear_kernel,
        inner // tile,
        [
            held(base.shape),
            held(entries.shape),
            held(front.shape),
            held(attended.shape),
            held(grad.shape),
            held(gain.shape),
            held(output.shape),
            pl.BlockSpec((width, tile), lambda j: (0, j)),
            pl.BlockSpec((tile, width), lambda j: (j, 0)),
        ],
        [
            held((total, width)),
            pl.BlockSpec((total, tile), lambda j: (0, j)),
            held(wide),
            held(triple),
            held((total, width)),
            held((total // size, size, width)),
            whole_block((1, width)),
        ],
        [
            high,
            jax.ShapeDtypeStruct((total, inner), BF),
            jax.ShapeDtypeStruct(wide, BF),
            jax.ShapeDtypeStruct(triple, BF),
            high,
            jax.ShapeDtypeStruct((total // size, size, width), BF),
            jax.ShapeDtypeStruct((1, width), F32),
        ],
        [pltpu.VMEM((total, width), F32)],
        "codec_rear",
    )(base, entries, front, attended, grad, gain, output, expand, contract)


def codec_result_kernel(mixed_ref, active_ref, live_ref, contract_ref, out_ref, total):
    positions, size, _ = out_ref.shape

    @pl.when(pl.program_id(0) == 0)
    def _():
        total[...] = mixed_ref[...]

    total[...] += matmul(active_ref[...], contract_ref[...])

    @pl.when(pl.program_id(0) == pl.num_programs(0) - 1)
    def _():
        for t in range(positions):
            out_ref[t] = (total[size * t : size * (t + 1)] * live_ref[...]).astype(BF)


def codec_result(mixed, active, live, contract):
    total, width = mixed.shape
    size = live.shape[0]
    inner = active.shape[1]
    tile = FF_TILE
    shape = (total // size, size, width)
    return dense_call(
        codec_result_kernel,
        inner // tile,
        [
            held(mixed.shape),
            pl.BlockSpec((total, tile), lambda j: (0, j)),
            held(live.shape),
            pl.BlockSpec((tile, width), lambda j: (j, 0)),
        ],
        whole_block(shape),
        jax.ShapeDtypeStruct(shape, BF),
        [pltpu.VMEM((total, width), F32)],
        "codec_result",
    )(mixed, active, live, contract)


def codec_front_grads_kernel(
    grad_ref, base_ref, entries_ref, gain_ref, mixed_grad_ref, weight_ref,
    base_grad_ref, entry_grad_ref, gain_grad_ref, total,
):
    positions = entries_ref.shape[0] + 1
    size = base_ref.shape[0]

    @pl.when(pl.program_id(0) == 0)
    def _():
        total[...] = jnp.zeros_like(total)

    total[...] += inner_right(grad_ref[...], weight_ref[...])

    @pl.when(pl.program_id(0) == pl.num_programs(0) - 1)
    def _():
        base = base_ref[...].astype(F32)
        gain_grads = jnp.zeros_like(gain_grad_ref)
        base_grad = jnp.zeros_like(base)
        for t in range(positions):
            own = slice(size * t, size * (t + 1))
            hidden = base if t == 0 else base + entries_ref[t - 1].astype(F32)
            part, gain_grad = rms_grads(hidden, gain_ref[...], total[own])
            gain_grads = gain_grads + gain_grad
            grad = mixed_grad_ref[own] + part
            base_grad = base_grad + grad
            if t > 0:
                entry_grad_ref[size * (t - 1) : size * t] = grad.astype(BF)
        base_grad_ref[...] = base_grad.astype(BF)
        gain_grad_ref[...] = gain_grads


def codec_front_grads(grad, base, entries, gain, mixed_grad, weight):
    size, width = base.shape
    total = grad.shape[0]
    tile = width // 2
    return dense_call(
        codec_front_grads_kernel,
        grad.shape[1] // tile,
        [
            pl.BlockSpec((total, tile), lambda j: (0, j)),
            held(base.shape),
            held(entries.shape),
            held(gain.shape),
            held(mixed_grad.shape),
            pl.BlockSpec((width, tile), lambda j: (0, j)),
        ],
        [whole_block((size, width)), whole_block((total - size, width)), whole_block((1, width))],
        [
            jax.ShapeDtypeStruct((size, width), BF),
            jax.ShapeDtypeStruct((total - size, width), BF),
            jax.ShapeDtypeStruct((1, width), F32),
        ],
        [pltpu.VMEM((total, width), F32)],
        "codec_front_grads",
    )(grad, base, entries, gain, mixed_grad, weight)


def shards_general(
    frames,
    segments,
    padding,
    codec_tokens,
    codebooks,
    frame_prenorm,
    frame_project,
    frame_output,
    frame_postnorm,
    frame_expand,
    frame_contract,
    codec_prenorm,
    codec_project,
    codec_output,
    codec_postnorm,
    codec_expand,
    codec_contract,
    cotangent,
):
    place = Place()
    row_count, frames_dev, width = frames.shape
    frame_total = row_count * frames_dev
    positions = cotangent.shape[2]
    gains = lax.all_gather(
        jnp.stack([frame_prenorm, frame_postnorm, codec_prenorm, codec_postnorm]),
        "mp",
        axis=1,
        tiled=True,
    )
    frame_weights = (
        gains[0],
        gather_weight(frame_project, place),
        gather_weight(frame_output, place),
        gains[1],
        gather_weight(frame_expand, place),
        gather_weight(frame_contract, place),
    )
    codec_weights = (
        gains[2],
        gather_weight(codec_project, place),
        gather_weight(codec_output, place),
        gains[3],
        gather_weight(codec_expand, place),
        gather_weight(codec_contract, place),
    )
    table = gather_weight(codebooks, place)

    hidden = frames.astype(F32).reshape(frame_total, width)
    normed, projected = front_pass(hidden, frame_weights)
    attended, attention_back = frame_attention(
        projected.reshape(row_count, frames_dev, 3 * width), segments, place
    )
    attended = attended.reshape(frame_total, width)
    frame_result, frame_saved = rear_pass(hidden, attended, frame_weights)
    base = frame_result.astype(BF).astype(F32)

    table_rows = codec_tokens.reshape(positions - 1, frame_total) + (
        jnp.arange(positions - 1, dtype=jnp.int32) * CODES
    )[:, None]
    embedded = table[table_rows].astype(F32)
    codec_hidden = jnp.concatenate([base[None], base[None] + embedded], axis=0).reshape(
        positions * frame_total, width
    )
    codec_normed, codec_projected = front_pass(codec_hidden, codec_weights)
    marks = (
        jnp.arange(width)[:, None] // HEAD == jnp.arange(HEADS)[None, :]
    ).astype(F32)
    view = codec_projected.reshape(positions, frame_total, 3, width)
    queries, keys, values = ([view[t, :, part] for t in range(positions)] for part in range(3))
    soft = codec_softmax(queries, keys, marks)
    codec_attended = jnp.concatenate(codec_attend(soft, values, marks), axis=0)
    codec_result, codec_saved = rear_pass(codec_hidden, codec_attended, codec_weights)
    live = padding.reshape(frame_total).astype(F32)[None, :, None]
    output = jnp.transpose(
        (codec_result.reshape(positions, frame_total, width) * live).astype(BF), (1, 0, 2)
    ).reshape(row_count, frames_dev, positions, width)

    codec_grad = (
        jnp.transpose(cotangent.reshape(frame_total, positions, width), (1, 0, 2)).astype(F32) * live
    ).reshape(positions * frame_total, width)
    mixed_grad, attended_grad, codec_postnorm_grad, contract_in, expand_in, output_in = rear_grads(
        codec_grad, codec_saved, codec_weights
    )
    codec_contract_part = weight_grad(codec_saved[3], contract_in, place, True)
    codec_expand_part = weight_grad(codec_saved[1], expand_in, place, False)
    codec_output_part = weight_grad(codec_attended, output_in, place, True)
    grad_view = attended_grad.reshape(positions, frame_total, width)
    codec_projected_grad = codec_attend_grads(
        soft, queries, keys, values, [grad_view[t] for t in range(positions)], marks
    )
    codec_project_part = weight_grad(codec_normed, codec_projected_grad, place, True)
    input_grad, codec_prenorm_grad = front_grads(
        codec_hidden, codec_projected_grad, mixed_grad, codec_weights
    )
    input_grad = input_grad.reshape(positions, frame_total, width)
    chosen = (
        table_rows.reshape(-1)[:, None] == jnp.arange(table.shape[0], dtype=jnp.int32)[None, :]
    ).astype(BF)
    table_part = weight_grad(chosen, input_grad[1:].reshape(-1, width).astype(BF), place, False)
    base_grad = jnp.sum(input_grad, axis=0).astype(BF).astype(F32)

    (codec_contract_grad,) = finish_grads([codec_contract_part], place)
    codec_expand_grad, codec_output_grad, codec_project_grad = finish_grads(
        [codec_expand_part, codec_output_part, codec_project_part], place
    )
    (table_grad,) = finish_grads([table_part], place)

    frame_mixed_grad, frame_attended_grad, frame_postnorm_grad, contract_in, expand_in, output_in = (
        rear_grads(base_grad, frame_saved, frame_weights)
    )
    frame_projected_grad = attention_back(
        frame_attended_grad.reshape(row_count, frames_dev, width)
    ).reshape(frame_total, 3 * width)
    frame_contract_part = weight_grad(frame_saved[3], contract_in, place, True)
    frame_expand_part = weight_grad(frame_saved[1], expand_in, place, False)
    frame_output_part = weight_grad(attended, output_in, place, True)
    frame_project_part = weight_grad(normed, frame_projected_grad, place, True)
    frames_grad, frame_prenorm_grad = front_grads(
        hidden, frame_projected_grad, frame_mixed_grad, frame_weights
    )
    (frame_contract_grad,) = finish_grads([frame_contract_part], place)
    frame_expand_grad, frame_output_grad = finish_grads(
        [frame_expand_part, frame_output_part], place
    )
    (frame_project_grad,) = finish_grads([frame_project_part], place)
    gain_sums = sum_everywhere(
        jnp.stack(
            [frame_prenorm_grad, frame_postnorm_grad, codec_prenorm_grad, codec_postnorm_grad]
        ),
        place,
    )
    return (
        output,
        frames_grad.reshape(row_count, frames_dev, width),
        table_grad,
        gain_sums[0],
        frame_project_grad,
        frame_output_grad,
        gain_sums[1],
        frame_expand_grad,
        frame_contract_grad,
        gain_sums[2],
        codec_project_grad,
        codec_output_grad,
        gain_sums[3],
        codec_expand_grad,
        codec_contract_grad,
    )


class Pair:
    def __init__(self, own):
        self.own = own
        self.other = swap(own, "mp", 1)
        self.age = 0

    def both(self):
        return (self.own, self.other)


class Chain:
    def __init__(self):
        self.last = ()
        self.pending = []

    def pair(self, own):
        made = Pair(own)
        self.pending.append(made)
        return made

    def enter(self, *values):
        due = [made for made in self.pending if made.age >= 3]
        self.pending = [made for made in self.pending if made.age < 3]
        for made in self.pending:
            made.age += 1
        came = tuple(made.other for made in due)
        held = lax.optimization_barrier(tuple(values) + came + self.last)
        for made, other in zip(due, held[len(values) :]):
            made.other = other
        return held[0] if len(values) == 1 else held[: len(values)]

    def leave(self, *values):
        self.last = values


class Gather:
    def __init__(self, members, spots, whole=False):
        self.members = members
        self.spots = spots
        self.whole = whole
        self.pack, self.quarter = pack_call(members, spots)

    def start(self, chain):
        self.came = swap(chain.enter(self.pack if self.whole else self.quarter), "mp", 2)
        self.near = chain.pair(self.pack)

    def spread(self, chain):
        self.came = chain.enter(self.came)
        chain.leave(self.came)
        if self.whole:
            self.far = chain.pair(self.came)
            return
        self.over_x = swap(self.came, "seq", 1)
        self.over_n = swap(self.came, "seq", 2)

    def cross(self, chain):
        self.over_x, self.over_n = chain.enter(self.over_x, self.over_n)
        chain.leave(self.over_x, self.over_n)
        half = self.over_x.shape[0] // 2
        self.ends = (swap(self.over_n[:half], "seq", 1), swap(self.over_x[half:], "seq", 2))

    def close(self, chain):
        ends = chain.enter(*self.ends)
        parts = ((0, 0), (1, 0), (2, 0), (3, 0), (3, ends[0].shape[0]))
        far = far_pack([self.came, self.over_x, self.over_n, *ends], parts, self.spots)
        chain.leave(far)
        self.far = far

    def send(self, chain):
        self.far = Pair(chain.enter(self.far))

    def join(self, chain):
        packs = chain.enter(*self.near.both(), *self.far.both())
        outs = join_weights(self.members, packs, self.spots)
        chain.leave(*outs)
        return outs


def load(block, riders):
    if riders is None:
        return block
    high = riders.astype(BF)
    low = (riders - high.astype(F32)).astype(BF)
    return jnp.concatenate(
        [part.reshape(-1, LANES) for part in (block, high, low)], axis=0
    )


def unload(message, shape, riders):
    if riders is None:
        return message, None
    rows = message.shape[0] - 2 * riders.size // LANES
    high, low = (
        part.astype(F32).reshape(riders.shape) for part in jnp.split(message[rows:], 2, axis=0)
    )
    return message[:rows].reshape(shape), riders + (high + low)


class Reduce:
    def __init__(self, stages, blocks, riders=None):
        self.stages = stages
        self.keep = blocks[1]
        self.riders = riders
        self.came = []
        self.shape = blocks[0].shape
        self.coming = swap(load(blocks[0], riders), *BITS[stages[0]])

    def arrive(self, chain):
        self.coming = chain.enter(self.coming)
        chain.leave(self.coming)

    def take(self, chain):
        self.keep, self.coming, *self.came = chain.enter(self.keep, self.coming, *self.came)
        block, self.riders = unload(self.coming, self.shape, self.riders)
        self.came.append(block)

    def total(self, last):
        at = len(self.came) - 1
        spot = (1,) * at + ((0,) if not last else ())
        value = self.keep[spot].astype(F32) if spot else self.keep.astype(F32)
        for level, came in enumerate(self.came):
            value = value + came[spot[level:]].astype(F32)
        return value

    def give(self, chain):
        self.take(chain)
        given = self.total(False).astype(BF)
        self.shape = given.shape
        return given

    def step(self, chain):
        given = self.give(chain)
        message = load(given, self.riders)
        chain.leave(message)
        self.coming = swap(message, *BITS[self.stages[len(self.came)]])

    def result(self):
        return self.total(True)


def finish(sums, chain):
    given = jnp.concatenate([one.give(chain) for one in sums], axis=0)
    riders = sums[-1].riders
    message = load(given, riders)
    chain.leave(message)
    message = swap(message, *BITS["f"])

    def take():
        came, total = unload(message, given.shape, riders)
        start = 0
        for one in sums:
            size = one.shape[-3]
            one.came.append(came[start : start + size])
            start += size
        sums[-1].riders = total

    return take


def shards(
    frames,
    segments,
    padding,
    codec_tokens,
    codebooks,
    frame_prenorm,
    frame_project,
    frame_output,
    frame_postnorm,
    frame_expand,
    frame_contract,
    codec_prenorm,
    codec_project,
    codec_output,
    codec_postnorm,
    codec_expand,
    codec_contract,
    cotangent,
):
    place = Place()
    chain = Chain()
    order = grad_order(place)
    spots = jnp.stack([place.mp, place.seq % 4]).astype(jnp.int32)
    row_count, frames_dev, width = frames.shape
    frame_total = row_count * frames_dev
    positions = cotangent.shape[2]
    count = place.seq_count

    gain_rows = jnp.pad(
        jnp.concatenate([frame_prenorm, frame_postnorm, codec_prenorm, codec_postnorm])[None],
        ((0, 127), (0, 0)),
    )
    first = Gather([frame_project, gain_rows], spots)
    first.start(chain)
    chain.leave(first.quarter)
    second = Gather([frame_expand, frame_contract, frame_output], spots)
    second.quarter = chain.enter(second.quarter)
    chain.leave(second.quarter)
    every_segment = lax.all_to_all(
        jnp.broadcast_to(segments[None], (count, row_count, frames_dev)),
        "seq",
        split_axis=0,
        concat_axis=0,
        tiled=True,
    )
    every_segment = jnp.transpose(every_segment, (1, 0, 2)).reshape(row_count, count * frames_dev)
    codes = codec_tokens.reshape(1, (positions - 1) * frame_total) + jnp.repeat(
        jnp.arange(positions - 1, dtype=jnp.int32) * CODES, frame_total
    )
    codes_pair = chain.pair(codes)
    every_segment = chain.enter(every_segment)
    chain.leave(every_segment)
    live = padding.reshape(frame_total).astype(F32)[:, None]
    first.spread(chain)
    second.start(chain)
    contract_in = (
        jnp.transpose(chain.enter(cotangent).reshape(frame_total, positions, width), (1, 0, 2))
        * live.astype(BF)[None]
    ).reshape(positions * frame_total, width)
    chain.leave(contract_in)
    first.cross(chain)
    fourth = Gather([codec_expand, codec_contract, codec_output], spots)
    fourth.quarter = chain.enter(fourth.quarter)
    chain.leave(fourth.quarter)
    second.spread(chain)
    fourth.start(chain)
    third = Gather([codec_project, codebooks], spots, True)
    third.pack = chain.enter(third.pack)
    chain.leave(third.pack)
    third.start(chain)
    first.close(chain)
    first.send(chain)

    frame_project_all, gains = first.join(chain)
    gains = jnp.transpose(
        gains.reshape(place.mp_count, -1, 4, width // 4)[:, 0], (1, 0, 2)
    ).reshape(4, 1, width).astype(F32)
    hidden = frames.reshape(frame_total, width)
    normed, packed = frame_front(hidden, chain.enter(gains[0]), frame_project_all, row_count)
    packed, second.over_x, second.over_n, fourth.came = chain.enter(
        packed, second.over_x, second.over_n, fourth.came
    )
    chain.leave(packed)
    packed = lax.all_to_all(packed, "seq", split_axis=0, concat_axis=0, tiled=True)
    second.cross(chain)
    packed, *second.ends = chain.enter(packed, *second.ends)
    chain.leave(packed)
    second.close(chain)
    second.send(chain)
    fourth.spread(chain)
    contract_pair = Pair(contract_in)
    packed = chain.enter(packed)
    attended = frame_attend_call(packed, every_segment)
    chain.leave(attended)
    attended, second.far.other = chain.enter(attended, second.far.other)
    chain.leave(attended)
    attended = lax.all_to_all(attended, "seq", split_axis=0, concat_axis=0, tiled=True)
    frame_expand_all, frame_contract_all, frame_output_all = second.join(chain)
    attended, fourth.over_x, fourth.over_n = chain.enter(attended, fourth.over_x, fourth.over_n)
    chain.leave(attended)
    fourth.cross(chain)
    frame_kept, mixed, slope, base = frame_rear(
        hidden,
        normed,
        chain.enter(attended),
        gains[1],
        frame_output_all,
        frame_expand_all,
        frame_contract_all,
    )
    chain.leave(base)

    base, third.came, *fourth.ends = chain.enter(base, third.came, *fourth.ends)
    chain.leave(base)
    third.spread(chain)
    fourth.close(chain)
    codec_project_all, table = third.join(chain)
    fourth.send(chain)
    frame_kept = Pair(chain.enter(frame_kept))
    entries = table[codes.reshape(positions - 1, frame_total)]
    codec_normed, codec_packed = codec_front(chain.enter(base), entries, gains[2], codec_project_all)
    chain.leave(codec_packed)
    codec_packed, contract_pair.other = chain.enter(codec_packed, contract_pair.other)
    codec_attended = codec_attend_call(codec_packed).reshape(positions * frame_total, width)
    chain.leave(codec_attended)
    codec_expand_all, codec_contract_all, codec_output_all = fourth.join(chain)
    codec_attended, frame_kept.other = chain.enter(codec_attended, frame_kept.other)
    chain.leave(codec_attended)
    (
        codec_mixed,
        codec_activated,
        codec_expand_kept,
        codec_kept,
        mixed_grad,
        attended_grad,
        codec_postnorm_grad,
    ) = codec_rear(
        base,
        entries,
        codec_normed,
        chain.enter(codec_attended),
        contract_in,
        gains[3],
        codec_output_all,
        codec_expand_all,
        codec_contract_all,
    )
    chain.leave(codec_activated)

    inner = codec_activated.shape[1]
    activated_pair = chain.pair(codec_activated)
    codec_expand_kept = chain.pair(codec_expand_kept)
    projected_grad = codec_attend_grads_call(codec_packed, chain.enter(attended_grad)).reshape(
        positions * frame_total, 3 * width
    )
    chain.leave(projected_grad)
    base_grad, table_in, codec_prenorm_grad = codec_front_grads(
        chain.enter(projected_grad), base, entries, gains[2], mixed_grad, codec_project_all
    )
    chain.leave(base_grad)
    frame_grads_kept, frame_mixed_grad, grads, frame_postnorm_grad = frame_rear_grads(
        chain.enter(base_grad),
        slope,
        mixed,
        gains[1],
        frame_output_all,
        frame_expand_all,
        frame_contract_all,
        row_count,
    )
    chain.leave(grads)

    activated_pair.other, codec_expand_kept.other, grads, frame_grads_kept = chain.enter(
        activated_pair.other, codec_expand_kept.other, grads, frame_grads_kept
    )
    chain.leave(grads)
    grads = lax.all_to_all(grads, "seq", split_axis=0, concat_axis=0, tiled=True)
    frame_grads_kept = Pair(frame_grads_kept)
    contract_stages = tuple("ynxf")
    contract_blocks = grad_columns(
        (chain.enter(*activated_pair.both()), 0, inner),
        (contract_pair.both(), 0, width),
        order,
        contract_stages,
        4,
        0,
    )
    chain.leave(*contract_blocks)
    expand_stages = tuple("xnyf")
    arrays = chain.enter(*codec_expand_kept.both())
    expand_blocks = grad_rows((arrays, 0, width), (arrays, width, inner), order, expand_stages, 4, 0)
    chain.leave(*expand_blocks)

    grads, frame_grads_kept.other = chain.enter(grads, frame_grads_kept.other)
    chain.leave(grads)
    contract_sum = Reduce(contract_stages, chain.enter(*contract_blocks))
    expand_sum = Reduce(expand_stages, chain.enter(*expand_blocks))
    codec_kept = Pair(chain.enter(codec_kept))
    projected_pair = Pair(chain.enter(projected_grad))
    packed_grad = frame_attend_grads_call(packed, chain.enter(grads), every_segment)
    chain.leave(packed_grad)
    kept, arrays = frame_kept.both(), chain.enter(*frame_grads_kept.both())
    frame_contract_blocks = grad_columns(
        (kept, 3 * width, inner), (arrays, 0, width), order, contract_stages, 4, 0
    )
    chain.leave(*frame_contract_blocks)
    frame_expand_stages = tuple("xynf")
    arrays = chain.enter(*arrays)
    blocks = grad_rows(
        (kept, 2 * width, width), (arrays, width, inner), order, frame_expand_stages, 5, 0
    )
    frame_expand_blocks = grad_rows(
        (kept, width, width), (arrays, width + inner, width), order, frame_expand_stages, 5, 4, blocks
    )
    chain.leave(*frame_expand_blocks)

    packed_grad, codec_kept.other, projected_pair.other = chain.enter(
        packed_grad, codec_kept.other, projected_pair.other
    )
    chain.leave(packed_grad)
    contract_sum.arrive(chain)
    expand_sum.arrive(chain)
    packed_grad = lax.all_to_all(packed_grad, "seq", split_axis=0, concat_axis=0, tiled=True)
    contract_sum.step(chain)
    expand_sum.step(chain)
    frame_contract_sum = Reduce(contract_stages, chain.enter(*frame_contract_blocks))
    frame_expand_sum = Reduce(frame_expand_stages, chain.enter(*frame_expand_blocks))
    table_pair = Pair(chain.enter(table_in))
    project_stages = tuple("yxnf")
    arrays = chain.enter(*codec_kept.both())
    blocks = grad_rows(
        (arrays, 0, width), (projected_pair.both(), 0, 3 * width), order, project_stages, 4, 0
    )
    project_blocks = grad_rows(
        (arrays, width, width), (arrays, 2 * width, width), order, project_stages, 4, 3, blocks
    )
    chain.leave(*project_blocks)
    table_stages = tuple("xynf")
    table_blocks = grad_table(
        jnp.concatenate(codes_pair.both(), axis=1),
        chain.enter(*table_pair.both()),
        order,
        table_stages,
        codebooks.shape[0],
        2,
        0,
    )
    chain.leave(*table_blocks)
    output = codec_result(codec_mixed, chain.enter(codec_activated), live, codec_contract_all)
    chain.leave(output)
    output = jnp.transpose(output, (1, 0, 2)).reshape(row_count, frames_dev, positions, width)

    packed_grad, contract_sum.coming, expand_sum.coming, frame_contract_sum.coming = chain.enter(
        packed_grad, contract_sum.coming, expand_sum.coming, frame_contract_sum.coming
    )
    packed_grad, frame_expand_sum.coming = chain.enter(packed_grad, frame_expand_sum.coming)
    chain.leave(packed_grad)
    frame_contract_sum.step(chain)
    frame_expand_sum.step(chain)
    frame_projected_grad, frames_grad, frame_prenorm_grad = frame_front_grads(
        chain.enter(packed_grad), hidden, gains[0], frame_mixed_grad, frame_project_all
    )
    chain.leave(frames_grad)
    frame_projected_pair = Pair(frame_projected_grad)
    gain_pair = Pair(
        jnp.concatenate(
            [frame_prenorm_grad, frame_postnorm_grad, codec_prenorm_grad, codec_postnorm_grad]
        )
    )
    frame_projected_pair.other, gain_pair.other = chain.enter(
        frame_projected_pair.other, gain_pair.other
    )
    chain.leave(gain_pair.other)
    blocks = grad_rows(
        (kept, 0, width),
        (chain.enter(*frame_projected_pair.both()), 0, 3 * width),
        order,
        table_stages,
        3,
        0,
    )
    chain.leave(*blocks)
    riders = gain_pair.own + gain_pair.other
    frame_project_sum = Reduce(table_stages, blocks, chain.enter(riders))
    project_sum = Reduce(project_stages, chain.enter(*project_blocks))
    contract_sum.step(chain)
    expand_sum.step(chain)
    frame_contract_sum.step(chain)
    frame_expand_sum.step(chain)
    table_sum = Reduce(table_stages, chain.enter(*table_blocks))
    take_first = finish([contract_sum, expand_sum], chain)
    frame_project_sum.step(chain)
    take_second = finish([frame_contract_sum, frame_expand_sum], chain)
    project_sum.step(chain)
    table_sum.step(chain)
    frame_project_sum.step(chain)
    project_sum.step(chain)
    table_sum.step(chain)
    take_third = finish([frame_project_sum], chain)
    take_fourth = finish([project_sum, table_sum], chain)
    take_first()
    take_second()
    take_third()
    take_fourth()

    height = frame_project.shape[0]
    project_units = project_sum.result()
    frame_expand_units = frame_expand_sum.result()
    gain_sums = frame_project_sum.riders
    return (
        output,
        frames_grad.reshape(row_count, frames_dev, width),
        rows_from_units(table_sum.result(), codebooks.shape[0]),
        gain_sums[0],
        rows_from_units(frame_project_sum.result(), height),
        rows_from_units(frame_expand_units[4:], height),
        gain_sums[1],
        rows_from_units(frame_expand_units[:4], height),
        columns_from_units(frame_contract_sum.result()),
        gain_sums[2],
        rows_from_units(project_units[:3], height),
        rows_from_units(project_units[3:], height),
        gain_sums[3],
        rows_from_units(expand_sum.result(), height),
        columns_from_units(contract_sum.result()),
    )


def solution(mesh):
    placed = (
        P("mp", "seq", None),
        P("mp", "seq"),
        P("mp", "seq"),
        P(None, "mp", "seq"),
        P("mp", None),
        P("mp"),
        P("mp", None),
        P("mp", None),
        P("mp"),
        P("mp", None),
        P("mp", None),
        P("mp"),
        P("mp", None),
        P("mp", None),
        P("mp"),
        P("mp", None),
        P("mp", None),
        P("mp", "seq", None, None),
    )
    small = mesh.shape["seq"] == 8 and mesh.shape["mp"] == 4
    return jax.shard_map(
        shards if small else shards_general,
        mesh=mesh,
        in_specs=placed,
        out_specs=(
            P("mp", "seq", None, None),
            P("mp", "seq", None),
            P("mp", "seq"),
            P(),
            P("mp", "seq"),
            P("mp", "seq"),
            P(),
            P("mp", "seq"),
            P("mp", "seq"),
            P(),
            P("mp", "seq"),
            P("mp", "seq"),
            P(),
            P("mp", "seq"),
            P("mp", "seq"),
        ),
        check_vma=False,
    )
```

```python
import functools

import jax
import jax.numpy as jnp
from jax import lax
from jax.experimental import pallas as pl
from jax.experimental.pallas import tpu as pltpu
from jax.sharding import PartitionSpec as P

HEADS = 16
HEAD = 64
CODES = 1024


EPSILON = 1e-05
MASKED = -1e30
FACTOR = HEAD ** (-0.5)

BF = jnp.bfloat16
F32 = jnp.float32


def rms_scale(values, gain_vec):
    return (
        values * lax.rsqrt(jnp.mean(values * values, axis=-1, keepdims=True) + EPSILON) * gain_vec
    )


def matmul(former, latter):
    return jnp.dot(former, latter, preferred_element_type=F32)


def inner_left(former, latter):
    return lax.dot_general(former, latter, (((0,), (0,)), ((), ())), preferred_element_type=F32)


def inner_right(former, latter):
    return lax.dot_general(former, latter, (((1,), (1,)), ((), ())), preferred_element_type=F32)


def split_heads(values):
    return values.reshape(values.shape[:-1] + (-1, HEAD))


def swap(values, axis, bit):
    return lax.ppermute(values, axis, [(i, i ^ bit) for i in range(lax.axis_size(axis))])


def pick(values, index, axis):
    return lax.dynamic_index_in_dim(values, index, axis, keepdims=False)


class Place:
    def __init__(self):
        self.seq_count = lax.axis_size("seq")
        self.mp_count = lax.axis_size("mp")
        self.seq = lax.axis_index("seq")
        self.mp = lax.axis_index("mp")
        self.seq_low = self.seq % 2


def gather_weight(shard, place):
    height, breadth = shard.shape
    half = height // 2
    mine = lax.dynamic_slice(shard, (place.seq_low * half, 0), (half, breadth))
    first = swap(mine, "mp", 2)
    second = swap(first, "seq", 1)
    near_other = swap(shard, "mp", 1)
    far = jnp.zeros((height, breadth), shard.dtype)
    far = lax.dynamic_update_slice(far, first, (place.seq_low * half, 0))
    far = lax.dynamic_update_slice(far, second, ((1 - place.seq_low) * half, 0))
    far_other = swap(far, "mp", 1)
    whole = jnp.zeros((height * place.mp_count, breadth), shard.dtype)
    for flip, piece in ((0, shard), (1, near_other), (2, far), (3, far_other)):
        whole = lax.dynamic_update_slice(whole, piece, ((place.mp ^ flip) * height, 0))
    return whole


def line_scatter(blocks, place):
    count = place.seq_count // 2
    position = place.seq // 2
    size = 2 * count
    state = blocks
    up_in = down_in = None
    for step in range(1, count):
        up_index = jnp.clip(count - step + position, 0, count - 1)
        down_index = jnp.clip(step - 1 - (count - 1 - position), 0, count - 1)
        up_perm = [(i, i + 2) for i in range(size - 2) if i // 2 < step]
        down_perm = [(i, i - 2) for i in range(2, size) if (count - 1 - i // 2) < step]
        up_out = pick(blocks, up_index, 1)
        down_out = pick(blocks, down_index, 1)
        if up_in is not None:
            up_out = up_out + up_in
            down_out = down_out + down_in
        up_in = lax.ppermute(up_out, "seq", up_perm)
        down_in = lax.ppermute(down_out, "seq", down_perm)
    own = pick(blocks, position, 1).astype(F32)
    return own + up_in.astype(F32) + down_in.astype(F32)


def weight_grad(former, latter, place, seq_first):
    height = former.shape[1] // place.mp_count
    rows = former.shape[0]
    breadth = latter.shape[1] // place.seq_count
    low = place.seq_low
    view = latter.reshape(rows, place.seq_count // 2, 2, breadth)
    half = breadth * (place.seq_count // 2)
    give = pick(view, 1 - low, 2).reshape(rows, half)
    keep = pick(view, low, 2).reshape(rows, half)
    both = jnp.concatenate([give, keep], axis=1)

    def columns(flip):
        return lax.dynamic_slice(former, (0, (place.mp ^ flip) * height), (rows, height))

    own, other, far, far_other = (columns(flip) for flip in (0, 1, 2, 3))
    part = inner_left(jnp.concatenate([far_other, other], axis=1), both).astype(BF)
    part = swap(part, "mp", 1).astype(F32)
    if seq_first:
        send = inner_left(jnp.concatenate([far, own], axis=1), give) + part[:, :half]
        low_in = swap(send.astype(BF), "seq", 1).astype(F32)
        send = inner_left(far, keep) + part[:height, half:] + low_in[:height]
        far_in = swap(send.astype(BF), "mp", 2).astype(F32)
        total = inner_left(own, keep) + part[height:, half:] + low_in[height:] + far_in
    else:
        send = inner_left(far, both) + part[:height]
        far_in = swap(send.astype(BF), "mp", 2).astype(F32)
        send = inner_left(own, give) + part[height:, :half] + far_in[:, :half]
        low_in = swap(send.astype(BF), "seq", 1).astype(F32)
        total = inner_left(own, keep) + part[height:, half:] + far_in[:, half:] + low_in
    return total.astype(BF).reshape(height, place.seq_count // 2, breadth)


def finish_grads(partials, place):
    sizes = [part.shape[2] for part in partials]
    total = line_scatter(jnp.concatenate(partials, axis=2), place)
    pieces, start = [], 0
    for size in sizes:
        pieces.append(total[:, start : start + size])
        start += size
    return pieces


def sum_everywhere(values, place):
    for axis, count in (("mp", place.mp_count), ("seq", place.seq_count)):
        bit = 1
        while bit < count:
            values = values + swap(values, axis, bit)
            bit *= 2
    return values


def front_pass(hidden, weights):
    normed = rms_scale(hidden, weights[0].astype(F32)).astype(BF)
    projected = matmul(normed, weights[1]).astype(BF)
    return (normed, projected)


def rear_pass(hidden, attended, weights):
    mixed_sum = hidden + matmul(attended, weights[2])
    normed_two = rms_scale(mixed_sum, weights[3].astype(F32)).astype(BF)
    expanded = matmul(normed_two, weights[4])
    activated = jax.nn.gelu(expanded).astype(BF)
    result = mixed_sum + matmul(activated, weights[5])
    return (result, (mixed_sum, normed_two, expanded, activated))


def rear_grads(result_grad, saved_state, weights):
    mixed_sum, normed_two, expanded, activated = saved_state
    contract_input = result_grad.astype(BF)
    active_grad = inner_right(contract_input, weights[5])
    expand_input = jax.vjp(jax.nn.gelu, expanded)[1](active_grad)[0].astype(BF)
    normed_grad = inner_right(expand_input, weights[4])
    mixed_part, postnorm_grad = jax.vjp(rms_scale, mixed_sum, weights[3].astype(F32))[1](
        normed_grad
    )
    mixed_grad = result_grad + mixed_part
    output_input = mixed_grad.astype(BF)
    attended_grad = inner_right(output_input, weights[2]).astype(BF)
    return (mixed_grad, attended_grad, postnorm_grad, contract_input, expand_input, output_input)


def front_grads(hidden, projected_grad, mixed_grad, weights):
    normed_grad = inner_right(projected_grad, weights[1])
    hidden_part, prenorm_grad = jax.vjp(rms_scale, hidden, weights[0].astype(F32))[1](normed_grad)
    return (mixed_grad + hidden_part, prenorm_grad)


def portions_of(queries, keys, allowed):
    scores = jnp.einsum("ihd,jhd->hij", queries, keys, preferred_element_type=F32) * FACTOR
    return jax.nn.softmax(jnp.where(allowed[None], scores, MASKED), axis=-1)


def attend(queries, keys, values, allowed):
    portions = portions_of(queries, keys, allowed)
    return jnp.einsum(
        "hij,jhd->ihd", portions.astype(BF), values, preferred_element_type=F32
    ).astype(BF)


def attend_grads(queries, keys, values, allowed, out_grad):
    portions = portions_of(queries, keys, allowed)
    portion_grad = jnp.einsum("ihd,jhd->hij", out_grad, values, preferred_element_type=F32)
    score_grad = (
        portions * (portion_grad - jnp.sum(portions * portion_grad, axis=-1, keepdims=True))
    ).astype(BF)
    query_grad = (
        jnp.einsum("hij,jhd->ihd", score_grad, keys, preferred_element_type=F32) * FACTOR
    )
    key_grad = (
        jnp.einsum("hij,ihd->jhd", score_grad, queries, preferred_element_type=F32) * FACTOR
    )
    value_grad = jnp.einsum("hij,ihd->jhd", portions.astype(BF), out_grad, preferred_element_type=F32)
    return query_grad, key_grad, value_grad


def to_heads(values, place):
    rows, own, parts, width = values.shape
    count = place.seq_count
    view = values.reshape(rows, own, parts, count, width // count)
    moved = lax.all_to_all(
        jnp.transpose(view, (3, 0, 1, 2, 4)), "seq", split_axis=0, concat_axis=0, tiled=True
    )
    return jnp.transpose(moved, (1, 0, 2, 3, 4)).reshape(rows, count * own, parts, width // count)


def to_frames(values, place):
    rows, total, parts, width = values.shape
    count = place.seq_count
    view = values.reshape(rows, count, total // count, parts, width)
    moved = lax.all_to_all(
        jnp.transpose(view, (1, 0, 2, 3, 4)), "seq", split_axis=0, concat_axis=0, tiled=True
    )
    return jnp.transpose(moved, (1, 2, 3, 0, 4)).reshape(
        rows, total // count, parts, count * width
    )


def allowed_of(query_seg, key_seg, query_pos, key_pos):
    return (query_seg[:, None] == key_seg[None, :]) & (key_pos[None, :] <= query_pos[:, None])


def frame_attention(projected, segments, place):
    rows, own, triple = projected.shape
    width = triple // 3
    parts = projected.reshape(rows, own, 3, width)
    every_segment = lax.all_gather(segments, "seq", axis=1, tiled=True)
    every_pos = jnp.arange(own * place.seq_count)
    if HEADS % place.seq_count == 0:
        packed = to_heads(parts, place)
        sets = [split_heads(packed[:, :, part]) for part in range(3)]

        def one_row(items):
            queries, keys, values, segs = items
            return attend(queries, keys, values, allowed_of(segs, segs, every_pos, every_pos))

        attended = lax.map(one_row, (*sets, every_segment))
        attended = to_frames(attended.reshape(rows, own * place.seq_count, 1, -1), place)

        def backward(out_grad):
            grads = to_heads(out_grad.reshape(rows, own, 1, width), place)[:, :, 0]

            def one_row(items):
                queries, keys, values, segs, grad = items
                return attend_grads(
                    queries, keys, values, allowed_of(segs, segs, every_pos, every_pos), grad
                )

            found = lax.map(one_row, (*sets, every_segment, split_heads(grads)))
            packed_grad = jnp.stack(
                [grad.reshape(rows, own * place.seq_count, -1) for grad in found], axis=2
            ).astype(BF)
            return to_frames(packed_grad, place).reshape(rows, own, triple)

        return attended.reshape(rows, own, width), backward

    keys = lax.all_gather(parts[:, :, 1], "seq", axis=1, tiled=True)
    values = lax.all_gather(parts[:, :, 2], "seq", axis=1, tiled=True)
    sets = (split_heads(parts[:, :, 0]), split_heads(keys), split_heads(values))
    own_pos = place.seq * own + jnp.arange(own)

    def one_row(items):
        row_q, row_k, row_v, own_segs, segs = items
        return attend(row_q, row_k, row_v, allowed_of(own_segs, segs, own_pos, every_pos))

    attended = lax.map(one_row, (*sets, segments, every_segment)).reshape(rows, own, width)

    def backward(out_grad):
        def one_row(items):
            row_q, row_k, row_v, own_segs, segs, grad = items
            allowed = allowed_of(own_segs, segs, own_pos, every_pos)
            return attend_grads(row_q, row_k, row_v, allowed, grad)

        query_grad, key_grad, value_grad = lax.map(
            one_row, (*sets, segments, every_segment, split_heads(out_grad))
        )
        both = jnp.stack([key_grad.reshape(rows, -1, width), value_grad.reshape(rows, -1, width)], 2)
        both = lax.psum_scatter(both, "seq", scatter_dimension=1, tiled=True)
        parts_grad = [query_grad.reshape(rows, own, width), both[:, :, 0], both[:, :, 1]]
        return jnp.concatenate(parts_grad, axis=-1).astype(BF)

    return attended, backward


def head_sums(values, marks):
    return jnp.dot(values, marks, precision=lax.Precision.HIGHEST, preferred_element_type=F32)


def head_spread(values, marks):
    return lax.dot_general(
        values.astype(BF), marks.astype(BF), (((1,), (1,)), ((), ())), preferred_element_type=F32
    )


def codec_softmax(queries, keys, marks):
    result = []
    for later in range(len(queries)):
        scores = [
            head_sums(queries[later].astype(F32) * keys[earlier].astype(F32), marks) * FACTOR
            for earlier in range(later + 1)
        ]
        top = scores[0]
        for score in scores[1:]:
            top = jnp.maximum(top, score)
        powers = [jnp.exp(score - top) for score in scores]
        total = sum(powers)
        result.append([power / total for power in powers])
    return result


def codec_attend(soft, values, marks):
    result = []
    for row in soft:
        total = 0.0
        for earlier, portion in enumerate(row):
            total = total + head_spread(portion, marks) * values[earlier].astype(F32)
        result.append(total.astype(BF))
    return result


def codec_attend_grads(soft, queries, keys, values, grads, marks):
    count = len(queries)
    query_grad = []
    key_grad = [0.0] * count
    value_grad = [0.0] * count
    for later in range(count):
        grad = grads[later].astype(F32)
        portion_grads = [
            head_sums(grad * values[earlier].astype(F32), marks) for earlier in range(later + 1)
        ]
        mean = sum(soft[later][i] * portion_grads[i] for i in range(later + 1))
        total = 0.0
        for earlier in range(later + 1):
            score_grad = soft[later][earlier] * (portion_grads[earlier] - mean)
            wide = head_spread(score_grad, marks)
            total = total + wide * keys[earlier].astype(F32)
            key_grad[earlier] = key_grad[earlier] + wide * queries[later].astype(F32)
            value_grad[earlier] = value_grad[earlier] + head_spread(soft[later][earlier], marks) * grad
        query_grad.append(total * FACTOR)
    return jnp.concatenate(
        [
            jnp.concatenate(
                [query_grad[t], key_grad[t] * FACTOR, value_grad[t]], axis=-1
            ).astype(BF)
            for t in range(count)
        ],
        axis=0,
    )


LANES = 128
TILE = 256
VMEM_LIMIT = 48 * 1024 * 1024
HINT = pl.CostEstimate(flops=1, bytes_accessed=1, transcendentals=0)


def whole_block(shape):
    return pl.BlockSpec(shape, lambda *_: (0,) * len(shape))


def causal_tiles(length):
    tile = min(TILE, length)
    return [(start, tile, start + tile) for start in range(0, length, tile)]


def head_masks(dtype):
    lane = lax.broadcasted_iota(jnp.int32, (1, LANES), 1)
    return [((lane // HEAD) == head).astype(dtype) for head in range(LANES // HEAD)]


def frame_attend_kernel(packed_ref, seg_col_ref, seg_row_ref, out_ref):
    chunks, _, own, _ = packed_ref.shape
    length = chunks * own
    packed = packed_ref[...].reshape(length, 3 * LANES)
    queries, keys, values = (packed[:, LANES * i : LANES * (i + 1)] for i in range(3))
    masks = head_masks(BF)
    lane = lax.broadcasted_iota(jnp.int32, (1, LANES), 1)
    for start, tile, end in causal_tiles(length):
        query_pos = start + lax.broadcasted_iota(jnp.int32, (tile, end), 0)
        key_pos = lax.broadcasted_iota(jnp.int32, (tile, end), 1)
        allowed = (seg_col_ref[0, start:end] == seg_row_ref[0, :, :end]) & (key_pos <= query_pos)
        result = jnp.zeros((tile, LANES), F32)
        for head, mask in enumerate(masks):
            scores = inner_right(queries[start:end] * mask, keys[:end]) * FACTOR
            scores = jnp.where(allowed, scores, MASKED)
            powers = jnp.exp(scores - jnp.max(scores, axis=1, keepdims=True))
            portions = powers / jnp.sum(powers, axis=1, keepdims=True)
            found = matmul(portions.astype(BF), values[:end])
            result = jnp.where(lane // HEAD == head, found, result)
        out_ref[start // own : end // own, 0] = result.astype(BF).reshape(tile // own, own, LANES)


def frame_attend_grads_kernel(packed_ref, grad_ref, seg_col_ref, seg_row_ref, out_ref, key_sum, value_sum):
    chunks, _, own, _ = packed_ref.shape
    length = chunks * own
    packed = packed_ref[...].reshape(length, 3 * LANES)
    queries, keys, values = (packed[:, LANES * i : LANES * (i + 1)] for i in range(3))
    grads = grad_ref[...].reshape(length, LANES)
    masks = head_masks(BF)
    lane = lax.broadcasted_iota(jnp.int32, (1, LANES), 1)
    key_sum[...] = jnp.zeros_like(key_sum)
    value_sum[...] = jnp.zeros_like(value_sum)
    for start, tile, end in causal_tiles(length):
        key_pos = lax.broadcasted_iota(jnp.int32, (end, tile), 0)
        query_pos = start + lax.broadcasted_iota(jnp.int32, (end, tile), 1)
        allowed = (seg_col_ref[0, :end] == seg_row_ref[0, :, start:end]) & (key_pos <= query_pos)
        query_grad = jnp.zeros((tile, LANES), F32)
        for head, mask in enumerate(masks):
            query = queries[start:end] * mask
            grad = grads[start:end] * mask
            scores = inner_right(keys[:end], query) * FACTOR
            scores = jnp.where(allowed, scores, MASKED)
            powers = jnp.exp(scores - jnp.max(scores, axis=0, keepdims=True))
            portions = powers / jnp.sum(powers, axis=0, keepdims=True)
            portion_grad = inner_right(values[:end], grad)
            mean = jnp.sum(portions * portion_grad, axis=0, keepdims=True)
            score_grad = (portions * (portion_grad - mean)).astype(BF)
            key_sum[:end] += matmul(score_grad, query)
            value_sum[:end] += matmul(portions.astype(BF), grad)
            found = inner_left(score_grad, keys[:end])
            query_grad = jnp.where(lane // HEAD == head, found, query_grad)
        out_ref[start // own : end // own, 0, :, :LANES] = (
            (query_grad * FACTOR).astype(BF).reshape(tile // own, own, LANES)
        )
    out_ref[:, 0, :, LANES : 2 * LANES] = (key_sum[...] * FACTOR).astype(BF).reshape(chunks, own, LANES)
    out_ref[:, 0, :, 2 * LANES :] = value_sum[...].astype(BF).reshape(chunks, own, LANES)


def row_spec(chunks, own, breadth):
    return pl.BlockSpec((chunks, 1, own, breadth), lambda row: (0, row, 0, 0))


def segment_specs(length):
    return [
        pl.BlockSpec((1, length, 1), lambda row: (row, 0, 0)),
        pl.BlockSpec((1, 1, length), lambda row: (row, 0, 0)),
    ]


def frame_attend_call(packed, segments):
    chunks, rows, own, _ = packed.shape
    length = chunks * own
    return pl.pallas_call(
        frame_attend_kernel,
        grid=(rows,),
        in_specs=[row_spec(chunks, own, 3 * LANES), *segment_specs(length)],
        out_specs=row_spec(chunks, own, LANES),
        out_shape=jax.ShapeDtypeStruct((chunks, rows, own, LANES), BF),
        compiler_params=pltpu.CompilerParams(vmem_limit_bytes=VMEM_LIMIT),
        cost_estimate=HINT,
        name="frame_attend",
    )(packed, segments[:, :, None], segments[:, None, :])


def frame_attend_grads_call(packed, grads, segments):
    chunks, rows, own, _ = packed.shape
    length = chunks * own
    return pl.pallas_call(
        frame_attend_grads_kernel,
        grid=(rows,),
        in_specs=[
            row_spec(chunks, own, 3 * LANES),
            row_spec(chunks, own, LANES),
            *segment_specs(length),
        ],
        out_specs=row_spec(chunks, own, 3 * LANES),
        out_shape=jax.ShapeDtypeStruct((chunks, rows, own, 3 * LANES), BF),
        scratch_shapes=[pltpu.VMEM((length, LANES), F32), pltpu.VMEM((length, LANES), F32)],
        compiler_params=pltpu.CompilerParams(vmem_limit_bytes=VMEM_LIMIT),
        cost_estimate=HINT,
        name="frame_attend_grads",
    )(packed, grads, segments[:, :, None], segments[:, None, :])


def position_pairs(positions):
    return [(later, earlier) for later in range(1, positions) for earlier in range(later + 1)]


def codec_sums(products, marks):
    stacked = jnp.concatenate(products, axis=0)
    high = stacked.astype(BF)
    low = (stacked - high.astype(F32)).astype(BF)
    total = matmul(high, marks) + matmul(low, marks)
    size = products[0].shape[0]
    return [total[size * i : size * (i + 1)] for i in range(len(products))]


def codec_spread(portions, marks):
    stacked = jnp.concatenate([portion.astype(BF) for portion in portions], axis=0)
    total = inner_right(stacked, marks)
    size = portions[0].shape[0]
    return [total[size * i : size * (i + 1)] for i in range(len(portions))]


def codec_portions(queries, keys, marks, pairs):
    scores = codec_sums(
        [queries[later].astype(F32) * keys[earlier].astype(F32) for later, earlier in pairs], marks
    )
    scores = dict(zip(pairs, [score * FACTOR for score in scores]))
    portions = {}
    for later in range(1, len(queries)):
        row = [scores[later, earlier] for earlier in range(later + 1)]
        top = functools.reduce(jnp.maximum, row)
        powers = [jnp.exp(score - top) for score in row]
        total = functools.reduce(jnp.add, powers)
        for earlier in range(later + 1):
            portions[later, earlier] = powers[earlier] / total
    return portions


def codec_parts(packed_ref, width):
    positions = packed_ref.shape[0]
    return [
        [packed_ref[t, :, width * part : width * (part + 1)] for t in range(positions)]
        for part in range(3)
    ]


def codec_attend_kernel(packed_ref, normed_ref, marks_ref, out_ref):
    positions, _, width = normed_ref.shape
    out_ref[:, :, :width] = normed_ref[...]
    queries, keys, values = codec_parts(packed_ref, width)
    marks = marks_ref[...]
    pairs = position_pairs(positions)
    portions = codec_portions(queries, keys, marks, pairs)
    wide = dict(zip(pairs, codec_spread([portions[pair] for pair in pairs], marks)))
    out_ref[0, :, width:] = values[0]
    for later in range(1, positions):
        terms = [wide[later, e] * values[e].astype(F32) for e in range(later + 1)]
        out_ref[later, :, width:] = functools.reduce(jnp.add, terms).astype(BF)


def codec_attend_grads_kernel(packed_ref, grad_ref, marks_ref, out_ref):
    positions, _, width = grad_ref.shape
    queries, keys, values = codec_parts(packed_ref, width)
    marks = marks_ref[...]
    pairs = position_pairs(positions)
    portions = codec_portions(queries, keys, marks, pairs)
    grads = [grad_ref[t].astype(F32) for t in range(positions)]
    portion_grads = dict(
        zip(
            pairs,
            codec_sums([grads[later] * values[earlier].astype(F32) for later, earlier in pairs], marks),
        )
    )
    score_grads = {}
    for later in range(1, positions):
        mean = functools.reduce(
            jnp.add, [portions[later, e] * portion_grads[later, e] for e in range(later + 1)]
        )
        for e in range(later + 1):
            score_grads[later, e] = portions[later, e] * (portion_grads[later, e] - mean)
    wide = dict(zip(pairs, codec_spread([portions[pair] for pair in pairs], marks)))
    wide_grads = dict(zip(pairs, codec_spread([score_grads[pair] for pair in pairs], marks)))
    zero = jnp.zeros_like(grads[0])
    for t in range(positions):
        query_grad = key_grad = zero
        value_grad = grads[0] if t == 0 else zero
        for later, earlier in pairs:
            if later == t:
                query_grad = query_grad + wide_grads[later, earlier] * keys[earlier].astype(F32)
            if earlier == t:
                key_grad = key_grad + wide_grads[later, earlier] * queries[later].astype(F32)
                value_grad = value_grad + wide[later, earlier] * grads[later]
        out_ref[t, :, :width] = (query_grad * FACTOR).astype(BF)
        out_ref[t, :, width : 2 * width] = (key_grad * FACTOR).astype(BF)
        out_ref[t, :, 2 * width :] = value_grad.astype(BF)


def codec_tile(frame_total):
    return 64 if frame_total % 64 == 0 else frame_total


def codec_spec(positions, tile, breadth):
    return pl.BlockSpec((positions, tile, breadth), lambda i: (0, i, 0))


def head_marks(width):
    return (
        jnp.arange(width)[:, None] // HEAD == jnp.arange(LANES)[None, :]
    ).astype(BF)


def codec_attend_call(packed, normed):
    positions, total, triple = packed.shape
    width = triple // 3
    tile = codec_tile(total)
    return pl.pallas_call(
        codec_attend_kernel,
        grid=(total // tile,),
        in_specs=[
            codec_spec(positions, tile, triple),
            codec_spec(positions, tile, width),
            whole_block((width, LANES)),
        ],
        out_specs=codec_spec(positions, tile, 2 * width),
        out_shape=jax.ShapeDtypeStruct((positions, total, 2 * width), BF),
        compiler_params=pltpu.CompilerParams(vmem_limit_bytes=VMEM_LIMIT),
        cost_estimate=HINT,
        name="codec_attend",
    )(packed, normed.reshape(positions, total, width), head_marks(width))


def codec_attend_grads_call(packed, grads):
    positions, total, triple = packed.shape
    width = triple // 3
    tile = codec_tile(total)
    return pl.pallas_call(
        codec_attend_grads_kernel,
        grid=(total // tile,),
        in_specs=[
            codec_spec(positions, tile, triple),
            codec_spec(positions, tile, width),
            whole_block((width, LANES)),
        ],
        out_specs=codec_spec(positions, tile, triple),
        out_shape=jax.ShapeDtypeStruct((positions, total, triple), BF),
        compiler_params=pltpu.CompilerParams(vmem_limit_bytes=VMEM_LIMIT),
        cost_estimate=HINT,
        name="codec_attend_grads",
    )(packed, grads, head_marks(width))


BITS = {"y": ("mp", 2), "x": ("seq", 1), "n": ("seq", 2), "f": ("seq", 4)}


def grad_order(place):
    flips = []
    for bits in ((1, 2, 4), (2, 1, 4), (1, 2, 4)):
        for step in range(8):
            flips.append(sum(bit for at, bit in enumerate(bits) if not (step >> (2 - at)) & 1))
    return jnp.stack(
        [place.mp ^ 2, place.mp] + [place.seq ^ flip for flip in flips] + [place.seq]
    ).astype(jnp.int32)


STEPS = {"y": (2, "xnf"), "n": (10, "nxf"), "x": (18, "xnf")}
OWN_SEQ = 26


def keep_flags(order_ref, seq):
    change = order_ref[OWN_SEQ] ^ seq
    return {"x": 1 - (change & 1), "n": 1 - ((change >> 1) & 1), "f": 1 - ((change >> 2) & 1)}


def grad_rows_kernel(stages, wide, order_ref, far_own, far_rec, own_own, own_rec, latter_own, latter_rec, *refs):
    send_ref, keep_ref, turned = refs[-3:]
    rows = latter_own.shape[0]
    height = far_own.shape[1]

    @pl.when(pl.program_id(0) == 0)
    def _():
        for at, (own, rec) in enumerate(((far_own, far_rec), (own_own, own_rec))):
            turned[height * at : height * (at + 1), :rows] = own[...].T
            turned[height * at : height * (at + 1), rows:] = rec[...].T

    total = matmul(turned[:, :rows], latter_own[...]) + matmul(turned[:, rows:], latter_rec[...])
    store = grad_store_wide if wide else grad_store
    store(stages, order_ref, total.astype(BF), height, send_ref, keep_ref)


def grad_store_wide(stages, order_ref, total, height, send_ref, keep_ref):
    units = height // TILE
    chunks = total.shape[1] // 8 // LANES
    for seq in range(8):
        flags = keep_flags(order_ref, seq)
        for chunk in range(chunks):
            first = (seq * chunks + chunk) * LANES
            for unit in range(units):
                at = chunk * units + unit
                for kept in range(2):
                    start = height * kept + unit * TILE
                    value = total[start : start + TILE, first : first + LANES]
                    spot = {**flags, "y": kept}
                    where = tuple(spot[stage] for stage in stages[1:])
                    for target, when in ((send_ref, 0), (keep_ref, 1)):

                        @pl.when(spot[stages[0]] == when)
                        def _(target=target, where=where, at=at, value=value):
                            target[(*where, at)] = value


def grad_store(stages, order_ref, total, height, send_ref, keep_ref):
    chunks = total.shape[1] // LANES
    for chunk in range(chunks):
        value = total[:, chunk * LANES : (chunk + 1) * LANES]
        given, kept = value[:height], value[height:]
        if stages[0] == "y":
            send_ref[0, 0, 0, chunk] = given
            keep_ref[0, 0, 0, chunk] = kept
        else:
            spots = [tuple(side if stage == "y" else 0 for stage in stages[1:]) for side in range(2)]
            for target, when in ((send_ref, pl.program_id(0) < 4), (keep_ref, pl.program_id(0) >= 4)):

                @pl.when(when)
                def _(target=target, given=given, kept=kept, chunk=chunk):
                    target[(*spots[0], chunk)] = given
                    target[(*spots[1], chunk)] = kept


def grad_buffers(units):
    return [jax.ShapeDtypeStruct((2, 2, 2, units, TILE, LANES), BF)] * 2


def grad_call(kernel, order, arrays, in_specs, out_specs, units, into, steps, scratch, flops, name):
    aliases = {}
    moved = 2 * sum(array.size for array in arrays)
    if into is not None:
        aliases = {len(arrays) + 1: 0, len(arrays) + 2: 1}
        in_specs = in_specs + [pl.BlockSpec(memory_space=pl.ANY)] * 2
        arrays = arrays + list(into)
    return pl.pallas_call(
        kernel,
        grid_spec=pltpu.PrefetchScalarGridSpec(
            num_scalar_prefetch=1,
            grid=(steps,),
            in_specs=in_specs,
            out_specs=out_specs,
            scratch_shapes=[scratch],
        ),
        out_shape=grad_buffers(units),
        input_output_aliases=aliases,
        compiler_params=pltpu.CompilerParams(vmem_limit_bytes=VMEM_LIMIT),
        cost_estimate=HINT,
        name=name,
    )(order, *arrays)


def grad_rows(former, latter, order, stages, units, offset, into=None):
    former, skip, height = former
    latter, latter_skip, breadth = latter
    rows = latter[0].shape[0]
    height = height // 4
    skip = skip // height
    wide = breadth // 8 == LANES
    chunks = breadth // 8 // LANES
    steps = 1 if wide else 8
    arrays = [former[0], former[1], former[0], former[1], latter[0], latter[1]]
    former_specs = [
        pl.BlockSpec((rows, height), lambda j, t, at=at: (0, skip + t[at]), pipeline_mode=pl.Buffered(1))
        for at in (0, 0, 1, 1)
    ]
    if wide:
        latter_specs = [
            pl.BlockSpec((rows, breadth), lambda j, t: (0, latter_skip // breadth))
        ] * 2
        block = (2, 2, 2, 1, TILE, LANES)
        out_specs = [pl.BlockSpec(block, lambda j, t: (0, 0, 0, offset, 0, 0))] * 2
    else:
        base = offset // chunks
        table, names = STEPS[stages[0]]
        bits = {name: 2 - at for at, name in enumerate(names)}
        if stages[0] == "y":
            block = (1, 1, 1, chunks, TILE, LANES)

            def where(j):
                return tuple((j >> bits[stage]) & 1 for stage in stages[1:]) + (base, 0, 0)

            out_specs = [pl.BlockSpec(block, lambda j, t: where(j))] * 2
        else:
            block = tuple(2 if stage == "y" else 1 for stage in stages[1:]) + (chunks, TILE, LANES)

            def where(j):
                return tuple(
                    0 if stage == "y" else (j >> bits[stage]) & 1 for stage in stages[1:]
                ) + (base, 0, 0)

            out_specs = [
                pl.BlockSpec(block, lambda j, t: where(jnp.minimum(j, 3))),
                pl.BlockSpec(block, lambda j, t: where(jnp.maximum(j - 4, 0))),
            ]
        latter_specs = [
            pl.BlockSpec(
                (rows, breadth // 8),
                lambda j, t: (0, latter_skip // (breadth // 8) + t[table + j]),
            )
        ] * 2
    return grad_call(
        functools.partial(grad_rows_kernel, stages, wide),
        order,
        arrays,
        former_specs + latter_specs,
        out_specs,
        units,
        into,
        steps,
        pltpu.VMEM((2 * height, 2 * rows), BF),
        2 * 2 * rows * 2 * height * breadth,
        "grad_rows",
    )


def grad_columns_kernel(stages, order_ref, latter_own, latter_rec, former_own, former_rec, *refs):
    send_ref, keep_ref, turned = refs[-3:]
    rows = latter_own.shape[0]
    step = pl.program_id(0)

    @pl.when(step == 0)
    def _():
        turned[:, :rows] = latter_own[...].T
        turned[:, rows:] = latter_rec[...].T

    total = matmul(turned[:, :rows], former_own[...]) + matmul(turned[:, rows:], former_rec[...])
    total = total.astype(BF)
    chunks = total.shape[1] // LANES
    for target, when in ((send_ref, step < pl.num_programs(0) // 2), (keep_ref, step >= pl.num_programs(0) // 2)):

        @pl.when(when)
        def _(target=target):
            for seq in range(8):
                flags = keep_flags(order_ref, seq)
                where = tuple(flags[stage] for stage in stages[1:])
                for chunk in range(chunks):
                    half = (chunk % 2) * LANES
                    target[(*where, chunk // 2, slice(half, half + LANES))] = total[
                        seq * LANES : (seq + 1) * LANES, chunk * LANES : (chunk + 1) * LANES
                    ]


def grad_columns(former, latter, order, stages, units, offset, into=None):
    former, skip, height = former
    latter, latter_skip, breadth = latter
    rows = latter[0].shape[0]
    height = height // 4
    step = min(512, height)
    per = height // step
    block = (2, 2, 2, step // TILE, TILE, LANES)
    base = offset // (step // TILE)
    latter_specs = [
        pl.BlockSpec(
            (rows, breadth), lambda j, t: (0, latter_skip // breadth), pipeline_mode=pl.Buffered(1)
        )
    ] * 2
    former_specs = [
        pl.BlockSpec((rows, step), lambda j, t: (0, skip // step + t[j // per] * per + j % per))
    ] * 2
    out_specs = [
        pl.BlockSpec(block, lambda j, t: (0, 0, 0, base + jnp.minimum(j, per - 1), 0, 0)),
        pl.BlockSpec(block, lambda j, t: (0, 0, 0, base + jnp.maximum(j - per, 0), 0, 0)),
    ]
    return grad_call(
        functools.partial(grad_columns_kernel, stages),
        order,
        [latter[0], latter[1], former[0], former[1]],
        latter_specs + former_specs,
        out_specs,
        units,
        into,
        2 * per,
        pltpu.VMEM((breadth, 2 * rows), BF),
        2 * 2 * rows * 2 * height * breadth,
        "grad_columns",
    )


def grad_table_kernel(stages, height, order_ref, codes_ref, latter_own, latter_rec, *refs):
    send_ref, keep_ref, _ = refs[-3:]
    rows = latter_own.shape[0]
    parts = []
    for at in range(2):
        entry = order_ref[at] * height + lax.broadcasted_iota(jnp.int32, (height, 2 * rows), 0)
        parts.append((entry == codes_ref[...]).astype(F32).astype(BF))
    chosen = jnp.concatenate(parts, axis=0)
    total = matmul(chosen[:, :rows], latter_own[...]) + matmul(chosen[:, rows:], latter_rec[...])
    grad_store_wide(stages, order_ref, total.astype(BF), height, send_ref, keep_ref)


def grad_table(codes, latter, order, stages, height, units, offset, into=None):
    rows, breadth = latter[0].shape
    block = (2, 2, 2, height // TILE, TILE, LANES)
    base = offset // (height // TILE)
    return grad_call(
        functools.partial(grad_table_kernel, stages, height),
        order,
        [codes, latter[0], latter[1]],
        [whole_block(codes.shape), whole_block((rows, breadth)), whole_block((rows, breadth))],
        [pl.BlockSpec(block, lambda j, t: (0, 0, 0, base, 0, 0))] * 2,
        units,
        into,
        1,
        pltpu.VMEM((8, LANES), F32),
        2 * 2 * rows * 2 * height * breadth,
        "grad_table",
    )


def rows_from_units(units, height):
    tiles = height // TILE
    chunks = units.shape[0] // tiles
    return jnp.transpose(
        units.reshape(chunks, height, LANES), (1, 0, 2)
    ).reshape(height, chunks * LANES)


def columns_from_units(units):
    count = units.shape[0]
    return jnp.transpose(units.reshape(2 * count, LANES, LANES), (0, 2, 1)).reshape(count * TILE, LANES)


PACK = 1024


def pack_rows(members):
    return sum(member.shape[0] * (member.shape[1] // PACK) for member in members)


def pack_pieces(shapes):
    found, start = [], 0
    for at, (height, breadth) in enumerate(shapes):
        for column in range(breadth // PACK):
            found.append((at, column, height, start))
            start += height
    return found


def columns_of(column):
    return pl.ds(column * PACK, PACK)


def pack_kernel(place_ref, *refs):
    members, (pack_ref, quarter_ref, held, sems, out_sems) = refs[:-5], refs[-5:]
    rows = held.shape[0] // 4
    copies = []
    for number, (at, column, height, start) in enumerate(pack_pieces([m.shape for m in members])):
        copies.append(
            pltpu.make_async_copy(
                members[at].at[:, columns_of(column)], held.at[pl.ds(start, height)], sems.at[number]
            )
        )
    for copy in copies:
        copy.start()
    for copy in copies:
        copy.wait()
    mine = pl.ds(pl.multiple_of(place_ref[1] * rows, 16), rows)
    whole = pltpu.make_async_copy(held, pack_ref, out_sems.at[0])
    part = pltpu.make_async_copy(held.at[mine], quarter_ref, out_sems.at[1])
    part.start()
    whole.start()
    part.wait()
    whole.wait()


def pack_call(members, spots):
    rows = pack_rows(members)
    any_spec = pl.BlockSpec(memory_space=pl.ANY)
    count = len(pack_pieces([m.shape for m in members]))
    return pl.pallas_call(
        pack_kernel,
        in_specs=[pl.BlockSpec(memory_space=pltpu.SMEM)] + [any_spec] * len(members),
        out_specs=[any_spec] * 2,
        out_shape=[
            jax.ShapeDtypeStruct((rows, PACK), BF),
            jax.ShapeDtypeStruct((rows // 4, PACK), BF),
        ],
        scratch_shapes=[
            pltpu.VMEM((rows, PACK), BF),
            pltpu.SemaphoreType.DMA((count,)),
            pltpu.SemaphoreType.DMA((2,)),
        ],
        compiler_params=pltpu.CompilerParams(vmem_limit_bytes=VMEM_LIMIT),
        cost_estimate=HINT,
        name="pack_weights",
    )(spots, *members)


def far_kernel(parts, place_ref, *refs):
    pieces, (out_ref, held, sems, out_sem) = refs[:-4], refs[-4:]
    quarter = held.shape[0] // 4
    copies = []
    for number, (piece, (change, offset)) in enumerate(zip(pieces, parts)):
        start = (place_ref[1] ^ change) * quarter + offset
        copies.append(
            pltpu.make_async_copy(
                piece, held.at[pl.ds(pl.multiple_of(start, 16), piece.shape[0])], sems.at[number]
            )
        )
    for copy in copies:
        copy.start()
    for copy in copies:
        copy.wait()
    whole = pltpu.make_async_copy(held, out_ref, out_sem.at[0])
    whole.start()
    whole.wait()


def far_pack(pieces, parts, spots):
    rows = sum(piece.shape[0] for piece in pieces)
    any_spec = pl.BlockSpec(memory_space=pl.ANY)
    return pl.pallas_call(
        functools.partial(far_kernel, parts),
        in_specs=[pl.BlockSpec(memory_space=pltpu.SMEM)] + [any_spec] * len(pieces),
        out_specs=any_spec,
        out_shape=jax.ShapeDtypeStruct((rows, PACK), BF),
        scratch_shapes=[
            pltpu.VMEM((rows, PACK), BF),
            pltpu.SemaphoreType.DMA((len(pieces),)),
            pltpu.SemaphoreType.DMA((1,)),
        ],
        compiler_params=pltpu.CompilerParams(vmem_limit_bytes=VMEM_LIMIT),
        cost_estimate=HINT,
        name="far_pack",
    )(spots, *pieces)


def join_kernel(shapes, flips, place_ref, *refs):
    count = len(flips)
    packs = refs[:count]
    outs, (held, sems, out_sems) = refs[-3 - len(shapes) : -3], refs[-3:]
    rows = held.shape[0] // count
    for number, pack in enumerate(packs):
        pltpu.make_async_copy(pack, held.at[pl.ds(number * rows, rows)], sems.at[number]).start()
    copies = []
    for number, flip in enumerate(flips):
        pltpu.make_async_copy(
            packs[number], held.at[pl.ds(number * rows, rows)], sems.at[number]
        ).wait()
        for at, column, height, start in pack_pieces(shapes):
            target = pl.multiple_of((place_ref[0] ^ flip) * height, height)
            copies.append(
                pltpu.make_async_copy(
                    held.at[pl.ds(number * rows + start, height)],
                    outs[at].at[pl.ds(target, height), columns_of(column)],
                    out_sems.at[len(copies)],
                )
            )
            copies[-1].start()
    for copy in copies:
        copy.wait()


def join_weights(members, packs, flips, spots, into=None):
    shapes = [member.shape for member in members]
    rows = pack_rows(members)
    any_spec = pl.BlockSpec(memory_space=pl.ANY)
    outs = [jax.ShapeDtypeStruct((4 * height, breadth), BF) for height, breadth in shapes]
    count = len(flips)
    held = [] if into is None else list(into)
    return pl.pallas_call(
        functools.partial(join_kernel, shapes, flips),
        in_specs=[pl.BlockSpec(memory_space=pltpu.SMEM)] + [any_spec] * (count + len(held)),
        out_specs=[any_spec] * len(outs),
        out_shape=outs,
        input_output_aliases={1 + count + at: at for at in range(len(held))},
        scratch_shapes=[
            pltpu.VMEM((count * rows, PACK), BF),
            pltpu.SemaphoreType.DMA((count,)),
            pltpu.SemaphoreType.DMA((count * len(pack_pieces(shapes)),)),
        ],
        compiler_params=pltpu.CompilerParams(vmem_limit_bytes=VMEM_LIMIT),
        cost_estimate=HINT,
        name="join_weights",
    )(spots, *packs, *held)


WIDE_LIMIT = 58 * 1024 * 1024
GELU_A = 0.7978845608028654
GELU_B = 0.044715


def gelu_pair(values):
    square = values * values
    bent = jnp.tanh(GELU_A * values * (1.0 + GELU_B * square))
    half = 0.5 * (1.0 + bent)
    slope = half + 0.5 * values * (1.0 - bent * bent) * (GELU_A * (1.0 + 3.0 * GELU_B * square))
    return values * half, slope


def rms_grads(values, gain, grad):
    inverse = lax.rsqrt(jnp.mean(values * values, axis=-1, keepdims=True) + EPSILON)
    scaled = values * inverse
    inner = grad * gain
    part = inverse * (inner - scaled * jnp.mean(inner * scaled, axis=-1, keepdims=True))
    return part, jnp.sum(grad * scaled, axis=0, keepdims=True)


def held(shape):
    return pl.BlockSpec(
        shape, lambda *_: (0,) * len(shape), pipeline_mode=pl.Buffered(1)
    )


def dense_call(kernel, steps, in_specs, out_specs, out_shape, scratch, name):
    return pl.pallas_call(
        kernel,
        grid=(steps,),
        in_specs=in_specs,
        out_specs=out_specs,
        out_shape=out_shape,
        scratch_shapes=scratch,
        compiler_params=pltpu.CompilerParams(vmem_limit_bytes=WIDE_LIMIT),
        cost_estimate=HINT,
        name=name,
    )


def frame_front_kernel(hidden_ref, gain_ref, weight_ref, normed_ref, packed_ref):
    groups, rows, own, _ = packed_ref.shape

    @pl.when(pl.program_id(0) == 0)
    def _():
        normed_ref[...] = rms_scale(hidden_ref[...].astype(F32), gain_ref[...]).astype(BF)

    total = matmul(normed_ref[...], weight_ref[...]).astype(BF)
    for part in range(3):

        @pl.when(pl.program_id(0) == part)
        def _(part=part):
            for group in range(groups):
                packed_ref[group, :, :, LANES * part : LANES * (part + 1)] = total[
                    :, LANES * group : LANES * (group + 1)
                ].reshape(rows, own, LANES)


def frame_front(hidden, gain, weight, rows):
    total, width = hidden.shape
    groups = width // LANES
    shape = (groups, rows, total // rows, 3 * LANES)
    return dense_call(
        frame_front_kernel,
        3,
        [held(hidden.shape), held(gain.shape), pl.BlockSpec((width, width), lambda j: (0, j))],
        [whole_block((total, width)), whole_block(shape)],
        [jax.ShapeDtypeStruct((total, width), BF), jax.ShapeDtypeStruct(shape, BF)],
        [],
        "frame_front",
    )(hidden, gain, weight)


def frame_rear_kernel(
    hidden_ref, front_ref, packed_ref, gain_ref, output_ref, expand_ref, contract_ref,
    kept_ref, mixed_ref, slope_ref, base_ref, total, normed_ref,
):
    groups, rows, own, _ = packed_ref.shape
    width = groups * LANES
    tile = slope_ref.shape[1]

    @pl.when(pl.program_id(0) == 0)
    def _():
        for group in range(groups):
            kept_ref[:, width + LANES * group : width + LANES * (group + 1)] = packed_ref[
                group
            ].reshape(rows * own, LANES)
        attended = kept_ref[:, width : 2 * width]
        mixed = hidden_ref[...].astype(F32) + matmul(attended, output_ref[...])
        mixed_ref[...] = mixed
        total[...] = mixed
        normed_ref[...] = rms_scale(mixed, gain_ref[...]).astype(BF)
        kept_ref[:, :width] = front_ref[...]
        kept_ref[:, 2 * width : 3 * width] = normed_ref[...]

    active, slope = gelu_pair(matmul(normed_ref[...], expand_ref[...]))
    active = active.astype(BF)
    for step in range(4 * width // tile):

        @pl.when(pl.program_id(0) == step)
        def _(step=step):
            kept_ref[:, 3 * width + step * tile : 3 * width + (step + 1) * tile] = active

    slope_ref[...] = slope.astype(BF)
    total[...] += matmul(active, contract_ref[...])

    @pl.when(pl.program_id(0) == pl.num_programs(0) - 1)
    def _():
        base_ref[...] = total[...].astype(BF)


FF_TILE = 512
FRAME_TILE = 1024


def frame_rear(hidden, front, packed, gain, output, expand, contract):
    total, width = hidden.shape
    inner = expand.shape[1]
    tile = FRAME_TILE
    full = whole_block((total, width))
    kept = (total, 3 * width + inner)
    return dense_call(
        frame_rear_kernel,
        inner // tile,
        [
            held(hidden.shape),
            held(front.shape),
            held(packed.shape),
            held(gain.shape),
            held(output.shape),
            pl.BlockSpec((width, tile), lambda j: (0, j)),
            pl.BlockSpec((tile, width), lambda j: (j, 0)),
        ],
        [whole_block(kept), full, pl.BlockSpec((total, tile), lambda j: (0, j)), full],
        [
            jax.ShapeDtypeStruct(kept, BF),
            jax.ShapeDtypeStruct((total, width), F32),
            jax.ShapeDtypeStruct((total, inner), BF),
            jax.ShapeDtypeStruct((total, width), BF),
        ],
        [pltpu.VMEM((total, width), F32), pltpu.VMEM((total, width), BF)],
        "frame_rear",
    )(hidden, front, packed, gain, output, expand, contract)


def frame_rear_grads_kernel(
    grad_ref, slope_ref, mixed_ref, gain_ref, output_ref, expand_ref, contract_ref,
    kept_ref, mixed_grad_ref, packed_ref, gain_grad_ref, total,
):
    groups, rows, own, _ = packed_ref.shape
    width = groups * LANES
    tile = slope_ref.shape[1]
    grad = grad_ref[...]
    expand_in = (slope_ref[...].astype(F32) * inner_right(grad, contract_ref[...])).astype(BF)
    for step in range(4 * width // tile):

        @pl.when(pl.program_id(0) == step)
        def _(step=step):
            kept_ref[:, width + step * tile : width + (step + 1) * tile] = expand_in

    @pl.when(pl.program_id(0) == 0)
    def _():
        total[...] = jnp.zeros_like(total)
        kept_ref[:, :width] = grad

    total[...] += inner_right(expand_in, expand_ref[...])

    @pl.when(pl.program_id(0) == pl.num_programs(0) - 1)
    def _():
        part, gain_grad = rms_grads(mixed_ref[...], gain_ref[...], total[...])
        mixed_grad = grad.astype(F32) + part
        mixed_grad_ref[...] = mixed_grad
        gain_grad_ref[...] = gain_grad
        output_in = mixed_grad.astype(BF)
        kept_ref[:, 5 * width :] = output_in
        attended_grad = inner_right(output_in, output_ref[...]).astype(BF)
        for group in range(groups):
            packed_ref[group] = attended_grad[:, LANES * group : LANES * (group + 1)].reshape(
                rows, own, LANES
            )


def frame_rear_grads(grad, slope, mixed, gain, output, expand, contract, rows):
    total, width = grad.shape
    inner = expand.shape[1]
    tile = FRAME_TILE
    shape = (width // LANES, rows, total // rows, LANES)
    kept = (total, 2 * width + inner)
    full = whole_block((total, width))
    part = pl.BlockSpec((total, tile), lambda j: (0, j))
    return dense_call(
        frame_rear_grads_kernel,
        inner // tile,
        [
            held(grad.shape),
            part,
            held(mixed.shape),
            held(gain.shape),
            held(output.shape),
            pl.BlockSpec((width, tile), lambda j: (0, j)),
            pl.BlockSpec((tile, width), lambda j: (j, 0)),
        ],
        [whole_block(kept), full, whole_block(shape), whole_block((1, width))],
        [
            jax.ShapeDtypeStruct(kept, BF),
            jax.ShapeDtypeStruct((total, width), F32),
            jax.ShapeDtypeStruct(shape, BF),
            jax.ShapeDtypeStruct((1, width), F32),
        ],
        [pltpu.VMEM((total, width), F32)],
        "frame_rear_grads",
    )(grad, slope, mixed, gain, output, expand, contract)


def frame_front_grads_kernel(
    packed_ref, hidden_ref, gain_ref, mixed_grad_ref, weight_ref,
    projected_ref, grad_ref, gain_grad_ref, total,
):
    groups, rows, own, _ = packed_ref.shape

    @pl.when(pl.program_id(0) == 0)
    def _():
        total[...] = jnp.zeros_like(total)

    for part in range(3):

        @pl.when(pl.program_id(0) == part)
        def _(part=part):
            for group in range(groups):
                projected_ref[:, LANES * group : LANES * (group + 1)] = packed_ref[
                    group, :, :, LANES * part : LANES * (part + 1)
                ].reshape(rows * own, LANES)

    total[...] += inner_right(projected_ref[...], weight_ref[...])

    @pl.when(pl.program_id(0) == 2)
    def _():
        part, gain_grad = rms_grads(hidden_ref[...].astype(F32), gain_ref[...], total[...])
        grad_ref[...] = mixed_grad_ref[...] + part
        gain_grad_ref[...] = gain_grad


def frame_front_grads(packed, hidden, gain, mixed_grad, weight):
    total, width = hidden.shape
    return dense_call(
        frame_front_grads_kernel,
        3,
        [
            held(packed.shape),
            held(hidden.shape),
            held(gain.shape),
            held(mixed_grad.shape),
            pl.BlockSpec((width, width), lambda j: (0, j)),
        ],
        [
            pl.BlockSpec((total, width), lambda j: (0, j)),
            whole_block((total, width)),
            whole_block((1, width)),
        ],
        [
            jax.ShapeDtypeStruct((total, 3 * width), BF),
            jax.ShapeDtypeStruct((total, width), F32),
            jax.ShapeDtypeStruct((1, width), F32),
        ],
        [pltpu.VMEM((total, width), F32)],
        "frame_front_grads",
    )(packed, hidden, gain, mixed_grad, weight)


def codec_front_kernel(base_ref, entries_ref, gain_ref, weight_ref, normed_ref, packed_ref, normed):
    positions = packed_ref.shape[0]

    @pl.when(pl.program_id(0) == 0)
    def _():
        base = base_ref[...].astype(F32)
        size = base.shape[0]
        for t in range(positions):
            hidden = base if t == 0 else base + entries_ref[t - 1].astype(F32)
            normed[size * t : size * (t + 1)] = rms_scale(hidden, gain_ref[...]).astype(BF)
        normed_ref[...] = normed[...]

    total = matmul(normed[...], weight_ref[...]).astype(BF)
    packed_ref[...] = total.reshape(packed_ref.shape)


def codec_front(base, entries, gain, weight):
    total, width = base.shape
    positions = entries.shape[0] + 1
    return dense_call(
        codec_front_kernel,
        6,
        [
            held(base.shape),
            held(entries.shape),
            held(gain.shape),
            pl.BlockSpec((width, width // 2), lambda j: (0, j)),
        ],
        [
            whole_block((positions * total, width)),
            pl.BlockSpec((positions, total, width // 2), lambda j: (0, 0, j)),
        ],
        [
            jax.ShapeDtypeStruct((positions * total, width), BF),
            jax.ShapeDtypeStruct((positions, total, 3 * width), BF),
        ],
        [pltpu.VMEM((positions * total, width), BF)],
        "codec_front",
    )(base, entries, gain, weight)


def codec_rear_kernel(
    base_ref, entries_ref, attended_ref, grad_ref, gain_ref, output_ref, expand_ref, contract_ref,
    mixed_ref, active_ref, expand_kept_ref, kept_ref, mixed_grad_ref,
    attended_grad_ref, gain_grad_ref, total,
):
    width = total.shape[1]
    positions = entries_ref.shape[0] + 1
    size = base_ref.shape[0]

    @pl.when(pl.program_id(0) == 0)
    def _():
        base = base_ref[...].astype(F32)
        for t in range(positions):
            own = slice(size * t, size * (t + 1))
            hidden = base if t == 0 else base + entries_ref[t - 1].astype(F32)
            mixed = hidden + matmul(attended_ref[own], output_ref[...])
            mixed_ref[own] = mixed
            expand_kept_ref[own, :width] = rms_scale(mixed, gain_ref[...]).astype(BF)
        total[...] = jnp.zeros_like(total)

    active, slope = gelu_pair(matmul(expand_kept_ref[:, :width], expand_ref[...]))
    active_ref[...] = active.astype(BF)
    expand_in = (slope * inner_right(grad_ref[...], contract_ref[...])).astype(BF)
    tile = expand_in.shape[1]
    for step in range(4 * width // tile):

        @pl.when(pl.program_id(0) == step)
        def _(step=step):
            expand_kept_ref[:, width + step * tile : width + (step + 1) * tile] = expand_in

    total[...] += inner_right(expand_in, expand_ref[...])

    @pl.when(pl.program_id(0) == pl.num_programs(0) - 1)
    def _():
        gain_grads = jnp.zeros_like(gain_grad_ref)
        for t in range(positions):
            own = slice(size * t, size * (t + 1))
            part, gain_grad = rms_grads(mixed_ref[own], gain_ref[...], total[own])
            gain_grads = gain_grads + gain_grad
            mixed_grad = grad_ref[own].astype(F32) + part
            mixed_grad_ref[own] = mixed_grad
            output_in = mixed_grad.astype(BF)
            kept_ref[own] = output_in
            attended_grad_ref[t] = inner_right(output_in, output_ref[...]).astype(BF)
        gain_grad_ref[...] = gain_grads


def codec_rear(base, entries, kept, grad, gain, output, expand, contract):
    size, width = base.shape
    total = kept.shape[0]
    inner = expand.shape[1]
    tile = FF_TILE
    full = whole_block((total, width))
    wide = (total, width + inner)
    high = jax.ShapeDtypeStruct((total, width), F32)
    return dense_call(
        codec_rear_kernel,
        inner // tile,
        [
            held(base.shape),
            held(entries.shape),
            pl.BlockSpec((total, width), lambda j: (0, 1), pipeline_mode=pl.Buffered(1)),
            held(grad.shape),
            held(gain.shape),
            held(output.shape),
            pl.BlockSpec((width, tile), lambda j: (0, j)),
            pl.BlockSpec((tile, width), lambda j: (j, 0)),
        ],
        [
            held((total, width)),
            pl.BlockSpec((total, tile), lambda j: (0, j)),
            held(wide),
            held((total, width)),
            held((total, width)),
            held((total // size, size, width)),
            whole_block((1, width)),
        ],
        [
            high,
            jax.ShapeDtypeStruct((total, inner), BF),
            jax.ShapeDtypeStruct(wide, BF),
            jax.ShapeDtypeStruct((total, width), BF),
            high,
            jax.ShapeDtypeStruct((total // size, size, width), BF),
            jax.ShapeDtypeStruct((1, width), F32),
        ],
        [pltpu.VMEM((total, width), F32)],
        "codec_rear",
    )(base, entries, kept, grad, gain, output, expand, contract)


def codec_result_kernel(mixed_ref, active_ref, live_ref, contract_ref, out_ref, total):
    positions, size, _ = out_ref.shape

    @pl.when(pl.program_id(0) == 0)
    def _():
        total[...] = mixed_ref[...]

    total[...] += matmul(active_ref[...], contract_ref[...])

    @pl.when(pl.program_id(0) == pl.num_programs(0) - 1)
    def _():
        for t in range(positions):
            out_ref[t] = (total[size * t : size * (t + 1)] * live_ref[...]).astype(BF)


def codec_result(mixed, active, live, contract):
    total, width = mixed.shape
    size = live.shape[0]
    inner = active.shape[1]
    tile = FF_TILE
    shape = (total // size, size, width)
    return dense_call(
        codec_result_kernel,
        inner // tile,
        [
            held(mixed.shape),
            pl.BlockSpec((total, tile), lambda j: (0, j)),
            held(live.shape),
            pl.BlockSpec((tile, width), lambda j: (j, 0)),
        ],
        whole_block(shape),
        jax.ShapeDtypeStruct(shape, BF),
        [pltpu.VMEM((total, width), F32)],
        "codec_result",
    )(mixed, active, live, contract)


def codec_front_grads_kernel(
    grad_ref, base_ref, entries_ref, gain_ref, mixed_grad_ref, weight_ref,
    base_grad_ref, entry_grad_ref, gain_grad_ref, total,
):
    positions = entries_ref.shape[0] + 1
    size = base_ref.shape[0]

    @pl.when(pl.program_id(0) == 0)
    def _():
        total[...] = jnp.zeros_like(total)

    total[...] += inner_right(grad_ref[...], weight_ref[...])

    @pl.when(pl.program_id(0) == pl.num_programs(0) - 1)
    def _():
        base = base_ref[...].astype(F32)
        gain_grads = jnp.zeros_like(gain_grad_ref)
        base_grad = jnp.zeros_like(base)
        for t in range(positions):
            own = slice(size * t, size * (t + 1))
            hidden = base if t == 0 else base + entries_ref[t - 1].astype(F32)
            part, gain_grad = rms_grads(hidden, gain_ref[...], total[own])
            gain_grads = gain_grads + gain_grad
            grad = mixed_grad_ref[own] + part
            base_grad = base_grad + grad
            if t > 0:
                entry_grad_ref[size * (t - 1) : size * t] = grad.astype(BF)
        base_grad_ref[...] = base_grad.astype(BF)
        gain_grad_ref[...] = gain_grads


def codec_front_grads(grad, base, entries, gain, mixed_grad, weight):
    size, width = base.shape
    total = grad.shape[0]
    tile = width // 2
    return dense_call(
        codec_front_grads_kernel,
        grad.shape[1] // tile,
        [
            pl.BlockSpec((total, tile), lambda j: (0, j)),
            held(base.shape),
            held(entries.shape),
            held(gain.shape),
            held(mixed_grad.shape),
            pl.BlockSpec((width, tile), lambda j: (0, j)),
        ],
        [whole_block((size, width)), whole_block((total - size, width)), whole_block((1, width))],
        [
            jax.ShapeDtypeStruct((size, width), BF),
            jax.ShapeDtypeStruct((total - size, width), BF),
            jax.ShapeDtypeStruct((1, width), F32),
        ],
        [pltpu.VMEM((total, width), F32)],
        "codec_front_grads",
    )(grad, base, entries, gain, mixed_grad, weight)


def shards_general(
    frames,
    segments,
    padding,
    codec_tokens,
    codebooks,
    frame_prenorm,
    frame_project,
    frame_output,
    frame_postnorm,
    frame_expand,
    frame_contract,
    codec_prenorm,
    codec_project,
    codec_output,
    codec_postnorm,
    codec_expand,
    codec_contract,
    cotangent,
):
    place = Place()
    row_count, frames_dev, width = frames.shape
    frame_total = row_count * frames_dev
    positions = cotangent.shape[2]
    gains = lax.all_gather(
        jnp.stack([frame_prenorm, frame_postnorm, codec_prenorm, codec_postnorm]),
        "mp",
        axis=1,
        tiled=True,
    )
    frame_weights = (
        gains[0],
        gather_weight(frame_project, place),
        gather_weight(frame_output, place),
        gains[1],
        gather_weight(frame_expand, place),
        gather_weight(frame_contract, place),
    )
    codec_weights = (
        gains[2],
        gather_weight(codec_project, place),
        gather_weight(codec_output, place),
        gains[3],
        gather_weight(codec_expand, place),
        gather_weight(codec_contract, place),
    )
    table = gather_weight(codebooks, place)

    hidden = frames.astype(F32).reshape(frame_total, width)
    normed, projected = front_pass(hidden, frame_weights)
    attended, attention_back = frame_attention(
        projected.reshape(row_count, frames_dev, 3 * width), segments, place
    )
    attended = attended.reshape(frame_total, width)
    frame_result, frame_saved = rear_pass(hidden, attended, frame_weights)
    base = frame_result.astype(BF).astype(F32)

    table_rows = codec_tokens.reshape(positions - 1, frame_total) + (
        jnp.arange(positions - 1, dtype=jnp.int32) * CODES
    )[:, None]
    embedded = table[table_rows].astype(F32)
    codec_hidden = jnp.concatenate([base[None], base[None] + embedded], axis=0).reshape(
        positions * frame_total, width
    )
    codec_normed, codec_projected = front_pass(codec_hidden, codec_weights)
    marks = (
        jnp.arange(width)[:, None] // HEAD == jnp.arange(HEADS)[None, :]
    ).astype(F32)
    view = codec_projected.reshape(positions, frame_total, 3, width)
    queries, keys, values = ([view[t, :, part] for t in range(positions)] for part in range(3))
    soft = codec_softmax(queries, keys, marks)
    codec_attended = jnp.concatenate(codec_attend(soft, values, marks), axis=0)
    codec_result, codec_saved = rear_pass(codec_hidden, codec_attended, codec_weights)
    live = padding.reshape(frame_total).astype(F32)[None, :, None]
    output = jnp.transpose(
        (codec_result.reshape(positions, frame_total, width) * live).astype(BF), (1, 0, 2)
    ).reshape(row_count, frames_dev, positions, width)

    codec_grad = (
        jnp.transpose(cotangent.reshape(frame_total, positions, width), (1, 0, 2)).astype(F32) * live
    ).reshape(positions * frame_total, width)
    mixed_grad, attended_grad, codec_postnorm_grad, contract_in, expand_in, output_in = rear_grads(
        codec_grad, codec_saved, codec_weights
    )
    codec_contract_part = weight_grad(codec_saved[3], contract_in, place, True)
    codec_expand_part = weight_grad(codec_saved[1], expand_in, place, False)
    codec_output_part = weight_grad(codec_attended, output_in, place, True)
    grad_view = attended_grad.reshape(positions, frame_total, width)
    codec_projected_grad = codec_attend_grads(
        soft, queries, keys, values, [grad_view[t] for t in range(positions)], marks
    )
    codec_project_part = weight_grad(codec_normed, codec_projected_grad, place, True)
    input_grad, codec_prenorm_grad = front_grads(
        codec_hidden, codec_projected_grad, mixed_grad, codec_weights
    )
    input_grad = input_grad.reshape(positions, frame_total, width)
    chosen = (
        table_rows.reshape(-1)[:, None] == jnp.arange(table.shape[0], dtype=jnp.int32)[None, :]
    ).astype(BF)
    table_part = weight_grad(chosen, input_grad[1:].reshape(-1, width).astype(BF), place, False)
    base_grad = jnp.sum(input_grad, axis=0).astype(BF).astype(F32)

    (codec_contract_grad,) = finish_grads([codec_contract_part], place)
    codec_expand_grad, codec_output_grad, codec_project_grad = finish_grads(
        [codec_expand_part, codec_output_part, codec_project_part], place
    )
    (table_grad,) = finish_grads([table_part], place)

    frame_mixed_grad, frame_attended_grad, frame_postnorm_grad, contract_in, expand_in, output_in = (
        rear_grads(base_grad, frame_saved, frame_weights)
    )
    frame_projected_grad = attention_back(
        frame_attended_grad.reshape(row_count, frames_dev, width)
    ).reshape(frame_total, 3 * width)
    frame_contract_part = weight_grad(frame_saved[3], contract_in, place, True)
    frame_expand_part = weight_grad(frame_saved[1], expand_in, place, False)
    frame_output_part = weight_grad(attended, output_in, place, True)
    frame_project_part = weight_grad(normed, frame_projected_grad, place, True)
    frames_grad, frame_prenorm_grad = front_grads(
        hidden, frame_projected_grad, frame_mixed_grad, frame_weights
    )
    (frame_contract_grad,) = finish_grads([frame_contract_part], place)
    frame_expand_grad, frame_output_grad = finish_grads(
        [frame_expand_part, frame_output_part], place
    )
    (frame_project_grad,) = finish_grads([frame_project_part], place)
    gain_sums = sum_everywhere(
        jnp.stack(
            [frame_prenorm_grad, frame_postnorm_grad, codec_prenorm_grad, codec_postnorm_grad]
        ),
        place,
    )
    return (
        output,
        frames_grad.reshape(row_count, frames_dev, width),
        table_grad,
        gain_sums[0],
        frame_project_grad,
        frame_output_grad,
        gain_sums[1],
        frame_expand_grad,
        frame_contract_grad,
        gain_sums[2],
        codec_project_grad,
        codec_output_grad,
        gain_sums[3],
        codec_expand_grad,
        codec_contract_grad,
    )


class Pair:
    def __init__(self, own):
        self.own = own
        self.other = swap(own, "mp", 1)
        self.age = 0

    def both(self):
        return (self.own, self.other)


class Chain:
    def __init__(self):
        self.last = ()
        self.pending = []

    def pair(self, own):
        made = Pair(own)
        self.pending.append(made)
        return made

    def enter(self, *values):
        due = [made for made in self.pending if made.age >= 3]
        self.pending = [made for made in self.pending if made.age < 3]
        for made in self.pending:
            made.age += 1
        came = tuple(made.other for made in due)
        held = lax.optimization_barrier(tuple(values) + came + self.last)
        for made, other in zip(due, held[len(values) :]):
            made.other = other
        return held[0] if len(values) == 1 else held[: len(values)]

    def leave(self, *values):
        self.last = values


class Gather:
    def __init__(self, members, spots, whole=False):
        self.members = members
        self.spots = spots
        self.whole = whole
        self.pack, self.quarter = pack_call(members, spots)

    def start(self, chain):
        self.came = swap(chain.enter(self.pack if self.whole else self.quarter), "mp", 2)
        self.near = chain.pair(self.pack)

    def spread(self, chain):
        self.came = chain.enter(self.came)
        chain.leave(self.came)
        if self.whole:
            self.far = chain.pair(self.came)
            return
        self.over_x = swap(self.came, "seq", 1)
        self.over_n = swap(self.came, "seq", 2)

    def cross(self, chain):
        self.over_x, self.over_n = chain.enter(self.over_x, self.over_n)
        chain.leave(self.over_x, self.over_n)
        half = self.over_x.shape[0] // 2
        self.ends = (swap(self.over_n[:half], "seq", 1), swap(self.over_x[half:], "seq", 2))

    def close(self, chain):
        ends = chain.enter(*self.ends)
        parts = ((0, 0), (1, 0), (2, 0), (3, 0), (3, ends[0].shape[0]))
        far = far_pack([self.came, self.over_x, self.over_n, *ends], parts, self.spots)
        chain.leave(far)
        self.far = far

    def send(self, chain):
        self.far = Pair(chain.enter(self.far))

    def join_near(self, chain):
        packs = chain.enter(*self.near.both())
        self.outs = join_weights(self.members, packs, (0, 1), self.spots)
        chain.leave(*self.outs)

    def join(self, chain):
        packs = chain.enter(*self.far.both())
        outs = join_weights(self.members, packs, (2, 3), self.spots, self.outs)
        chain.leave(*outs)
        return outs


def load(block, riders):
    if riders is None:
        return block
    high = riders.astype(BF)
    low = (riders - high.astype(F32)).astype(BF)
    return jnp.concatenate(
        [part.reshape(-1, LANES) for part in (block, high, low)], axis=0
    )


def unload(message, shape, riders):
    if riders is None:
        return message, None
    rows = message.shape[0] - 2 * riders.size // LANES
    high, low = (
        part.astype(F32).reshape(riders.shape) for part in jnp.split(message[rows:], 2, axis=0)
    )
    return message[:rows].reshape(shape), riders + (high + low)


class Reduce:
    def __init__(self, stages, blocks, riders=None):
        self.stages = stages
        self.keep = blocks[1]
        self.riders = riders
        self.came = []
        self.shape = blocks[0].shape
        self.coming = swap(load(blocks[0], riders), *BITS[stages[0]])

    def arrive(self, chain):
        self.coming = chain.enter(self.coming)
        chain.leave(self.coming)

    def take(self, chain):
        self.keep, self.coming, *self.came = chain.enter(self.keep, self.coming, *self.came)
        block, self.riders = unload(self.coming, self.shape, self.riders)
        self.came.append(block)

    def total(self, last):
        at = len(self.came) - 1
        spot = (1,) * at + ((0,) if not last else ())
        value = self.keep[spot].astype(F32) if spot else self.keep.astype(F32)
        for level, came in enumerate(self.came):
            value = value + came[spot[level:]].astype(F32)
        return value

    def give(self, chain):
        self.take(chain)
        given = self.total(False).astype(BF)
        self.shape = given.shape
        return given

    def step(self, chain):
        given = self.give(chain)
        message = load(given, self.riders)
        chain.leave(message)
        self.coming = swap(message, *BITS[self.stages[len(self.came)]])

    def result(self):
        return self.total(True)


def finish(sums, chain):
    given = jnp.concatenate([one.give(chain) for one in sums], axis=0)
    riders = sums[-1].riders
    message = load(given, riders)
    chain.leave(message)
    message = swap(message, *BITS["f"])

    def take():
        held = chain.enter(message)
        chain.leave(held)
        came, total = unload(held, given.shape, riders)
        start = 0
        for one in sums:
            size = one.shape[-3]
            one.came.append(came[start : start + size])
            start += size
        sums[-1].riders = total

    return take


def shards(
    frames,
    segments,
    padding,
    codec_tokens,
    codebooks,
    frame_prenorm,
    frame_project,
    frame_output,
    frame_postnorm,
    frame_expand,
    frame_contract,
    codec_prenorm,
    codec_project,
    codec_output,
    codec_postnorm,
    codec_expand,
    codec_contract,
    cotangent,
):
    place = Place()
    chain = Chain()
    order = grad_order(place)
    spots = jnp.stack([place.mp, place.seq % 4]).astype(jnp.int32)
    row_count, frames_dev, width = frames.shape
    frame_total = row_count * frames_dev
    positions = cotangent.shape[2]
    count = place.seq_count

    gain_rows = jnp.pad(
        jnp.concatenate([frame_prenorm, frame_postnorm, codec_prenorm, codec_postnorm])[None],
        ((0, 127), (0, 0)),
    )
    first = Gather([frame_project, gain_rows], spots)
    first.start(chain)
    chain.leave(first.quarter)
    second = Gather([frame_expand, frame_contract, frame_output], spots)
    second.quarter = chain.enter(second.quarter)
    chain.leave(second.quarter)
    every_segment = lax.all_to_all(
        jnp.broadcast_to(segments[None], (count, row_count, frames_dev)),
        "seq",
        split_axis=0,
        concat_axis=0,
        tiled=True,
    )
    every_segment = jnp.transpose(every_segment, (1, 0, 2)).reshape(row_count, count * frames_dev)
    codes = codec_tokens.reshape(1, (positions - 1) * frame_total) + jnp.repeat(
        jnp.arange(positions - 1, dtype=jnp.int32) * CODES, frame_total
    )
    codes_pair = chain.pair(codes)
    every_segment = chain.enter(every_segment)
    chain.leave(every_segment)
    live = padding.reshape(frame_total).astype(F32)[:, None]
    first.spread(chain)
    second.start(chain)
    contract_in = (
        jnp.transpose(chain.enter(cotangent).reshape(frame_total, positions, width), (1, 0, 2))
        * live.astype(BF)[None]
    ).reshape(positions * frame_total, width)
    chain.leave(contract_in)
    first.join_near(chain)
    first.cross(chain)
    fourth = Gather([codec_expand, codec_contract, codec_output], spots)
    fourth.quarter = chain.enter(fourth.quarter)
    chain.leave(fourth.quarter)
    second.spread(chain)
    fourth.start(chain)
    third = Gather([codec_project, codebooks], spots, True)
    third.pack = chain.enter(third.pack)
    chain.leave(third.pack)
    third.start(chain)
    first.close(chain)
    first.send(chain)

    frame_project_all, gains = first.join(chain)
    gains = jnp.transpose(
        gains.reshape(place.mp_count, -1, 4, width // 4)[:, 0], (1, 0, 2)
    ).reshape(4, 1, width).astype(F32)
    hidden = frames.reshape(frame_total, width)
    normed, packed = frame_front(hidden, chain.enter(gains[0]), frame_project_all, row_count)
    packed, second.over_x, second.over_n, fourth.came = chain.enter(
        packed, second.over_x, second.over_n, fourth.came
    )
    chain.leave(packed)
    packed = lax.all_to_all(packed, "seq", split_axis=0, concat_axis=0, tiled=True)
    second.join_near(chain)
    third.join_near(chain)
    fourth.join_near(chain)
    second.cross(chain)
    packed, *second.ends = chain.enter(packed, *second.ends)
    chain.leave(packed)
    second.close(chain)
    second.send(chain)
    fourth.spread(chain)
    contract_pair = Pair(contract_in)
    packed = chain.enter(packed)
    attended = frame_attend_call(packed, every_segment)
    chain.leave(attended)
    attended, second.far.other = chain.enter(attended, second.far.other)
    chain.leave(attended)
    attended = lax.all_to_all(attended, "seq", split_axis=0, concat_axis=0, tiled=True)
    frame_expand_all, frame_contract_all, frame_output_all = second.join(chain)
    attended, fourth.over_x, fourth.over_n = chain.enter(attended, fourth.over_x, fourth.over_n)
    chain.leave(attended)
    fourth.cross(chain)
    frame_kept, mixed, slope, base = frame_rear(
        hidden,
        normed,
        chain.enter(attended),
        gains[1],
        frame_output_all,
        frame_expand_all,
        frame_contract_all,
    )
    chain.leave(base)

    base, third.came, *fourth.ends = chain.enter(base, third.came, *fourth.ends)
    chain.leave(base)
    third.spread(chain)
    fourth.close(chain)
    codec_project_all, table = third.join(chain)
    fourth.send(chain)
    frame_kept = Pair(chain.enter(frame_kept))
    entries = table[codes.reshape(positions - 1, frame_total)]
    codec_normed, codec_packed = codec_front(chain.enter(base), entries, gains[2], codec_project_all)
    chain.leave(codec_packed)
    codec_packed, contract_pair.other = chain.enter(codec_packed, contract_pair.other)
    codec_kept = codec_attend_call(codec_packed, codec_normed).reshape(
        positions * frame_total, 2 * width
    )
    chain.leave(codec_kept)
    codec_expand_all, codec_contract_all, codec_output_all = fourth.join(chain)
    codec_kept, frame_kept.other = chain.enter(codec_kept, frame_kept.other)
    chain.leave(codec_kept)
    (
        codec_mixed,
        codec_activated,
        codec_expand_kept,
        codec_output_in,
        mixed_grad,
        attended_grad,
        codec_postnorm_grad,
    ) = codec_rear(
        base,
        entries,
        chain.enter(codec_kept),
        contract_in,
        gains[3],
        codec_output_all,
        codec_expand_all,
        codec_contract_all,
    )
    chain.leave(codec_activated)

    inner = codec_activated.shape[1]
    activated_pair = chain.pair(codec_activated)
    codec_expand_kept = chain.pair(codec_expand_kept)
    projected_grad = codec_attend_grads_call(codec_packed, chain.enter(attended_grad)).reshape(
        positions * frame_total, 3 * width
    )
    chain.leave(projected_grad)
    base_grad, table_in, codec_prenorm_grad = codec_front_grads(
        chain.enter(projected_grad), base, entries, gains[2], mixed_grad, codec_project_all
    )
    chain.leave(base_grad)
    frame_grads_kept, frame_mixed_grad, grads, frame_postnorm_grad = frame_rear_grads(
        chain.enter(base_grad),
        slope,
        mixed,
        gains[1],
        frame_output_all,
        frame_expand_all,
        frame_contract_all,
        row_count,
    )
    chain.leave(grads)

    activated_pair.other, codec_expand_kept.other, grads, frame_grads_kept = chain.enter(
        activated_pair.other, codec_expand_kept.other, grads, frame_grads_kept
    )
    chain.leave(grads)
    grads = lax.all_to_all(grads, "seq", split_axis=0, concat_axis=0, tiled=True)
    frame_grads_kept = Pair(frame_grads_kept)
    contract_stages = tuple("ynxf")
    contract_blocks = grad_columns(
        (chain.enter(*activated_pair.both()), 0, inner),
        (contract_pair.both(), 0, width),
        order,
        contract_stages,
        4,
        0,
    )
    chain.leave(*contract_blocks)
    expand_stages = tuple("xnyf")
    arrays = chain.enter(*codec_expand_kept.both())
    expand_blocks = grad_rows((arrays, 0, width), (arrays, width, inner), order, expand_stages, 4, 0)
    chain.leave(*expand_blocks)

    grads, frame_grads_kept.other = chain.enter(grads, frame_grads_kept.other)
    chain.leave(grads)
    contract_sum = Reduce(contract_stages, chain.enter(*contract_blocks))
    expand_sum = Reduce(expand_stages, chain.enter(*expand_blocks))
    codec_kept = Pair(chain.enter(codec_kept))
    output_pair = Pair(chain.enter(codec_output_in))
    projected_pair = Pair(chain.enter(projected_grad))
    packed_grad = frame_attend_grads_call(packed, chain.enter(grads), every_segment)
    chain.leave(packed_grad)
    kept, arrays = frame_kept.both(), chain.enter(*frame_grads_kept.both())
    frame_contract_stages = tuple("yxnf")
    frame_contract_blocks = grad_columns(
        (kept, 3 * width, inner), (arrays, 0, width), order, frame_contract_stages, 4, 0
    )
    chain.leave(*frame_contract_blocks)
    frame_expand_stages = tuple("xnyf")
    arrays = chain.enter(*arrays)
    blocks = grad_rows(
        (kept, 2 * width, width), (arrays, width, inner), order, frame_expand_stages, 5, 0
    )
    frame_expand_blocks = grad_rows(
        (kept, width, width), (arrays, width + inner, width), order, frame_expand_stages, 5, 4, blocks
    )
    chain.leave(*frame_expand_blocks)

    packed_grad, codec_kept.other, projected_pair.other, output_pair.other = chain.enter(
        packed_grad, codec_kept.other, projected_pair.other, output_pair.other
    )
    chain.leave(packed_grad)
    contract_sum.arrive(chain)
    expand_sum.arrive(chain)
    packed_grad = lax.all_to_all(packed_grad, "seq", split_axis=0, concat_axis=0, tiled=True)
    contract_sum.step(chain)
    expand_sum.step(chain)
    frame_contract_sum = Reduce(frame_contract_stages, chain.enter(*frame_contract_blocks))
    frame_expand_sum = Reduce(frame_expand_stages, chain.enter(*frame_expand_blocks))
    table_pair = Pair(chain.enter(table_in))
    project_stages = tuple("ynxf")
    arrays = chain.enter(*codec_kept.both())
    blocks = grad_rows(
        (arrays, 0, width), (projected_pair.both(), 0, 3 * width), order, project_stages, 4, 0
    )
    project_blocks = grad_rows(
        (arrays, width, width), (output_pair.both(), 0, width), order, project_stages, 4, 3, blocks
    )
    chain.leave(*project_blocks)
    table_stages = tuple("xynf")
    table_blocks = grad_table(
        jnp.concatenate(codes_pair.both(), axis=1),
        chain.enter(*table_pair.both()),
        order,
        table_stages,
        codebooks.shape[0],
        2,
        0,
    )
    chain.leave(*table_blocks)
    project_sum = Reduce(project_stages, chain.enter(*project_blocks))
    table_sum = Reduce(table_stages, chain.enter(*table_blocks))
    output = codec_result(codec_mixed, chain.enter(codec_activated), live, codec_contract_all)
    chain.leave(output)
    output = jnp.transpose(output, (1, 0, 2)).reshape(row_count, frames_dev, positions, width)

    packed_grad, contract_sum.coming, expand_sum.coming, frame_contract_sum.coming = chain.enter(
        packed_grad, contract_sum.coming, expand_sum.coming, frame_contract_sum.coming
    )
    packed_grad, frame_expand_sum.coming = chain.enter(packed_grad, frame_expand_sum.coming)
    chain.leave(packed_grad)
    frame_contract_sum.step(chain)
    frame_expand_sum.step(chain)
    frame_projected_grad, frames_grad, frame_prenorm_grad = frame_front_grads(
        chain.enter(packed_grad), hidden, gains[0], frame_mixed_grad, frame_project_all
    )
    chain.leave(frames_grad)
    frame_projected_pair = Pair(frame_projected_grad)
    gain_pair = Pair(
        jnp.concatenate(
            [frame_prenorm_grad, frame_postnorm_grad, codec_prenorm_grad, codec_postnorm_grad]
        )
    )
    frame_projected_pair.other, gain_pair.other = chain.enter(
        frame_projected_pair.other, gain_pair.other
    )
    chain.leave(gain_pair.other)
    blocks = grad_rows(
        (kept, 0, width),
        (chain.enter(*frame_projected_pair.both()), 0, 3 * width),
        order,
        table_stages,
        3,
        0,
    )
    chain.leave(*blocks)
    riders = gain_pair.own + gain_pair.other
    frame_project_sum = Reduce(table_stages, blocks, chain.enter(riders))
    project_sum.step(chain)
    table_sum.step(chain)
    frame_expand_sum.step(chain)
    expand_sum.step(chain)
    frame_project_sum.step(chain)
    frame_contract_sum.step(chain)
    project_sum.step(chain)
    contract_sum.step(chain)
    take_second = finish([frame_contract_sum, frame_expand_sum], chain)
    table_sum.step(chain)
    frame_project_sum.step(chain)
    take_first = finish([contract_sum, expand_sum], chain)
    take_fourth = finish([project_sum, table_sum], chain)
    take_third = finish([frame_project_sum], chain)
    take_second()
    take_first()
    take_fourth()
    take_third()

    height = frame_project.shape[0]
    project_units = project_sum.result()
    frame_expand_units = frame_expand_sum.result()
    gain_sums = frame_project_sum.riders
    return (
        output,
        frames_grad.reshape(row_count, frames_dev, width),
        rows_from_units(table_sum.result(), codebooks.shape[0]),
        gain_sums[0],
        rows_from_units(frame_project_sum.result(), height),
        rows_from_units(frame_expand_units[4:], height),
        gain_sums[1],
        rows_from_units(frame_expand_units[:4], height),
        columns_from_units(frame_contract_sum.result()),
        gain_sums[2],
        rows_from_units(project_units[:3], height),
        rows_from_units(project_units[3:], height),
        gain_sums[3],
        rows_from_units(expand_sum.result(), height),
        columns_from_units(contract_sum.result()),
    )


def solution(mesh):
    placed = (
        P("mp", "seq", None),
        P("mp", "seq"),
        P("mp", "seq"),
        P(None, "mp", "seq"),
        P("mp", None),
        P("mp"),
        P("mp", None),
        P("mp", None),
        P("mp"),
        P("mp", None),
        P("mp", None),
        P("mp"),
        P("mp", None),
        P("mp", None),
        P("mp"),
        P("mp", None),
        P("mp", None),
        P("mp", "seq", None, None),
    )
    small = mesh.shape["seq"] == 8 and mesh.shape["mp"] == 4
    return jax.shard_map(
        shards if small else shards_general,
        mesh=mesh,
        in_specs=placed,
        out_specs=(
            P("mp", "seq", None, None),
            P("mp", "seq", None),
            P("mp", "seq"),
            P(),
            P("mp", "seq"),
            P("mp", "seq"),
            P(),
            P("mp", "seq"),
            P("mp", "seq"),
            P(),
            P("mp", "seq"),
            P("mp", "seq"),
            P(),
            P("mp", "seq"),
            P("mp", "seq"),
        ),
        check_vma=False,
    )
```

```python
import functools

import jax
import jax.numpy as jnp
from jax import lax
from jax.experimental import pallas as pl
from jax.experimental.pallas import tpu as pltpu
from jax.sharding import PartitionSpec as P

HEADS = 16
HEAD = 64
CODES = 1024


EPSILON = 1e-05
MASKED = -1e30
FACTOR = HEAD ** (-0.5)

BF = jnp.bfloat16
F32 = jnp.float32


def rms_scale(values, gain_vec):
    return (
        values * lax.rsqrt(jnp.mean(values * values, axis=-1, keepdims=True) + EPSILON) * gain_vec
    )


def matmul(former, latter):
    return jnp.dot(former, latter, preferred_element_type=F32)


def inner_left(former, latter):
    return lax.dot_general(former, latter, (((0,), (0,)), ((), ())), preferred_element_type=F32)


def inner_right(former, latter):
    return lax.dot_general(former, latter, (((1,), (1,)), ((), ())), preferred_element_type=F32)


def split_heads(values):
    return values.reshape(values.shape[:-1] + (-1, HEAD))


def swap(values, axis, bit):
    return lax.ppermute(values, axis, [(i, i ^ bit) for i in range(lax.axis_size(axis))])


def pick(values, index, axis):
    return lax.dynamic_index_in_dim(values, index, axis, keepdims=False)


class Place:
    def __init__(self):
        self.seq_count = lax.axis_size("seq")
        self.mp_count = lax.axis_size("mp")
        self.seq = lax.axis_index("seq")
        self.mp = lax.axis_index("mp")
        self.seq_low = self.seq % 2


def gather_weight(shard, place):
    height, breadth = shard.shape
    half = height // 2
    mine = lax.dynamic_slice(shard, (place.seq_low * half, 0), (half, breadth))
    first = swap(mine, "mp", 2)
    second = swap(first, "seq", 1)
    near_other = swap(shard, "mp", 1)
    far = jnp.zeros((height, breadth), shard.dtype)
    far = lax.dynamic_update_slice(far, first, (place.seq_low * half, 0))
    far = lax.dynamic_update_slice(far, second, ((1 - place.seq_low) * half, 0))
    far_other = swap(far, "mp", 1)
    whole = jnp.zeros((height * place.mp_count, breadth), shard.dtype)
    for flip, piece in ((0, shard), (1, near_other), (2, far), (3, far_other)):
        whole = lax.dynamic_update_slice(whole, piece, ((place.mp ^ flip) * height, 0))
    return whole


def line_scatter(blocks, place):
    count = place.seq_count // 2
    position = place.seq // 2
    size = 2 * count
    state = blocks
    up_in = down_in = None
    for step in range(1, count):
        up_index = jnp.clip(count - step + position, 0, count - 1)
        down_index = jnp.clip(step - 1 - (count - 1 - position), 0, count - 1)
        up_perm = [(i, i + 2) for i in range(size - 2) if i // 2 < step]
        down_perm = [(i, i - 2) for i in range(2, size) if (count - 1 - i // 2) < step]
        up_out = pick(blocks, up_index, 1)
        down_out = pick(blocks, down_index, 1)
        if up_in is not None:
            up_out = up_out + up_in
            down_out = down_out + down_in
        up_in = lax.ppermute(up_out, "seq", up_perm)
        down_in = lax.ppermute(down_out, "seq", down_perm)
    own = pick(blocks, position, 1).astype(F32)
    return own + up_in.astype(F32) + down_in.astype(F32)


def weight_grad(former, latter, place, seq_first):
    height = former.shape[1] // place.mp_count
    rows = former.shape[0]
    breadth = latter.shape[1] // place.seq_count
    low = place.seq_low
    view = latter.reshape(rows, place.seq_count // 2, 2, breadth)
    half = breadth * (place.seq_count // 2)
    give = pick(view, 1 - low, 2).reshape(rows, half)
    keep = pick(view, low, 2).reshape(rows, half)
    both = jnp.concatenate([give, keep], axis=1)

    def columns(flip):
        return lax.dynamic_slice(former, (0, (place.mp ^ flip) * height), (rows, height))

    own, other, far, far_other = (columns(flip) for flip in (0, 1, 2, 3))
    part = inner_left(jnp.concatenate([far_other, other], axis=1), both).astype(BF)
    part = swap(part, "mp", 1).astype(F32)
    if seq_first:
        send = inner_left(jnp.concatenate([far, own], axis=1), give) + part[:, :half]
        low_in = swap(send.astype(BF), "seq", 1).astype(F32)
        send = inner_left(far, keep) + part[:height, half:] + low_in[:height]
        far_in = swap(send.astype(BF), "mp", 2).astype(F32)
        total = inner_left(own, keep) + part[height:, half:] + low_in[height:] + far_in
    else:
        send = inner_left(far, both) + part[:height]
        far_in = swap(send.astype(BF), "mp", 2).astype(F32)
        send = inner_left(own, give) + part[height:, :half] + far_in[:, :half]
        low_in = swap(send.astype(BF), "seq", 1).astype(F32)
        total = inner_left(own, keep) + part[height:, half:] + far_in[:, half:] + low_in
    return total.astype(BF).reshape(height, place.seq_count // 2, breadth)


def finish_grads(partials, place):
    sizes = [part.shape[2] for part in partials]
    total = line_scatter(jnp.concatenate(partials, axis=2), place)
    pieces, start = [], 0
    for size in sizes:
        pieces.append(total[:, start : start + size])
        start += size
    return pieces


def sum_everywhere(values, place):
    for axis, count in (("mp", place.mp_count), ("seq", place.seq_count)):
        bit = 1
        while bit < count:
            values = values + swap(values, axis, bit)
            bit *= 2
    return values


def front_pass(hidden, weights):
    normed = rms_scale(hidden, weights[0].astype(F32)).astype(BF)
    projected = matmul(normed, weights[1]).astype(BF)
    return (normed, projected)


def rear_pass(hidden, attended, weights):
    mixed_sum = hidden + matmul(attended, weights[2])
    normed_two = rms_scale(mixed_sum, weights[3].astype(F32)).astype(BF)
    expanded = matmul(normed_two, weights[4])
    activated = jax.nn.gelu(expanded).astype(BF)
    result = mixed_sum + matmul(activated, weights[5])
    return (result, (mixed_sum, normed_two, expanded, activated))


def rear_grads(result_grad, saved_state, weights):
    mixed_sum, normed_two, expanded, activated = saved_state
    contract_input = result_grad.astype(BF)
    active_grad = inner_right(contract_input, weights[5])
    expand_input = jax.vjp(jax.nn.gelu, expanded)[1](active_grad)[0].astype(BF)
    normed_grad = inner_right(expand_input, weights[4])
    mixed_part, postnorm_grad = jax.vjp(rms_scale, mixed_sum, weights[3].astype(F32))[1](
        normed_grad
    )
    mixed_grad = result_grad + mixed_part
    output_input = mixed_grad.astype(BF)
    attended_grad = inner_right(output_input, weights[2]).astype(BF)
    return (mixed_grad, attended_grad, postnorm_grad, contract_input, expand_input, output_input)


def front_grads(hidden, projected_grad, mixed_grad, weights):
    normed_grad = inner_right(projected_grad, weights[1])
    hidden_part, prenorm_grad = jax.vjp(rms_scale, hidden, weights[0].astype(F32))[1](normed_grad)
    return (mixed_grad + hidden_part, prenorm_grad)


def portions_of(queries, keys, allowed):
    scores = jnp.einsum("ihd,jhd->hij", queries, keys, preferred_element_type=F32) * FACTOR
    return jax.nn.softmax(jnp.where(allowed[None], scores, MASKED), axis=-1)


def attend(queries, keys, values, allowed):
    portions = portions_of(queries, keys, allowed)
    return jnp.einsum(
        "hij,jhd->ihd", portions.astype(BF), values, preferred_element_type=F32
    ).astype(BF)


def attend_grads(queries, keys, values, allowed, out_grad):
    portions = portions_of(queries, keys, allowed)
    portion_grad = jnp.einsum("ihd,jhd->hij", out_grad, values, preferred_element_type=F32)
    score_grad = (
        portions * (portion_grad - jnp.sum(portions * portion_grad, axis=-1, keepdims=True))
    ).astype(BF)
    query_grad = (
        jnp.einsum("hij,jhd->ihd", score_grad, keys, preferred_element_type=F32) * FACTOR
    )
    key_grad = (
        jnp.einsum("hij,ihd->jhd", score_grad, queries, preferred_element_type=F32) * FACTOR
    )
    value_grad = jnp.einsum("hij,ihd->jhd", portions.astype(BF), out_grad, preferred_element_type=F32)
    return query_grad, key_grad, value_grad


def to_heads(values, place):
    rows, own, parts, width = values.shape
    count = place.seq_count
    view = values.reshape(rows, own, parts, count, width // count)
    moved = lax.all_to_all(
        jnp.transpose(view, (3, 0, 1, 2, 4)), "seq", split_axis=0, concat_axis=0, tiled=True
    )
    return jnp.transpose(moved, (1, 0, 2, 3, 4)).reshape(rows, count * own, parts, width // count)


def to_frames(values, place):
    rows, total, parts, width = values.shape
    count = place.seq_count
    view = values.reshape(rows, count, total // count, parts, width)
    moved = lax.all_to_all(
        jnp.transpose(view, (1, 0, 2, 3, 4)), "seq", split_axis=0, concat_axis=0, tiled=True
    )
    return jnp.transpose(moved, (1, 2, 3, 0, 4)).reshape(
        rows, total // count, parts, count * width
    )


def allowed_of(query_seg, key_seg, query_pos, key_pos):
    return (query_seg[:, None] == key_seg[None, :]) & (key_pos[None, :] <= query_pos[:, None])


def frame_attention(projected, segments, place):
    rows, own, triple = projected.shape
    width = triple // 3
    parts = projected.reshape(rows, own, 3, width)
    every_segment = lax.all_gather(segments, "seq", axis=1, tiled=True)
    every_pos = jnp.arange(own * place.seq_count)
    if HEADS % place.seq_count == 0:
        packed = to_heads(parts, place)
        sets = [split_heads(packed[:, :, part]) for part in range(3)]

        def one_row(items):
            queries, keys, values, segs = items
            return attend(queries, keys, values, allowed_of(segs, segs, every_pos, every_pos))

        attended = lax.map(one_row, (*sets, every_segment))
        attended = to_frames(attended.reshape(rows, own * place.seq_count, 1, -1), place)

        def backward(out_grad):
            grads = to_heads(out_grad.reshape(rows, own, 1, width), place)[:, :, 0]

            def one_row(items):
                queries, keys, values, segs, grad = items
                return attend_grads(
                    queries, keys, values, allowed_of(segs, segs, every_pos, every_pos), grad
                )

            found = lax.map(one_row, (*sets, every_segment, split_heads(grads)))
            packed_grad = jnp.stack(
                [grad.reshape(rows, own * place.seq_count, -1) for grad in found], axis=2
            ).astype(BF)
            return to_frames(packed_grad, place).reshape(rows, own, triple)

        return attended.reshape(rows, own, width), backward

    keys = lax.all_gather(parts[:, :, 1], "seq", axis=1, tiled=True)
    values = lax.all_gather(parts[:, :, 2], "seq", axis=1, tiled=True)
    sets = (split_heads(parts[:, :, 0]), split_heads(keys), split_heads(values))
    own_pos = place.seq * own + jnp.arange(own)

    def one_row(items):
        row_q, row_k, row_v, own_segs, segs = items
        return attend(row_q, row_k, row_v, allowed_of(own_segs, segs, own_pos, every_pos))

    attended = lax.map(one_row, (*sets, segments, every_segment)).reshape(rows, own, width)

    def backward(out_grad):
        def one_row(items):
            row_q, row_k, row_v, own_segs, segs, grad = items
            allowed = allowed_of(own_segs, segs, own_pos, every_pos)
            return attend_grads(row_q, row_k, row_v, allowed, grad)

        query_grad, key_grad, value_grad = lax.map(
            one_row, (*sets, segments, every_segment, split_heads(out_grad))
        )
        both = jnp.stack([key_grad.reshape(rows, -1, width), value_grad.reshape(rows, -1, width)], 2)
        both = lax.psum_scatter(both, "seq", scatter_dimension=1, tiled=True)
        parts_grad = [query_grad.reshape(rows, own, width), both[:, :, 0], both[:, :, 1]]
        return jnp.concatenate(parts_grad, axis=-1).astype(BF)

    return attended, backward


def head_sums(values, marks):
    return jnp.dot(values, marks, precision=lax.Precision.HIGHEST, preferred_element_type=F32)


def head_spread(values, marks):
    return lax.dot_general(
        values.astype(BF), marks.astype(BF), (((1,), (1,)), ((), ())), preferred_element_type=F32
    )


def codec_softmax(queries, keys, marks):
    result = []
    for later in range(len(queries)):
        scores = [
            head_sums(queries[later].astype(F32) * keys[earlier].astype(F32), marks) * FACTOR
            for earlier in range(later + 1)
        ]
        top = scores[0]
        for score in scores[1:]:
            top = jnp.maximum(top, score)
        powers = [jnp.exp(score - top) for score in scores]
        total = sum(powers)
        result.append([power / total for power in powers])
    return result


def codec_attend(soft, values, marks):
    result = []
    for row in soft:
        total = 0.0
        for earlier, portion in enumerate(row):
            total = total + head_spread(portion, marks) * values[earlier].astype(F32)
        result.append(total.astype(BF))
    return result


def codec_attend_grads(soft, queries, keys, values, grads, marks):
    count = len(queries)
    query_grad = []
    key_grad = [0.0] * count
    value_grad = [0.0] * count
    for later in range(count):
        grad = grads[later].astype(F32)
        portion_grads = [
            head_sums(grad * values[earlier].astype(F32), marks) for earlier in range(later + 1)
        ]
        mean = sum(soft[later][i] * portion_grads[i] for i in range(later + 1))
        total = 0.0
        for earlier in range(later + 1):
            score_grad = soft[later][earlier] * (portion_grads[earlier] - mean)
            wide = head_spread(score_grad, marks)
            total = total + wide * keys[earlier].astype(F32)
            key_grad[earlier] = key_grad[earlier] + wide * queries[later].astype(F32)
            value_grad[earlier] = value_grad[earlier] + head_spread(soft[later][earlier], marks) * grad
        query_grad.append(total * FACTOR)
    return jnp.concatenate(
        [
            jnp.concatenate(
                [query_grad[t], key_grad[t] * FACTOR, value_grad[t]], axis=-1
            ).astype(BF)
            for t in range(count)
        ],
        axis=0,
    )


LANES = 128
TILE = 256
VMEM_LIMIT = 48 * 1024 * 1024
HINT = pl.CostEstimate(flops=1, bytes_accessed=1, transcendentals=0)


def whole_block(shape):
    return pl.BlockSpec(shape, lambda *_: (0,) * len(shape))


def causal_tiles(length):
    tile = min(TILE, length)
    return [(start, tile, start + tile) for start in range(0, length, tile)]


def head_masks(dtype):
    lane = lax.broadcasted_iota(jnp.int32, (1, LANES), 1)
    return [((lane // HEAD) == head).astype(dtype) for head in range(LANES // HEAD)]


def frame_attend_kernel(packed_ref, seg_col_ref, seg_row_ref, out_ref):
    chunks, _, own, _ = packed_ref.shape
    length = chunks * own
    packed = packed_ref[...].reshape(length, 3 * LANES)
    queries, keys, values = (packed[:, LANES * i : LANES * (i + 1)] for i in range(3))
    masks = head_masks(BF)
    lane = lax.broadcasted_iota(jnp.int32, (1, LANES), 1)
    for start, tile, end in causal_tiles(length):
        query_pos = start + lax.broadcasted_iota(jnp.int32, (tile, end), 0)
        key_pos = lax.broadcasted_iota(jnp.int32, (tile, end), 1)
        allowed = (seg_col_ref[0, start:end] == seg_row_ref[0, :, :end]) & (key_pos <= query_pos)
        result = jnp.zeros((tile, LANES), F32)
        for head, mask in enumerate(masks):
            scores = inner_right(queries[start:end] * mask, keys[:end]) * FACTOR
            scores = jnp.where(allowed, scores, MASKED)
            powers = jnp.exp(scores - jnp.max(scores, axis=1, keepdims=True))
            portions = powers / jnp.sum(powers, axis=1, keepdims=True)
            found = matmul(portions.astype(BF), values[:end])
            result = jnp.where(lane // HEAD == head, found, result)
        out_ref[start // own : end // own, 0] = result.astype(BF).reshape(tile // own, own, LANES)


def frame_attend_grads_kernel(packed_ref, grad_ref, seg_col_ref, seg_row_ref, out_ref, key_sum, value_sum):
    chunks, _, own, _ = packed_ref.shape
    length = chunks * own
    packed = packed_ref[...].reshape(length, 3 * LANES)
    queries, keys, values = (packed[:, LANES * i : LANES * (i + 1)] for i in range(3))
    grads = grad_ref[...].reshape(length, LANES)
    masks = head_masks(BF)
    lane = lax.broadcasted_iota(jnp.int32, (1, LANES), 1)
    key_sum[...] = jnp.zeros_like(key_sum)
    value_sum[...] = jnp.zeros_like(value_sum)
    for start, tile, end in causal_tiles(length):
        key_pos = lax.broadcasted_iota(jnp.int32, (end, tile), 0)
        query_pos = start + lax.broadcasted_iota(jnp.int32, (end, tile), 1)
        allowed = (seg_col_ref[0, :end] == seg_row_ref[0, :, start:end]) & (key_pos <= query_pos)
        query_grad = jnp.zeros((tile, LANES), F32)
        for head, mask in enumerate(masks):
            query = queries[start:end] * mask
            grad = grads[start:end] * mask
            scores = inner_right(keys[:end], query) * FACTOR
            scores = jnp.where(allowed, scores, MASKED)
            powers = jnp.exp(scores - jnp.max(scores, axis=0, keepdims=True))
            portions = powers / jnp.sum(powers, axis=0, keepdims=True)
            portion_grad = inner_right(values[:end], grad)
            mean = jnp.sum(portions * portion_grad, axis=0, keepdims=True)
            score_grad = (portions * (portion_grad - mean)).astype(BF)
            key_sum[:end] += matmul(score_grad, query)
            value_sum[:end] += matmul(portions.astype(BF), grad)
            found = inner_left(score_grad, keys[:end])
            query_grad = jnp.where(lane // HEAD == head, found, query_grad)
        out_ref[start // own : end // own, 0, :, :LANES] = (
            (query_grad * FACTOR).astype(BF).reshape(tile // own, own, LANES)
        )
    out_ref[:, 0, :, LANES : 2 * LANES] = (key_sum[...] * FACTOR).astype(BF).reshape(chunks, own, LANES)
    out_ref[:, 0, :, 2 * LANES :] = value_sum[...].astype(BF).reshape(chunks, own, LANES)


def row_spec(chunks, own, breadth):
    return pl.BlockSpec((chunks, 1, own, breadth), lambda row: (0, row, 0, 0))


def segment_specs(length):
    return [
        pl.BlockSpec((1, length, 1), lambda row: (row, 0, 0)),
        pl.BlockSpec((1, 1, length), lambda row: (row, 0, 0)),
    ]


def frame_attend_call(packed, segments):
    chunks, rows, own, _ = packed.shape
    length = chunks * own
    return pl.pallas_call(
        frame_attend_kernel,
        grid=(rows,),
        in_specs=[row_spec(chunks, own, 3 * LANES), *segment_specs(length)],
        out_specs=row_spec(chunks, own, LANES),
        out_shape=jax.ShapeDtypeStruct((chunks, rows, own, LANES), BF),
        compiler_params=pltpu.CompilerParams(vmem_limit_bytes=VMEM_LIMIT),
        cost_estimate=HINT,
        name="frame_attend",
    )(packed, segments[:, :, None], segments[:, None, :])


def frame_attend_grads_call(packed, grads, segments):
    chunks, rows, own, _ = packed.shape
    length = chunks * own
    return pl.pallas_call(
        frame_attend_grads_kernel,
        grid=(rows,),
        in_specs=[
            row_spec(chunks, own, 3 * LANES),
            row_spec(chunks, own, LANES),
            *segment_specs(length),
        ],
        out_specs=row_spec(chunks, own, 3 * LANES),
        out_shape=jax.ShapeDtypeStruct((chunks, rows, own, 3 * LANES), BF),
        scratch_shapes=[pltpu.VMEM((length, LANES), F32), pltpu.VMEM((length, LANES), F32)],
        compiler_params=pltpu.CompilerParams(vmem_limit_bytes=VMEM_LIMIT),
        cost_estimate=HINT,
        name="frame_attend_grads",
    )(packed, grads, segments[:, :, None], segments[:, None, :])


def position_pairs(positions):
    return [(later, earlier) for later in range(1, positions) for earlier in range(later + 1)]


def codec_sums(products, marks):
    stacked = jnp.concatenate(products, axis=0)
    high = stacked.astype(BF)
    low = (stacked - high.astype(F32)).astype(BF)
    total = matmul(high, marks) + matmul(low, marks)
    size = products[0].shape[0]
    return [total[size * i : size * (i + 1)] for i in range(len(products))]


def codec_spread(portions, marks):
    stacked = jnp.concatenate([portion.astype(BF) for portion in portions], axis=0)
    total = inner_right(stacked, marks)
    size = portions[0].shape[0]
    return [total[size * i : size * (i + 1)] for i in range(len(portions))]


def codec_portions(queries, keys, marks, pairs):
    scores = codec_sums(
        [queries[later].astype(F32) * keys[earlier].astype(F32) for later, earlier in pairs], marks
    )
    scores = dict(zip(pairs, [score * FACTOR for score in scores]))
    portions = {}
    for later in range(1, len(queries)):
        row = [scores[later, earlier] for earlier in range(later + 1)]
        top = functools.reduce(jnp.maximum, row)
        powers = [jnp.exp(score - top) for score in row]
        total = functools.reduce(jnp.add, powers)
        for earlier in range(later + 1):
            portions[later, earlier] = powers[earlier] / total
    return portions


def codec_parts(packed_ref, width):
    positions = packed_ref.shape[0]
    return [
        [packed_ref[t, :, width * part : width * (part + 1)] for t in range(positions)]
        for part in range(3)
    ]


def codec_attend_kernel(packed_ref, normed_ref, marks_ref, out_ref):
    positions, _, width = normed_ref.shape
    out_ref[:, :, :width] = normed_ref[...]
    queries, keys, values = codec_parts(packed_ref, width)
    marks = marks_ref[...]
    pairs = position_pairs(positions)
    portions = codec_portions(queries, keys, marks, pairs)
    wide = dict(zip(pairs, codec_spread([portions[pair] for pair in pairs], marks)))
    out_ref[0, :, width:] = values[0]
    for later in range(1, positions):
        terms = [wide[later, e] * values[e].astype(F32) for e in range(later + 1)]
        out_ref[later, :, width:] = functools.reduce(jnp.add, terms).astype(BF)


def codec_attend_grads_kernel(packed_ref, grad_ref, marks_ref, out_ref):
    positions, _, width = grad_ref.shape
    queries, keys, values = codec_parts(packed_ref, width)
    marks = marks_ref[...]
    pairs = position_pairs(positions)
    portions = codec_portions(queries, keys, marks, pairs)
    grads = [grad_ref[t].astype(F32) for t in range(positions)]
    portion_grads = dict(
        zip(
            pairs,
            codec_sums([grads[later] * values[earlier].astype(F32) for later, earlier in pairs], marks),
        )
    )
    score_grads = {}
    for later in range(1, positions):
        mean = functools.reduce(
            jnp.add, [portions[later, e] * portion_grads[later, e] for e in range(later + 1)]
        )
        for e in range(later + 1):
            score_grads[later, e] = portions[later, e] * (portion_grads[later, e] - mean)
    wide = dict(zip(pairs, codec_spread([portions[pair] for pair in pairs], marks)))
    wide_grads = dict(zip(pairs, codec_spread([score_grads[pair] for pair in pairs], marks)))
    zero = jnp.zeros_like(grads[0])
    for t in range(positions):
        query_grad = key_grad = zero
        value_grad = grads[0] if t == 0 else zero
        for later, earlier in pairs:
            if later == t:
                query_grad = query_grad + wide_grads[later, earlier] * keys[earlier].astype(F32)
            if earlier == t:
                key_grad = key_grad + wide_grads[later, earlier] * queries[later].astype(F32)
                value_grad = value_grad + wide[later, earlier] * grads[later]
        out_ref[t, :, :width] = (query_grad * FACTOR).astype(BF)
        out_ref[t, :, width : 2 * width] = (key_grad * FACTOR).astype(BF)
        out_ref[t, :, 2 * width :] = value_grad.astype(BF)


def codec_tile(frame_total):
    return 64 if frame_total % 64 == 0 else frame_total


def codec_spec(positions, tile, breadth):
    return pl.BlockSpec((positions, tile, breadth), lambda i: (0, i, 0))


def head_marks(width):
    return (
        jnp.arange(width)[:, None] // HEAD == jnp.arange(LANES)[None, :]
    ).astype(BF)


def codec_attend_call(packed, normed):
    positions, total, triple = packed.shape
    width = triple // 3
    tile = codec_tile(total)
    return pl.pallas_call(
        codec_attend_kernel,
        grid=(total // tile,),
        in_specs=[
            codec_spec(positions, tile, triple),
            codec_spec(positions, tile, width),
            whole_block((width, LANES)),
        ],
        out_specs=codec_spec(positions, tile, 2 * width),
        out_shape=jax.ShapeDtypeStruct((positions, total, 2 * width), BF),
        compiler_params=pltpu.CompilerParams(vmem_limit_bytes=VMEM_LIMIT),
        cost_estimate=HINT,
        name="codec_attend",
    )(packed, normed.reshape(positions, total, width), head_marks(width))


def codec_attend_grads_call(packed, grads):
    positions, total, triple = packed.shape
    width = triple // 3
    tile = codec_tile(total)
    return pl.pallas_call(
        codec_attend_grads_kernel,
        grid=(total // tile,),
        in_specs=[
            codec_spec(positions, tile, triple),
            codec_spec(positions, tile, width),
            whole_block((width, LANES)),
        ],
        out_specs=codec_spec(positions, tile, triple),
        out_shape=jax.ShapeDtypeStruct((positions, total, triple), BF),
        compiler_params=pltpu.CompilerParams(vmem_limit_bytes=VMEM_LIMIT),
        cost_estimate=HINT,
        name="codec_attend_grads",
    )(packed, grads, head_marks(width))


BITS = {"y": ("mp", 2), "x": ("seq", 1), "n": ("seq", 2), "f": ("seq", 4)}


def grad_order(place):
    flips = []
    for bits in ((1, 2, 4), (2, 1, 4), (1, 2, 4)):
        for step in range(8):
            flips.append(sum(bit for at, bit in enumerate(bits) if not (step >> (2 - at)) & 1))
    return jnp.stack(
        [place.mp ^ 2, place.mp] + [place.seq ^ flip for flip in flips] + [place.seq]
    ).astype(jnp.int32)


STEPS = {"y": (2, "xnf"), "n": (10, "nxf"), "x": (18, "xnf")}
OWN_SEQ = 26


def keep_flags(order_ref, seq):
    change = order_ref[OWN_SEQ] ^ seq
    return {"x": 1 - (change & 1), "n": 1 - ((change >> 1) & 1), "f": 1 - ((change >> 2) & 1)}


def grad_rows_kernel(stages, wide, order_ref, far_own, far_rec, own_own, own_rec, latter_own, latter_rec, *refs):
    send_ref, keep_ref, turned = refs[-3:]
    rows = latter_own.shape[0]
    height = far_own.shape[1]

    @pl.when(pl.program_id(0) == 0)
    def _():
        for at, (own, rec) in enumerate(((far_own, far_rec), (own_own, own_rec))):
            turned[height * at : height * (at + 1), :rows] = own[...].T
            turned[height * at : height * (at + 1), rows:] = rec[...].T

    total = matmul(turned[:, :rows], latter_own[...]) + matmul(turned[:, rows:], latter_rec[...])
    store = grad_store_wide if wide else grad_store
    store(stages, order_ref, total.astype(BF), height, send_ref, keep_ref)


def grad_store_wide(stages, order_ref, total, height, send_ref, keep_ref):
    units = height // TILE
    chunks = total.shape[1] // 8 // LANES
    for seq in range(8):
        flags = keep_flags(order_ref, seq)
        for chunk in range(chunks):
            first = (seq * chunks + chunk) * LANES
            for unit in range(units):
                at = chunk * units + unit
                for kept in range(2):
                    start = height * kept + unit * TILE
                    value = total[start : start + TILE, first : first + LANES]
                    spot = {**flags, "y": kept}
                    where = tuple(spot[stage] for stage in stages[1:])
                    for target, when in ((send_ref, 0), (keep_ref, 1)):

                        @pl.when(spot[stages[0]] == when)
                        def _(target=target, where=where, at=at, value=value):
                            target[(*where, at)] = value


def grad_store(stages, order_ref, total, height, send_ref, keep_ref):
    chunks = total.shape[1] // LANES
    for chunk in range(chunks):
        value = total[:, chunk * LANES : (chunk + 1) * LANES]
        given, kept = value[:height], value[height:]
        if stages[0] == "y":
            send_ref[0, 0, 0, chunk] = given
            keep_ref[0, 0, 0, chunk] = kept
        else:
            spots = [tuple(side if stage == "y" else 0 for stage in stages[1:]) for side in range(2)]
            for target, when in ((send_ref, pl.program_id(0) < 4), (keep_ref, pl.program_id(0) >= 4)):

                @pl.when(when)
                def _(target=target, given=given, kept=kept, chunk=chunk):
                    target[(*spots[0], chunk)] = given
                    target[(*spots[1], chunk)] = kept


def grad_buffers(units):
    return [jax.ShapeDtypeStruct((2, 2, 2, units, TILE, LANES), BF)] * 2


def grad_call(kernel, order, arrays, in_specs, out_specs, units, into, steps, scratch, flops, name):
    aliases = {}
    moved = 2 * sum(array.size for array in arrays)
    if into is not None:
        aliases = {len(arrays) + 1: 0, len(arrays) + 2: 1}
        in_specs = in_specs + [pl.BlockSpec(memory_space=pl.ANY)] * 2
        arrays = arrays + list(into)
    return pl.pallas_call(
        kernel,
        grid_spec=pltpu.PrefetchScalarGridSpec(
            num_scalar_prefetch=1,
            grid=(steps,),
            in_specs=in_specs,
            out_specs=out_specs,
            scratch_shapes=[scratch],
        ),
        out_shape=grad_buffers(units),
        input_output_aliases=aliases,
        compiler_params=pltpu.CompilerParams(vmem_limit_bytes=VMEM_LIMIT),
        cost_estimate=HINT,
        name=name,
    )(order, *arrays)


def grad_rows(former, latter, order, stages, units, offset, into=None):
    former, skip, height = former
    latter, latter_skip, breadth = latter
    rows = latter[0].shape[0]
    height = height // 4
    skip = skip // height
    wide = breadth // 8 == LANES
    chunks = breadth // 8 // LANES
    steps = 1 if wide else 8
    arrays = [former[0], former[1], former[0], former[1], latter[0], latter[1]]
    former_specs = [
        pl.BlockSpec((rows, height), lambda j, t, at=at: (0, skip + t[at]), pipeline_mode=pl.Buffered(1))
        for at in (0, 0, 1, 1)
    ]
    if wide:
        latter_specs = [
            pl.BlockSpec((rows, breadth), lambda j, t: (0, latter_skip // breadth))
        ] * 2
        block = (2, 2, 2, 1, TILE, LANES)
        out_specs = [pl.BlockSpec(block, lambda j, t: (0, 0, 0, offset, 0, 0))] * 2
    else:
        base = offset // chunks
        table, names = STEPS[stages[0]]
        bits = {name: 2 - at for at, name in enumerate(names)}
        if stages[0] == "y":
            block = (1, 1, 1, chunks, TILE, LANES)

            def where(j):
                return tuple((j >> bits[stage]) & 1 for stage in stages[1:]) + (base, 0, 0)

            out_specs = [pl.BlockSpec(block, lambda j, t: where(j))] * 2
        else:
            block = tuple(2 if stage == "y" else 1 for stage in stages[1:]) + (chunks, TILE, LANES)

            def where(j):
                return tuple(
                    0 if stage == "y" else (j >> bits[stage]) & 1 for stage in stages[1:]
                ) + (base, 0, 0)

            out_specs = [
                pl.BlockSpec(block, lambda j, t: where(jnp.minimum(j, 3))),
                pl.BlockSpec(block, lambda j, t: where(jnp.maximum(j - 4, 0))),
            ]
        latter_specs = [
            pl.BlockSpec(
                (rows, breadth // 8),
                lambda j, t: (0, latter_skip // (breadth // 8) + t[table + j]),
            )
        ] * 2
    return grad_call(
        functools.partial(grad_rows_kernel, stages, wide),
        order,
        arrays,
        former_specs + latter_specs,
        out_specs,
        units,
        into,
        steps,
        pltpu.VMEM((2 * height, 2 * rows), BF),
        2 * 2 * rows * 2 * height * breadth,
        "grad_rows",
    )


def grad_columns_kernel(stages, order_ref, latter_own, latter_rec, former_own, former_rec, *refs):
    send_ref, keep_ref, turned = refs[-3:]
    rows = latter_own.shape[0]
    step = pl.program_id(0)

    @pl.when(step == 0)
    def _():
        turned[:, :rows] = latter_own[...].T
        turned[:, rows:] = latter_rec[...].T

    total = matmul(turned[:, :rows], former_own[...]) + matmul(turned[:, rows:], former_rec[...])
    total = total.astype(BF)
    chunks = total.shape[1] // LANES
    for target, when in ((send_ref, step < pl.num_programs(0) // 2), (keep_ref, step >= pl.num_programs(0) // 2)):

        @pl.when(when)
        def _(target=target):
            for seq in range(8):
                flags = keep_flags(order_ref, seq)
                where = tuple(flags[stage] for stage in stages[1:])
                for chunk in range(chunks):
                    half = (chunk % 2) * LANES
                    target[(*where, chunk // 2, slice(half, half + LANES))] = total[
                        seq * LANES : (seq + 1) * LANES, chunk * LANES : (chunk + 1) * LANES
                    ]


def grad_columns(former, latter, order, stages, units, offset, into=None):
    former, skip, height = former
    latter, latter_skip, breadth = latter
    rows = latter[0].shape[0]
    height = height // 4
    step = min(512, height)
    per = height // step
    block = (2, 2, 2, step // TILE, TILE, LANES)
    base = offset // (step // TILE)
    latter_specs = [
        pl.BlockSpec(
            (rows, breadth), lambda j, t: (0, latter_skip // breadth), pipeline_mode=pl.Buffered(1)
        )
    ] * 2
    former_specs = [
        pl.BlockSpec((rows, step), lambda j, t: (0, skip // step + t[j // per] * per + j % per))
    ] * 2
    out_specs = [
        pl.BlockSpec(block, lambda j, t: (0, 0, 0, base + jnp.minimum(j, per - 1), 0, 0)),
        pl.BlockSpec(block, lambda j, t: (0, 0, 0, base + jnp.maximum(j - per, 0), 0, 0)),
    ]
    return grad_call(
        functools.partial(grad_columns_kernel, stages),
        order,
        [latter[0], latter[1], former[0], former[1]],
        latter_specs + former_specs,
        out_specs,
        units,
        into,
        2 * per,
        pltpu.VMEM((breadth, 2 * rows), BF),
        2 * 2 * rows * 2 * height * breadth,
        "grad_columns",
    )


def grad_table_kernel(stages, height, order_ref, codes_ref, latter_own, latter_rec, *refs):
    send_ref, keep_ref, _ = refs[-3:]
    rows = latter_own.shape[0]
    parts = []
    for at in range(2):
        entry = order_ref[at] * height + lax.broadcasted_iota(jnp.int32, (height, 2 * rows), 0)
        parts.append((entry == codes_ref[...]).astype(F32).astype(BF))
    chosen = jnp.concatenate(parts, axis=0)
    total = matmul(chosen[:, :rows], latter_own[...]) + matmul(chosen[:, rows:], latter_rec[...])
    grad_store_wide(stages, order_ref, total.astype(BF), height, send_ref, keep_ref)


def grad_table(codes, latter, order, stages, height, units, offset, into=None):
    rows, breadth = latter[0].shape
    block = (2, 2, 2, height // TILE, TILE, LANES)
    base = offset // (height // TILE)
    return grad_call(
        functools.partial(grad_table_kernel, stages, height),
        order,
        [codes, latter[0], latter[1]],
        [whole_block(codes.shape), whole_block((rows, breadth)), whole_block((rows, breadth))],
        [pl.BlockSpec(block, lambda j, t: (0, 0, 0, base, 0, 0))] * 2,
        units,
        into,
        1,
        pltpu.VMEM((8, LANES), F32),
        2 * 2 * rows * 2 * height * breadth,
        "grad_table",
    )


def rows_from_units(units, height):
    tiles = height // TILE
    chunks = units.shape[0] // tiles
    return jnp.transpose(
        units.reshape(chunks, height, LANES), (1, 0, 2)
    ).reshape(height, chunks * LANES)


def columns_from_units(units):
    count = units.shape[0]
    return jnp.transpose(units.reshape(2 * count, LANES, LANES), (0, 2, 1)).reshape(count * TILE, LANES)


PACK = 1024


def pack_rows(members):
    return sum(member.shape[0] * (member.shape[1] // PACK) for member in members)


def pack_pieces(shapes):
    found, start = [], 0
    for at, (height, breadth) in enumerate(shapes):
        for column in range(breadth // PACK):
            found.append((at, column, height, start))
            start += height
    return found


def columns_of(column):
    return pl.ds(column * PACK, PACK)


def pack_kernel(place_ref, *refs):
    members, (pack_ref, quarter_ref, held, sems, out_sems) = refs[:-5], refs[-5:]
    rows = held.shape[0] // 4
    copies = []
    for number, (at, column, height, start) in enumerate(pack_pieces([m.shape for m in members])):
        copies.append(
            pltpu.make_async_copy(
                members[at].at[:, columns_of(column)], held.at[pl.ds(start, height)], sems.at[number]
            )
        )
    for copy in copies:
        copy.start()
    for copy in copies:
        copy.wait()
    mine = pl.ds(pl.multiple_of(place_ref[1] * rows, 16), rows)
    whole = pltpu.make_async_copy(held, pack_ref, out_sems.at[0])
    part = pltpu.make_async_copy(held.at[mine], quarter_ref, out_sems.at[1])
    part.start()
    whole.start()
    part.wait()
    whole.wait()


def pack_call(members, spots):
    rows = pack_rows(members)
    any_spec = pl.BlockSpec(memory_space=pl.ANY)
    count = len(pack_pieces([m.shape for m in members]))
    return pl.pallas_call(
        pack_kernel,
        in_specs=[pl.BlockSpec(memory_space=pltpu.SMEM)] + [any_spec] * len(members),
        out_specs=[any_spec] * 2,
        out_shape=[
            jax.ShapeDtypeStruct((rows, PACK), BF),
            jax.ShapeDtypeStruct((rows // 4, PACK), BF),
        ],
        scratch_shapes=[
            pltpu.VMEM((rows, PACK), BF),
            pltpu.SemaphoreType.DMA((count,)),
            pltpu.SemaphoreType.DMA((2,)),
        ],
        compiler_params=pltpu.CompilerParams(vmem_limit_bytes=VMEM_LIMIT),
        cost_estimate=HINT,
        name="pack_weights",
    )(spots, *members)


def far_kernel(parts, place_ref, *refs):
    pieces, (out_ref, held, sems, out_sem) = refs[:-4], refs[-4:]
    quarter = held.shape[0] // 4
    copies = []
    for number, (piece, (change, offset)) in enumerate(zip(pieces, parts)):
        start = (place_ref[1] ^ change) * quarter + offset
        copies.append(
            pltpu.make_async_copy(
                piece, held.at[pl.ds(pl.multiple_of(start, 16), piece.shape[0])], sems.at[number]
            )
        )
    for copy in copies:
        copy.start()
    for copy in copies:
        copy.wait()
    whole = pltpu.make_async_copy(held, out_ref, out_sem.at[0])
    whole.start()
    whole.wait()


def far_pack(pieces, parts, spots):
    rows = sum(piece.shape[0] for piece in pieces)
    any_spec = pl.BlockSpec(memory_space=pl.ANY)
    return pl.pallas_call(
        functools.partial(far_kernel, parts),
        in_specs=[pl.BlockSpec(memory_space=pltpu.SMEM)] + [any_spec] * len(pieces),
        out_specs=any_spec,
        out_shape=jax.ShapeDtypeStruct((rows, PACK), BF),
        scratch_shapes=[
            pltpu.VMEM((rows, PACK), BF),
            pltpu.SemaphoreType.DMA((len(pieces),)),
            pltpu.SemaphoreType.DMA((1,)),
        ],
        compiler_params=pltpu.CompilerParams(vmem_limit_bytes=VMEM_LIMIT),
        cost_estimate=HINT,
        name="far_pack",
    )(spots, *pieces)


def join_kernel(shapes, flips, place_ref, *refs):
    count = len(flips)
    packs = refs[:count]
    outs, (held, sems, out_sems) = refs[-3 - len(shapes) : -3], refs[-3:]
    rows = held.shape[0] // count
    for number, pack in enumerate(packs):
        pltpu.make_async_copy(pack, held.at[pl.ds(number * rows, rows)], sems.at[number]).start()
    copies = []
    for number, flip in enumerate(flips):
        pltpu.make_async_copy(
            packs[number], held.at[pl.ds(number * rows, rows)], sems.at[number]
        ).wait()
        for at, column, height, start in pack_pieces(shapes):
            target = pl.multiple_of((place_ref[0] ^ flip) * height, height)
            copies.append(
                pltpu.make_async_copy(
                    held.at[pl.ds(number * rows + start, height)],
                    outs[at].at[pl.ds(target, height), columns_of(column)],
                    out_sems.at[len(copies)],
                )
            )
            copies[-1].start()
    for copy in copies:
        copy.wait()


def join_weights(members, packs, flips, spots, into=None):
    shapes = [member.shape for member in members]
    rows = pack_rows(members)
    any_spec = pl.BlockSpec(memory_space=pl.ANY)
    outs = [jax.ShapeDtypeStruct((4 * height, breadth), BF) for height, breadth in shapes]
    count = len(flips)
    held = [] if into is None else list(into)
    return pl.pallas_call(
        functools.partial(join_kernel, shapes, flips),
        in_specs=[pl.BlockSpec(memory_space=pltpu.SMEM)] + [any_spec] * (count + len(held)),
        out_specs=[any_spec] * len(outs),
        out_shape=outs,
        input_output_aliases={1 + count + at: at for at in range(len(held))},
        scratch_shapes=[
            pltpu.VMEM((count * rows, PACK), BF),
            pltpu.SemaphoreType.DMA((count,)),
            pltpu.SemaphoreType.DMA((count * len(pack_pieces(shapes)),)),
        ],
        compiler_params=pltpu.CompilerParams(vmem_limit_bytes=VMEM_LIMIT),
        cost_estimate=HINT,
        name="join_weights",
    )(spots, *packs, *held)


WIDE_LIMIT = 58 * 1024 * 1024
GELU_A = 0.7978845608028654
GELU_B = 0.044715


def gelu_pair(values):
    square = values * values
    bent = jnp.tanh(GELU_A * values * (1.0 + GELU_B * square))
    half = 0.5 * (1.0 + bent)
    slope = half + 0.5 * values * (1.0 - bent * bent) * (GELU_A * (1.0 + 3.0 * GELU_B * square))
    return values * half, slope


def rms_grads(values, gain, grad):
    inverse = lax.rsqrt(jnp.mean(values * values, axis=-1, keepdims=True) + EPSILON)
    scaled = values * inverse
    inner = grad * gain
    part = inverse * (inner - scaled * jnp.mean(inner * scaled, axis=-1, keepdims=True))
    return part, jnp.sum(grad * scaled, axis=0, keepdims=True)


def held(shape):
    return pl.BlockSpec(
        shape, lambda *_: (0,) * len(shape), pipeline_mode=pl.Buffered(1)
    )


def dense_call(kernel, steps, in_specs, out_specs, out_shape, scratch, name):
    return pl.pallas_call(
        kernel,
        grid=(steps,),
        in_specs=in_specs,
        out_specs=out_specs,
        out_shape=out_shape,
        scratch_shapes=scratch,
        compiler_params=pltpu.CompilerParams(vmem_limit_bytes=WIDE_LIMIT),
        cost_estimate=HINT,
        name=name,
    )


def frame_front_kernel(hidden_ref, gain_ref, weight_ref, normed_ref, packed_ref):
    groups, rows, own, _ = packed_ref.shape

    @pl.when(pl.program_id(0) == 0)
    def _():
        normed_ref[...] = rms_scale(hidden_ref[...].astype(F32), gain_ref[...]).astype(BF)

    total = matmul(normed_ref[...], weight_ref[...]).astype(BF)
    for part in range(3):

        @pl.when(pl.program_id(0) == part)
        def _(part=part):
            for group in range(groups):
                packed_ref[group, :, :, LANES * part : LANES * (part + 1)] = total[
                    :, LANES * group : LANES * (group + 1)
                ].reshape(rows, own, LANES)


def frame_front(hidden, gain, weight, rows):
    total, width = hidden.shape
    groups = width // LANES
    shape = (groups, rows, total // rows, 3 * LANES)
    return dense_call(
        frame_front_kernel,
        3,
        [held(hidden.shape), held(gain.shape), pl.BlockSpec((width, width), lambda j: (0, j))],
        [whole_block((total, width)), whole_block(shape)],
        [jax.ShapeDtypeStruct((total, width), BF), jax.ShapeDtypeStruct(shape, BF)],
        [],
        "frame_front",
    )(hidden, gain, weight)


def frame_rear_kernel(
    hidden_ref, front_ref, packed_ref, gain_ref, output_ref, expand_ref, contract_ref,
    kept_ref, mixed_ref, slope_ref, base_ref, total, normed_ref,
):
    groups, rows, own, _ = packed_ref.shape
    width = groups * LANES
    tile = slope_ref.shape[1]

    @pl.when(pl.program_id(0) == 0)
    def _():
        for group in range(groups):
            kept_ref[:, width + LANES * group : width + LANES * (group + 1)] = packed_ref[
                group
            ].reshape(rows * own, LANES)
        attended = kept_ref[:, width : 2 * width]
        mixed = hidden_ref[...].astype(F32) + matmul(attended, output_ref[...])
        mixed_ref[...] = mixed
        total[...] = mixed
        normed_ref[...] = rms_scale(mixed, gain_ref[...]).astype(BF)
        kept_ref[:, :width] = front_ref[...]
        kept_ref[:, 2 * width : 3 * width] = normed_ref[...]

    active, slope = gelu_pair(matmul(normed_ref[...], expand_ref[...]))
    active = active.astype(BF)
    for step in range(4 * width // tile):

        @pl.when(pl.program_id(0) == step)
        def _(step=step):
            kept_ref[:, 3 * width + step * tile : 3 * width + (step + 1) * tile] = active

    slope_ref[...] = slope.astype(BF)
    total[...] += matmul(active, contract_ref[...])

    @pl.when(pl.program_id(0) == pl.num_programs(0) - 1)
    def _():
        base_ref[...] = total[...].astype(BF)


FF_TILE = 512
FRAME_TILE = 1024


def frame_rear(hidden, front, packed, gain, output, expand, contract):
    total, width = hidden.shape
    inner = expand.shape[1]
    tile = FRAME_TILE
    full = whole_block((total, width))
    kept = (total, 3 * width + inner)
    return dense_call(
        frame_rear_kernel,
        inner // tile,
        [
            held(hidden.shape),
            held(front.shape),
            held(packed.shape),
            held(gain.shape),
            held(output.shape),
            pl.BlockSpec((width, tile), lambda j: (0, j)),
            pl.BlockSpec((tile, width), lambda j: (j, 0)),
        ],
        [whole_block(kept), full, pl.BlockSpec((total, tile), lambda j: (0, j)), full],
        [
            jax.ShapeDtypeStruct(kept, BF),
            jax.ShapeDtypeStruct((total, width), F32),
            jax.ShapeDtypeStruct((total, inner), BF),
            jax.ShapeDtypeStruct((total, width), BF),
        ],
        [pltpu.VMEM((total, width), F32), pltpu.VMEM((total, width), BF)],
        "frame_rear",
    )(hidden, front, packed, gain, output, expand, contract)


def frame_rear_grads_kernel(
    grad_ref, slope_ref, mixed_ref, gain_ref, output_ref, expand_ref, contract_ref,
    kept_ref, mixed_grad_ref, packed_ref, gain_grad_ref, total,
):
    groups, rows, own, _ = packed_ref.shape
    width = groups * LANES
    tile = slope_ref.shape[1]
    grad = grad_ref[...]
    expand_in = (slope_ref[...].astype(F32) * inner_right(grad, contract_ref[...])).astype(BF)
    for step in range(4 * width // tile):

        @pl.when(pl.program_id(0) == step)
        def _(step=step):
            kept_ref[:, width + step * tile : width + (step + 1) * tile] = expand_in

    @pl.when(pl.program_id(0) == 0)
    def _():
        total[...] = jnp.zeros_like(total)
        kept_ref[:, :width] = grad

    total[...] += inner_right(expand_in, expand_ref[...])

    @pl.when(pl.program_id(0) == pl.num_programs(0) - 1)
    def _():
        part, gain_grad = rms_grads(mixed_ref[...], gain_ref[...], total[...])
        mixed_grad = grad.astype(F32) + part
        mixed_grad_ref[...] = mixed_grad
        gain_grad_ref[...] = gain_grad
        output_in = mixed_grad.astype(BF)
        kept_ref[:, 5 * width :] = output_in
        attended_grad = inner_right(output_in, output_ref[...]).astype(BF)
        for group in range(groups):
            packed_ref[group] = attended_grad[:, LANES * group : LANES * (group + 1)].reshape(
                rows, own, LANES
            )


def frame_rear_grads(grad, slope, mixed, gain, output, expand, contract, rows):
    total, width = grad.shape
    inner = expand.shape[1]
    tile = FRAME_TILE
    shape = (width // LANES, rows, total // rows, LANES)
    kept = (total, 2 * width + inner)
    full = whole_block((total, width))
    part = pl.BlockSpec((total, tile), lambda j: (0, j))
    return dense_call(
        frame_rear_grads_kernel,
        inner // tile,
        [
            held(grad.shape),
            part,
            held(mixed.shape),
            held(gain.shape),
            held(output.shape),
            pl.BlockSpec((width, tile), lambda j: (0, j)),
            pl.BlockSpec((tile, width), lambda j: (j, 0)),
        ],
        [whole_block(kept), full, whole_block(shape), whole_block((1, width))],
        [
            jax.ShapeDtypeStruct(kept, BF),
            jax.ShapeDtypeStruct((total, width), F32),
            jax.ShapeDtypeStruct(shape, BF),
            jax.ShapeDtypeStruct((1, width), F32),
        ],
        [pltpu.VMEM((total, width), F32)],
        "frame_rear_grads",
    )(grad, slope, mixed, gain, output, expand, contract)


def frame_front_grads_kernel(
    packed_ref, hidden_ref, gain_ref, mixed_grad_ref, weight_ref,
    projected_ref, grad_ref, gain_grad_ref, total,
):
    groups, rows, own, _ = packed_ref.shape

    @pl.when(pl.program_id(0) == 0)
    def _():
        total[...] = jnp.zeros_like(total)

    for part in range(3):

        @pl.when(pl.program_id(0) == part)
        def _(part=part):
            for group in range(groups):
                projected_ref[:, LANES * group : LANES * (group + 1)] = packed_ref[
                    group, :, :, LANES * part : LANES * (part + 1)
                ].reshape(rows * own, LANES)

    total[...] += inner_right(projected_ref[...], weight_ref[...])

    @pl.when(pl.program_id(0) == 2)
    def _():
        part, gain_grad = rms_grads(hidden_ref[...].astype(F32), gain_ref[...], total[...])
        grad_ref[...] = mixed_grad_ref[...] + part
        gain_grad_ref[...] = gain_grad


def frame_front_grads(packed, hidden, gain, mixed_grad, weight):
    total, width = hidden.shape
    return dense_call(
        frame_front_grads_kernel,
        3,
        [
            held(packed.shape),
            held(hidden.shape),
            held(gain.shape),
            held(mixed_grad.shape),
            pl.BlockSpec((width, width), lambda j: (0, j)),
        ],
        [
            pl.BlockSpec((total, width), lambda j: (0, j)),
            whole_block((total, width)),
            whole_block((1, width)),
        ],
        [
            jax.ShapeDtypeStruct((total, 3 * width), BF),
            jax.ShapeDtypeStruct((total, width), F32),
            jax.ShapeDtypeStruct((1, width), F32),
        ],
        [pltpu.VMEM((total, width), F32)],
        "frame_front_grads",
    )(packed, hidden, gain, mixed_grad, weight)


def codec_front_kernel(base_ref, entries_ref, gain_ref, weight_ref, normed_ref, packed_ref, normed):
    positions = packed_ref.shape[0]

    @pl.when(pl.program_id(0) == 0)
    def _():
        base = base_ref[...].astype(F32)
        size = base.shape[0]
        for t in range(positions):
            hidden = base if t == 0 else base + entries_ref[t - 1].astype(F32)
            normed[size * t : size * (t + 1)] = rms_scale(hidden, gain_ref[...]).astype(BF)
        normed_ref[...] = normed[...]

    total = matmul(normed[...], weight_ref[...]).astype(BF)
    packed_ref[...] = total.reshape(packed_ref.shape)


def codec_front(base, entries, gain, weight):
    total, width = base.shape
    positions = entries.shape[0] + 1
    return dense_call(
        codec_front_kernel,
        6,
        [
            held(base.shape),
            held(entries.shape),
            held(gain.shape),
            pl.BlockSpec((width, width // 2), lambda j: (0, j)),
        ],
        [
            whole_block((positions * total, width)),
            pl.BlockSpec((positions, total, width // 2), lambda j: (0, 0, j)),
        ],
        [
            jax.ShapeDtypeStruct((positions * total, width), BF),
            jax.ShapeDtypeStruct((positions, total, 3 * width), BF),
        ],
        [pltpu.VMEM((positions * total, width), BF)],
        "codec_front",
    )(base, entries, gain, weight)


def codec_rear_kernel(
    base_ref, entries_ref, attended_ref, grad_ref, gain_ref, output_ref, expand_ref, contract_ref,
    mixed_ref, active_ref, expand_kept_ref, kept_ref, mixed_grad_ref,
    attended_grad_ref, gain_grad_ref, total,
):
    width = total.shape[1]
    positions = entries_ref.shape[0] + 1
    size = base_ref.shape[0]

    @pl.when(pl.program_id(0) == 0)
    def _():
        base = base_ref[...].astype(F32)
        for t in range(positions):
            own = slice(size * t, size * (t + 1))
            hidden = base if t == 0 else base + entries_ref[t - 1].astype(F32)
            mixed = hidden + matmul(attended_ref[own], output_ref[...])
            mixed_ref[own] = mixed
            expand_kept_ref[own, :width] = rms_scale(mixed, gain_ref[...]).astype(BF)
        total[...] = jnp.zeros_like(total)

    active, slope = gelu_pair(matmul(expand_kept_ref[:, :width], expand_ref[...]))
    active_ref[...] = active.astype(BF)
    expand_in = (slope * inner_right(grad_ref[...], contract_ref[...])).astype(BF)
    tile = expand_in.shape[1]
    for step in range(4 * width // tile):

        @pl.when(pl.program_id(0) == step)
        def _(step=step):
            expand_kept_ref[:, width + step * tile : width + (step + 1) * tile] = expand_in

    total[...] += inner_right(expand_in, expand_ref[...])

    @pl.when(pl.program_id(0) == pl.num_programs(0) - 1)
    def _():
        gain_grads = jnp.zeros_like(gain_grad_ref)
        for t in range(positions):
            own = slice(size * t, size * (t + 1))
            part, gain_grad = rms_grads(mixed_ref[own], gain_ref[...], total[own])
            gain_grads = gain_grads + gain_grad
            mixed_grad = grad_ref[own].astype(F32) + part
            mixed_grad_ref[own] = mixed_grad
            output_in = mixed_grad.astype(BF)
            kept_ref[own] = output_in
            attended_grad_ref[t] = inner_right(output_in, output_ref[...]).astype(BF)
        gain_grad_ref[...] = gain_grads


def codec_rear(base, entries, kept, grad, gain, output, expand, contract):
    size, width = base.shape
    total = kept.shape[0]
    inner = expand.shape[1]
    tile = FF_TILE
    full = whole_block((total, width))
    wide = (total, width + inner)
    high = jax.ShapeDtypeStruct((total, width), F32)
    return dense_call(
        codec_rear_kernel,
        inner // tile,
        [
            held(base.shape),
            held(entries.shape),
            pl.BlockSpec((total, width), lambda j: (0, 1), pipeline_mode=pl.Buffered(1)),
            held(grad.shape),
            held(gain.shape),
            held(output.shape),
            pl.BlockSpec((width, tile), lambda j: (0, j)),
            pl.BlockSpec((tile, width), lambda j: (j, 0)),
        ],
        [
            held((total, width)),
            pl.BlockSpec((total, tile), lambda j: (0, j)),
            held(wide),
            held((total, width)),
            held((total, width)),
            held((total // size, size, width)),
            whole_block((1, width)),
        ],
        [
            high,
            jax.ShapeDtypeStruct((total, inner), BF),
            jax.ShapeDtypeStruct(wide, BF),
            jax.ShapeDtypeStruct((total, width), BF),
            high,
            jax.ShapeDtypeStruct((total // size, size, width), BF),
            jax.ShapeDtypeStruct((1, width), F32),
        ],
        [pltpu.VMEM((total, width), F32)],
        "codec_rear",
    )(base, entries, kept, grad, gain, output, expand, contract)


def codec_result_kernel(mixed_ref, active_ref, live_ref, contract_ref, out_ref, total):
    positions, size, _ = out_ref.shape

    @pl.when(pl.program_id(0) == 0)
    def _():
        total[...] = mixed_ref[...]

    total[...] += matmul(active_ref[...], contract_ref[...])

    @pl.when(pl.program_id(0) == pl.num_programs(0) - 1)
    def _():
        for t in range(positions):
            out_ref[t] = (total[size * t : size * (t + 1)] * live_ref[...]).astype(BF)


def codec_result(mixed, active, live, contract):
    total, width = mixed.shape
    size = live.shape[0]
    inner = active.shape[1]
    tile = FF_TILE
    shape = (total // size, size, width)
    return dense_call(
        codec_result_kernel,
        inner // tile,
        [
            held(mixed.shape),
            pl.BlockSpec((total, tile), lambda j: (0, j)),
            held(live.shape),
            pl.BlockSpec((tile, width), lambda j: (j, 0)),
        ],
        whole_block(shape),
        jax.ShapeDtypeStruct(shape, BF),
        [pltpu.VMEM((total, width), F32)],
        "codec_result",
    )(mixed, active, live, contract)


def codec_front_grads_kernel(
    grad_ref, base_ref, entries_ref, gain_ref, mixed_grad_ref, weight_ref,
    base_grad_ref, entry_grad_ref, gain_grad_ref, total,
):
    positions = entries_ref.shape[0] + 1
    size = base_ref.shape[0]

    @pl.when(pl.program_id(0) == 0)
    def _():
        total[...] = jnp.zeros_like(total)

    total[...] += inner_right(grad_ref[...], weight_ref[...])

    @pl.when(pl.program_id(0) == pl.num_programs(0) - 1)
    def _():
        base = base_ref[...].astype(F32)
        gain_grads = jnp.zeros_like(gain_grad_ref)
        base_grad = jnp.zeros_like(base)
        for t in range(positions):
            own = slice(size * t, size * (t + 1))
            hidden = base if t == 0 else base + entries_ref[t - 1].astype(F32)
            part, gain_grad = rms_grads(hidden, gain_ref[...], total[own])
            gain_grads = gain_grads + gain_grad
            grad = mixed_grad_ref[own] + part
            base_grad = base_grad + grad
            if t > 0:
                entry_grad_ref[size * (t - 1) : size * t] = grad.astype(BF)
        base_grad_ref[...] = base_grad.astype(BF)
        gain_grad_ref[...] = gain_grads


def codec_front_grads(grad, base, entries, gain, mixed_grad, weight):
    size, width = base.shape
    total = grad.shape[0]
    tile = width // 2
    return dense_call(
        codec_front_grads_kernel,
        grad.shape[1] // tile,
        [
            pl.BlockSpec((total, tile), lambda j: (0, j)),
            held(base.shape),
            held(entries.shape),
            held(gain.shape),
            held(mixed_grad.shape),
            pl.BlockSpec((width, tile), lambda j: (0, j)),
        ],
        [whole_block((size, width)), whole_block((total - size, width)), whole_block((1, width))],
        [
            jax.ShapeDtypeStruct((size, width), BF),
            jax.ShapeDtypeStruct((total - size, width), BF),
            jax.ShapeDtypeStruct((1, width), F32),
        ],
        [pltpu.VMEM((total, width), F32)],
        "codec_front_grads",
    )(grad, base, entries, gain, mixed_grad, weight)


def shards_general(
    frames,
    segments,
    padding,
    codec_tokens,
    codebooks,
    frame_prenorm,
    frame_project,
    frame_output,
    frame_postnorm,
    frame_expand,
    frame_contract,
    codec_prenorm,
    codec_project,
    codec_output,
    codec_postnorm,
    codec_expand,
    codec_contract,
    cotangent,
):
    place = Place()
    row_count, frames_dev, width = frames.shape
    frame_total = row_count * frames_dev
    positions = cotangent.shape[2]
    gains = lax.all_gather(
        jnp.stack([frame_prenorm, frame_postnorm, codec_prenorm, codec_postnorm]),
        "mp",
        axis=1,
        tiled=True,
    )
    frame_weights = (
        gains[0],
        gather_weight(frame_project, place),
        gather_weight(frame_output, place),
        gains[1],
        gather_weight(frame_expand, place),
        gather_weight(frame_contract, place),
    )
    codec_weights = (
        gains[2],
        gather_weight(codec_project, place),
        gather_weight(codec_output, place),
        gains[3],
        gather_weight(codec_expand, place),
        gather_weight(codec_contract, place),
    )
    table = gather_weight(codebooks, place)

    hidden = frames.astype(F32).reshape(frame_total, width)
    normed, projected = front_pass(hidden, frame_weights)
    attended, attention_back = frame_attention(
        projected.reshape(row_count, frames_dev, 3 * width), segments, place
    )
    attended = attended.reshape(frame_total, width)
    frame_result, frame_saved = rear_pass(hidden, attended, frame_weights)
    base = frame_result.astype(BF).astype(F32)

    table_rows = codec_tokens.reshape(positions - 1, frame_total) + (
        jnp.arange(positions - 1, dtype=jnp.int32) * CODES
    )[:, None]
    embedded = table[table_rows].astype(F32)
    codec_hidden = jnp.concatenate([base[None], base[None] + embedded], axis=0).reshape(
        positions * frame_total, width
    )
    codec_normed, codec_projected = front_pass(codec_hidden, codec_weights)
    marks = (
        jnp.arange(width)[:, None] // HEAD == jnp.arange(HEADS)[None, :]
    ).astype(F32)
    view = codec_projected.reshape(positions, frame_total, 3, width)
    queries, keys, values = ([view[t, :, part] for t in range(positions)] for part in range(3))
    soft = codec_softmax(queries, keys, marks)
    codec_attended = jnp.concatenate(codec_attend(soft, values, marks), axis=0)
    codec_result, codec_saved = rear_pass(codec_hidden, codec_attended, codec_weights)
    live = padding.reshape(frame_total).astype(F32)[None, :, None]
    output = jnp.transpose(
        (codec_result.reshape(positions, frame_total, width) * live).astype(BF), (1, 0, 2)
    ).reshape(row_count, frames_dev, positions, width)

    codec_grad = (
        jnp.transpose(cotangent.reshape(frame_total, positions, width), (1, 0, 2)).astype(F32) * live
    ).reshape(positions * frame_total, width)
    mixed_grad, attended_grad, codec_postnorm_grad, contract_in, expand_in, output_in = rear_grads(
        codec_grad, codec_saved, codec_weights
    )
    codec_contract_part = weight_grad(codec_saved[3], contract_in, place, True)
    codec_expand_part = weight_grad(codec_saved[1], expand_in, place, False)
    codec_output_part = weight_grad(codec_attended, output_in, place, True)
    grad_view = attended_grad.reshape(positions, frame_total, width)
    codec_projected_grad = codec_attend_grads(
        soft, queries, keys, values, [grad_view[t] for t in range(positions)], marks
    )
    codec_project_part = weight_grad(codec_normed, codec_projected_grad, place, True)
    input_grad, codec_prenorm_grad = front_grads(
        codec_hidden, codec_projected_grad, mixed_grad, codec_weights
    )
    input_grad = input_grad.reshape(positions, frame_total, width)
    chosen = (
        table_rows.reshape(-1)[:, None] == jnp.arange(table.shape[0], dtype=jnp.int32)[None, :]
    ).astype(BF)
    table_part = weight_grad(chosen, input_grad[1:].reshape(-1, width).astype(BF), place, False)
    base_grad = jnp.sum(input_grad, axis=0).astype(BF).astype(F32)

    (codec_contract_grad,) = finish_grads([codec_contract_part], place)
    codec_expand_grad, codec_output_grad, codec_project_grad = finish_grads(
        [codec_expand_part, codec_output_part, codec_project_part], place
    )
    (table_grad,) = finish_grads([table_part], place)

    frame_mixed_grad, frame_attended_grad, frame_postnorm_grad, contract_in, expand_in, output_in = (
        rear_grads(base_grad, frame_saved, frame_weights)
    )
    frame_projected_grad = attention_back(
        frame_attended_grad.reshape(row_count, frames_dev, width)
    ).reshape(frame_total, 3 * width)
    frame_contract_part = weight_grad(frame_saved[3], contract_in, place, True)
    frame_expand_part = weight_grad(frame_saved[1], expand_in, place, False)
    frame_output_part = weight_grad(attended, output_in, place, True)
    frame_project_part = weight_grad(normed, frame_projected_grad, place, True)
    frames_grad, frame_prenorm_grad = front_grads(
        hidden, frame_projected_grad, frame_mixed_grad, frame_weights
    )
    (frame_contract_grad,) = finish_grads([frame_contract_part], place)
    frame_expand_grad, frame_output_grad = finish_grads(
        [frame_expand_part, frame_output_part], place
    )
    (frame_project_grad,) = finish_grads([frame_project_part], place)
    gain_sums = sum_everywhere(
        jnp.stack(
            [frame_prenorm_grad, frame_postnorm_grad, codec_prenorm_grad, codec_postnorm_grad]
        ),
        place,
    )
    return (
        output,
        frames_grad.reshape(row_count, frames_dev, width),
        table_grad,
        gain_sums[0],
        frame_project_grad,
        frame_output_grad,
        gain_sums[1],
        frame_expand_grad,
        frame_contract_grad,
        gain_sums[2],
        codec_project_grad,
        codec_output_grad,
        gain_sums[3],
        codec_expand_grad,
        codec_contract_grad,
    )


class Pair:
    def __init__(self, own):
        self.own = own
        self.other = swap(own, "mp", 1)
        self.age = 0

    def both(self):
        return (self.own, self.other)


class Chain:
    def __init__(self):
        self.last = ()
        self.pending = []

    def pair(self, own):
        made = Pair(own)
        self.pending.append(made)
        return made

    def enter(self, *values):
        due = [made for made in self.pending if made.age >= 3]
        self.pending = [made for made in self.pending if made.age < 3]
        for made in self.pending:
            made.age += 1
        came = tuple(made.other for made in due)
        held = lax.optimization_barrier(tuple(values) + came + self.last)
        for made, other in zip(due, held[len(values) :]):
            made.other = other
        return held[0] if len(values) == 1 else held[: len(values)]

    def leave(self, *values):
        self.last = values


class Gather:
    def __init__(self, members, spots, whole=False):
        self.members = members
        self.spots = spots
        self.whole = whole
        self.pack, self.quarter = pack_call(members, spots)

    def start(self, chain):
        self.came = swap(chain.enter(self.pack if self.whole else self.quarter), "mp", 2)
        self.near = chain.pair(self.pack)

    def spread(self, chain):
        self.came = chain.enter(self.came)
        chain.leave(self.came)
        if self.whole:
            self.far = chain.pair(self.came)
            return
        self.over_x = swap(self.came, "seq", 1)
        self.over_n = swap(self.came, "seq", 2)

    def cross(self, chain):
        self.over_x, self.over_n = chain.enter(self.over_x, self.over_n)
        chain.leave(self.over_x, self.over_n)
        half = self.over_x.shape[0] // 2
        self.ends = (swap(self.over_n[:half], "seq", 1), swap(self.over_x[half:], "seq", 2))

    def close(self, chain):
        ends = chain.enter(*self.ends)
        parts = ((0, 0), (1, 0), (2, 0), (3, 0), (3, ends[0].shape[0]))
        far = far_pack([self.came, self.over_x, self.over_n, *ends], parts, self.spots)
        chain.leave(far)
        self.far = far

    def send(self, chain):
        self.far = Pair(chain.enter(self.far))

    def join_near(self, chain):
        packs = chain.enter(*self.near.both())
        self.outs = join_weights(self.members, packs, (0, 1), self.spots)
        chain.leave(*self.outs)

    def join(self, chain):
        packs = chain.enter(*self.far.both())
        outs = join_weights(self.members, packs, (2, 3), self.spots, self.outs)
        chain.leave(*outs)
        return outs


def load(block, riders):
    if riders is None:
        return block
    high = riders.astype(BF)
    low = (riders - high.astype(F32)).astype(BF)
    return jnp.concatenate(
        [part.reshape(-1, LANES) for part in (block, high, low)], axis=0
    )


def unload(message, shape, riders):
    if riders is None:
        return message, None
    rows = message.shape[0] - 2 * riders.size // LANES
    high, low = (
        part.astype(F32).reshape(riders.shape) for part in jnp.split(message[rows:], 2, axis=0)
    )
    return message[:rows].reshape(shape), riders + (high + low)


class Reduce:
    def __init__(self, stages, blocks, riders=None):
        self.stages = stages
        self.keep = blocks[1]
        self.riders = riders
        self.came = []
        self.shape = blocks[0].shape
        self.coming = swap(load(blocks[0], riders), *BITS[stages[0]])

    def arrive(self, chain):
        self.coming = chain.enter(self.coming)
        chain.leave(self.coming)

    def take(self, chain):
        self.keep, self.coming, *self.came = chain.enter(self.keep, self.coming, *self.came)
        block, self.riders = unload(self.coming, self.shape, self.riders)
        self.came.append(block)

    def total(self, last):
        at = len(self.came) - 1
        spot = (1,) * at + ((0,) if not last else ())
        value = self.keep[spot].astype(F32) if spot else self.keep.astype(F32)
        for level, came in enumerate(self.came):
            value = value + came[spot[level:]].astype(F32)
        return value

    def give(self, chain):
        self.take(chain)
        given = self.total(False).astype(BF)
        self.shape = given.shape
        return given

    def step(self, chain):
        given = self.give(chain)
        message = load(given, self.riders)
        chain.leave(message)
        self.coming = swap(message, *BITS[self.stages[len(self.came)]])

    def result(self):
        return self.total(True)


def together(sums, chain, stage):
    given = [one.give(chain) for one in sums]
    message = jnp.concatenate(given, axis=-3)
    chain.leave(message)
    message = swap(message, *BITS[stage])

    def take():
        held = chain.enter(message)
        chain.leave(held)
        start = 0
        for one, part in zip(sums, given):
            size = part.shape[-3]
            one.coming = held[..., start : start + size, :, :]
            start += size

    return take


def finish(sums, chain):
    given = jnp.concatenate([one.give(chain) for one in sums], axis=0)
    riders = sums[-1].riders
    message = load(given, riders)
    chain.leave(message)
    message = swap(message, *BITS["f"])

    def take():
        held = chain.enter(message)
        chain.leave(held)
        came, total = unload(held, given.shape, riders)
        start = 0
        for one in sums:
            size = one.shape[-3]
            one.came.append(came[start : start + size])
            start += size
        sums[-1].riders = total

    return take


def shards(
    frames,
    segments,
    padding,
    codec_tokens,
    codebooks,
    frame_prenorm,
    frame_project,
    frame_output,
    frame_postnorm,
    frame_expand,
    frame_contract,
    codec_prenorm,
    codec_project,
    codec_output,
    codec_postnorm,
    codec_expand,
    codec_contract,
    cotangent,
):
    place = Place()
    chain = Chain()
    order = grad_order(place)
    spots = jnp.stack([place.mp, place.seq % 4]).astype(jnp.int32)
    row_count, frames_dev, width = frames.shape
    frame_total = row_count * frames_dev
    positions = cotangent.shape[2]
    count = place.seq_count

    gain_rows = jnp.pad(
        jnp.concatenate([frame_prenorm, frame_postnorm, codec_prenorm, codec_postnorm])[None],
        ((0, 127), (0, 0)),
    )
    first = Gather([frame_project, gain_rows], spots)
    chain.leave(first.quarter)
    first.start(chain)
    members = chain.enter(frame_expand, frame_contract, frame_output)
    second = Gather(members, spots)
    chain.leave(second.quarter)
    codes = codec_tokens.reshape(1, (positions - 1) * frame_total) + jnp.repeat(
        jnp.arange(positions - 1, dtype=jnp.int32) * CODES, frame_total
    )
    live = padding.reshape(frame_total).astype(F32)[:, None]
    first.spread(chain)
    second.start(chain)
    every_segment = lax.all_to_all(
        jnp.broadcast_to(chain.enter(segments)[None], (count, row_count, frames_dev)),
        "seq",
        split_axis=0,
        concat_axis=0,
        tiled=True,
    )
    every_segment = jnp.transpose(every_segment, (1, 0, 2)).reshape(row_count, count * frames_dev)
    every_segment = chain.enter(every_segment)
    chain.leave(every_segment)
    fourth = Gather(chain.enter(codec_expand, codec_contract, codec_output), spots)
    chain.leave(fourth.quarter)
    contract_in = (
        jnp.transpose(chain.enter(cotangent).reshape(frame_total, positions, width), (1, 0, 2))
        * live.astype(BF)[None]
    ).reshape(positions * frame_total, width)
    chain.leave(contract_in)
    first.join_near(chain)
    first.cross(chain)
    third = Gather(chain.enter(codec_project, codebooks), spots, True)
    chain.leave(third.pack)
    first.close(chain)
    second.spread(chain)
    first.send(chain)
    fourth.start(chain)
    third.start(chain)

    frame_project_all, gains = first.join(chain)
    gains = jnp.transpose(
        gains.reshape(place.mp_count, -1, 4, width // 4)[:, 0], (1, 0, 2)
    ).reshape(4, 1, width).astype(F32)
    hidden = frames.reshape(frame_total, width)
    normed, packed = frame_front(hidden, chain.enter(gains[0]), frame_project_all, row_count)
    packed, second.over_x, second.over_n, fourth.came = chain.enter(
        packed, second.over_x, second.over_n, fourth.came
    )
    chain.leave(packed)
    packed = lax.all_to_all(packed, "seq", split_axis=0, concat_axis=0, tiled=True)
    second.join_near(chain)
    third.join_near(chain)
    fourth.join_near(chain)
    second.cross(chain)
    packed, *second.ends = chain.enter(packed, *second.ends)
    chain.leave(packed)
    second.close(chain)
    second.send(chain)
    fourth.spread(chain)
    contract_pair = Pair(contract_in)
    codes_pair = Pair(chain.enter(codes))
    packed = chain.enter(packed)
    attended = frame_attend_call(packed, every_segment)
    chain.leave(attended)
    attended, second.far.other = chain.enter(attended, second.far.other)
    chain.leave(attended)
    attended = lax.all_to_all(attended, "seq", split_axis=0, concat_axis=0, tiled=True)
    frame_expand_all, frame_contract_all, frame_output_all = second.join(chain)
    attended, fourth.over_x, fourth.over_n = chain.enter(attended, fourth.over_x, fourth.over_n)
    chain.leave(attended)
    fourth.cross(chain)
    frame_kept, mixed, slope, base = frame_rear(
        hidden,
        normed,
        chain.enter(attended),
        gains[1],
        frame_output_all,
        frame_expand_all,
        frame_contract_all,
    )
    chain.leave(base)

    base, third.came, *fourth.ends = chain.enter(base, third.came, *fourth.ends)
    chain.leave(base)
    third.spread(chain)
    fourth.close(chain)
    codec_project_all, table = third.join(chain)
    fourth.send(chain)
    frame_kept = Pair(chain.enter(frame_kept))
    entries = table[codes.reshape(positions - 1, frame_total)]
    codec_normed, codec_packed = codec_front(chain.enter(base), entries, gains[2], codec_project_all)
    chain.leave(codec_packed)
    codec_packed, contract_pair.other = chain.enter(codec_packed, contract_pair.other)
    codec_kept = codec_attend_call(codec_packed, codec_normed).reshape(
        positions * frame_total, 2 * width
    )
    chain.leave(codec_kept)
    codec_expand_all, codec_contract_all, codec_output_all = fourth.join(chain)
    codec_kept, frame_kept.other = chain.enter(codec_kept, frame_kept.other)
    chain.leave(codec_kept)
    (
        codec_mixed,
        codec_activated,
        codec_expand_kept,
        codec_output_in,
        mixed_grad,
        attended_grad,
        codec_postnorm_grad,
    ) = codec_rear(
        base,
        entries,
        chain.enter(codec_kept),
        contract_in,
        gains[3],
        codec_output_all,
        codec_expand_all,
        codec_contract_all,
    )
    chain.leave(codec_activated)

    inner = codec_activated.shape[1]
    activated_pair = chain.pair(codec_activated)
    codec_expand_kept = chain.pair(codec_expand_kept)
    projected_grad = codec_attend_grads_call(codec_packed, chain.enter(attended_grad)).reshape(
        positions * frame_total, 3 * width
    )
    chain.leave(projected_grad)
    base_grad, table_in, codec_prenorm_grad = codec_front_grads(
        chain.enter(projected_grad), base, entries, gains[2], mixed_grad, codec_project_all
    )
    chain.leave(base_grad)
    frame_grads_kept, frame_mixed_grad, grads, frame_postnorm_grad = frame_rear_grads(
        chain.enter(base_grad),
        slope,
        mixed,
        gains[1],
        frame_output_all,
        frame_expand_all,
        frame_contract_all,
        row_count,
    )
    chain.leave(grads)

    activated_pair.other, codec_expand_kept.other, grads, frame_grads_kept = chain.enter(
        activated_pair.other, codec_expand_kept.other, grads, frame_grads_kept
    )
    chain.leave(grads)
    grads = lax.all_to_all(grads, "seq", split_axis=0, concat_axis=0, tiled=True)
    frame_grads_kept = Pair(frame_grads_kept)
    contract_stages = tuple("ynxf")
    contract_blocks = grad_columns(
        (chain.enter(*activated_pair.both()), 0, inner),
        (contract_pair.both(), 0, width),
        order,
        contract_stages,
        4,
        0,
    )
    chain.leave(*contract_blocks)
    expand_stages = tuple("xnyf")
    arrays = chain.enter(*codec_expand_kept.both())
    expand_blocks = grad_rows((arrays, 0, width), (arrays, width, inner), order, expand_stages, 4, 0)
    chain.leave(*expand_blocks)

    grads, frame_grads_kept.other = chain.enter(grads, frame_grads_kept.other)
    chain.leave(grads)
    contract_sum = Reduce(contract_stages, chain.enter(*contract_blocks))
    expand_sum = Reduce(expand_stages, chain.enter(*expand_blocks))
    codec_kept = Pair(chain.enter(codec_kept))
    output_pair = Pair(chain.enter(codec_output_in))
    projected_pair = Pair(chain.enter(projected_grad))
    packed_grad = frame_attend_grads_call(packed, chain.enter(grads), every_segment)
    chain.leave(packed_grad)
    kept, arrays = frame_kept.both(), chain.enter(*frame_grads_kept.both())
    frame_contract_stages = tuple("yxnf")
    frame_contract_blocks = grad_columns(
        (kept, 3 * width, inner), (arrays, 0, width), order, frame_contract_stages, 4, 0
    )
    chain.leave(*frame_contract_blocks)
    frame_expand_stages = tuple("xnyf")
    arrays = chain.enter(*arrays)
    blocks = grad_rows(
        (kept, 2 * width, width), (arrays, width, inner), order, frame_expand_stages, 5, 0
    )
    frame_expand_blocks = grad_rows(
        (kept, width, width), (arrays, width + inner, width), order, frame_expand_stages, 5, 4, blocks
    )
    chain.leave(*frame_expand_blocks)

    packed_grad, codec_kept.other, projected_pair.other, output_pair.other = chain.enter(
        packed_grad, codec_kept.other, projected_pair.other, output_pair.other
    )
    chain.leave(packed_grad)
    contract_sum.arrive(chain)
    expand_sum.arrive(chain)
    packed_grad = lax.all_to_all(packed_grad, "seq", split_axis=0, concat_axis=0, tiled=True)
    take_both = together([contract_sum, expand_sum], chain, "n")
    frame_contract_sum = Reduce(frame_contract_stages, chain.enter(*frame_contract_blocks))
    frame_expand_sum = Reduce(frame_expand_stages, chain.enter(*frame_expand_blocks))
    table_pair = Pair(chain.enter(table_in))
    project_stages = tuple("ynxf")
    arrays = chain.enter(*codec_kept.both())
    blocks = grad_rows(
        (arrays, 0, width), (projected_pair.both(), 0, 3 * width), order, project_stages, 4, 0
    )
    project_blocks = grad_rows(
        (arrays, width, width), (output_pair.both(), 0, width), order, project_stages, 4, 3, blocks
    )
    chain.leave(*project_blocks)
    table_stages = tuple("xynf")
    table_blocks = grad_table(
        jnp.concatenate(codes_pair.both(), axis=1),
        chain.enter(*table_pair.both()),
        order,
        table_stages,
        codebooks.shape[0],
        2,
        0,
    )
    chain.leave(*table_blocks)
    project_sum = Reduce(project_stages, chain.enter(*project_blocks))
    table_sum = Reduce(table_stages, chain.enter(*table_blocks))
    packed_grad = chain.enter(packed_grad)
    chain.leave(packed_grad)
    frame_projected_grad, frames_grad, frame_prenorm_grad = frame_front_grads(
        chain.enter(packed_grad), hidden, gains[0], frame_mixed_grad, frame_project_all
    )
    chain.leave(frames_grad)
    frame_projected_pair = Pair(frame_projected_grad)
    gain_pair = Pair(
        jnp.concatenate(
            [frame_prenorm_grad, frame_postnorm_grad, codec_prenorm_grad, codec_postnorm_grad]
        )
    )
    frame_projected_pair.other, gain_pair.other = chain.enter(
        frame_projected_pair.other, gain_pair.other
    )
    chain.leave(gain_pair.other)
    blocks = grad_rows(
        (kept, 0, width),
        (chain.enter(*frame_projected_pair.both()), 0, 3 * width),
        order,
        table_stages,
        3,
        0,
    )
    chain.leave(*blocks)
    riders = gain_pair.own + gain_pair.other
    frame_project_sum = Reduce(table_stages, blocks, chain.enter(riders))
    frame_expand_sum.arrive(chain)
    frame_contract_sum.step(chain)
    frame_expand_sum.step(chain)
    output = codec_result(codec_mixed, chain.enter(codec_activated), live, codec_contract_all)
    chain.leave(output)
    output = jnp.transpose(output, (1, 0, 2)).reshape(row_count, frames_dev, positions, width)

    project_sum.step(chain)
    take_both()
    table_sum.step(chain)
    take_expand = together([expand_sum, frame_expand_sum], chain, "y")
    frame_project_sum.step(chain)
    frame_contract_sum.step(chain)
    project_sum.step(chain)
    contract_sum.step(chain)
    take_expand()
    take_second = finish([frame_contract_sum, frame_expand_sum], chain)
    table_sum.step(chain)
    frame_project_sum.step(chain)
    take_first = finish([contract_sum, expand_sum], chain)
    take_fourth = finish([project_sum, table_sum], chain)
    take_third = finish([frame_project_sum], chain)
    take_second()
    take_first()
    take_fourth()
    take_third()

    height = frame_project.shape[0]
    project_units = project_sum.result()
    frame_expand_units = frame_expand_sum.result()
    gain_sums = frame_project_sum.riders
    return (
        output,
        frames_grad.reshape(row_count, frames_dev, width),
        rows_from_units(table_sum.result(), codebooks.shape[0]),
        gain_sums[0],
        rows_from_units(frame_project_sum.result(), height),
        rows_from_units(frame_expand_units[4:], height),
        gain_sums[1],
        rows_from_units(frame_expand_units[:4], height),
        columns_from_units(frame_contract_sum.result()),
        gain_sums[2],
        rows_from_units(project_units[:3], height),
        rows_from_units(project_units[3:], height),
        gain_sums[3],
        rows_from_units(expand_sum.result(), height),
        columns_from_units(contract_sum.result()),
    )


def solution(mesh):
    placed = (
        P("mp", "seq", None),
        P("mp", "seq"),
        P("mp", "seq"),
        P(None, "mp", "seq"),
        P("mp", None),
        P("mp"),
        P("mp", None),
        P("mp", None),
        P("mp"),
        P("mp", None),
        P("mp", None),
        P("mp"),
        P("mp", None),
        P("mp", None),
        P("mp"),
        P("mp", None),
        P("mp", None),
        P("mp", "seq", None, None),
    )
    small = mesh.shape["seq"] == 8 and mesh.shape["mp"] == 4
    return jax.shard_map(
        shards if small else shards_general,
        mesh=mesh,
        in_specs=placed,
        out_specs=(
            P("mp", "seq", None, None),
            P("mp", "seq", None),
            P("mp", "seq"),
            P(),
            P("mp", "seq"),
            P("mp", "seq"),
            P(),
            P("mp", "seq"),
            P("mp", "seq"),
            P(),
            P("mp", "seq"),
            P("mp", "seq"),
            P(),
            P("mp", "seq"),
            P("mp", "seq"),
        ),
        check_vma=False,
    )
```

```python
import functools

import jax
import jax.numpy as jnp
from jax import lax
from jax.experimental import pallas as pl
from jax.experimental.pallas import tpu as pltpu
from jax.sharding import PartitionSpec as P

HEADS = 16
HEAD = 64
CODES = 1024


EPSILON = 1e-05
MASKED = -1e30
FACTOR = HEAD ** (-0.5)

BF = jnp.bfloat16
F32 = jnp.float32


def rms_scale(values, gain_vec):
    return (
        values * lax.rsqrt(jnp.mean(values * values, axis=-1, keepdims=True) + EPSILON) * gain_vec
    )


def matmul(former, latter):
    return jnp.dot(former, latter, preferred_element_type=F32)


def inner_left(former, latter):
    return lax.dot_general(former, latter, (((0,), (0,)), ((), ())), preferred_element_type=F32)


def inner_right(former, latter):
    return lax.dot_general(former, latter, (((1,), (1,)), ((), ())), preferred_element_type=F32)


def split_heads(values):
    return values.reshape(values.shape[:-1] + (-1, HEAD))


def swap(values, axis, bit):
    return lax.ppermute(values, axis, [(i, i ^ bit) for i in range(lax.axis_size(axis))])


def pick(values, index, axis):
    return lax.dynamic_index_in_dim(values, index, axis, keepdims=False)


class Place:
    def __init__(self):
        self.seq_count = lax.axis_size("seq")
        self.mp_count = lax.axis_size("mp")
        self.seq = lax.axis_index("seq")
        self.mp = lax.axis_index("mp")
        self.seq_low = self.seq % 2


def gather_weight(shard, place):
    height, breadth = shard.shape
    half = height // 2
    mine = lax.dynamic_slice(shard, (place.seq_low * half, 0), (half, breadth))
    first = swap(mine, "mp", 2)
    second = swap(first, "seq", 1)
    near_other = swap(shard, "mp", 1)
    far = jnp.zeros((height, breadth), shard.dtype)
    far = lax.dynamic_update_slice(far, first, (place.seq_low * half, 0))
    far = lax.dynamic_update_slice(far, second, ((1 - place.seq_low) * half, 0))
    far_other = swap(far, "mp", 1)
    whole = jnp.zeros((height * place.mp_count, breadth), shard.dtype)
    for flip, piece in ((0, shard), (1, near_other), (2, far), (3, far_other)):
        whole = lax.dynamic_update_slice(whole, piece, ((place.mp ^ flip) * height, 0))
    return whole


def line_scatter(blocks, place):
    count = place.seq_count // 2
    position = place.seq // 2
    size = 2 * count
    state = blocks
    up_in = down_in = None
    for step in range(1, count):
        up_index = jnp.clip(count - step + position, 0, count - 1)
        down_index = jnp.clip(step - 1 - (count - 1 - position), 0, count - 1)
        up_perm = [(i, i + 2) for i in range(size - 2) if i // 2 < step]
        down_perm = [(i, i - 2) for i in range(2, size) if (count - 1 - i // 2) < step]
        up_out = pick(blocks, up_index, 1)
        down_out = pick(blocks, down_index, 1)
        if up_in is not None:
            up_out = up_out + up_in
            down_out = down_out + down_in
        up_in = lax.ppermute(up_out, "seq", up_perm)
        down_in = lax.ppermute(down_out, "seq", down_perm)
    own = pick(blocks, position, 1).astype(F32)
    return own + up_in.astype(F32) + down_in.astype(F32)


def weight_grad(former, latter, place, seq_first):
    height = former.shape[1] // place.mp_count
    rows = former.shape[0]
    breadth = latter.shape[1] // place.seq_count
    low = place.seq_low
    view = latter.reshape(rows, place.seq_count // 2, 2, breadth)
    half = breadth * (place.seq_count // 2)
    give = pick(view, 1 - low, 2).reshape(rows, half)
    keep = pick(view, low, 2).reshape(rows, half)
    both = jnp.concatenate([give, keep], axis=1)

    def columns(flip):
        return lax.dynamic_slice(former, (0, (place.mp ^ flip) * height), (rows, height))

    own, other, far, far_other = (columns(flip) for flip in (0, 1, 2, 3))
    part = inner_left(jnp.concatenate([far_other, other], axis=1), both).astype(BF)
    part = swap(part, "mp", 1).astype(F32)
    if seq_first:
        send = inner_left(jnp.concatenate([far, own], axis=1), give) + part[:, :half]
        low_in = swap(send.astype(BF), "seq", 1).astype(F32)
        send = inner_left(far, keep) + part[:height, half:] + low_in[:height]
        far_in = swap(send.astype(BF), "mp", 2).astype(F32)
        total = inner_left(own, keep) + part[height:, half:] + low_in[height:] + far_in
    else:
        send = inner_left(far, both) + part[:height]
        far_in = swap(send.astype(BF), "mp", 2).astype(F32)
        send = inner_left(own, give) + part[height:, :half] + far_in[:, :half]
        low_in = swap(send.astype(BF), "seq", 1).astype(F32)
        total = inner_left(own, keep) + part[height:, half:] + far_in[:, half:] + low_in
    return total.astype(BF).reshape(height, place.seq_count // 2, breadth)


def finish_grads(partials, place):
    sizes = [part.shape[2] for part in partials]
    total = line_scatter(jnp.concatenate(partials, axis=2), place)
    pieces, start = [], 0
    for size in sizes:
        pieces.append(total[:, start : start + size])
        start += size
    return pieces


def sum_everywhere(values, place):
    for axis, count in (("mp", place.mp_count), ("seq", place.seq_count)):
        bit = 1
        while bit < count:
            values = values + swap(values, axis, bit)
            bit *= 2
    return values


def front_pass(hidden, weights):
    normed = rms_scale(hidden, weights[0].astype(F32)).astype(BF)
    projected = matmul(normed, weights[1]).astype(BF)
    return (normed, projected)


def rear_pass(hidden, attended, weights):
    mixed_sum = hidden + matmul(attended, weights[2])
    normed_two = rms_scale(mixed_sum, weights[3].astype(F32)).astype(BF)
    expanded = matmul(normed_two, weights[4])
    activated = jax.nn.gelu(expanded).astype(BF)
    result = mixed_sum + matmul(activated, weights[5])
    return (result, (mixed_sum, normed_two, expanded, activated))


def rear_grads(result_grad, saved_state, weights):
    mixed_sum, normed_two, expanded, activated = saved_state
    contract_input = result_grad.astype(BF)
    active_grad = inner_right(contract_input, weights[5])
    expand_input = jax.vjp(jax.nn.gelu, expanded)[1](active_grad)[0].astype(BF)
    normed_grad = inner_right(expand_input, weights[4])
    mixed_part, postnorm_grad = jax.vjp(rms_scale, mixed_sum, weights[3].astype(F32))[1](
        normed_grad
    )
    mixed_grad = result_grad + mixed_part
    output_input = mixed_grad.astype(BF)
    attended_grad = inner_right(output_input, weights[2]).astype(BF)
    return (mixed_grad, attended_grad, postnorm_grad, contract_input, expand_input, output_input)


def front_grads(hidden, projected_grad, mixed_grad, weights):
    normed_grad = inner_right(projected_grad, weights[1])
    hidden_part, prenorm_grad = jax.vjp(rms_scale, hidden, weights[0].astype(F32))[1](normed_grad)
    return (mixed_grad + hidden_part, prenorm_grad)


def portions_of(queries, keys, allowed):
    scores = jnp.einsum("ihd,jhd->hij", queries, keys, preferred_element_type=F32) * FACTOR
    return jax.nn.softmax(jnp.where(allowed[None], scores, MASKED), axis=-1)


def attend(queries, keys, values, allowed):
    portions = portions_of(queries, keys, allowed)
    return jnp.einsum(
        "hij,jhd->ihd", portions.astype(BF), values, preferred_element_type=F32
    ).astype(BF)


def attend_grads(queries, keys, values, allowed, out_grad):
    portions = portions_of(queries, keys, allowed)
    portion_grad = jnp.einsum("ihd,jhd->hij", out_grad, values, preferred_element_type=F32)
    score_grad = (
        portions * (portion_grad - jnp.sum(portions * portion_grad, axis=-1, keepdims=True))
    ).astype(BF)
    query_grad = (
        jnp.einsum("hij,jhd->ihd", score_grad, keys, preferred_element_type=F32) * FACTOR
    )
    key_grad = (
        jnp.einsum("hij,ihd->jhd", score_grad, queries, preferred_element_type=F32) * FACTOR
    )
    value_grad = jnp.einsum("hij,ihd->jhd", portions.astype(BF), out_grad, preferred_element_type=F32)
    return query_grad, key_grad, value_grad


def to_heads(values, place):
    rows, own, parts, width = values.shape
    count = place.seq_count
    view = values.reshape(rows, own, parts, count, width // count)
    moved = lax.all_to_all(
        jnp.transpose(view, (3, 0, 1, 2, 4)), "seq", split_axis=0, concat_axis=0, tiled=True
    )
    return jnp.transpose(moved, (1, 0, 2, 3, 4)).reshape(rows, count * own, parts, width // count)


def to_frames(values, place):
    rows, total, parts, width = values.shape
    count = place.seq_count
    view = values.reshape(rows, count, total // count, parts, width)
    moved = lax.all_to_all(
        jnp.transpose(view, (1, 0, 2, 3, 4)), "seq", split_axis=0, concat_axis=0, tiled=True
    )
    return jnp.transpose(moved, (1, 2, 3, 0, 4)).reshape(
        rows, total // count, parts, count * width
    )


def allowed_of(query_seg, key_seg, query_pos, key_pos):
    return (query_seg[:, None] == key_seg[None, :]) & (key_pos[None, :] <= query_pos[:, None])


def frame_attention(projected, segments, place):
    rows, own, triple = projected.shape
    width = triple // 3
    parts = projected.reshape(rows, own, 3, width)
    every_segment = lax.all_gather(segments, "seq", axis=1, tiled=True)
    every_pos = jnp.arange(own * place.seq_count)
    if HEADS % place.seq_count == 0:
        packed = to_heads(parts, place)
        sets = [split_heads(packed[:, :, part]) for part in range(3)]

        def one_row(items):
            queries, keys, values, segs = items
            return attend(queries, keys, values, allowed_of(segs, segs, every_pos, every_pos))

        attended = lax.map(one_row, (*sets, every_segment))
        attended = to_frames(attended.reshape(rows, own * place.seq_count, 1, -1), place)

        def backward(out_grad):
            grads = to_heads(out_grad.reshape(rows, own, 1, width), place)[:, :, 0]

            def one_row(items):
                queries, keys, values, segs, grad = items
                return attend_grads(
                    queries, keys, values, allowed_of(segs, segs, every_pos, every_pos), grad
                )

            found = lax.map(one_row, (*sets, every_segment, split_heads(grads)))
            packed_grad = jnp.stack(
                [grad.reshape(rows, own * place.seq_count, -1) for grad in found], axis=2
            ).astype(BF)
            return to_frames(packed_grad, place).reshape(rows, own, triple)

        return attended.reshape(rows, own, width), backward

    keys = lax.all_gather(parts[:, :, 1], "seq", axis=1, tiled=True)
    values = lax.all_gather(parts[:, :, 2], "seq", axis=1, tiled=True)
    sets = (split_heads(parts[:, :, 0]), split_heads(keys), split_heads(values))
    own_pos = place.seq * own + jnp.arange(own)

    def one_row(items):
        row_q, row_k, row_v, own_segs, segs = items
        return attend(row_q, row_k, row_v, allowed_of(own_segs, segs, own_pos, every_pos))

    attended = lax.map(one_row, (*sets, segments, every_segment)).reshape(rows, own, width)

    def backward(out_grad):
        def one_row(items):
            row_q, row_k, row_v, own_segs, segs, grad = items
            allowed = allowed_of(own_segs, segs, own_pos, every_pos)
            return attend_grads(row_q, row_k, row_v, allowed, grad)

        query_grad, key_grad, value_grad = lax.map(
            one_row, (*sets, segments, every_segment, split_heads(out_grad))
        )
        both = jnp.stack([key_grad.reshape(rows, -1, width), value_grad.reshape(rows, -1, width)], 2)
        both = lax.psum_scatter(both, "seq", scatter_dimension=1, tiled=True)
        parts_grad = [query_grad.reshape(rows, own, width), both[:, :, 0], both[:, :, 1]]
        return jnp.concatenate(parts_grad, axis=-1).astype(BF)

    return attended, backward


def head_sums(values, marks):
    return jnp.dot(values, marks, precision=lax.Precision.HIGHEST, preferred_element_type=F32)


def head_spread(values, marks):
    return lax.dot_general(
        values.astype(BF), marks.astype(BF), (((1,), (1,)), ((), ())), preferred_element_type=F32
    )


def codec_softmax(queries, keys, marks):
    result = []
    for later in range(len(queries)):
        scores = [
            head_sums(queries[later].astype(F32) * keys[earlier].astype(F32), marks) * FACTOR
            for earlier in range(later + 1)
        ]
        top = scores[0]
        for score in scores[1:]:
            top = jnp.maximum(top, score)
        powers = [jnp.exp(score - top) for score in scores]
        total = sum(powers)
        result.append([power / total for power in powers])
    return result


def codec_attend(soft, values, marks):
    result = []
    for row in soft:
        total = 0.0
        for earlier, portion in enumerate(row):
            total = total + head_spread(portion, marks) * values[earlier].astype(F32)
        result.append(total.astype(BF))
    return result


def codec_attend_grads(soft, queries, keys, values, grads, marks):
    count = len(queries)
    query_grad = []
    key_grad = [0.0] * count
    value_grad = [0.0] * count
    for later in range(count):
        grad = grads[later].astype(F32)
        portion_grads = [
            head_sums(grad * values[earlier].astype(F32), marks) for earlier in range(later + 1)
        ]
        mean = sum(soft[later][i] * portion_grads[i] for i in range(later + 1))
        total = 0.0
        for earlier in range(later + 1):
            score_grad = soft[later][earlier] * (portion_grads[earlier] - mean)
            wide = head_spread(score_grad, marks)
            total = total + wide * keys[earlier].astype(F32)
            key_grad[earlier] = key_grad[earlier] + wide * queries[later].astype(F32)
            value_grad[earlier] = value_grad[earlier] + head_spread(soft[later][earlier], marks) * grad
        query_grad.append(total * FACTOR)
    return jnp.concatenate(
        [
            jnp.concatenate(
                [query_grad[t], key_grad[t] * FACTOR, value_grad[t]], axis=-1
            ).astype(BF)
            for t in range(count)
        ],
        axis=0,
    )


LANES = 128
TILE = 256
VMEM_LIMIT = 48 * 1024 * 1024
HINT = pl.CostEstimate(flops=1, bytes_accessed=1, transcendentals=0)


def whole_block(shape):
    return pl.BlockSpec(shape, lambda *_: (0,) * len(shape))


def causal_tiles(length):
    tile = min(TILE, length)
    return [(start, tile, start + tile) for start in range(0, length, tile)]


def head_masks(dtype):
    lane = lax.broadcasted_iota(jnp.int32, (1, LANES), 1)
    return [((lane // HEAD) == head).astype(dtype) for head in range(LANES // HEAD)]


def frame_attend_kernel(packed_ref, seg_col_ref, seg_row_ref, out_ref):
    chunks, _, own, _ = packed_ref.shape
    length = chunks * own
    packed = packed_ref[...].reshape(length, 3 * LANES)
    queries, keys, values = (packed[:, LANES * i : LANES * (i + 1)] for i in range(3))
    masks = head_masks(BF)
    lane = lax.broadcasted_iota(jnp.int32, (1, LANES), 1)
    for start, tile, end in causal_tiles(length):
        query_pos = start + lax.broadcasted_iota(jnp.int32, (tile, end), 0)
        key_pos = lax.broadcasted_iota(jnp.int32, (tile, end), 1)
        allowed = (seg_col_ref[0, start:end] == seg_row_ref[0, :, :end]) & (key_pos <= query_pos)
        result = jnp.zeros((tile, LANES), F32)
        for head, mask in enumerate(masks):
            scores = inner_right(queries[start:end] * mask, keys[:end]) * FACTOR
            scores = jnp.where(allowed, scores, MASKED)
            powers = jnp.exp(scores - jnp.max(scores, axis=1, keepdims=True))
            portions = powers / jnp.sum(powers, axis=1, keepdims=True)
            found = matmul(portions.astype(BF), values[:end])
            result = jnp.where(lane // HEAD == head, found, result)
        out_ref[start // own : end // own, 0] = result.astype(BF).reshape(tile // own, own, LANES)


def frame_attend_grads_kernel(packed_ref, grad_ref, seg_col_ref, seg_row_ref, out_ref, key_sum, value_sum):
    chunks, _, own, _ = packed_ref.shape
    length = chunks * own
    packed = packed_ref[...].reshape(length, 3 * LANES)
    queries, keys, values = (packed[:, LANES * i : LANES * (i + 1)] for i in range(3))
    grads = grad_ref[...].reshape(length, LANES)
    masks = head_masks(BF)
    lane = lax.broadcasted_iota(jnp.int32, (1, LANES), 1)
    key_sum[...] = jnp.zeros_like(key_sum)
    value_sum[...] = jnp.zeros_like(value_sum)
    for start, tile, end in causal_tiles(length):
        key_pos = lax.broadcasted_iota(jnp.int32, (end, tile), 0)
        query_pos = start + lax.broadcasted_iota(jnp.int32, (end, tile), 1)
        allowed = (seg_col_ref[0, :end] == seg_row_ref[0, :, start:end]) & (key_pos <= query_pos)
        query_grad = jnp.zeros((tile, LANES), F32)
        for head, mask in enumerate(masks):
            query = queries[start:end] * mask
            grad = grads[start:end] * mask
            scores = inner_right(keys[:end], query) * FACTOR
            scores = jnp.where(allowed, scores, MASKED)
            powers = jnp.exp(scores - jnp.max(scores, axis=0, keepdims=True))
            portions = powers / jnp.sum(powers, axis=0, keepdims=True)
            portion_grad = inner_right(values[:end], grad)
            mean = jnp.sum(portions * portion_grad, axis=0, keepdims=True)
            score_grad = (portions * (portion_grad - mean)).astype(BF)
            key_sum[:end] += matmul(score_grad, query)
            value_sum[:end] += matmul(portions.astype(BF), grad)
            found = inner_left(score_grad, keys[:end])
            query_grad = jnp.where(lane // HEAD == head, found, query_grad)
        out_ref[start // own : end // own, 0, :, :LANES] = (
            (query_grad * FACTOR).astype(BF).reshape(tile // own, own, LANES)
        )
    out_ref[:, 0, :, LANES : 2 * LANES] = (key_sum[...] * FACTOR).astype(BF).reshape(chunks, own, LANES)
    out_ref[:, 0, :, 2 * LANES :] = value_sum[...].astype(BF).reshape(chunks, own, LANES)


def row_spec(chunks, own, breadth):
    return pl.BlockSpec((chunks, 1, own, breadth), lambda row: (0, row, 0, 0))


def segment_specs(length):
    return [
        pl.BlockSpec((1, length, 1), lambda row: (row, 0, 0)),
        pl.BlockSpec((1, 1, length), lambda row: (row, 0, 0)),
    ]


def frame_attend_call(packed, segments):
    chunks, rows, own, _ = packed.shape
    length = chunks * own
    return pl.pallas_call(
        frame_attend_kernel,
        grid=(rows,),
        in_specs=[row_spec(chunks, own, 3 * LANES), *segment_specs(length)],
        out_specs=row_spec(chunks, own, LANES),
        out_shape=jax.ShapeDtypeStruct((chunks, rows, own, LANES), BF),
        compiler_params=pltpu.CompilerParams(vmem_limit_bytes=VMEM_LIMIT),
        cost_estimate=HINT,
        name="frame_attend",
    )(packed, segments[:, :, None], segments[:, None, :])


def frame_attend_grads_call(packed, grads, segments):
    chunks, rows, own, _ = packed.shape
    length = chunks * own
    return pl.pallas_call(
        frame_attend_grads_kernel,
        grid=(rows,),
        in_specs=[
            row_spec(chunks, own, 3 * LANES),
            row_spec(chunks, own, LANES),
            *segment_specs(length),
        ],
        out_specs=row_spec(chunks, own, 3 * LANES),
        out_shape=jax.ShapeDtypeStruct((chunks, rows, own, 3 * LANES), BF),
        scratch_shapes=[pltpu.VMEM((length, LANES), F32), pltpu.VMEM((length, LANES), F32)],
        compiler_params=pltpu.CompilerParams(vmem_limit_bytes=VMEM_LIMIT),
        cost_estimate=HINT,
        name="frame_attend_grads",
    )(packed, grads, segments[:, :, None], segments[:, None, :])


def position_pairs(positions):
    return [(later, earlier) for later in range(1, positions) for earlier in range(later + 1)]


def codec_sums(products, marks):
    stacked = jnp.concatenate(products, axis=0)
    high = stacked.astype(BF)
    low = (stacked - high.astype(F32)).astype(BF)
    total = matmul(high, marks) + matmul(low, marks)
    size = products[0].shape[0]
    return [total[size * i : size * (i + 1)] for i in range(len(products))]


def codec_spread(portions, marks):
    stacked = jnp.concatenate([portion.astype(BF) for portion in portions], axis=0)
    total = inner_right(stacked, marks)
    size = portions[0].shape[0]
    return [total[size * i : size * (i + 1)] for i in range(len(portions))]


def codec_portions(queries, keys, marks, pairs):
    scores = codec_sums(
        [queries[later].astype(F32) * keys[earlier].astype(F32) for later, earlier in pairs], marks
    )
    scores = dict(zip(pairs, [score * FACTOR for score in scores]))
    portions = {}
    for later in range(1, len(queries)):
        row = [scores[later, earlier] for earlier in range(later + 1)]
        top = functools.reduce(jnp.maximum, row)
        powers = [jnp.exp(score - top) for score in row]
        total = functools.reduce(jnp.add, powers)
        for earlier in range(later + 1):
            portions[later, earlier] = powers[earlier] / total
    return portions


def codec_parts(packed_ref, width):
    positions = packed_ref.shape[0]
    return [
        [packed_ref[t, :, width * part : width * (part + 1)] for t in range(positions)]
        for part in range(3)
    ]


def codec_attend_kernel(packed_ref, normed_ref, marks_ref, out_ref):
    positions, _, width = normed_ref.shape
    out_ref[:, :, :width] = normed_ref[...]
    queries, keys, values = codec_parts(packed_ref, width)
    marks = marks_ref[...]
    pairs = position_pairs(positions)
    portions = codec_portions(queries, keys, marks, pairs)
    wide = dict(zip(pairs, codec_spread([portions[pair] for pair in pairs], marks)))
    out_ref[0, :, width:] = values[0]
    for later in range(1, positions):
        terms = [wide[later, e] * values[e].astype(F32) for e in range(later + 1)]
        out_ref[later, :, width:] = functools.reduce(jnp.add, terms).astype(BF)


def codec_attend_grads_kernel(packed_ref, grad_ref, marks_ref, out_ref):
    positions, _, width = grad_ref.shape
    queries, keys, values = codec_parts(packed_ref, width)
    marks = marks_ref[...]
    pairs = position_pairs(positions)
    portions = codec_portions(queries, keys, marks, pairs)
    grads = [grad_ref[t].astype(F32) for t in range(positions)]
    portion_grads = dict(
        zip(
            pairs,
            codec_sums([grads[later] * values[earlier].astype(F32) for later, earlier in pairs], marks),
        )
    )
    score_grads = {}
    for later in range(1, positions):
        mean = functools.reduce(
            jnp.add, [portions[later, e] * portion_grads[later, e] for e in range(later + 1)]
        )
        for e in range(later + 1):
            score_grads[later, e] = portions[later, e] * (portion_grads[later, e] - mean)
    wide = dict(zip(pairs, codec_spread([portions[pair] for pair in pairs], marks)))
    wide_grads = dict(zip(pairs, codec_spread([score_grads[pair] for pair in pairs], marks)))
    zero = jnp.zeros_like(grads[0])
    for t in range(positions):
        query_grad = key_grad = zero
        value_grad = grads[0] if t == 0 else zero
        for later, earlier in pairs:
            if later == t:
                query_grad = query_grad + wide_grads[later, earlier] * keys[earlier].astype(F32)
            if earlier == t:
                key_grad = key_grad + wide_grads[later, earlier] * queries[later].astype(F32)
                value_grad = value_grad + wide[later, earlier] * grads[later]
        out_ref[t, :, :width] = (query_grad * FACTOR).astype(BF)
        out_ref[t, :, width : 2 * width] = (key_grad * FACTOR).astype(BF)
        out_ref[t, :, 2 * width :] = value_grad.astype(BF)


def codec_tile(frame_total):
    return 64 if frame_total % 64 == 0 else frame_total


def codec_spec(positions, tile, breadth):
    return pl.BlockSpec((positions, tile, breadth), lambda i: (0, i, 0))


def head_marks(width):
    return (
        jnp.arange(width)[:, None] // HEAD == jnp.arange(LANES)[None, :]
    ).astype(BF)


def codec_attend_call(packed, normed):
    positions, total, triple = packed.shape
    width = triple // 3
    tile = codec_tile(total)
    return pl.pallas_call(
        codec_attend_kernel,
        grid=(total // tile,),
        in_specs=[
            codec_spec(positions, tile, triple),
            codec_spec(positions, tile, width),
            whole_block((width, LANES)),
        ],
        out_specs=codec_spec(positions, tile, 2 * width),
        out_shape=jax.ShapeDtypeStruct((positions, total, 2 * width), BF),
        compiler_params=pltpu.CompilerParams(vmem_limit_bytes=VMEM_LIMIT),
        cost_estimate=HINT,
        name="codec_attend",
    )(packed, normed.reshape(positions, total, width), head_marks(width))


def codec_attend_grads_call(packed, grads):
    positions, total, triple = packed.shape
    width = triple // 3
    tile = codec_tile(total)
    return pl.pallas_call(
        codec_attend_grads_kernel,
        grid=(total // tile,),
        in_specs=[
            codec_spec(positions, tile, triple),
            codec_spec(positions, tile, width),
            whole_block((width, LANES)),
        ],
        out_specs=codec_spec(positions, tile, triple),
        out_shape=jax.ShapeDtypeStruct((positions, total, triple), BF),
        compiler_params=pltpu.CompilerParams(vmem_limit_bytes=VMEM_LIMIT),
        cost_estimate=HINT,
        name="codec_attend_grads",
    )(packed, grads, head_marks(width))


BITS = {"y": ("mp", 2), "x": ("seq", 1), "n": ("seq", 2), "f": ("seq", 4)}


def grad_order(place):
    flips = []
    for bits in ((1, 2, 4), (2, 1, 4), (1, 2, 4)):
        for step in range(8):
            flips.append(sum(bit for at, bit in enumerate(bits) if not (step >> (2 - at)) & 1))
    return jnp.stack(
        [place.mp ^ 2, place.mp] + [place.seq ^ flip for flip in flips] + [place.seq]
    ).astype(jnp.int32)


STEPS = {"y": (2, "xnf"), "n": (10, "nxf"), "x": (18, "xnf")}
OWN_SEQ = 26


def keep_flags(order_ref, seq):
    change = order_ref[OWN_SEQ] ^ seq
    return {"x": 1 - (change & 1), "n": 1 - ((change >> 1) & 1), "f": 1 - ((change >> 2) & 1)}


def grad_rows_kernel(stages, wide, order_ref, far_own, far_rec, own_own, own_rec, latter_own, latter_rec, *refs):
    send_ref, keep_ref, turned = refs[-3:]
    rows = latter_own.shape[0]
    height = far_own.shape[1]

    @pl.when(pl.program_id(0) == 0)
    def _():
        for at, (own, rec) in enumerate(((far_own, far_rec), (own_own, own_rec))):
            turned[height * at : height * (at + 1), :rows] = own[...].T
            turned[height * at : height * (at + 1), rows:] = rec[...].T

    total = matmul(turned[:, :rows], latter_own[...]) + matmul(turned[:, rows:], latter_rec[...])
    store = grad_store_wide if wide else grad_store
    store(stages, order_ref, total.astype(BF), height, send_ref, keep_ref)


def grad_store_wide(stages, order_ref, total, height, send_ref, keep_ref):
    units = height // TILE
    chunks = total.shape[1] // 8 // LANES
    for seq in range(8):
        flags = keep_flags(order_ref, seq)
        for chunk in range(chunks):
            first = (seq * chunks + chunk) * LANES
            for unit in range(units):
                at = chunk * units + unit
                for kept in range(2):
                    start = height * kept + unit * TILE
                    value = total[start : start + TILE, first : first + LANES]
                    spot = {**flags, "y": kept}
                    where = tuple(spot[stage] for stage in stages[1:])
                    for target, when in ((send_ref, 0), (keep_ref, 1)):

                        @pl.when(spot[stages[0]] == when)
                        def _(target=target, where=where, at=at, value=value):
                            target[(*where, at)] = value


def grad_store(stages, order_ref, total, height, send_ref, keep_ref):
    chunks = total.shape[1] // LANES
    for chunk in range(chunks):
        value = total[:, chunk * LANES : (chunk + 1) * LANES]
        given, kept = value[:height], value[height:]
        if stages[0] == "y":
            send_ref[0, 0, 0, chunk] = given
            keep_ref[0, 0, 0, chunk] = kept
        else:
            spots = [tuple(side if stage == "y" else 0 for stage in stages[1:]) for side in range(2)]
            for target, when in ((send_ref, pl.program_id(0) < 4), (keep_ref, pl.program_id(0) >= 4)):

                @pl.when(when)
                def _(target=target, given=given, kept=kept, chunk=chunk):
                    target[(*spots[0], chunk)] = given
                    target[(*spots[1], chunk)] = kept


def grad_buffers(units):
    return [jax.ShapeDtypeStruct((2, 2, 2, units, TILE, LANES), BF)] * 2


def grad_call(kernel, order, arrays, in_specs, out_specs, units, into, steps, scratch, flops, name):
    aliases = {}
    moved = 2 * sum(array.size for array in arrays)
    if into is not None:
        aliases = {len(arrays) + 1: 0, len(arrays) + 2: 1}
        in_specs = in_specs + [pl.BlockSpec(memory_space=pl.ANY)] * 2
        arrays = arrays + list(into)
    return pl.pallas_call(
        kernel,
        grid_spec=pltpu.PrefetchScalarGridSpec(
            num_scalar_prefetch=1,
            grid=(steps,),
            in_specs=in_specs,
            out_specs=out_specs,
            scratch_shapes=[scratch],
        ),
        out_shape=grad_buffers(units),
        input_output_aliases=aliases,
        compiler_params=pltpu.CompilerParams(vmem_limit_bytes=VMEM_LIMIT),
        cost_estimate=HINT,
        name=name,
    )(order, *arrays)


def grad_rows(former, latter, order, stages, units, offset, into=None):
    former, skip, height = former
    latter, latter_skip, breadth = latter
    rows = latter[0].shape[0]
    height = height // 4
    skip = skip // height
    wide = breadth // 8 == LANES
    chunks = breadth // 8 // LANES
    steps = 1 if wide else 8
    arrays = [former[0], former[1], former[0], former[1], latter[0], latter[1]]
    former_specs = [
        pl.BlockSpec((rows, height), lambda j, t, at=at: (0, skip + t[at]), pipeline_mode=pl.Buffered(1))
        for at in (0, 0, 1, 1)
    ]
    if wide:
        latter_specs = [
            pl.BlockSpec((rows, breadth), lambda j, t: (0, latter_skip // breadth))
        ] * 2
        block = (2, 2, 2, 1, TILE, LANES)
        out_specs = [pl.BlockSpec(block, lambda j, t: (0, 0, 0, offset, 0, 0))] * 2
    else:
        base = offset // chunks
        table, names = STEPS[stages[0]]
        bits = {name: 2 - at for at, name in enumerate(names)}
        if stages[0] == "y":
            block = (1, 1, 1, chunks, TILE, LANES)

            def where(j):
                return tuple((j >> bits[stage]) & 1 for stage in stages[1:]) + (base, 0, 0)

            out_specs = [pl.BlockSpec(block, lambda j, t: where(j))] * 2
        else:
            block = tuple(2 if stage == "y" else 1 for stage in stages[1:]) + (chunks, TILE, LANES)

            def where(j):
                return tuple(
                    0 if stage == "y" else (j >> bits[stage]) & 1 for stage in stages[1:]
                ) + (base, 0, 0)

            out_specs = [
                pl.BlockSpec(block, lambda j, t: where(jnp.minimum(j, 3))),
                pl.BlockSpec(block, lambda j, t: where(jnp.maximum(j - 4, 0))),
            ]
        latter_specs = [
            pl.BlockSpec(
                (rows, breadth // 8),
                lambda j, t: (0, latter_skip // (breadth // 8) + t[table + j]),
            )
        ] * 2
    return grad_call(
        functools.partial(grad_rows_kernel, stages, wide),
        order,
        arrays,
        former_specs + latter_specs,
        out_specs,
        units,
        into,
        steps,
        pltpu.VMEM((2 * height, 2 * rows), BF),
        2 * 2 * rows * 2 * height * breadth,
        "grad_rows",
    )


def grad_columns_kernel(stages, order_ref, latter_own, latter_rec, former_own, former_rec, *refs):
    send_ref, keep_ref, turned = refs[-3:]
    rows = latter_own.shape[0]
    step = pl.program_id(0)

    @pl.when(step == 0)
    def _():
        turned[:, :rows] = latter_own[...].T
        turned[:, rows:] = latter_rec[...].T

    total = matmul(turned[:, :rows], former_own[...]) + matmul(turned[:, rows:], former_rec[...])
    total = total.astype(BF)
    chunks = total.shape[1] // LANES
    for target, when in ((send_ref, step < pl.num_programs(0) // 2), (keep_ref, step >= pl.num_programs(0) // 2)):

        @pl.when(when)
        def _(target=target):
            for seq in range(8):
                flags = keep_flags(order_ref, seq)
                where = tuple(flags[stage] for stage in stages[1:])
                for chunk in range(chunks):
                    half = (chunk % 2) * LANES
                    target[(*where, chunk // 2, slice(half, half + LANES))] = total[
                        seq * LANES : (seq + 1) * LANES, chunk * LANES : (chunk + 1) * LANES
                    ]


def grad_columns(former, latter, order, stages, units, offset, into=None):
    former, skip, height = former
    latter, latter_skip, breadth = latter
    rows = latter[0].shape[0]
    height = height // 4
    step = min(512, height)
    per = height // step
    block = (2, 2, 2, step // TILE, TILE, LANES)
    base = offset // (step // TILE)
    latter_specs = [
        pl.BlockSpec(
            (rows, breadth), lambda j, t: (0, latter_skip // breadth), pipeline_mode=pl.Buffered(1)
        )
    ] * 2
    former_specs = [
        pl.BlockSpec((rows, step), lambda j, t: (0, skip // step + t[j // per] * per + j % per))
    ] * 2
    out_specs = [
        pl.BlockSpec(block, lambda j, t: (0, 0, 0, base + jnp.minimum(j, per - 1), 0, 0)),
        pl.BlockSpec(block, lambda j, t: (0, 0, 0, base + jnp.maximum(j - per, 0), 0, 0)),
    ]
    return grad_call(
        functools.partial(grad_columns_kernel, stages),
        order,
        [latter[0], latter[1], former[0], former[1]],
        latter_specs + former_specs,
        out_specs,
        units,
        into,
        2 * per,
        pltpu.VMEM((breadth, 2 * rows), BF),
        2 * 2 * rows * 2 * height * breadth,
        "grad_columns",
    )


def grad_table_kernel(stages, height, order_ref, codes_ref, latter_own, latter_rec, *refs):
    send_ref, keep_ref, _ = refs[-3:]
    rows = latter_own.shape[0]
    parts = []
    for at in range(2):
        entry = order_ref[at] * height + lax.broadcasted_iota(jnp.int32, (height, 2 * rows), 0)
        parts.append((entry == codes_ref[...]).astype(F32).astype(BF))
    chosen = jnp.concatenate(parts, axis=0)
    total = matmul(chosen[:, :rows], latter_own[...]) + matmul(chosen[:, rows:], latter_rec[...])
    grad_store_wide(stages, order_ref, total.astype(BF), height, send_ref, keep_ref)


def grad_table(codes, latter, order, stages, height, units, offset, into=None):
    rows, breadth = latter[0].shape
    block = (2, 2, 2, height // TILE, TILE, LANES)
    base = offset // (height // TILE)
    return grad_call(
        functools.partial(grad_table_kernel, stages, height),
        order,
        [codes, latter[0], latter[1]],
        [whole_block(codes.shape), whole_block((rows, breadth)), whole_block((rows, breadth))],
        [pl.BlockSpec(block, lambda j, t: (0, 0, 0, base, 0, 0))] * 2,
        units,
        into,
        1,
        pltpu.VMEM((8, LANES), F32),
        2 * 2 * rows * 2 * height * breadth,
        "grad_table",
    )


def rows_from_units(units, height):
    tiles = height // TILE
    chunks = units.shape[0] // tiles
    return jnp.transpose(
        units.reshape(chunks, height, LANES), (1, 0, 2)
    ).reshape(height, chunks * LANES)


def columns_from_units(units):
    count = units.shape[0]
    return jnp.transpose(units.reshape(2 * count, LANES, LANES), (0, 2, 1)).reshape(count * TILE, LANES)


PACK = 1024


def pack_rows(members):
    return sum(member.shape[0] * (member.shape[1] // PACK) for member in members)


def pack_pieces(shapes):
    found, start = [], 0
    for at, (height, breadth) in enumerate(shapes):
        for column in range(breadth // PACK):
            found.append((at, column, height, start))
            start += height
    return found


def columns_of(column):
    return pl.ds(column * PACK, PACK)


def pack_kernel(place_ref, *refs):
    members, (pack_ref, quarter_ref, held, sems, out_sems) = refs[:-5], refs[-5:]
    rows = held.shape[0] // 4
    copies = []
    for number, (at, column, height, start) in enumerate(pack_pieces([m.shape for m in members])):
        copies.append(
            pltpu.make_async_copy(
                members[at].at[:, columns_of(column)], held.at[pl.ds(start, height)], sems.at[number]
            )
        )
    for copy in copies:
        copy.start()
    for copy in copies:
        copy.wait()
    mine = pl.ds(pl.multiple_of(place_ref[1] * rows, 16), rows)
    whole = pltpu.make_async_copy(held, pack_ref, out_sems.at[0])
    part = pltpu.make_async_copy(held.at[mine], quarter_ref, out_sems.at[1])
    part.start()
    whole.start()
    part.wait()
    whole.wait()


def pack_call(members, spots):
    rows = pack_rows(members)
    any_spec = pl.BlockSpec(memory_space=pl.ANY)
    count = len(pack_pieces([m.shape for m in members]))
    return pl.pallas_call(
        pack_kernel,
        in_specs=[pl.BlockSpec(memory_space=pltpu.SMEM)] + [any_spec] * len(members),
        out_specs=[any_spec] * 2,
        out_shape=[
            jax.ShapeDtypeStruct((rows, PACK), BF),
            jax.ShapeDtypeStruct((rows // 4, PACK), BF),
        ],
        scratch_shapes=[
            pltpu.VMEM((rows, PACK), BF),
            pltpu.SemaphoreType.DMA((count,)),
            pltpu.SemaphoreType.DMA((2,)),
        ],
        compiler_params=pltpu.CompilerParams(vmem_limit_bytes=VMEM_LIMIT),
        cost_estimate=HINT,
        name="pack_weights",
    )(spots, *members)


def far_kernel(parts, place_ref, *refs):
    pieces, (out_ref, held, sems, out_sem) = refs[:-4], refs[-4:]
    quarter = held.shape[0] // 4
    copies = []
    for number, (piece, (change, offset)) in enumerate(zip(pieces, parts)):
        start = (place_ref[1] ^ change) * quarter + offset
        copies.append(
            pltpu.make_async_copy(
                piece, held.at[pl.ds(pl.multiple_of(start, 16), piece.shape[0])], sems.at[number]
            )
        )
    for copy in copies:
        copy.start()
    for copy in copies:
        copy.wait()
    whole = pltpu.make_async_copy(held, out_ref, out_sem.at[0])
    whole.start()
    whole.wait()


def far_pack(pieces, parts, spots):
    rows = sum(piece.shape[0] for piece in pieces)
    any_spec = pl.BlockSpec(memory_space=pl.ANY)
    return pl.pallas_call(
        functools.partial(far_kernel, parts),
        in_specs=[pl.BlockSpec(memory_space=pltpu.SMEM)] + [any_spec] * len(pieces),
        out_specs=any_spec,
        out_shape=jax.ShapeDtypeStruct((rows, PACK), BF),
        scratch_shapes=[
            pltpu.VMEM((rows, PACK), BF),
            pltpu.SemaphoreType.DMA((len(pieces),)),
            pltpu.SemaphoreType.DMA((1,)),
        ],
        compiler_params=pltpu.CompilerParams(vmem_limit_bytes=VMEM_LIMIT),
        cost_estimate=HINT,
        name="far_pack",
    )(spots, *pieces)


def join_kernel(shapes, flips, place_ref, *refs):
    count = len(flips)
    packs = refs[:count]
    outs, (held, sems, out_sems) = refs[-3 - len(shapes) : -3], refs[-3:]
    rows = held.shape[0] // count
    for number, pack in enumerate(packs):
        pltpu.make_async_copy(pack, held.at[pl.ds(number * rows, rows)], sems.at[number]).start()
    copies = []
    for number, flip in enumerate(flips):
        pltpu.make_async_copy(
            packs[number], held.at[pl.ds(number * rows, rows)], sems.at[number]
        ).wait()
        for at, column, height, start in pack_pieces(shapes):
            target = pl.multiple_of((place_ref[0] ^ flip) * height, height)
            copies.append(
                pltpu.make_async_copy(
                    held.at[pl.ds(number * rows + start, height)],
                    outs[at].at[pl.ds(target, height), columns_of(column)],
                    out_sems.at[len(copies)],
                )
            )
            copies[-1].start()
    for copy in copies:
        copy.wait()


def join_weights(members, packs, flips, spots, into=None):
    shapes = [member.shape for member in members]
    rows = pack_rows(members)
    any_spec = pl.BlockSpec(memory_space=pl.ANY)
    outs = [jax.ShapeDtypeStruct((4 * height, breadth), BF) for height, breadth in shapes]
    count = len(flips)
    held = [] if into is None else list(into)
    return pl.pallas_call(
        functools.partial(join_kernel, shapes, flips),
        in_specs=[pl.BlockSpec(memory_space=pltpu.SMEM)] + [any_spec] * (count + len(held)),
        out_specs=[any_spec] * len(outs),
        out_shape=outs,
        input_output_aliases={1 + count + at: at for at in range(len(held))},
        scratch_shapes=[
            pltpu.VMEM((count * rows, PACK), BF),
            pltpu.SemaphoreType.DMA((count,)),
            pltpu.SemaphoreType.DMA((count * len(pack_pieces(shapes)),)),
        ],
        compiler_params=pltpu.CompilerParams(vmem_limit_bytes=VMEM_LIMIT),
        cost_estimate=HINT,
        name="join_weights",
    )(spots, *packs, *held)


WIDE_LIMIT = 58 * 1024 * 1024
GELU_A = 0.7978845608028654
GELU_B = 0.044715


def gelu_pair(values):
    square = values * values
    bent = jnp.tanh(GELU_A * values * (1.0 + GELU_B * square))
    half = 0.5 * (1.0 + bent)
    slope = half + 0.5 * values * (1.0 - bent * bent) * (GELU_A * (1.0 + 3.0 * GELU_B * square))
    return values * half, slope


def rms_grads(values, gain, grad):
    inverse = lax.rsqrt(jnp.mean(values * values, axis=-1, keepdims=True) + EPSILON)
    scaled = values * inverse
    inner = grad * gain
    part = inverse * (inner - scaled * jnp.mean(inner * scaled, axis=-1, keepdims=True))
    return part, jnp.sum(grad * scaled, axis=0, keepdims=True)


def held(shape):
    return pl.BlockSpec(
        shape, lambda *_: (0,) * len(shape), pipeline_mode=pl.Buffered(1)
    )


def dense_call(kernel, steps, in_specs, out_specs, out_shape, scratch, name):
    return pl.pallas_call(
        kernel,
        grid=(steps,),
        in_specs=in_specs,
        out_specs=out_specs,
        out_shape=out_shape,
        scratch_shapes=scratch,
        compiler_params=pltpu.CompilerParams(vmem_limit_bytes=WIDE_LIMIT),
        cost_estimate=HINT,
        name=name,
    )


def frame_front_kernel(hidden_ref, gain_ref, weight_ref, normed_ref, packed_ref):
    groups, rows, own, _ = packed_ref.shape

    @pl.when(pl.program_id(0) == 0)
    def _():
        normed_ref[...] = rms_scale(hidden_ref[...].astype(F32), gain_ref[...]).astype(BF)

    total = matmul(normed_ref[...], weight_ref[...]).astype(BF)
    for part in range(3):

        @pl.when(pl.program_id(0) == part)
        def _(part=part):
            for group in range(groups):
                packed_ref[group, :, :, LANES * part : LANES * (part + 1)] = total[
                    :, LANES * group : LANES * (group + 1)
                ].reshape(rows, own, LANES)


def frame_front(hidden, gain, weight, rows):
    total, width = hidden.shape
    groups = width // LANES
    shape = (groups, rows, total // rows, 3 * LANES)
    return dense_call(
        frame_front_kernel,
        3,
        [held(hidden.shape), held(gain.shape), pl.BlockSpec((width, width), lambda j: (0, j))],
        [whole_block((total, width)), whole_block(shape)],
        [jax.ShapeDtypeStruct((total, width), BF), jax.ShapeDtypeStruct(shape, BF)],
        [],
        "frame_front",
    )(hidden, gain, weight)


def frame_rear_kernel(
    hidden_ref, front_ref, packed_ref, gain_ref, output_ref, expand_ref, contract_ref,
    kept_ref, mixed_ref, slope_ref, base_ref, total, normed_ref,
):
    groups, rows, own, _ = packed_ref.shape
    width = groups * LANES
    tile = slope_ref.shape[1]

    @pl.when(pl.program_id(0) == 0)
    def _():
        for group in range(groups):
            kept_ref[:, width + LANES * group : width + LANES * (group + 1)] = packed_ref[
                group
            ].reshape(rows * own, LANES)
        attended = kept_ref[:, width : 2 * width]
        mixed = hidden_ref[...].astype(F32) + matmul(attended, output_ref[...])
        mixed_ref[...] = mixed
        total[...] = mixed
        normed_ref[...] = rms_scale(mixed, gain_ref[...]).astype(BF)
        kept_ref[:, :width] = front_ref[...]
        kept_ref[:, 2 * width : 3 * width] = normed_ref[...]

    active, slope = gelu_pair(matmul(normed_ref[...], expand_ref[...]))
    active = active.astype(BF)
    for step in range(4 * width // tile):

        @pl.when(pl.program_id(0) == step)
        def _(step=step):
            kept_ref[:, 3 * width + step * tile : 3 * width + (step + 1) * tile] = active

    slope_ref[...] = slope.astype(BF)
    total[...] += matmul(active, contract_ref[...])

    @pl.when(pl.program_id(0) == pl.num_programs(0) - 1)
    def _():
        base_ref[...] = total[...].astype(BF)


FF_TILE = 512
FRAME_TILE = 1024


def frame_rear(hidden, front, packed, gain, output, expand, contract):
    total, width = hidden.shape
    inner = expand.shape[1]
    tile = FRAME_TILE
    full = whole_block((total, width))
    kept = (total, 3 * width + inner)
    return dense_call(
        frame_rear_kernel,
        inner // tile,
        [
            held(hidden.shape),
            held(front.shape),
            held(packed.shape),
            held(gain.shape),
            held(output.shape),
            pl.BlockSpec((width, tile), lambda j: (0, j)),
            pl.BlockSpec((tile, width), lambda j: (j, 0)),
        ],
        [whole_block(kept), full, pl.BlockSpec((total, tile), lambda j: (0, j)), full],
        [
            jax.ShapeDtypeStruct(kept, BF),
            jax.ShapeDtypeStruct((total, width), F32),
            jax.ShapeDtypeStruct((total, inner), BF),
            jax.ShapeDtypeStruct((total, width), BF),
        ],
        [pltpu.VMEM((total, width), F32), pltpu.VMEM((total, width), BF)],
        "frame_rear",
    )(hidden, front, packed, gain, output, expand, contract)


def frame_rear_grads_kernel(
    grad_ref, slope_ref, mixed_ref, gain_ref, output_ref, expand_ref, contract_ref,
    kept_ref, mixed_grad_ref, packed_ref, gain_grad_ref, total,
):
    groups, rows, own, _ = packed_ref.shape
    width = groups * LANES
    tile = slope_ref.shape[1]
    grad = grad_ref[...]
    expand_in = (slope_ref[...].astype(F32) * inner_right(grad, contract_ref[...])).astype(BF)
    for step in range(4 * width // tile):

        @pl.when(pl.program_id(0) == step)
        def _(step=step):
            kept_ref[:, width + step * tile : width + (step + 1) * tile] = expand_in

    @pl.when(pl.program_id(0) == 0)
    def _():
        total[...] = jnp.zeros_like(total)
        kept_ref[:, :width] = grad

    total[...] += inner_right(expand_in, expand_ref[...])

    @pl.when(pl.program_id(0) == pl.num_programs(0) - 1)
    def _():
        part, gain_grad = rms_grads(mixed_ref[...], gain_ref[...], total[...])
        mixed_grad = grad.astype(F32) + part
        mixed_grad_ref[...] = mixed_grad
        gain_grad_ref[...] = gain_grad
        output_in = mixed_grad.astype(BF)
        kept_ref[:, 5 * width :] = output_in
        attended_grad = inner_right(output_in, output_ref[...]).astype(BF)
        for group in range(groups):
            packed_ref[group] = attended_grad[:, LANES * group : LANES * (group + 1)].reshape(
                rows, own, LANES
            )


def frame_rear_grads(grad, slope, mixed, gain, output, expand, contract, rows):
    total, width = grad.shape
    inner = expand.shape[1]
    tile = FRAME_TILE
    shape = (width // LANES, rows, total // rows, LANES)
    kept = (total, 2 * width + inner)
    full = whole_block((total, width))
    part = pl.BlockSpec((total, tile), lambda j: (0, j))
    return dense_call(
        frame_rear_grads_kernel,
        inner // tile,
        [
            held(grad.shape),
            part,
            held(mixed.shape),
            held(gain.shape),
            held(output.shape),
            pl.BlockSpec((width, tile), lambda j: (0, j)),
            pl.BlockSpec((tile, width), lambda j: (j, 0)),
        ],
        [whole_block(kept), full, whole_block(shape), whole_block((1, width))],
        [
            jax.ShapeDtypeStruct(kept, BF),
            jax.ShapeDtypeStruct((total, width), F32),
            jax.ShapeDtypeStruct(shape, BF),
            jax.ShapeDtypeStruct((1, width), F32),
        ],
        [pltpu.VMEM((total, width), F32)],
        "frame_rear_grads",
    )(grad, slope, mixed, gain, output, expand, contract)


def frame_front_grads_kernel(
    packed_ref, hidden_ref, gain_ref, mixed_grad_ref, weight_ref,
    projected_ref, grad_ref, gain_grad_ref, total,
):
    groups, rows, own, _ = packed_ref.shape

    @pl.when(pl.program_id(0) == 0)
    def _():
        total[...] = jnp.zeros_like(total)

    for part in range(3):

        @pl.when(pl.program_id(0) == part)
        def _(part=part):
            for group in range(groups):
                projected_ref[:, LANES * group : LANES * (group + 1)] = packed_ref[
                    group, :, :, LANES * part : LANES * (part + 1)
                ].reshape(rows * own, LANES)

    total[...] += inner_right(projected_ref[...], weight_ref[...])

    @pl.when(pl.program_id(0) == 2)
    def _():
        part, gain_grad = rms_grads(hidden_ref[...].astype(F32), gain_ref[...], total[...])
        grad_ref[...] = mixed_grad_ref[...] + part
        gain_grad_ref[...] = gain_grad


def frame_front_grads(packed, hidden, gain, mixed_grad, weight):
    total, width = hidden.shape
    return dense_call(
        frame_front_grads_kernel,
        3,
        [
            held(packed.shape),
            held(hidden.shape),
            held(gain.shape),
            held(mixed_grad.shape),
            pl.BlockSpec((width, width), lambda j: (0, j)),
        ],
        [
            pl.BlockSpec((total, width), lambda j: (0, j)),
            whole_block((total, width)),
            whole_block((1, width)),
        ],
        [
            jax.ShapeDtypeStruct((total, 3 * width), BF),
            jax.ShapeDtypeStruct((total, width), F32),
            jax.ShapeDtypeStruct((1, width), F32),
        ],
        [pltpu.VMEM((total, width), F32)],
        "frame_front_grads",
    )(packed, hidden, gain, mixed_grad, weight)


def codec_front_kernel(base_ref, entries_ref, gain_ref, weight_ref, normed_ref, packed_ref, normed):
    positions = packed_ref.shape[0]

    @pl.when(pl.program_id(0) == 0)
    def _():
        base = base_ref[...].astype(F32)
        size = base.shape[0]
        for t in range(positions):
            hidden = base if t == 0 else base + entries_ref[t - 1].astype(F32)
            normed[size * t : size * (t + 1)] = rms_scale(hidden, gain_ref[...]).astype(BF)
        normed_ref[...] = normed[...]

    total = matmul(normed[...], weight_ref[...]).astype(BF)
    packed_ref[...] = total.reshape(packed_ref.shape)


def codec_front(base, entries, gain, weight):
    total, width = base.shape
    positions = entries.shape[0] + 1
    return dense_call(
        codec_front_kernel,
        6,
        [
            held(base.shape),
            held(entries.shape),
            held(gain.shape),
            pl.BlockSpec((width, width // 2), lambda j: (0, j)),
        ],
        [
            whole_block((positions * total, width)),
            pl.BlockSpec((positions, total, width // 2), lambda j: (0, 0, j)),
        ],
        [
            jax.ShapeDtypeStruct((positions * total, width), BF),
            jax.ShapeDtypeStruct((positions, total, 3 * width), BF),
        ],
        [pltpu.VMEM((positions * total, width), BF)],
        "codec_front",
    )(base, entries, gain, weight)


def codec_rear_kernel(
    base_ref, entries_ref, attended_ref, grad_ref, gain_ref, output_ref, expand_ref, contract_ref,
    mixed_ref, active_ref, expand_kept_ref, kept_ref, mixed_grad_ref,
    attended_grad_ref, gain_grad_ref, total,
):
    width = total.shape[1]
    positions = entries_ref.shape[0] + 1
    size = base_ref.shape[0]

    @pl.when(pl.program_id(0) == 0)
    def _():
        base = base_ref[...].astype(F32)
        for t in range(positions):
            own = slice(size * t, size * (t + 1))
            hidden = base if t == 0 else base + entries_ref[t - 1].astype(F32)
            mixed = hidden + matmul(attended_ref[own], output_ref[...])
            mixed_ref[own] = mixed
            expand_kept_ref[own, :width] = rms_scale(mixed, gain_ref[...]).astype(BF)
        total[...] = jnp.zeros_like(total)

    active, slope = gelu_pair(matmul(expand_kept_ref[:, :width], expand_ref[...]))
    active_ref[...] = active.astype(BF)
    expand_in = (slope * inner_right(grad_ref[...], contract_ref[...])).astype(BF)
    tile = expand_in.shape[1]
    for step in range(4 * width // tile):

        @pl.when(pl.program_id(0) == step)
        def _(step=step):
            expand_kept_ref[:, width + step * tile : width + (step + 1) * tile] = expand_in

    total[...] += inner_right(expand_in, expand_ref[...])

    @pl.when(pl.program_id(0) == pl.num_programs(0) - 1)
    def _():
        gain_grads = jnp.zeros_like(gain_grad_ref)
        for t in range(positions):
            own = slice(size * t, size * (t + 1))
            part, gain_grad = rms_grads(mixed_ref[own], gain_ref[...], total[own])
            gain_grads = gain_grads + gain_grad
            mixed_grad = grad_ref[own].astype(F32) + part
            mixed_grad_ref[own] = mixed_grad
            output_in = mixed_grad.astype(BF)
            kept_ref[own] = output_in
            attended_grad_ref[t] = inner_right(output_in, output_ref[...]).astype(BF)
        gain_grad_ref[...] = gain_grads


def codec_rear(base, entries, kept, grad, gain, output, expand, contract):
    size, width = base.shape
    total = kept.shape[0]
    inner = expand.shape[1]
    tile = FF_TILE
    full = whole_block((total, width))
    wide = (total, width + inner)
    high = jax.ShapeDtypeStruct((total, width), F32)
    return dense_call(
        codec_rear_kernel,
        inner // tile,
        [
            held(base.shape),
            held(entries.shape),
            pl.BlockSpec((total, width), lambda j: (0, 1), pipeline_mode=pl.Buffered(1)),
            held(grad.shape),
            held(gain.shape),
            held(output.shape),
            pl.BlockSpec((width, tile), lambda j: (0, j)),
            pl.BlockSpec((tile, width), lambda j: (j, 0)),
        ],
        [
            held((total, width)),
            pl.BlockSpec((total, tile), lambda j: (0, j)),
            held(wide),
            held((total, width)),
            held((total, width)),
            held((total // size, size, width)),
            whole_block((1, width)),
        ],
        [
            high,
            jax.ShapeDtypeStruct((total, inner), BF),
            jax.ShapeDtypeStruct(wide, BF),
            jax.ShapeDtypeStruct((total, width), BF),
            high,
            jax.ShapeDtypeStruct((total // size, size, width), BF),
            jax.ShapeDtypeStruct((1, width), F32),
        ],
        [pltpu.VMEM((total, width), F32)],
        "codec_rear",
    )(base, entries, kept, grad, gain, output, expand, contract)


def codec_result_kernel(mixed_ref, active_ref, live_ref, contract_ref, out_ref, total):
    positions, size, _ = out_ref.shape

    @pl.when(pl.program_id(0) == 0)
    def _():
        total[...] = mixed_ref[...]

    total[...] += matmul(active_ref[...], contract_ref[...])

    @pl.when(pl.program_id(0) == pl.num_programs(0) - 1)
    def _():
        for t in range(positions):
            out_ref[t] = (total[size * t : size * (t + 1)] * live_ref[...]).astype(BF)


def codec_result(mixed, active, live, contract):
    total, width = mixed.shape
    size = live.shape[0]
    inner = active.shape[1]
    tile = FF_TILE
    shape = (total // size, size, width)
    return dense_call(
        codec_result_kernel,
        inner // tile,
        [
            held(mixed.shape),
            pl.BlockSpec((total, tile), lambda j: (0, j)),
            held(live.shape),
            pl.BlockSpec((tile, width), lambda j: (j, 0)),
        ],
        whole_block(shape),
        jax.ShapeDtypeStruct(shape, BF),
        [pltpu.VMEM((total, width), F32)],
        "codec_result",
    )(mixed, active, live, contract)


def codec_front_grads_kernel(
    grad_ref, base_ref, entries_ref, gain_ref, mixed_grad_ref, weight_ref,
    base_grad_ref, entry_grad_ref, gain_grad_ref, total,
):
    positions = entries_ref.shape[0] + 1
    size = base_ref.shape[0]

    @pl.when(pl.program_id(0) == 0)
    def _():
        total[...] = jnp.zeros_like(total)

    total[...] += inner_right(grad_ref[...], weight_ref[...])

    @pl.when(pl.program_id(0) == pl.num_programs(0) - 1)
    def _():
        base = base_ref[...].astype(F32)
        gain_grads = jnp.zeros_like(gain_grad_ref)
        base_grad = jnp.zeros_like(base)
        for t in range(positions):
            own = slice(size * t, size * (t + 1))
            hidden = base if t == 0 else base + entries_ref[t - 1].astype(F32)
            part, gain_grad = rms_grads(hidden, gain_ref[...], total[own])
            gain_grads = gain_grads + gain_grad
            grad = mixed_grad_ref[own] + part
            base_grad = base_grad + grad
            if t > 0:
                entry_grad_ref[size * (t - 1) : size * t] = grad.astype(BF)
        base_grad_ref[...] = base_grad.astype(BF)
        gain_grad_ref[...] = gain_grads


def codec_front_grads(grad, base, entries, gain, mixed_grad, weight):
    size, width = base.shape
    total = grad.shape[0]
    tile = width // 2
    return dense_call(
        codec_front_grads_kernel,
        grad.shape[1] // tile,
        [
            pl.BlockSpec((total, tile), lambda j: (0, j)),
            held(base.shape),
            held(entries.shape),
            held(gain.shape),
            held(mixed_grad.shape),
            pl.BlockSpec((width, tile), lambda j: (0, j)),
        ],
        [whole_block((size, width)), whole_block((total - size, width)), whole_block((1, width))],
        [
            jax.ShapeDtypeStruct((size, width), BF),
            jax.ShapeDtypeStruct((total - size, width), BF),
            jax.ShapeDtypeStruct((1, width), F32),
        ],
        [pltpu.VMEM((total, width), F32)],
        "codec_front_grads",
    )(grad, base, entries, gain, mixed_grad, weight)


def shards_general(
    frames,
    segments,
    padding,
    codec_tokens,
    codebooks,
    frame_prenorm,
    frame_project,
    frame_output,
    frame_postnorm,
    frame_expand,
    frame_contract,
    codec_prenorm,
    codec_project,
    codec_output,
    codec_postnorm,
    codec_expand,
    codec_contract,
    cotangent,
):
    place = Place()
    row_count, frames_dev, width = frames.shape
    frame_total = row_count * frames_dev
    positions = cotangent.shape[2]
    gains = lax.all_gather(
        jnp.stack([frame_prenorm, frame_postnorm, codec_prenorm, codec_postnorm]),
        "mp",
        axis=1,
        tiled=True,
    )
    frame_weights = (
        gains[0],
        gather_weight(frame_project, place),
        gather_weight(frame_output, place),
        gains[1],
        gather_weight(frame_expand, place),
        gather_weight(frame_contract, place),
    )
    codec_weights = (
        gains[2],
        gather_weight(codec_project, place),
        gather_weight(codec_output, place),
        gains[3],
        gather_weight(codec_expand, place),
        gather_weight(codec_contract, place),
    )
    table = gather_weight(codebooks, place)

    hidden = frames.astype(F32).reshape(frame_total, width)
    normed, projected = front_pass(hidden, frame_weights)
    attended, attention_back = frame_attention(
        projected.reshape(row_count, frames_dev, 3 * width), segments, place
    )
    attended = attended.reshape(frame_total, width)
    frame_result, frame_saved = rear_pass(hidden, attended, frame_weights)
    base = frame_result.astype(BF).astype(F32)

    table_rows = codec_tokens.reshape(positions - 1, frame_total) + (
        jnp.arange(positions - 1, dtype=jnp.int32) * CODES
    )[:, None]
    embedded = table[table_rows].astype(F32)
    codec_hidden = jnp.concatenate([base[None], base[None] + embedded], axis=0).reshape(
        positions * frame_total, width
    )
    codec_normed, codec_projected = front_pass(codec_hidden, codec_weights)
    marks = (
        jnp.arange(width)[:, None] // HEAD == jnp.arange(HEADS)[None, :]
    ).astype(F32)
    view = codec_projected.reshape(positions, frame_total, 3, width)
    queries, keys, values = ([view[t, :, part] for t in range(positions)] for part in range(3))
    soft = codec_softmax(queries, keys, marks)
    codec_attended = jnp.concatenate(codec_attend(soft, values, marks), axis=0)
    codec_result, codec_saved = rear_pass(codec_hidden, codec_attended, codec_weights)
    live = padding.reshape(frame_total).astype(F32)[None, :, None]
    output = jnp.transpose(
        (codec_result.reshape(positions, frame_total, width) * live).astype(BF), (1, 0, 2)
    ).reshape(row_count, frames_dev, positions, width)

    codec_grad = (
        jnp.transpose(cotangent.reshape(frame_total, positions, width), (1, 0, 2)).astype(F32) * live
    ).reshape(positions * frame_total, width)
    mixed_grad, attended_grad, codec_postnorm_grad, contract_in, expand_in, output_in = rear_grads(
        codec_grad, codec_saved, codec_weights
    )
    codec_contract_part = weight_grad(codec_saved[3], contract_in, place, True)
    codec_expand_part = weight_grad(codec_saved[1], expand_in, place, False)
    codec_output_part = weight_grad(codec_attended, output_in, place, True)
    grad_view = attended_grad.reshape(positions, frame_total, width)
    codec_projected_grad = codec_attend_grads(
        soft, queries, keys, values, [grad_view[t] for t in range(positions)], marks
    )
    codec_project_part = weight_grad(codec_normed, codec_projected_grad, place, True)
    input_grad, codec_prenorm_grad = front_grads(
        codec_hidden, codec_projected_grad, mixed_grad, codec_weights
    )
    input_grad = input_grad.reshape(positions, frame_total, width)
    chosen = (
        table_rows.reshape(-1)[:, None] == jnp.arange(table.shape[0], dtype=jnp.int32)[None, :]
    ).astype(BF)
    table_part = weight_grad(chosen, input_grad[1:].reshape(-1, width).astype(BF), place, False)
    base_grad = jnp.sum(input_grad, axis=0).astype(BF).astype(F32)

    (codec_contract_grad,) = finish_grads([codec_contract_part], place)
    codec_expand_grad, codec_output_grad, codec_project_grad = finish_grads(
        [codec_expand_part, codec_output_part, codec_project_part], place
    )
    (table_grad,) = finish_grads([table_part], place)

    frame_mixed_grad, frame_attended_grad, frame_postnorm_grad, contract_in, expand_in, output_in = (
        rear_grads(base_grad, frame_saved, frame_weights)
    )
    frame_projected_grad = attention_back(
        frame_attended_grad.reshape(row_count, frames_dev, width)
    ).reshape(frame_total, 3 * width)
    frame_contract_part = weight_grad(frame_saved[3], contract_in, place, True)
    frame_expand_part = weight_grad(frame_saved[1], expand_in, place, False)
    frame_output_part = weight_grad(attended, output_in, place, True)
    frame_project_part = weight_grad(normed, frame_projected_grad, place, True)
    frames_grad, frame_prenorm_grad = front_grads(
        hidden, frame_projected_grad, frame_mixed_grad, frame_weights
    )
    (frame_contract_grad,) = finish_grads([frame_contract_part], place)
    frame_expand_grad, frame_output_grad = finish_grads(
        [frame_expand_part, frame_output_part], place
    )
    (frame_project_grad,) = finish_grads([frame_project_part], place)
    gain_sums = sum_everywhere(
        jnp.stack(
            [frame_prenorm_grad, frame_postnorm_grad, codec_prenorm_grad, codec_postnorm_grad]
        ),
        place,
    )
    return (
        output,
        frames_grad.reshape(row_count, frames_dev, width),
        table_grad,
        gain_sums[0],
        frame_project_grad,
        frame_output_grad,
        gain_sums[1],
        frame_expand_grad,
        frame_contract_grad,
        gain_sums[2],
        codec_project_grad,
        codec_output_grad,
        gain_sums[3],
        codec_expand_grad,
        codec_contract_grad,
    )


class Pair:
    def __init__(self, own):
        self.own = own
        self.other = swap(own, "mp", 1)
        self.age = 0

    def both(self):
        return (self.own, self.other)


class Chain:
    def __init__(self):
        self.last = ()
        self.pending = []

    def pair(self, own):
        made = Pair(own)
        self.pending.append(made)
        return made

    def enter(self, *values):
        due = [made for made in self.pending if made.age >= 3]
        self.pending = [made for made in self.pending if made.age < 3]
        for made in self.pending:
            made.age += 1
        came = tuple(made.other for made in due)
        held = lax.optimization_barrier(tuple(values) + came + self.last)
        for made, other in zip(due, held[len(values) :]):
            made.other = other
        return held[0] if len(values) == 1 else held[: len(values)]

    def leave(self, *values):
        self.last = values


class Gather:
    def __init__(self, members, spots, whole=False):
        self.members = members
        self.spots = spots
        self.whole = whole
        self.pack, self.quarter = pack_call(members, spots)

    def start(self, chain):
        self.came = swap(chain.enter(self.pack if self.whole else self.quarter), "mp", 2)

    def send_near(self, chain):
        self.near = Pair(chain.enter(self.pack))

    def spread(self, chain):
        self.came = chain.enter(self.came)
        chain.leave(self.came)
        if self.whole:
            self.far = chain.pair(self.came)
            return
        self.over_x = swap(self.came, "seq", 1)
        self.over_n = swap(self.came, "seq", 2)

    def cross(self, chain):
        self.over_x, self.over_n = chain.enter(self.over_x, self.over_n)
        chain.leave(self.over_x, self.over_n)
        half = self.over_x.shape[0] // 2
        self.ends = (swap(self.over_n[:half], "seq", 1), swap(self.over_x[half:], "seq", 2))

    def close(self, chain):
        ends = chain.enter(*self.ends)
        parts = ((0, 0), (1, 0), (2, 0), (3, 0), (3, ends[0].shape[0]))
        far = far_pack([self.came, self.over_x, self.over_n, *ends], parts, self.spots)
        chain.leave(far)
        self.far = far

    def send(self, chain):
        self.far = Pair(chain.enter(self.far))

    def join_near(self, chain):
        packs = chain.enter(*self.near.both())
        self.outs = join_weights(self.members, packs, (0, 1), self.spots)
        chain.leave(*self.outs)

    def join(self, chain):
        packs = chain.enter(*self.far.both())
        outs = join_weights(self.members, packs, (2, 3), self.spots, self.outs)
        chain.leave(*outs)
        return outs


def load(block, riders):
    if riders is None:
        return block
    high = riders.astype(BF)
    low = (riders - high.astype(F32)).astype(BF)
    return jnp.concatenate(
        [part.reshape(-1, LANES) for part in (block, high, low)], axis=0
    )


def unload(message, shape, riders):
    if riders is None:
        return message, None
    rows = message.shape[0] - 2 * riders.size // LANES
    high, low = (
        part.astype(F32).reshape(riders.shape) for part in jnp.split(message[rows:], 2, axis=0)
    )
    return message[:rows].reshape(shape), riders + (high + low)


class Reduce:
    def __init__(self, stages, blocks, riders=None):
        self.stages = stages
        self.keep = blocks[1]
        self.riders = riders
        self.came = []
        self.shape = blocks[0].shape
        self.coming = swap(load(blocks[0], riders), *BITS[stages[0]])

    def arrive(self, chain):
        self.coming = chain.enter(self.coming)
        chain.leave(self.coming)

    def take(self, chain):
        self.keep, self.coming, *self.came = chain.enter(self.keep, self.coming, *self.came)
        block, self.riders = unload(self.coming, self.shape, self.riders)
        self.came.append(block)

    def total(self, last):
        at = len(self.came) - 1
        spot = (1,) * at + ((0,) if not last else ())
        value = self.keep[spot].astype(F32) if spot else self.keep.astype(F32)
        for level, came in enumerate(self.came):
            value = value + came[spot[level:]].astype(F32)
        return value

    def give(self, chain):
        self.take(chain)
        given = self.total(False).astype(BF)
        self.shape = given.shape
        return given

    def step(self, chain):
        given = self.give(chain)
        message = load(given, self.riders)
        chain.leave(message)
        self.coming = swap(message, *BITS[self.stages[len(self.came)]])

    def result(self):
        return self.total(True)


def together(sums, chain, stage):
    given = [one.give(chain) for one in sums]
    message = jnp.concatenate(given, axis=-3)
    chain.leave(message)
    message = swap(message, *BITS[stage])

    def take():
        held = chain.enter(message)
        chain.leave(held)
        start = 0
        for one, part in zip(sums, given):
            size = part.shape[-3]
            one.coming = held[..., start : start + size, :, :]
            start += size

    return take


def finish(sums, chain):
    given = jnp.concatenate([one.give(chain) for one in sums], axis=0)
    riders = sums[-1].riders
    message = load(given, riders)
    chain.leave(message)
    message = swap(message, *BITS["f"])

    def take():
        held = chain.enter(message)
        chain.leave(held)
        came, total = unload(held, given.shape, riders)
        start = 0
        for one in sums:
            size = one.shape[-3]
            one.came.append(came[start : start + size])
            start += size
        sums[-1].riders = total

    return take


def shards(
    frames,
    segments,
    padding,
    codec_tokens,
    codebooks,
    frame_prenorm,
    frame_project,
    frame_output,
    frame_postnorm,
    frame_expand,
    frame_contract,
    codec_prenorm,
    codec_project,
    codec_output,
    codec_postnorm,
    codec_expand,
    codec_contract,
    cotangent,
):
    place = Place()
    chain = Chain()
    order = grad_order(place)
    spots = jnp.stack([place.mp, place.seq % 4]).astype(jnp.int32)
    row_count, frames_dev, width = frames.shape
    frame_total = row_count * frames_dev
    positions = cotangent.shape[2]
    count = place.seq_count

    gain_rows = jnp.pad(
        jnp.concatenate([frame_prenorm, frame_postnorm, codec_prenorm, codec_postnorm])[None],
        ((0, 127), (0, 0)),
    )
    first = Gather([frame_project, gain_rows], spots)
    chain.leave(first.quarter)
    first.start(chain)
    first.send_near(chain)
    members = chain.enter(frame_expand, frame_contract, frame_output)
    second = Gather(members, spots)
    chain.leave(second.quarter)
    codes = codec_tokens.reshape(1, (positions - 1) * frame_total) + jnp.repeat(
        jnp.arange(positions - 1, dtype=jnp.int32) * CODES, frame_total
    )
    live = padding.reshape(frame_total).astype(F32)[:, None]
    every_segment = lax.all_to_all(
        jnp.broadcast_to(chain.enter(segments)[None], (count, row_count, frames_dev)),
        "seq",
        split_axis=0,
        concat_axis=0,
        tiled=True,
    )
    every_segment = jnp.transpose(every_segment, (1, 0, 2)).reshape(row_count, count * frames_dev)
    every_segment = chain.enter(every_segment)
    chain.leave(every_segment)
    first.spread(chain)
    second.start(chain)
    contract_in = (
        jnp.transpose(chain.enter(cotangent).reshape(frame_total, positions, width), (1, 0, 2))
        * live.astype(BF)[None]
    ).reshape(positions * frame_total, width)
    chain.leave(contract_in)
    first.join_near(chain)
    first.cross(chain)
    fourth = Gather(chain.enter(codec_expand, codec_contract, codec_output), spots)
    chain.leave(fourth.quarter)
    third = Gather(chain.enter(codec_project, codebooks), spots, True)
    chain.leave(third.pack)
    first.close(chain)
    second.spread(chain)
    first.send(chain)
    fourth.start(chain)
    third.start(chain)

    frame_project_all, gains = first.join(chain)
    gains = jnp.transpose(
        gains.reshape(place.mp_count, -1, 4, width // 4)[:, 0], (1, 0, 2)
    ).reshape(4, 1, width).astype(F32)
    hidden = frames.reshape(frame_total, width)
    normed, packed = frame_front(hidden, chain.enter(gains[0]), frame_project_all, row_count)
    packed, second.over_x, second.over_n, fourth.came = chain.enter(
        packed, second.over_x, second.over_n, fourth.came
    )
    chain.leave(packed)
    packed = lax.all_to_all(packed, "seq", split_axis=0, concat_axis=0, tiled=True)
    second.send_near(chain)
    third.send_near(chain)
    fourth.send_near(chain)
    second.join_near(chain)
    third.join_near(chain)
    fourth.join_near(chain)
    second.cross(chain)
    packed, *second.ends = chain.enter(packed, *second.ends)
    chain.leave(packed)
    second.close(chain)
    second.send(chain)
    fourth.spread(chain)
    contract_pair = Pair(contract_in)
    codes_pair = Pair(chain.enter(codes))
    packed = chain.enter(packed)
    attended = frame_attend_call(packed, every_segment)
    chain.leave(attended)
    attended, second.far.other = chain.enter(attended, second.far.other)
    chain.leave(attended)
    attended = lax.all_to_all(attended, "seq", split_axis=0, concat_axis=0, tiled=True)
    frame_expand_all, frame_contract_all, frame_output_all = second.join(chain)
    attended, fourth.over_x, fourth.over_n = chain.enter(attended, fourth.over_x, fourth.over_n)
    chain.leave(attended)
    fourth.cross(chain)
    frame_kept, mixed, slope, base = frame_rear(
        hidden,
        normed,
        chain.enter(attended),
        gains[1],
        frame_output_all,
        frame_expand_all,
        frame_contract_all,
    )
    chain.leave(base)

    base, third.came, *fourth.ends = chain.enter(base, third.came, *fourth.ends)
    chain.leave(base)
    third.spread(chain)
    fourth.close(chain)
    codec_project_all, table = third.join(chain)
    fourth.send(chain)
    frame_kept = Pair(chain.enter(frame_kept))
    entries = table[codes.reshape(positions - 1, frame_total)]
    codec_normed, codec_packed = codec_front(chain.enter(base), entries, gains[2], codec_project_all)
    chain.leave(codec_packed)
    codec_packed, contract_pair.other = chain.enter(codec_packed, contract_pair.other)
    codec_kept = codec_attend_call(codec_packed, codec_normed).reshape(
        positions * frame_total, 2 * width
    )
    chain.leave(codec_kept)
    codec_expand_all, codec_contract_all, codec_output_all = fourth.join(chain)
    codec_kept, frame_kept.other = chain.enter(codec_kept, frame_kept.other)
    chain.leave(codec_kept)
    (
        codec_mixed,
        codec_activated,
        codec_expand_kept,
        codec_output_in,
        mixed_grad,
        attended_grad,
        codec_postnorm_grad,
    ) = codec_rear(
        base,
        entries,
        chain.enter(codec_kept),
        contract_in,
        gains[3],
        codec_output_all,
        codec_expand_all,
        codec_contract_all,
    )
    chain.leave(codec_activated)

    inner = codec_activated.shape[1]
    activated_pair = chain.pair(codec_activated)
    codec_expand_kept = chain.pair(codec_expand_kept)
    projected_grad = codec_attend_grads_call(codec_packed, chain.enter(attended_grad)).reshape(
        positions * frame_total, 3 * width
    )
    chain.leave(projected_grad)
    base_grad, table_in, codec_prenorm_grad = codec_front_grads(
        chain.enter(projected_grad), base, entries, gains[2], mixed_grad, codec_project_all
    )
    chain.leave(base_grad)
    frame_grads_kept, frame_mixed_grad, grads, frame_postnorm_grad = frame_rear_grads(
        chain.enter(base_grad),
        slope,
        mixed,
        gains[1],
        frame_output_all,
        frame_expand_all,
        frame_contract_all,
        row_count,
    )
    chain.leave(grads)

    activated_pair.other, codec_expand_kept.other, grads, frame_grads_kept = chain.enter(
        activated_pair.other, codec_expand_kept.other, grads, frame_grads_kept
    )
    chain.leave(grads)
    grads = lax.all_to_all(grads, "seq", split_axis=0, concat_axis=0, tiled=True)
    frame_grads_kept = Pair(frame_grads_kept)
    contract_stages = tuple("ynxf")
    contract_blocks = grad_columns(
        (chain.enter(*activated_pair.both()), 0, inner),
        (contract_pair.both(), 0, width),
        order,
        contract_stages,
        4,
        0,
    )
    chain.leave(*contract_blocks)
    expand_stages = tuple("xnyf")
    arrays = chain.enter(*codec_expand_kept.both())
    expand_blocks = grad_rows((arrays, 0, width), (arrays, width, inner), order, expand_stages, 4, 0)
    chain.leave(*expand_blocks)

    grads, frame_grads_kept.other = chain.enter(grads, frame_grads_kept.other)
    chain.leave(grads)
    contract_sum = Reduce(contract_stages, chain.enter(*contract_blocks))
    expand_sum = Reduce(expand_stages, chain.enter(*expand_blocks))
    codec_kept = Pair(chain.enter(codec_kept))
    output_pair = Pair(chain.enter(codec_output_in))
    projected_pair = Pair(chain.enter(projected_grad))
    packed_grad = frame_attend_grads_call(packed, chain.enter(grads), every_segment)
    chain.leave(packed_grad)
    kept, arrays = frame_kept.both(), chain.enter(*frame_grads_kept.both())
    frame_contract_stages = tuple("yxnf")
    frame_contract_blocks = grad_columns(
        (kept, 3 * width, inner), (arrays, 0, width), order, frame_contract_stages, 4, 0
    )
    chain.leave(*frame_contract_blocks)
    frame_expand_stages = tuple("xnyf")
    arrays = chain.enter(*arrays)
    blocks = grad_rows(
        (kept, 2 * width, width), (arrays, width, inner), order, frame_expand_stages, 5, 0
    )
    frame_expand_blocks = grad_rows(
        (kept, width, width), (arrays, width + inner, width), order, frame_expand_stages, 5, 4, blocks
    )
    chain.leave(*frame_expand_blocks)

    packed_grad, codec_kept.other, projected_pair.other, output_pair.other = chain.enter(
        packed_grad, codec_kept.other, projected_pair.other, output_pair.other
    )
    chain.leave(packed_grad)
    contract_sum.arrive(chain)
    expand_sum.arrive(chain)
    packed_grad = lax.all_to_all(packed_grad, "seq", split_axis=0, concat_axis=0, tiled=True)
    take_both = together([contract_sum, expand_sum], chain, "n")
    frame_contract_sum = Reduce(frame_contract_stages, chain.enter(*frame_contract_blocks))
    frame_expand_sum = Reduce(frame_expand_stages, chain.enter(*frame_expand_blocks))
    table_pair = Pair(chain.enter(table_in))
    project_stages = tuple("ynxf")
    arrays = chain.enter(*codec_kept.both())
    blocks = grad_rows(
        (arrays, 0, width), (projected_pair.both(), 0, 3 * width), order, project_stages, 4, 0
    )
    project_blocks = grad_rows(
        (arrays, width, width), (output_pair.both(), 0, width), order, project_stages, 4, 3, blocks
    )
    chain.leave(*project_blocks)
    table_stages = tuple("xynf")
    table_blocks = grad_table(
        jnp.concatenate(codes_pair.both(), axis=1),
        chain.enter(*table_pair.both()),
        order,
        table_stages,
        codebooks.shape[0],
        2,
        0,
    )
    chain.leave(*table_blocks)
    project_sum = Reduce(project_stages, chain.enter(*project_blocks))
    table_sum = Reduce(table_stages, chain.enter(*table_blocks))
    packed_grad = chain.enter(packed_grad)
    chain.leave(packed_grad)
    frame_projected_grad, frames_grad, frame_prenorm_grad = frame_front_grads(
        chain.enter(packed_grad), hidden, gains[0], frame_mixed_grad, frame_project_all
    )
    chain.leave(frames_grad)
    frame_projected_pair = Pair(frame_projected_grad)
    gain_pair = Pair(
        jnp.concatenate(
            [frame_prenorm_grad, frame_postnorm_grad, codec_prenorm_grad, codec_postnorm_grad]
        )
    )
    frame_projected_pair.other, gain_pair.other = chain.enter(
        frame_projected_pair.other, gain_pair.other
    )
    chain.leave(gain_pair.other)
    blocks = grad_rows(
        (kept, 0, width),
        (chain.enter(*frame_projected_pair.both()), 0, 3 * width),
        order,
        table_stages,
        3,
        0,
    )
    chain.leave(*blocks)
    riders = gain_pair.own + gain_pair.other
    frame_project_sum = Reduce(table_stages, blocks, chain.enter(riders))
    frame_expand_sum.arrive(chain)
    frame_contract_sum.step(chain)
    frame_expand_sum.step(chain)
    output = codec_result(codec_mixed, chain.enter(codec_activated), live, codec_contract_all)
    chain.leave(output)
    output = jnp.transpose(output, (1, 0, 2)).reshape(row_count, frames_dev, positions, width)

    project_sum.step(chain)
    take_both()
    table_sum.step(chain)
    take_expand = together([expand_sum, frame_expand_sum], chain, "y")
    frame_project_sum.step(chain)
    frame_contract_sum.step(chain)
    project_sum.step(chain)
    contract_sum.step(chain)
    take_expand()
    take_second = finish([frame_contract_sum, frame_expand_sum], chain)
    table_sum.step(chain)
    frame_project_sum.step(chain)
    take_first = finish([contract_sum, expand_sum], chain)
    take_fourth = finish([project_sum, table_sum], chain)
    take_third = finish([frame_project_sum], chain)
    take_second()
    take_first()
    take_fourth()
    take_third()

    height = frame_project.shape[0]
    project_units = project_sum.result()
    frame_expand_units = frame_expand_sum.result()
    gain_sums = frame_project_sum.riders
    return (
        output,
        frames_grad.reshape(row_count, frames_dev, width),
        rows_from_units(table_sum.result(), codebooks.shape[0]),
        gain_sums[0],
        rows_from_units(frame_project_sum.result(), height),
        rows_from_units(frame_expand_units[4:], height),
        gain_sums[1],
        rows_from_units(frame_expand_units[:4], height),
        columns_from_units(frame_contract_sum.result()),
        gain_sums[2],
        rows_from_units(project_units[:3], height),
        rows_from_units(project_units[3:], height),
        gain_sums[3],
        rows_from_units(expand_sum.result(), height),
        columns_from_units(contract_sum.result()),
    )


def solution(mesh):
    placed = (
        P("mp", "seq", None),
        P("mp", "seq"),
        P("mp", "seq"),
        P(None, "mp", "seq"),
        P("mp", None),
        P("mp"),
        P("mp", None),
        P("mp", None),
        P("mp"),
        P("mp", None),
        P("mp", None),
        P("mp"),
        P("mp", None),
        P("mp", None),
        P("mp"),
        P("mp", None),
        P("mp", None),
        P("mp", "seq", None, None),
    )
    small = mesh.shape["seq"] == 8 and mesh.shape["mp"] == 4
    return jax.shard_map(
        shards if small else shards_general,
        mesh=mesh,
        in_specs=placed,
        out_specs=(
            P("mp", "seq", None, None),
            P("mp", "seq", None),
            P("mp", "seq"),
            P(),
            P("mp", "seq"),
            P("mp", "seq"),
            P(),
            P("mp", "seq"),
            P("mp", "seq"),
            P(),
            P("mp", "seq"),
            P("mp", "seq"),
            P(),
            P("mp", "seq"),
            P("mp", "seq"),
        ),
        check_vma=False,
    )
```
